32 devices in a mesh: batch: 4 (over y, x), seq: 8 (over z, core).
Axes of the slice: x: 2, y: 2, z: 4, core: 2. Of those that a mesh axis runs over, the one named last changes fastest.
Arguments:
- frames: bfloat16 [4, 2048, 768], P('batch', 'seq'), may hold values from -6 to 6
- cotangent: bfloat16 [4, 2048, 768], P('batch', 'seq'), may hold values from -6 to 6
- modulation: float32 [4, 3, 6, 768], P('batch'), may hold values from -3 to 3
- lengths: int32 [4, 3], P('batch'), may hold values from 1 to 1024, 2048 in all within a row
- text: bfloat16 [4, 3, 256, 1024], P('batch'), may hold values from -6 to 6
- text_len: int32 [4, 3], P('batch'), may hold values from 80 to 256
- w_qkv: bfloat16 [768, 2304], replicated, may hold values from -0.21875 to 0.21875
- w_o: bfloat16 [768, 768], replicated, may hold values from -2.5 to 2.5
- w_cq: bfloat16 [768, 768], replicated, may hold values from -0.21875 to 0.21875
- w_ckv: bfloat16 [1024, 1536], replicated, may hold values from -0.1875 to 0.1875
- w_co: bfloat16 [768, 768], replicated, may hold values from -1.25 to 1.25
- w_up: bfloat16 [768, 3072], replicated, may hold values from -0.21875 to 0.21875
- w_down: bfloat16 [3072, 768], replicated, may hold values from -0.109375 to 0.109375
Outputs:
- out: bfloat16 [4, 2048, 768], P('batch', 'seq')
- frames_grad: float32 [4, 2048, 768], P('batch', 'seq')
- modulation_grad: float32 [4, 3, 3, 768], P('batch', None, None, 'seq')
- modulation_mlp_grad: float32 [4, 3, 3, 768], P('batch', None, None, 'seq')
- text_grad: float32 [4, 3, 256, 1024], P('batch', None, 'seq')
- w_qkv_grad: float32 [768, 2304], P('seq', 'batch')
- w_o_grad: float32 [768, 768], P('seq', 'batch')
- w_cq_grad: float32 [768, 768], P('seq', 'batch')
- w_ckv_grad: float32 [1024, 1536], P('seq', 'batch')
- w_co_grad: float32 [768, 768], P('seq', 'batch')
- w_up_grad: float32 [768, 3072], P('seq', 'batch')
- w_down_grad: float32 [3072, 768], P('seq', 'batch')
The draws below stay inside these ranges and needn't reach their ends.
Inputs may be any that keep to these rules, and one draw needn't show every extreme that they name: The 3 lengths of a group sum to 2048, and the longest is exactly min(1024, 2048). text slots at or beyond text_len are padding.
All inputs are finite; a program needn't handle non-finite values.
Results may differ from the reference program's by a relative error of at most 0.025.
Values may be sent and summed in bfloat16 or wider, within the bound.
No kernel may reach another device: no remote copies, remote signals or barrier semaphores. Data moves between devices by JAX's collectives and lax.ppermute only.
A program may use at most 256 MiB of HBM per device.

```python
import math
import jax
import jax.numpy as jnp
import numpy as np
from jax import lax

D = 768
H = 12
HD = 64
FF = 3072
CT = 1024
TXT = 256
MAXLEN = 1024
GROUP = 2048
GROUPS = 4
ITEMS = 3


def touch_ends(entries, key, least, top_value):
    extent = entries.shape
    spot = [jax.random.randint(jax.random.fold_in(key, axis), (), 0, extent[axis]) for axis in range(len(extent))]
    entries = entries.at[tuple(spot)].set(least)
    longest = extent.index(max(extent))
    spot[longest] = (spot[longest] + 1) % extent[longest]
    return entries.at[tuple(spot)].set(top_value)


def level_of(rng, dims, shards, low, high):
    loudness, own = 1.0, jax.random.fold_in(rng, 6)
    for dim, blocks in shards:
        heights = jnp.exp(jax.random.uniform(jax.random.fold_in(own, dim), (blocks,), jnp.float32, low / len(shards), high / len(shards)))
        loudness = loudness * jnp.repeat(heights, dims[dim] // blocks).reshape([-1 if axis == dim else 1 for axis in range(len(dims))])
    return loudness


def split_up(amount, total, bound, lean):
    weights = [(1 << 20) // math.isqrt(rank ** lean) + 1 for rank in range(2, amount + 1)]
    rest, counts = total - bound - (amount - 1), [1] * (amount - 1)
    while rest > 0:
        candidates = [i for i in range(amount - 1) if counts[i] < bound]
        mass, budget = sum([weights[i] for i in candidates]), rest
        for i in candidates:
            extra = min(bound - counts[i], max(1, budget * weights[i] // mass), rest)
            counts[i] = counts[i] + extra
            rest = rest - extra
    return np.array([bound] + counts)


def uneven(stream_key, amount, total, bound, skew):
    if amount == 2:
        one = jax.random.randint(stream_key, (), max(1, total - bound), min(bound, total - 1) + 1)
        return jnp.stack([one, total - one])
    tallies = jnp.asarray(split_up(amount, total, bound, skew), jnp.int32)
    twos = (amount - 1) // 2
    giver, receiver = tallies[1:1 + 2 * twos:2], tallies[2:2 + 2 * twos:2]
    slack = jnp.minimum(giver - 1, bound - receiver)
    shifted = jax.random.randint(jax.random.fold_in(stream_key, 1), (twos,), 0, 1 << 20) % (slack + 1)
    tallies = tallies.at[1:1 + 2 * twos:2].set(giver - shifted).at[2:2 + 2 * twos:2].set(receiver + shifted)
    return tallies[jax.random.permutation(jax.random.fold_in(stream_key, 2), amount)]


def noise(rng, shape, spread, limit, cuts=(), kind=jnp.bfloat16):
    array = spread * jax.random.normal(rng, shape, jnp.float32)
    if cuts:
        array = array * level_of(rng, shape, cuts, -0.22, 0.18)
    return jnp.clip(array, -limit, limit).astype(kind)


def setup_inputs(seed: int = 0) -> dict:
    splits = jax.random.split(jax.random.key(seed), 14)
    return {
        "frames": noise(splits[0], (GROUPS, GROUP, D), 1.0, 6.0, ((0, 4), (1, 8))),
        "cotangent": noise(splits[1], (GROUPS, GROUP, D), 1.0, 6.0, ((0, 4), (1, 8))),
        "modulation": noise(splits[2], (GROUPS, ITEMS, 6, D), 0.5, 3.0, ((0, 4),), jnp.float32),
        "lengths": jax.vmap(lambda own: uneven(own, ITEMS, GROUP, min(MAXLEN, GROUP), 2))(jax.random.split(splits[3], GROUPS)).reshape((GROUPS, ITEMS)).astype(jnp.int32),
        "text": noise(splits[4], (GROUPS, ITEMS, TXT, CT), 1.0, 6.0, ((0, 4),)),
        "text_len": touch_ends(jax.random.randint(splits[5], (GROUPS, ITEMS), TXT * 5 // 16, TXT + 1), jax.random.fold_in(splits[5], 1), TXT * 5 // 16, TXT).astype(jnp.int32),
        "w_qkv": noise(splits[6], (D, 3 * D), D ** -0.5, 0.21875),
        "w_o": noise(splits[7], (D, D), (max(4, D // 128)) ** -0.5, 2.5),
        "w_cq": noise(splits[8], (D, D), D ** -0.5, 0.21875),
        "w_ckv": noise(splits[9], (CT, 2 * D), CT ** -0.5, 0.1875),
        "w_co": noise(splits[10], (D, D), (max(4, D // 32)) ** -0.5, 1.25),
        "w_up": noise(splits[11], (D, FF), D ** -0.5, 0.21875),
        "w_down": noise(splits[12], (FF, D), FF ** -0.5, 0.109375),
    }


@jax.custom_vjp
def low(v):
    return lax.optimization_barrier(v.astype(jnp.bfloat16)).astype(jnp.float32)

@jax.custom_vjp
def low_back(v):
    return v

def low_keep(v):
    return (low(v), None)

def low_pass(kept, grad):
    return (grad,)

def back_keep(v):
    return (v, None)

def back_low(kept, grad):
    return (low(grad),)
low.defvjp(low_keep, low_pass)
low_back.defvjp(back_keep, back_low)
highest = lax.Precision.HIGHEST
epsilon = 1e-06
negative = -1e+30

def matmul(left, right):
    return jnp.dot(left, right, precision=highest, preferred_element_type=jnp.float32)

def layer_norm(values):
    centred = values - lax.optimization_barrier(jnp.mean(values, axis=-1, keepdims=True))
    return centred * lax.rsqrt(lax.optimization_barrier(jnp.mean(centred * centred, axis=-1, keepdims=True)) + epsilon)

def item_ids(positions, ends):
    return lax.optimization_barrier(jnp.sum((positions[:, None] >= ends[None, :]).astype(jnp.int32), axis=1))

def block_forward(inputs, modulation, text, w_qkv, w_o, w_cq, w_ckv, w_co, w_up, w_down, segment, text_live):
    group = inputs.shape[0]
    scale = HD ** (-0.5)
    one_hot = (segment[:, None] == jnp.arange(ITEMS, dtype=jnp.int32)[None, :]).astype(jnp.float32)
    per_frame = matmul(one_hot, modulation.reshape(ITEMS, 6 * D)).reshape(group, 6, D)
    hidden_one = low(layer_norm(inputs) * (1.0 + per_frame[:, 1]) + per_frame[:, 0])
    projected = low(low_back(matmul(hidden_one, w_qkv)))
    queries = projected[:, :D].reshape(group, H, HD)
    keys = projected[:, D:2 * D].reshape(group, H, HD)
    values = projected[:, 2 * D:].reshape(group, H, HD)
    row_block = 512 if group % 512 == 0 else group
    blocks = group // row_block

    def self_block(pieces):
        query_rows, query_items = pieces
        scores = low_back(jnp.einsum('qhd,khd->qhk', query_rows, keys, precision=highest) * scale)
        allowed = (query_items[:, None] == segment[None, :])[:, None, :]
        probs = jax.nn.softmax(jnp.where(allowed, scores, negative), axis=-1)
        return jnp.einsum('qhk,khd->qhd', low(probs), values, precision=highest)
    attended = lax.map(jax.checkpoint(self_block), (queries.reshape(blocks, row_block, H, HD), segment.reshape(blocks, row_block)))
    attended = low(low_back(attended.reshape(group, D)))
    branch_one = low_back(matmul(attended, w_o))
    after_attn = inputs + per_frame[:, 2] * branch_one
    cross_in = low(layer_norm(after_attn))
    cross_queries = low(low_back(matmul(cross_in, w_cq))).reshape(group, H, HD)
    text_proj = low(low_back(matmul(text.reshape(ITEMS * TXT, CT), w_ckv)))
    text_keys = text_proj[:, :D].reshape(ITEMS * TXT, H, HD)
    text_values = text_proj[:, D:].reshape(ITEMS * TXT, H, HD)
    text_items = jnp.arange(ITEMS * TXT, dtype=jnp.int32) // TXT
    live_flat = text_live.reshape(ITEMS * TXT)

    def cross_block(pieces):
        query_rows, query_items = pieces
        scores = low_back(jnp.einsum('qhd,khd->qhk', query_rows, text_keys, precision=highest) * scale)
        allowed = ((query_items[:, None] == text_items[None, :]) & live_flat[None, :])[:, None, :]
        probs = jax.nn.softmax(jnp.where(allowed, scores, negative), axis=-1)
        return jnp.einsum('qhk,khd->qhd', low(probs), text_values, precision=highest)
    cross_out = lax.map(jax.checkpoint(cross_block), (cross_queries.reshape(blocks, row_block, H, HD), segment.reshape(blocks, row_block)))
    cross_out = low(low_back(cross_out.reshape(group, D)))
    after_cross = after_attn + low_back(matmul(cross_out, w_co))
    hidden_two = low(layer_norm(after_cross) * (1.0 + per_frame[:, 4]) + per_frame[:, 3])
    pre_act = low_back(matmul(hidden_two, w_up))
    activated = low(jax.nn.gelu(pre_act, approximate=True))
    branch_three = low_back(matmul(activated, w_down))
    return after_cross + per_frame[:, 5] * branch_three

def reference(frames, cotangent, modulation, lengths, text, text_len, w_qkv, w_o, w_cq, w_ckv, w_co, w_up, w_down):
    weights = (w_qkv.astype(jnp.float32), w_o.astype(jnp.float32), w_cq.astype(jnp.float32), w_ckv.astype(jnp.float32), w_co.astype(jnp.float32), w_up.astype(jnp.float32), w_down.astype(jnp.float32))

    def group_pass(totals, pieces):
        group_frames, group_cot, group_mod, group_len, group_text, group_tlen = pieces
        ends = jnp.cumsum(group_len).astype(jnp.int32)
        segment = item_ids(jnp.arange(GROUP, dtype=jnp.int32), ends)
        text_live = jnp.arange(TXT, dtype=jnp.int32)[None, :] < group_tlen[:, None]

        def forward(inputs, mod_in, text_in, wa, wb, wc, wd, we, wf, wg):
            return block_forward(inputs, mod_in, text_in, wa, wb, wc, wd, we, wf, wg, segment, text_live)
        result, pullback = jax.vjp(forward, group_frames.astype(jnp.float32), group_mod, group_text.astype(jnp.float32), weights[0], weights[1], weights[2], weights[3], weights[4], weights[5], weights[6])
        grads = pullback(group_cot.astype(jnp.float32))
        new_totals = tuple((total + grad for total, grad in zip(totals, grads[3:])))
        return (new_totals, (result.astype(jnp.bfloat16), grads[0], grads[1][:, :3], grads[1][:, 3:], grads[2]))
    start_totals = tuple((jnp.zeros(weight.shape, jnp.float32) for weight in weights))
    totals, stacked = lax.scan(group_pass, start_totals, (frames, cotangent, modulation, lengths, text, text_len))
    return (stacked[0], stacked[1], stacked[2], stacked[3], stacked[4], totals[0], totals[1], totals[2], totals[3], totals[4], totals[5], totals[6])
```

```python
from functools import partial

import jax
import jax.numpy as jnp
from jax import lax
from jax.experimental import pallas as pl
from jax.experimental.pallas import tpu as pltpu
from jax.sharding import PartitionSpec as P

H = 12
LONGEST = 1024

epsilon = 1e-06
far = -1e30
LSE_LANE = 8
DELTA_LANE = 44
MIB = 1 << 20


def layer_norm(values):
    centred = values - jnp.mean(values, axis=-1, keepdims=True)
    inverse = lax.rsqrt(jnp.mean(centred * centred, axis=-1, keepdims=True) + epsilon)
    return (centred * inverse, inverse)


def norm_back(grad_normed, normed, inverse):
    return inverse * (
        grad_normed
        - jnp.mean(grad_normed, axis=-1, keepdims=True)
        - normed * jnp.mean(grad_normed * normed, axis=-1, keepdims=True)
    )


def contract_rows(left, right):
    return lax.dot_general(
        left, right, (((0,), (0,)), ((), ())), preferred_element_type=jnp.float32
    )


def times_transposed(left, right):
    return lax.dot_general(
        left, right, (((1,), (1,)), ((), ())), preferred_element_type=jnp.float32
    )


class Frame:
    def __init__(self, meta, items, count, shards):
        self.position = meta[0]
        self.items = items
        self.count = count
        self.shards = shards
        self.ends = []
        total = jnp.int32(0)
        for item in range(items):
            total = total + meta[1 + item]
            self.ends.append(total)
        self.text_len = [meta[1 + items + item] for item in range(items)]
        self.first = self.item_of(self.position * count)
        self.last = self.item_of(self.position * count + count - 1)
        self.low = jnp.int32(0)
        self.high = jnp.int32(0)
        for item in range(items):
            start = self.ends[item] - meta[1 + item]
            self.low = jnp.where(self.first == item, start, self.low)
            self.high = jnp.where(self.last == item, self.ends[item], self.high)

    def item_of(self, place):
        found = jnp.int32(0)
        for end in self.ends:
            found = found + (place >= end).astype(jnp.int32)
        return found

    def items_of_rows(self, base, rows):
        place = base + lax.broadcasted_iota(jnp.int32, (rows, 1), 0)
        found = jnp.zeros((rows, 1), jnp.int32)
        for end in self.ends:
            found = found + (place >= end).astype(jnp.int32)
        return found

    def base(self, block):
        pair = block // 2
        hop = (pair + 1) // 2
        step = jnp.where(pair % 2 == 1, -hop, hop)
        chip = self.position // 2 + step
        device = chip * 2 + (self.position % 2 + block % 2) % 2
        start = device * self.count
        live = (chip >= 0) & (chip < self.shards // 2)
        return start, live & (start < self.high) & (start + self.count > self.low)


def lanes(rows):
    return lax.broadcasted_iota(jnp.int32, (rows, 128), 1)


def minus_ones(rows, base, head):
    lane = lanes(rows)
    start = base + 3 * head
    return jnp.where((lane >= start) & (lane < start + 3), -1.0, 0.0)


def keep_head(values, half):
    lane = lanes(values.shape[0])
    return jnp.where((lane // 64) == half, values.astype(jnp.float32), 0.0)


def beside(left, right):
    return jnp.concatenate([left.astype(jnp.bfloat16), right.astype(jnp.bfloat16)], axis=1)


def pieces(values):
    high = values.astype(jnp.bfloat16).astype(jnp.float32)
    rest = values - high
    middle = rest.astype(jnp.bfloat16).astype(jnp.float32)
    return high, middle, rest - middle


def dot(left, right):
    return jnp.dot(left, right, preferred_element_type=jnp.float32)


def window_bias(frame, block):
    base, _ = frame.base(block)
    item = frame.items_of_rows(base, frame.count)
    lane = lanes(frame.count)
    return jnp.where((lane != item) & (lane < frame.items), far, 0.0)


def text_bias(frame, block, rows):
    slot = lax.broadcasted_iota(jnp.int32, (rows, 1), 0)
    length = jnp.int32(0)
    for item in range(frame.items):
        length = jnp.where(block == item, frame.text_len[item], length)
    lane = lanes(rows)
    dead = (lane != block) | (slot >= length)
    return jnp.where(dead & (lane < frame.items), far, 0.0)


def block_rule(frame, kind, rows):
    if kind == "frames":
        return (
            lambda block: frame.base(block)[1],
            lambda block: window_bias(frame, block),
        )
    return (
        lambda block: (block >= frame.first) & (block <= frame.last),
        lambda block: text_bias(frame, block, rows),
    )


def project_kernel(items, shards, blocks, columns, meta, mod_ref, w_ref, *refs):
    x_refs, out_ref = refs[:-1], refs[-1]
    count = x_refs[0].shape[0]
    frame = Frame(meta, items, count, shards)
    for number, block in enumerate(blocks):
        base, live = frame.base(jnp.int32(block))

        @pl.when(live)
        def _(number=number, base=base):
            normed, _ = layer_norm(x_refs[number][...].astype(jnp.float32))
            item = frame.items_of_rows(base, count)
            shift = jnp.zeros_like(normed)
            scale = jnp.zeros_like(normed)
            for i in range(items):
                shift = jnp.where(item == i, mod_ref[i, 0:1, :], shift)
                scale = jnp.where(item == i, mod_ref[i, 1:2, :], scale)
            hidden = (normed * (1.0 + scale) + shift).astype(jnp.bfloat16)
            for c in range(columns):
                part = w_ref[:, c * 768 : (c + 1) * 768]
                out_ref[number * count : (number + 1) * count, c * 768 : (c + 1) * 768] = dot(
                    hidden, part
                ).astype(jnp.bfloat16)


def project(meta, modulation, weight, x_blocks, blocks, items, shards, name):
    count, width = x_blocks[0].shape
    columns = weight.shape[1] // width
    return pl.pallas_call(
        partial(project_kernel, items, shards, blocks, columns),
        out_shape=jax.ShapeDtypeStruct((len(blocks) * count, weight.shape[1]), jnp.bfloat16),
        in_specs=[pl.BlockSpec(memory_space=pltpu.SMEM)]
        + [pl.BlockSpec(memory_space=pltpu.VMEM)] * (2 + len(blocks)),
        out_specs=pl.BlockSpec(memory_space=pltpu.VMEM),
        compiler_params=pltpu.CompilerParams(vmem_limit_bytes=40 * MIB),
        cost_estimate=pl.CostEstimate(
            flops=len(blocks) * count * width * weight.shape[1],
            bytes_accessed=2 * len(blocks) * count * (width + weight.shape[1]),
            transcendentals=0,
        ),
        name=name,
    )(meta, modulation, weight, *x_blocks)


def attend_kernel(items, shards, kind, blocks, meta, q_ref, k_ref, v_ref, o_ref, low_ref, f_ref, qa, s, m, l, acc):
    count = q_ref.shape[0]
    rows = k_ref.shape[0] // blocks
    frame = Frame(meta, items, count, shards)
    active, bias = block_rule(frame, kind, rows)
    pair = pl.program_id(0)
    lane = lanes(count)
    own = frame.items_of_rows(frame.position * count, count)
    q = q_ref[...]
    for h in range(2):
        qa[h] = beside(keep_head(q, h) * 0.125, (lane == own).astype(jnp.float32))
        m[h] = jnp.full((count, 128), far, jnp.float32)
        l[h] = jnp.zeros((count, 128), jnp.float32)
        acc[h] = jnp.zeros((count, 128), jnp.float32)

    @pl.loop(0, blocks)
    def _(block):
        @pl.when(active(block))
        def _():
            keys = beside(k_ref[pl.ds(pl.multiple_of(block * rows, rows), rows), :], bias(block))
            for h in range(2):
                scores = times_transposed(qa[h], keys)
                s[h, block] = scores
                m[h] = jnp.maximum(m[h], jnp.maximum(scores[:, :128], scores[:, 128:]))

    top = [jnp.max(m[h], axis=1, keepdims=True) for h in range(2)]

    @pl.loop(0, blocks)
    def _(block):
        @pl.when(active(block))
        def _():
            values = v_ref[pl.ds(pl.multiple_of(block * rows, rows), rows), :]
            for h in range(2):
                probs = jnp.exp(s[h, block] - top[h])
                l[h] = l[h] + (probs[:, :128] + probs[:, 128:])
                acc[h] = acc[h] + dot(probs.astype(jnp.bfloat16), values)

    out = []
    features = jnp.where(pair == 0, (lane == own).astype(jnp.float32), f_ref[...].astype(jnp.float32))
    for h in range(2):
        total = jnp.sum(l[h], axis=1, keepdims=True)
        out.append(acc[h] / total)
        start = LSE_LANE + 3 * (2 * pair + h)
        for number, piece in enumerate(pieces(top[h] + jnp.log(total))):
            features = jnp.where(lane == start + number, piece, features)
    result = jnp.where(lane < 64, out[0], out[1])
    o_ref[...] = result
    low_ref[...] = result.astype(jnp.bfloat16)
    f_ref[...] = features.astype(jnp.bfloat16)


def attend(meta, queries, kv, kind, blocks, items, shards, name):
    count, width = queries.shape
    pairs = width // 128
    total = kv.shape[0]
    rows = total // blocks
    column = lambda offset: (lambda p: (0, p + offset))
    tile = pl.BlockSpec((count, 128), column(0))
    return pl.pallas_call(
        partial(attend_kernel, items, shards, kind, blocks),
        grid=(pairs,),
        out_shape=(
            jax.ShapeDtypeStruct((count, width), jnp.float32),
            jax.ShapeDtypeStruct((count, width), jnp.bfloat16),
            jax.ShapeDtypeStruct((count, 128), jnp.bfloat16),
        ),
        in_specs=[
            pl.BlockSpec(memory_space=pltpu.SMEM),
            tile,
            pl.BlockSpec((total, 128), column(0)),
            pl.BlockSpec((total, 128), column(pairs)),
        ],
        out_specs=(tile, tile, pl.BlockSpec((count, 128), lambda p: (0, 0))),
        scratch_shapes=[
            pltpu.VMEM((2, count, 256), jnp.bfloat16),
            pltpu.VMEM((2, blocks, count, rows), jnp.float32),
            pltpu.VMEM((2, count, 128), jnp.float32),
            pltpu.VMEM((2, count, 128), jnp.float32),
            pltpu.VMEM((2, count, 128), jnp.float32),
        ],
        compiler_params=pltpu.CompilerParams(vmem_limit_bytes=40 * MIB),
        cost_estimate=pl.CostEstimate(
            flops=2 * count * total * width,
            bytes_accessed=4 * total * width,
            transcendentals=count * total * H // 2,
        ),
        name=name,
    )(meta, queries, kv, kv)


def query_grad_kernel(items, shards, kind, blocks, meta, q_ref, do_ref, f_ref, k_ref, v_ref, dq_ref, qa, da, acc):
    count = q_ref.shape[0]
    rows = k_ref.shape[0] // blocks
    frame = Frame(meta, items, count, shards)
    active, bias = block_rule(frame, kind, rows)
    pair = pl.program_id(0)
    features = f_ref[...]
    for h in range(2):
        qa[h] = beside(keep_head(q_ref[...], h) * 0.125, features)
        da[h] = beside(keep_head(do_ref[...], h), features)
        acc[h] = jnp.zeros((count, 128), jnp.float32)

    @pl.loop(0, blocks)
    def _(block):
        @pl.when(active(block))
        def _():
            here = pl.ds(pl.multiple_of(block * rows, rows), rows)
            keys, values, mask = k_ref[here, :], v_ref[here, :], bias(block)
            for h in range(2):
                head = 2 * pair + h
                probs = jnp.exp(
                    times_transposed(qa[h], beside(keys, mask + minus_ones(rows, LSE_LANE, head)))
                )
                slope = times_transposed(da[h], beside(values, minus_ones(rows, DELTA_LANE, head)))
                acc[h] = acc[h] + dot((probs * slope).astype(jnp.bfloat16), keys)

    dq_ref[...] = (jnp.where(lanes(count) < 64, acc[0], acc[1]) * 0.125).astype(jnp.bfloat16)


def query_grad(meta, queries, grad_out, features, kv, kind, blocks, items, shards, name):
    count, width = queries.shape
    pairs = width // 128
    total = kv.shape[0]
    column = lambda offset: (lambda p: (0, p + offset))
    tile = pl.BlockSpec((count, 128), column(0))
    return pl.pallas_call(
        partial(query_grad_kernel, items, shards, kind, blocks),
        grid=(pairs,),
        out_shape=jax.ShapeDtypeStruct((count, width), jnp.bfloat16),
        in_specs=[
            pl.BlockSpec(memory_space=pltpu.SMEM),
            tile,
            tile,
            pl.BlockSpec((count, 128), lambda p: (0, 0)),
            pl.BlockSpec((total, 128), column(0)),
            pl.BlockSpec((total, 128), column(pairs)),
        ],
        out_specs=tile,
        scratch_shapes=[
            pltpu.VMEM((2, count, 256), jnp.bfloat16),
            pltpu.VMEM((2, count, 256), jnp.bfloat16),
            pltpu.VMEM((2, count, 128), jnp.float32),
        ],
        compiler_params=pltpu.CompilerParams(vmem_limit_bytes=40 * MIB),
        cost_estimate=pl.CostEstimate(
            flops=3 * count * total * width,
            bytes_accessed=4 * total * width,
            transcendentals=count * total * H // 2,
        ),
        name=name,
    )(meta, queries, grad_out, features, kv, kv)


def key_grad_tile(frame, pair, k, v, mask, visit, dk_acc, dv_acc, ka, va):
    rows = k.shape[0]
    for h in range(2):
        head = 2 * pair + h
        ka[h] = beside(keep_head(k, h), mask + minus_ones(rows, LSE_LANE, head))
        va[h] = beside(keep_head(v, h), minus_ones(rows, DELTA_LANE, head))
        dk_acc[h] = jnp.zeros((rows, 128), jnp.float32)
        dv_acc[h] = jnp.zeros((rows, 128), jnp.float32)

    def step(q, do, features):
        q = (q.astype(jnp.float32) * 0.125).astype(jnp.bfloat16)
        q_wide = beside(q, features)
        do_wide = beside(do, features)
        for h in range(2):
            probs = jnp.exp(times_transposed(ka[h], q_wide))
            slope = times_transposed(va[h], do_wide)
            dv_acc[h] = dv_acc[h] + dot(probs.astype(jnp.bfloat16), do)
            dk_acc[h] = dk_acc[h] + dot((probs * slope).astype(jnp.bfloat16), q)

    visit(step)
    lane = lanes(rows)
    return (
        jnp.where(lane < 64, dk_acc[0], dk_acc[1]),
        jnp.where(lane < 64, dv_acc[0], dv_acc[1]),
    )


def frame_key_grad_kernel(items, shards, blocks, meta, q_ref, do_ref, f_ref, k_ref, v_ref, dk_ref, dv_ref, ka, va, dka, dva):
    count = k_ref.shape[0]
    frame = Frame(meta, items, count, shards)

    def visit(step):
        @pl.loop(0, blocks)
        def _(block):
            @pl.when(frame.base(block)[1])
            def _():
                here = pl.ds(pl.multiple_of(block * count, count), count)
                step(q_ref[here, :], do_ref[here, :], f_ref[here, :])

    dk, dv = key_grad_tile(
        frame, pl.program_id(0), k_ref[...], v_ref[...], window_bias(frame, jnp.int32(0)), visit, dka, dva, ka, va
    )
    dk_ref[...] = dk.astype(jnp.bfloat16)
    dv_ref[...] = dv.astype(jnp.bfloat16)


def key_scratch(rows):
    return [
        pltpu.VMEM((2, rows, 256), jnp.bfloat16),
        pltpu.VMEM((2, rows, 256), jnp.bfloat16),
        pltpu.VMEM((2, rows, 128), jnp.float32),
        pltpu.VMEM((2, rows, 128), jnp.float32),
    ]


def frame_key_grad(meta, q_window, do_window, kv, count, blocks, items, shards, name):
    total, width = q_window.shape
    pairs = width // 128
    column = lambda offset: (lambda p: (0, p + offset))
    tile = pl.BlockSpec((count, 128), column(0))
    wide = pl.BlockSpec((total, 128), column(0))
    return pl.pallas_call(
        partial(frame_key_grad_kernel, items, shards, blocks),
        grid=(pairs,),
        out_shape=(jax.ShapeDtypeStruct((count, width), jnp.bfloat16),) * 2,
        in_specs=[
            pl.BlockSpec(memory_space=pltpu.SMEM),
            wide,
            wide,
            pl.BlockSpec((total, 128), lambda p: (0, pairs)),
            tile,
            pl.BlockSpec((count, 128), column(pairs)),
        ],
        out_specs=(tile, tile),
        scratch_shapes=key_scratch(count),
        compiler_params=pltpu.CompilerParams(vmem_limit_bytes=40 * MIB),
        cost_estimate=pl.CostEstimate(
            flops=4 * count * total * width,
            bytes_accessed=4 * total * width,
            transcendentals=count * total * H // 2,
        ),
        name=name,
    )(meta, q_window, do_window, do_window, kv, kv)


def text_key_grad_kernel(items, shards, meta, q_ref, do_ref, f_ref, k_ref, v_ref, dk_ref, dv_ref, ka, va, dka, dva):
    count = q_ref.shape[0]
    rows = k_ref.shape[0] // items
    frame = Frame(meta, items, count, shards)
    for item in range(items):
        here = slice(item * rows, (item + 1) * rows)
        live = (item >= frame.first) & (item <= frame.last)

        @pl.when(live)
        def _(item=item, here=here):
            dk, dv = key_grad_tile(
                frame,
                pl.program_id(0),
                k_ref[here, :],
                v_ref[here, :],
                text_bias(frame, jnp.int32(item), rows),
                lambda step: step(q_ref[...], do_ref[...], f_ref[...]),
                dka,
                dva,
                ka,
                va,
            )
            dk_ref[here, :] = dk.astype(jnp.bfloat16)
            dv_ref[here, :] = dv.astype(jnp.bfloat16)

        @pl.when(jnp.logical_not(live))
        def _(here=here):
            dk_ref[here, :] = jnp.zeros((rows, 128), jnp.bfloat16)
            dv_ref[here, :] = jnp.zeros((rows, 128), jnp.bfloat16)


def text_key_grad(meta, queries, grad_out, features, kv, items, shards, name):
    count, width = queries.shape
    pairs = width // 128
    total = kv.shape[0]
    column = lambda offset: (lambda p: (0, p + offset))
    tile = pl.BlockSpec((count, 128), column(0))
    wide = pl.BlockSpec((total, 128), column(0))
    return pl.pallas_call(
        partial(text_key_grad_kernel, items, shards),
        grid=(pairs,),
        out_shape=(jax.ShapeDtypeStruct((total, width), jnp.bfloat16),) * 2,
        in_specs=[
            pl.BlockSpec(memory_space=pltpu.SMEM),
            tile,
            tile,
            pl.BlockSpec((count, 128), lambda p: (0, 0)),
            wide,
            pl.BlockSpec((total, 128), column(pairs)),
        ],
        out_specs=(wide, wide),
        scratch_shapes=key_scratch(total // items),
        compiler_params=pltpu.CompilerParams(vmem_limit_bytes=40 * MIB),
        cost_estimate=pl.CostEstimate(
            flops=4 * count * total * width,
            bytes_accessed=8 * total * width,
            transcendentals=count * total * H // 2,
        ),
        name=name,
    )(meta, queries, grad_out, features, kv, kv)


def with_deltas(features, grad_out, attn_exact):
    width = attn_exact.shape[1]
    lane = jnp.arange(128)[None, :]
    head = (jnp.arange(width) // (width // H))[:, None]
    pick = ((lane >= DELTA_LANE) & ((lane - DELTA_LANE) // 3 == head)).astype(jnp.float32)
    delta = jnp.dot(
        grad_out.astype(jnp.float32) * attn_exact,
        pick,
        precision=lax.Precision.HIGHEST,
        preferred_element_type=jnp.float32,
    )
    high = lax.reduce_precision(delta, 8, 7)
    middle = lax.reduce_precision(delta - high, 8, 7)
    which = (lane - DELTA_LANE) % 3
    piece = jnp.where(which == 0, high, jnp.where(which == 1, middle, delta - high - middle))
    inside = (lane >= DELTA_LANE) & (lane < DELTA_LANE + 3 * H)
    return jnp.where(inside, piece.astype(jnp.bfloat16), features)


def gather_window(own, reach, shards):
    swap = [(i, i ^ 1) for i in range(shards)]
    up = [(i, i + 2) for i in range(shards - 2)]
    down = [(i + 2, i) for i in range(shards - 2)]
    blocks = [own, lax.ppermute(own, "seq", swap)]
    below, above = own, own
    for _ in range(reach):
        below = lax.ppermute(below, "seq", up)
        above = lax.ppermute(above, "seq", down)
        blocks += [below, lax.ppermute(below, "seq", swap)]
        blocks += [above, lax.ppermute(above, "seq", swap)]
    return blocks


def body(
    frames,
    cotangent,
    modulation,
    lengths,
    text,
    text_len,
    w_qkv,
    w_o,
    w_cq,
    w_ckv,
    w_co,
    w_up,
    w_down,
):
    local = frames[0]
    count, width = local.shape
    items = lengths.shape[1]
    text_rows, text_width = text.shape[2:]
    shards = lax.axis_size("seq")
    position = lax.axis_index("seq")
    reach = min(-(-(LONGEST - 1) // (2 * count)), shards // 2 - 1)
    blocks = 2 + 4 * reach
    meta = jnp.concatenate([position[None].astype(jnp.int32), lengths[0], text_len[0]])
    item_range = jnp.arange(items, dtype=jnp.int32)
    ends = jnp.sum(jnp.where(item_range[None, :] <= item_range[:, None], lengths[0][None, :], 0), axis=1)
    place = position * count + jnp.arange(count, dtype=jnp.int32)
    query_items = jnp.sum((place[:, None] >= ends[None, :]).astype(jnp.int32), axis=1)[:, None]
    one_hot = (query_items == item_range[None, :]).astype(jnp.float32)
    mod = modulation[0]

    def per_frame(which):
        found = jnp.broadcast_to(mod[0, which][None, :], (count, width))
        for item in range(1, items):
            found = jnp.where(query_items == item, mod[item, which][None, :], found)
        return found

    window = gather_window(local, reach, shards)
    inputs = local.astype(jnp.float32)
    normed_one, inverse_one = layer_norm(inputs)
    hidden_one = (normed_one * (1.0 + per_frame(1)) + per_frame(0)).astype(jnp.bfloat16)
    queries = jnp.dot(hidden_one, w_qkv[:, :width], preferred_element_type=jnp.float32).astype(jnp.bfloat16)
    text_proj = jnp.dot(
        text[0].reshape(items * text_rows, text_width), w_ckv, preferred_element_type=jnp.float32
    ).astype(jnp.bfloat16)
    kv = project(meta, mod, w_qkv[:, width:], window, tuple(range(blocks)), items, shards, "project_keys")
    attn_exact, attended, features = attend(meta, queries, kv, "frames", blocks, items, shards, "self_attend")
    branch_one = jnp.dot(attended, w_o, preferred_element_type=jnp.float32)
    after_attn = inputs + per_frame(2) * branch_one
    normed_cross, inverse_cross = layer_norm(after_attn)
    cross_in = normed_cross.astype(jnp.bfloat16)
    cross_queries = jnp.dot(cross_in, w_cq, preferred_element_type=jnp.float32).astype(jnp.bfloat16)
    cross_exact, cross_out, cross_features = attend(
        meta, cross_queries, text_proj, "text", items, items, shards, "cross_attend"
    )
    branch_two = jnp.dot(cross_out, w_co, preferred_element_type=jnp.float32)
    after_cross = after_attn + branch_two
    normed_two, inverse_two = layer_norm(after_cross)
    hidden_two = (normed_two * (1.0 + per_frame(4)) + per_frame(3)).astype(jnp.bfloat16)
    pre_act = jnp.dot(hidden_two, w_up, preferred_element_type=jnp.float32)
    activated, gelu_back = jax.vjp(partial(jax.nn.gelu, approximate=True), pre_act)
    activated_low = activated.astype(jnp.bfloat16)
    branch_three = jnp.dot(activated_low, w_down, preferred_element_type=jnp.float32)
    gate_two = per_frame(5)
    result = after_cross + gate_two * branch_three
    grad_out = cotangent[0].astype(jnp.float32)
    grad_branch_three = (grad_out * gate_two).astype(jnp.bfloat16)
    grad_w_down = contract_rows(activated_low, grad_branch_three)
    grad_pre = gelu_back(times_transposed(grad_branch_three, w_down))[0].astype(jnp.bfloat16)
    grad_w_up = contract_rows(hidden_two, grad_pre)
    grad_hidden_two = times_transposed(grad_pre, w_up)
    grad_cross = grad_out + norm_back(grad_hidden_two * (1.0 + per_frame(4)), normed_two, inverse_two)
    grad_branch_two = grad_cross.astype(jnp.bfloat16)
    grad_w_co = contract_rows(cross_out, grad_branch_two)
    grad_cross_out = times_transposed(grad_branch_two, w_co).astype(jnp.bfloat16)
    cross_features = with_deltas(cross_features, grad_cross_out, cross_exact)
    grad_cross_queries = query_grad(
        meta, cross_queries, grad_cross_out, cross_features, text_proj, "text", items, items, shards, "cross_query_grad"
    )
    grad_text_keys, grad_text_values = text_key_grad(
        meta, cross_queries, grad_cross_out, cross_features, text_proj, items, shards, "cross_key_grad"
    )
    grad_w_cq = contract_rows(cross_in, grad_cross_queries)
    grad_attn_res = grad_cross + norm_back(
        times_transposed(grad_cross_queries, w_cq), normed_cross, inverse_cross
    )
    grad_branch_one = (grad_attn_res * per_frame(2)).astype(jnp.bfloat16)
    grad_w_o = contract_rows(attended, grad_branch_one)
    grad_attended = times_transposed(grad_branch_one, w_o).astype(jnp.bfloat16)
    features = with_deltas(features, grad_attended, attn_exact)
    grad_queries = query_grad(
        meta, queries, grad_attended, features, kv, "frames", blocks, items, shards, "self_query_grad"
    )
    do_window = jnp.concatenate(
        gather_window(jnp.concatenate([grad_attended, features], axis=1), reach, shards), axis=0
    )
    q_window = project(meta, mod, w_qkv[:, :width], window, tuple(range(blocks)), items, shards, "project_queries")
    grad_keys, grad_values = frame_key_grad(
        meta, q_window, do_window, kv, count, blocks, items, shards, "self_key_grad"
    )
    grad_projected = jnp.concatenate([grad_queries, grad_keys, grad_values], axis=1)
    grad_w_qkv = contract_rows(hidden_one, grad_projected)
    grad_hidden_one = times_transposed(grad_projected, w_qkv)
    grad_inputs = grad_attn_res + norm_back(
        grad_hidden_one * (1.0 + per_frame(1)), normed_one, inverse_one
    )

    def item_sum(values):
        return lax.dot_general(
            one_hot,
            values,
            (((0,), (0,)), ((), ())),
            precision=lax.Precision.HIGHEST,
            preferred_element_type=jnp.float32,
        )

    item_terms = jnp.stack(
        [
            item_sum(grad_hidden_one),
            item_sum(grad_hidden_one * normed_one),
            item_sum(grad_attn_res * branch_one),
            item_sum(grad_hidden_two),
            item_sum(grad_hidden_two * normed_two),
            item_sum(grad_out * branch_three),
        ],
        axis=1,
    )[None]
    text_terms = jnp.concatenate([grad_text_keys, grad_text_values], axis=1)
    share_rows = text_rows // shards
    text_terms = text_terms.reshape(items, shards, share_rows, 2 * width).transpose(1, 0, 2, 3)
    text_grad_low = lax.psum_scatter(
        text_terms.reshape(shards * items * share_rows, 2 * width), "seq", scatter_dimension=0, tiled=True
    )
    item_share = lax.psum_scatter(item_terms, "seq", scatter_dimension=3, tiled=True)
    text_mine = lax.dynamic_slice_in_dim(text[0], position * share_rows, share_rows, 1).reshape(
        items * share_rows, text_width
    )
    grad_text = times_transposed(text_grad_low, w_ckv).reshape(1, items, share_rows, text_width)
    grad_w_ckv = contract_rows(text_mine, text_grad_low)

    def reduce_weight(grad):
        part = lax.psum_scatter(grad.astype(jnp.bfloat16), "seq", scatter_dimension=0, tiled=True)
        return lax.psum_scatter(part, "batch", scatter_dimension=1, tiled=True).astype(jnp.float32)

    return (
        result.astype(jnp.bfloat16)[None],
        grad_inputs[None],
        item_share[:, :, :3],
        item_share[:, :, 3:],
        grad_text,
        reduce_weight(grad_w_qkv),
        reduce_weight(grad_w_o),
        reduce_weight(grad_w_cq),
        reduce_weight(grad_w_ckv),
        reduce_weight(grad_w_co),
        reduce_weight(grad_w_up),
        reduce_weight(grad_w_down),
    )


def solution(mesh):
    in_specs = (
        P("batch", "seq", None),
        P("batch", "seq", None),
        P("batch", None, None, None),
        P("batch", None),
        P("batch", None, None, None),
        P("batch", None),
        P(),
        P(),
        P(),
        P(),
        P(),
        P(),
        P(),
    )
    out_specs = (
        P("batch", "seq", None),
        P("batch", "seq", None),
        P("batch", None, None, "seq"),
        P("batch", None, None, "seq"),
        P("batch", None, "seq", None),
        P("seq", "batch"),
        P("seq", "batch"),
        P("seq", "batch"),
        P("seq", "batch"),
        P("seq", "batch"),
        P("seq", "batch"),
        P("seq", "batch"),
    )
    return jax.shard_map(body, mesh=mesh, in_specs=in_specs, out_specs=out_specs, check_vma=False)
```

```python
from functools import partial

import jax
import jax.numpy as jnp
from jax import lax
from jax.experimental import pallas as pl
from jax.experimental.pallas import tpu as pltpu
from jax.sharding import PartitionSpec as P

H = 12
LONGEST = 1024

epsilon = 1e-06
far = -1e30
LSE_LANE = 8
DELTA_LANE = 44
MIB = 1 << 20


def layer_norm(values):
    centred = values - jnp.mean(values, axis=-1, keepdims=True)
    inverse = lax.rsqrt(jnp.mean(centred * centred, axis=-1, keepdims=True) + epsilon)
    return (centred * inverse, inverse)


def norm_back(grad_normed, normed, inverse):
    return inverse * (
        grad_normed
        - jnp.mean(grad_normed, axis=-1, keepdims=True)
        - normed * jnp.mean(grad_normed * normed, axis=-1, keepdims=True)
    )


def contract_rows(left, right):
    return lax.dot_general(
        left, right, (((0,), (0,)), ((), ())), preferred_element_type=jnp.float32
    )


def times_transposed(left, right):
    return lax.dot_general(
        left, right, (((1,), (1,)), ((), ())), preferred_element_type=jnp.float32
    )


class Frame:
    def __init__(self, meta, items, count, shards):
        self.position = meta[0]
        self.items = items
        self.count = count
        self.shards = shards
        self.ends = []
        total = jnp.int32(0)
        for item in range(items):
            total = total + meta[1 + item]
            self.ends.append(total)
        self.text_len = [meta[1 + items + item] for item in range(items)]
        self.first = self.item_of(self.position * count)
        self.last = self.item_of(self.position * count + count - 1)
        self.low = jnp.int32(0)
        self.high = jnp.int32(0)
        for item in range(items):
            start = self.ends[item] - meta[1 + item]
            self.low = jnp.where(self.first == item, start, self.low)
            self.high = jnp.where(self.last == item, self.ends[item], self.high)

    def item_of(self, place):
        found = jnp.int32(0)
        for end in self.ends:
            found = found + (place >= end).astype(jnp.int32)
        return found

    def items_of_rows(self, base, rows):
        place = base + lax.broadcasted_iota(jnp.int32, (rows, 1), 0)
        found = jnp.zeros((rows, 1), jnp.int32)
        for end in self.ends:
            found = found + (place >= end).astype(jnp.int32)
        return found

    def base(self, block):
        pair = block // 2
        hop = (pair + 1) // 2
        step = jnp.where(pair % 2 == 1, -hop, hop)
        chip = self.position // 2 + step
        device = chip * 2 + (self.position % 2 + block % 2) % 2
        start = device * self.count
        live = (chip >= 0) & (chip < self.shards // 2)
        return start, live & (start < self.high) & (start + self.count > self.low)


def lanes(rows):
    return lax.broadcasted_iota(jnp.int32, (rows, 128), 1)


def lse_lanes(lane):
    return (lane >= LSE_LANE) & (lane < DELTA_LANE)


def delta_lanes(lane):
    return (lane >= DELTA_LANE) & (lane < DELTA_LANE + 3 * H)


def head_lanes(lane, base, head):
    start = base + 3 * head
    return (lane >= start) & (lane < start + 3)


def beside(left, right):
    return jnp.concatenate([left.astype(jnp.bfloat16), right.astype(jnp.bfloat16)], axis=1)


def pieces(values):
    high = values.astype(jnp.bfloat16).astype(jnp.float32)
    rest = values - high
    middle = rest.astype(jnp.bfloat16).astype(jnp.float32)
    return high, middle, rest - middle


def dot(left, right):
    return jnp.dot(left, right, preferred_element_type=jnp.float32)


def stack_heads(target, values, features):
    rows = values.shape[0]
    half = lanes(rows) // 64
    wide = values.astype(jnp.float32)
    for h in range(2):
        target[h * rows : (h + 1) * rows, :] = beside(jnp.where(half == h, wide, 0.0), features[h])


def merge_heads(stacked):
    rows = stacked.shape[0] // 2
    return jnp.where(lanes(rows) < 64, stacked[:rows], stacked[rows:])


def window_bias(frame, block):
    base, _ = frame.base(block)
    item = frame.items_of_rows(base, frame.count)
    lane = lanes(frame.count)
    return jnp.where((lane != item) & (lane < frame.items), far, 0.0)


def text_bias(frame, block, rows):
    slot = lax.broadcasted_iota(jnp.int32, (rows, 1), 0)
    length = jnp.int32(0)
    for item in range(frame.items):
        length = jnp.where(block == item, frame.text_len[item], length)
    lane = lanes(rows)
    dead = (lane != block) | (slot >= length)
    return jnp.where(dead & (lane < frame.items), far, 0.0)


def block_rule(frame, kind, rows):
    if kind == "frames":
        return (
            lambda block: frame.base(block)[1],
            lambda block: window_bias(frame, block),
        )
    return (
        lambda block: (block >= frame.first) & (block <= frame.last),
        lambda block: text_bias(frame, block, rows),
    )


def rows_of(block, rows):
    return pl.ds(pl.multiple_of(block * rows, rows), rows)


def each_active(blocks, active, step):
    @pl.loop(0, blocks)
    def _(block):
        @pl.when(active(block))
        def _():
            step(block)


def fill_bias(blocks, rows, active, bias, target, with_lse):
    @pl.when(pl.program_id(0) == 0)
    def _():
        def step(block):
            mask = bias(block)
            if with_lse:
                mask = jnp.where(lse_lanes(lanes(rows)), -1.0, mask)
            target[rows_of(block, rows), :] = mask.astype(jnp.bfloat16)

        each_active(blocks, active, step)


def project_kernel(items, shards, blocks, meta, mod_ref, *refs):
    w_refs, x_refs = refs[:2], refs[2:-2]
    hidden_ref, out_ref = refs[-2:]
    count, width = x_refs[0].shape
    frame = Frame(meta, items, count, shards)
    for number, block in enumerate(blocks):
        base, live = frame.base(jnp.int32(block))

        @pl.when(live)
        def _(number=number, base=base):
            normed, _ = layer_norm(x_refs[number][...].astype(jnp.float32))
            item = frame.items_of_rows(base, count)
            shift = jnp.zeros_like(normed)
            scale = jnp.zeros_like(normed)
            for i in range(items):
                shift = jnp.where(item == i, mod_ref[i, 0:1, :], shift)
                scale = jnp.where(item == i, mod_ref[i, 1:2, :], scale)
            hidden = (normed * (1.0 + scale) + shift).astype(jnp.bfloat16)
            here = slice(number * count, (number + 1) * count)
            hidden_ref[here, :] = hidden
            for c in range(2):
                out_ref[here, c * width : (c + 1) * width] = dot(hidden, w_refs[c][...]).astype(jnp.bfloat16)


def project(meta, modulation, weight, x_blocks, blocks, items, shards, name):
    count, width = x_blocks[0].shape
    total = len(blocks) * count
    whole = pl.BlockSpec(memory_space=pltpu.VMEM)
    return pl.pallas_call(
        partial(project_kernel, items, shards, blocks),
        grid=(1,),
        out_shape=(
            jax.ShapeDtypeStruct((total, width), jnp.bfloat16),
            jax.ShapeDtypeStruct((total, 2 * width), jnp.bfloat16),
        ),
        in_specs=[
            pl.BlockSpec(memory_space=pltpu.SMEM),
            whole,
            pl.BlockSpec((width, width), lambda i: (0, 1), pipeline_mode=pl.Buffered(1)),
            pl.BlockSpec((width, width), lambda i: (0, 2), pipeline_mode=pl.Buffered(1)),
        ]
        + [whole] * len(blocks),
        out_specs=(whole, whole),
        compiler_params=pltpu.CompilerParams(vmem_limit_bytes=40 * MIB),
        cost_estimate=pl.CostEstimate(
            flops=2 * total * width * width,
            bytes_accessed=2 * 4 * total * width,
            transcendentals=0,
        ),
        name=name,
    )(meta, modulation, weight, weight, *x_blocks)


def window_queries_kernel(items, shards, blocks, meta, h_ref, w_ref, q_ref):
    count = h_ref.shape[0] // blocks
    frame = Frame(meta, items, count, shards)

    def step(block):
        here = rows_of(block, count)
        q = dot(h_ref[here, :], w_ref[...]).astype(jnp.bfloat16)
        q_ref[here, :] = (q.astype(jnp.float32) * 0.125).astype(jnp.bfloat16)

    each_active(blocks, lambda block: frame.base(block)[1], step)


def window_queries(meta, hidden, weight, blocks, items, shards):
    total, width = hidden.shape
    whole = pl.BlockSpec(memory_space=pltpu.VMEM)
    return pl.pallas_call(
        partial(window_queries_kernel, items, shards, blocks),
        grid=(1,),
        out_shape=jax.ShapeDtypeStruct((total, width), jnp.bfloat16),
        in_specs=[
            pl.BlockSpec(memory_space=pltpu.SMEM),
            whole,
            pl.BlockSpec((width, width), lambda i: (0, 0), pipeline_mode=pl.Buffered(1)),
        ],
        out_specs=whole,
        compiler_params=pltpu.CompilerParams(vmem_limit_bytes=40 * MIB),
        cost_estimate=pl.CostEstimate(flops=total * width * width, bytes_accessed=4 * total * width, transcendentals=0),
        name="window_queries",
    )(meta, hidden, weight)


def attend_kernel(items, shards, kind, blocks, meta, q_ref, k_ref, v_ref, o_ref, low_ref, f_ref, qa, bias_ref, s, m, l, acc):
    count = q_ref.shape[0]
    rows = k_ref.shape[0] // blocks
    frame = Frame(meta, items, count, shards)
    active, bias = block_rule(frame, kind, rows)
    pair = pl.program_id(0)
    lane = lanes(count)
    own = frame.items_of_rows(frame.position * count, count)
    own_item = (lane == own).astype(jnp.float32)
    fill_bias(blocks, rows, active, bias, bias_ref, False)
    stack_heads(qa, q_ref[...], [own_item, own_item])
    m[...] = jnp.full((2 * count, 128), far, jnp.float32)
    l[...] = jnp.zeros((2 * count, 128), jnp.float32)
    acc[...] = jnp.zeros((2 * count, 128), jnp.float32)

    def score(block):
        here = rows_of(block, rows)
        scores = times_transposed(qa[...], jnp.concatenate([k_ref[here, :], bias_ref[here, :]], axis=1))
        s[block] = scores
        m[...] = jnp.maximum(m[...], jnp.maximum(scores[:, :128], scores[:, 128:]))

    each_active(blocks, active, score)
    top = jnp.max(m[...], axis=1, keepdims=True)
    m[...] = jnp.broadcast_to(top, (2 * count, 128))

    def weigh(block):
        here = rows_of(block, rows)
        high = m[...]
        left = jnp.exp(s[block, :, :128] - high)
        right = jnp.exp(s[block, :, 128:] - high)
        l[...] = l[...] + (left + right)
        acc[...] = acc[...] + dot(beside(left, right), v_ref[here, :])

    each_active(blocks, active, weigh)
    total = jnp.sum(l[...], axis=1, keepdims=True)
    result = merge_heads(acc[...] / total)
    lse = top + jnp.log(total)
    features = jnp.where(pair == 0, own_item, f_ref[...].astype(jnp.float32))
    for h in range(2):
        start = LSE_LANE + 3 * (2 * pair + h)
        for number, piece in enumerate(pieces(lse[h * count : (h + 1) * count])):
            features = jnp.where(lane == start + number, piece, features)
    o_ref[...] = result
    low_ref[...] = result.astype(jnp.bfloat16)
    f_ref[...] = features.astype(jnp.bfloat16)


def attend(meta, queries, kv, kind, blocks, items, shards, name):
    count, width = queries.shape
    pairs = width // 128
    total = kv.shape[0]
    rows = total // blocks
    column = lambda offset: (lambda p: (0, p + offset))
    tile = pl.BlockSpec((count, 128), column(0))
    return pl.pallas_call(
        partial(attend_kernel, items, shards, kind, blocks),
        grid=(pairs,),
        out_shape=(
            jax.ShapeDtypeStruct((count, width), jnp.float32),
            jax.ShapeDtypeStruct((count, width), jnp.bfloat16),
            jax.ShapeDtypeStruct((count, 128), jnp.bfloat16),
        ),
        in_specs=[
            pl.BlockSpec(memory_space=pltpu.SMEM),
            tile,
            pl.BlockSpec((total, 128), column(0)),
            pl.BlockSpec((total, 128), column(pairs)),
        ],
        out_specs=(tile, tile, pl.BlockSpec((count, 128), lambda p: (0, 0))),
        scratch_shapes=[
            pltpu.VMEM((2 * count, 256), jnp.bfloat16),
            pltpu.VMEM((total, 128), jnp.bfloat16),
            pltpu.VMEM((blocks, 2 * count, rows), jnp.float32),
            pltpu.VMEM((2 * count, 128), jnp.float32),
            pltpu.VMEM((2 * count, 128), jnp.float32),
            pltpu.VMEM((2 * count, 128), jnp.float32),
        ],
        compiler_params=pltpu.CompilerParams(vmem_limit_bytes=40 * MIB),
        cost_estimate=pl.CostEstimate(
            flops=2 * count * total * width,
            bytes_accessed=4 * total * width,
            transcendentals=count * total * H // 2,
        ),
        name=name,
    )(meta, queries, kv, kv)


def query_side(pair, f_ref, q_ref, do_ref, qa, da):
    lane = lanes(q_ref.shape[0])
    features = f_ref[...].astype(jnp.float32)
    heads = [2 * pair, 2 * pair + 1]
    stack_heads(
        qa,
        q_ref[...],
        [jnp.where((lane < LSE_LANE) | head_lanes(lane, LSE_LANE, head), features, 0.0) for head in heads],
    )
    stack_heads(
        da, do_ref[...], [jnp.where(head_lanes(lane, DELTA_LANE, head), features, 0.0) for head in heads]
    )


def query_step(qa, da, keys, values, bias):
    minus = jnp.where(delta_lanes(lanes(keys.shape[0])), -1.0, 0.0)
    probs = jnp.exp(times_transposed(qa[...], jnp.concatenate([keys, bias], axis=1)))
    slope = times_transposed(da[...], beside(values, minus))
    return dot((probs * slope).astype(jnp.bfloat16), keys)


def key_side(frame, pair, k, v, mask, ka, va):
    lane = lanes(k.shape[0])
    heads = [2 * pair, 2 * pair + 1]
    stack_heads(ka, k, [jnp.where(head_lanes(lane, LSE_LANE, head), -1.0, mask) for head in heads])
    stack_heads(va, v, [jnp.where(head_lanes(lane, DELTA_LANE, head), -1.0, 0.0) for head in heads])


def key_step(ka, va, q, do, features):
    probs = jnp.exp(times_transposed(ka[...], jnp.concatenate([q, features], axis=1)))
    slope = times_transposed(va[...], jnp.concatenate([do, features], axis=1))
    return dot((probs * slope).astype(jnp.bfloat16), q), dot(probs.astype(jnp.bfloat16), do)


def query_grad_kernel(items, shards, blocks, meta, q_ref, do_ref, f_ref, k_ref, v_ref, dq_ref, qa, da, bias_ref, acc):
    count = q_ref.shape[0]
    rows = k_ref.shape[0] // blocks
    frame = Frame(meta, items, count, shards)
    active, bias = block_rule(frame, "frames", rows)
    fill_bias(blocks, rows, active, bias, bias_ref, True)
    query_side(pl.program_id(0), f_ref, q_ref, do_ref, qa, da)
    acc[...] = jnp.zeros((2 * count, 128), jnp.float32)

    def step(block):
        here = rows_of(block, rows)
        acc[...] = acc[...] + query_step(qa, da, k_ref[here, :], v_ref[here, :], bias_ref[here, :])

    each_active(blocks, active, step)
    dq_ref[...] = (merge_heads(acc[...]) * 0.125).astype(jnp.bfloat16)


def query_grad(meta, queries, grad_out, features, kv, blocks, items, shards, name):
    count, width = queries.shape
    pairs = width // 128
    total = kv.shape[0]
    column = lambda offset: (lambda p: (0, p + offset))
    tile = pl.BlockSpec((count, 128), column(0))
    return pl.pallas_call(
        partial(query_grad_kernel, items, shards, blocks),
        grid=(pairs,),
        out_shape=jax.ShapeDtypeStruct((count, width), jnp.bfloat16),
        in_specs=[
            pl.BlockSpec(memory_space=pltpu.SMEM),
            tile,
            tile,
            pl.BlockSpec((count, 128), lambda p: (0, 0)),
            pl.BlockSpec((total, 128), column(0)),
            pl.BlockSpec((total, 128), column(pairs)),
        ],
        out_specs=tile,
        scratch_shapes=[
            pltpu.VMEM((2 * count, 256), jnp.bfloat16),
            pltpu.VMEM((2 * count, 256), jnp.bfloat16),
            pltpu.VMEM((total, 128), jnp.bfloat16),
            pltpu.VMEM((2 * count, 128), jnp.float32),
        ],
        compiler_params=pltpu.CompilerParams(vmem_limit_bytes=40 * MIB),
        cost_estimate=pl.CostEstimate(
            flops=3 * count * total * width,
            bytes_accessed=4 * total * width,
            transcendentals=count * total * H // 2,
        ),
        name=name,
    )(meta, queries, grad_out, features, kv, kv)


def frame_key_grad_kernel(items, shards, blocks, meta, q_ref, do_ref, f_ref, k_ref, v_ref, dk_ref, dv_ref, ka, va, dka, dva):
    count = k_ref.shape[0]
    frame = Frame(meta, items, count, shards)
    key_side(frame, pl.program_id(0), k_ref[...], v_ref[...], window_bias(frame, jnp.int32(0)), ka, va)
    dka[...] = jnp.zeros((2 * count, 128), jnp.float32)
    dva[...] = jnp.zeros((2 * count, 128), jnp.float32)

    def step(block):
        here = rows_of(block, count)
        dk, dv = key_step(ka, va, q_ref[here, :], do_ref[here, :], f_ref[here, :])
        dka[...] = dka[...] + dk
        dva[...] = dva[...] + dv

    each_active(blocks, lambda block: frame.base(block)[1], step)
    dk_ref[...] = merge_heads(dka[...]).astype(jnp.bfloat16)
    dv_ref[...] = merge_heads(dva[...]).astype(jnp.bfloat16)


def frame_key_grad(meta, q_window, do_window, kv, count, blocks, items, shards, name):
    total, width = q_window.shape
    pairs = width // 128
    column = lambda offset: (lambda p: (0, p + offset))
    tile = pl.BlockSpec((count, 128), column(0))
    wide = pl.BlockSpec((total, 128), column(0))
    return pl.pallas_call(
        partial(frame_key_grad_kernel, items, shards, blocks),
        grid=(pairs,),
        out_shape=(jax.ShapeDtypeStruct((count, width), jnp.bfloat16),) * 2,
        in_specs=[
            pl.BlockSpec(memory_space=pltpu.SMEM),
            wide,
            wide,
            pl.BlockSpec((total, 128), lambda p: (0, pairs)),
            tile,
            pl.BlockSpec((count, 128), column(pairs)),
        ],
        out_specs=(tile, tile),
        scratch_shapes=[pltpu.VMEM((2 * count, 256), jnp.bfloat16)] * 2
        + [pltpu.VMEM((2 * count, 128), jnp.float32)] * 2,
        compiler_params=pltpu.CompilerParams(vmem_limit_bytes=40 * MIB),
        cost_estimate=pl.CostEstimate(
            flops=4 * count * total * width,
            bytes_accessed=4 * total * width,
            transcendentals=count * total * H // 2,
        ),
        name=name,
    )(meta, q_window, do_window, do_window, kv, kv)


def text_grad_kernel(items, shards, meta, q_ref, do_ref, f_ref, k_ref, v_ref, dq_ref, dkv_ref, qa, da, ka, va, acc):
    count = q_ref.shape[0]
    rows = k_ref.shape[0] // items
    share = rows // shards
    frame = Frame(meta, items, count, shards)
    pair = pl.program_id(0)
    query_side(pair, f_ref, q_ref, do_ref, qa, da)
    acc[...] = jnp.zeros((2 * count, 128), jnp.float32)

    @pl.loop(0, items)
    def _(item):
        here = rows_of(item, rows)
        live = (item >= frame.first) & (item <= frame.last)
        target = pl.ds(pl.multiple_of(item * share, share), share)

        @pl.when(live)
        def _():
            keys, values = k_ref[here, :], v_ref[here, :]
            mask = text_bias(frame, item, rows)
            bias = jnp.where(lse_lanes(lanes(rows)), -1.0, mask).astype(jnp.bfloat16)
            acc[...] = acc[...] + query_step(qa, da, keys, values, bias)
            key_side(frame, pair, keys, values, mask, ka, va)
            grads = key_step(ka, va, q_ref[...], do_ref[...], f_ref[...])
            for which, grad in enumerate(grads):
                merged = merge_heads(grad).astype(jnp.bfloat16)
                for piece in range(shards):
                    dkv_ref[which, piece ^ frame.position, target, :] = merged[piece * share : (piece + 1) * share]

        @pl.when(jnp.logical_not(live))
        def _():
            for which in range(2):
                for piece in range(shards):
                    dkv_ref[which, piece, target, :] = jnp.zeros((share, 128), jnp.bfloat16)

    dq_ref[...] = (merge_heads(acc[...]) * 0.125).astype(jnp.bfloat16)


def text_grad(meta, queries, grad_out, features, kv, items, shards, name):
    count, width = queries.shape
    pairs = width // 128
    total = kv.shape[0]
    column = lambda offset: (lambda p: (0, p + offset))
    tile = pl.BlockSpec((count, 128), column(0))
    rows = total // items
    return pl.pallas_call(
        partial(text_grad_kernel, items, shards),
        grid=(pairs,),
        out_shape=(
            jax.ShapeDtypeStruct((count, width), jnp.bfloat16),
            jax.ShapeDtypeStruct((2, shards, total // shards, width), jnp.bfloat16),
        ),
        in_specs=[
            pl.BlockSpec(memory_space=pltpu.SMEM),
            tile,
            tile,
            pl.BlockSpec((count, 128), lambda p: (0, 0)),
            pl.BlockSpec((total, 128), column(0)),
            pl.BlockSpec((total, 128), column(pairs)),
        ],
        out_specs=(tile, pl.BlockSpec((2, shards, total // shards, 128), lambda p: (0, 0, 0, p))),
        scratch_shapes=[pltpu.VMEM((2 * count, 256), jnp.bfloat16)] * 2
        + [pltpu.VMEM((2 * rows, 256), jnp.bfloat16)] * 2
        + [pltpu.VMEM((2 * count, 128), jnp.float32)],
        compiler_params=pltpu.CompilerParams(vmem_limit_bytes=40 * MIB),
        cost_estimate=pl.CostEstimate(
            flops=7 * count * rows * 2 * width,
            bytes_accessed=8 * total * width,
            transcendentals=count * rows * H * 2,
        ),
        name=name,
    )(meta, queries, grad_out, features, kv, kv)


UNIT = 192


def turned(x_ref, start, width):
    eye = (
        lax.broadcasted_iota(jnp.int32, (width, width), 0) == lax.broadcasted_iota(jnp.int32, (width, width), 1)
    ).astype(jnp.bfloat16)
    return times_transposed(eye, x_ref[:, pl.ds(pl.multiple_of(start, 128), width)]).astype(jnp.bfloat16)


def turned_rows(x_ref, core):
    row = lax.broadcasted_iota(jnp.int32, (384, 768), 0)
    column = lax.broadcasted_iota(jnp.int32, (384, 768), 1)
    chip = (row >= 96).astype(jnp.int32) + (row >= 192).astype(jnp.int32) + (row >= 288).astype(jnp.int32)
    pick = (column == row + 96 * (chip + core)).astype(jnp.bfloat16)
    return times_transposed(pick, x_ref[...]).astype(jnp.bfloat16)


def pack_kernel(items, kinds, firsts, meta, *refs):
    position = meta[0]
    core, chip = position % 2, position // 2
    mine = meta[1 + 2 * items]
    inputs = refs[: 4 * len(kinds)]
    outputs = refs[4 * len(kinds) :]

    def store(group, owner, owner_chip, row, values):
        relative = owner ^ mine
        first = firsts[group]
        low = values.astype(jnp.bfloat16)
        where = ((relative >> (1 - first)) % 2, owner_chip ^ chip, slice(row, row + values.shape[0]))

        @pl.when((relative >> first) % 2 == 1)
        def _():
            outputs[2 * group][where] = low

        @pl.when((relative >> first) % 2 == 0)
        def _():
            outputs[2 * group + 1][where] = low

    def store_split(group, pair, row, values, chips):
        rolled = pltpu.roll(values, UNIT, 1)
        each = values.shape[0] // len(chips)
        left = lax.broadcasted_iota(jnp.int32, (each // 2, 384), 1) < UNIT
        for number, owner_chip in enumerate(chips):
            upper = slice(number * each, number * each + each // 2)
            lower = slice(number * each + each // 2, (number + 1) * each)
            store(group, 2 * pair, owner_chip, row, jnp.where(left, values[upper], rolled[lower]))
            store(group, 2 * pair + 1, owner_chip, row, jnp.where(left, rolled[upper], values[lower]))

    row = 0
    for number, kind in enumerate(kinds):
        x_own, x_sib, y_own, y_sib = inputs[4 * number : 4 * number + 4]

        def product(own, sib, column):
            here = pl.ds(column * 384, 384) if isinstance(column, int) else pl.ds(pl.multiple_of(column * 384, 128), 384)
            return dot(own, y_own[:, here]) + dot(sib, y_sib[:, here])

        if kind == "down":
            for owner_chip in range(4):
                start = owner_chip * 768 + core * 384
                own, sib = turned(x_own, start, 384), turned(x_sib, start, 384)
                for pair in range(2):
                    store_split(0, pair, row, product(own, sib, pair), [owner_chip])
            row += 192
        elif kind == "text":
            for owner_chip in range(4):
                start = owner_chip * 256 + core * 128
                own, sib = turned(x_own, start, 128), turned(x_sib, start, 128)
                for owner in range(4):
                    store(0, owner, owner_chip, row, product(own, sib, owner))
            row += 128
        else:
            own, sib = turned_rows(x_own, core), turned_rows(x_sib, core)
            if kind == "square":
                for pair in range(2):
                    store_split(0, pair, row, product(own, sib, pair), range(4))
                row += 48
            elif kind == "up":
                for column in range(8):
                    values = product(own, sib, column)
                    for owner_chip in range(4):
                        store(
                            0,
                            column // 2,
                            owner_chip,
                            row + (column % 2) * 96,
                            values[owner_chip * 96 : (owner_chip + 1) * 96],
                        )
                row += 192
            elif kind == "qkv":
                for owner, column in enumerate((0, 2, 3, 5)):
                    values = product(own, sib, column)
                    for owner_chip in range(4):
                        store(0, owner, owner_chip, 0, values[owner_chip * 96 : (owner_chip + 1) * 96])
                for pair, column in enumerate((1, 4)):
                    store_split(1, pair, 0, product(own, sib, column), range(4))


PACKED_ROWS = {"down": 192, "text": 128, "square": 48, "up": 192}


def pack(meta, kinds, operands, firsts, items, name):
    group_rows = [96, 48] if kinds == ("qkv",) else [sum(PACKED_ROWS[kind] for kind in kinds)]
    whole = pl.BlockSpec(memory_space=pltpu.VMEM)
    shapes = [jax.ShapeDtypeStruct((2, 4, rows, 384), jnp.bfloat16) for rows in group_rows for _ in range(2)]
    return pl.pallas_call(
        partial(pack_kernel, items, kinds, firsts),
        out_shape=tuple(shapes),
        in_specs=[pl.BlockSpec(memory_space=pltpu.SMEM)] + [whole] * len(operands),
        out_specs=tuple([whole] * len(shapes)),
        compiler_params=pltpu.CompilerParams(vmem_limit_bytes=40 * MIB),
        cost_estimate=pl.CostEstimate(
            flops=2 * 512 * 16 * sum(group_rows) * 384,
            bytes_accessed=32 * sum(group_rows) * 384,
            transcendentals=0,
        ),
        name=name,
    )(meta, *operands)


def trade(values, axis, bit):
    size = lax.axis_size(axis)
    return lax.ppermute(values, axis, [(i, i ^ (1 << bit)) for i in range(size)])


def halve(keep, send, axis, bit):
    total = keep.astype(jnp.float32) + trade(send, axis, bit).astype(jnp.float32)
    return total


def reduce_packed(send, keep, first):
    part = halve(keep, send, "batch", first).astype(jnp.bfloat16)
    part = halve(part[0], part[1], "batch", 1 - first).astype(jnp.bfloat16)
    part = part.reshape(2, 2, *part.shape[1:])
    part = halve(part[:, 0], part[:, 1], "seq", 1).astype(jnp.bfloat16)
    return halve(part[0], part[1], "seq", 2)


def unsplit(rows):
    return jnp.concatenate([rows[:, :UNIT], rows[:, UNIT:]], axis=0)


def with_deltas(features, grad_out, attn_exact):
    width = attn_exact.shape[1]
    lane = jnp.arange(128)[None, :]
    head = (jnp.arange(width) // (width // H))[:, None]
    pick = ((lane >= DELTA_LANE) & ((lane - DELTA_LANE) // 3 == head)).astype(jnp.float32)
    delta = jnp.dot(
        grad_out.astype(jnp.float32) * attn_exact,
        pick,
        precision=lax.Precision.HIGHEST,
        preferred_element_type=jnp.float32,
    )
    high = lax.reduce_precision(delta, 8, 7)
    middle = lax.reduce_precision(delta - high, 8, 7)
    which = (lane - DELTA_LANE) % 3
    piece = jnp.where(which == 0, high, jnp.where(which == 1, middle, delta - high - middle))
    inside = (lane >= DELTA_LANE) & (lane < DELTA_LANE + 3 * H)
    return jnp.where(inside, piece.astype(jnp.bfloat16), features)


def gather_window(own, reach, shards):
    swap = [(i, i ^ 1) for i in range(shards)]
    up = [(i, i + 2) for i in range(shards - 2)]
    down = [(i + 2, i) for i in range(shards - 2)]
    blocks = [own, lax.ppermute(own, "seq", swap)]
    below, above = own, own
    for _ in range(reach):
        below = lax.ppermute(below, "seq", up)
        above = lax.ppermute(above, "seq", down)
        blocks += [below, lax.ppermute(below, "seq", swap)]
        blocks += [above, lax.ppermute(above, "seq", swap)]
    return blocks


def body(
    frames,
    cotangent,
    modulation,
    lengths,
    text,
    text_len,
    w_qkv,
    w_o,
    w_cq,
    w_ckv,
    w_co,
    w_up,
    w_down,
):
    local = frames[0]
    count, width = local.shape
    items = lengths.shape[1]
    text_rows, text_width = text.shape[2:]
    shards = lax.axis_size("seq")
    position = lax.axis_index("seq")
    reach = min(-(-(LONGEST - 1) // (2 * count)), shards // 2 - 1)
    blocks = 2 + 4 * reach
    meta = jnp.concatenate(
        [position[None].astype(jnp.int32), lengths[0], text_len[0], lax.axis_index("batch")[None].astype(jnp.int32)]
    )
    item_range = jnp.arange(items, dtype=jnp.int32)
    ends = jnp.sum(jnp.where(item_range[None, :] <= item_range[:, None], lengths[0][None, :], 0), axis=1)
    place = position * count + jnp.arange(count, dtype=jnp.int32)
    query_items = jnp.sum((place[:, None] >= ends[None, :]).astype(jnp.int32), axis=1)[:, None]
    one_hot = (query_items == item_range[None, :]).astype(jnp.float32)
    mod = modulation[0]

    def per_frame(which):
        found = jnp.broadcast_to(mod[0, which][None, :], (count, width))
        for item in range(1, items):
            found = jnp.where(query_items == item, mod[item, which][None, :], found)
        return found

    swap = [(i, i ^ 1) for i in range(shards)]

    def sibling(values):
        return lax.ppermute(values, "seq", swap)

    fast = shards == 8 and lax.axis_size("batch") == 4 and width == 768
    window = gather_window(local, reach, shards)
    inputs = local.astype(jnp.float32)
    normed_one, inverse_one = layer_norm(inputs)
    hidden_one = (normed_one * (1.0 + per_frame(1)) + per_frame(0)).astype(jnp.bfloat16)
    queries = jnp.dot(hidden_one, w_qkv[:, :width], preferred_element_type=jnp.float32).astype(jnp.bfloat16)
    queries = (queries.astype(jnp.float32) * 0.125).astype(jnp.bfloat16)
    text_proj = jnp.dot(
        text[0].reshape(items * text_rows, text_width), w_ckv, preferred_element_type=jnp.float32
    ).astype(jnp.bfloat16)
    hidden_window, kv = project(meta, mod, w_qkv, window, tuple(range(blocks)), items, shards, "project_keys")
    attn_exact, attended, features = attend(meta, queries, kv, "frames", blocks, items, shards, "self_attend")
    branch_one = jnp.dot(attended, w_o, preferred_element_type=jnp.float32)
    after_attn = inputs + per_frame(2) * branch_one
    normed_cross, inverse_cross = layer_norm(after_attn)
    cross_in = normed_cross.astype(jnp.bfloat16)
    cross_queries = jnp.dot(cross_in, w_cq, preferred_element_type=jnp.float32).astype(jnp.bfloat16)
    cross_queries = (cross_queries.astype(jnp.float32) * 0.125).astype(jnp.bfloat16)
    cross_exact, cross_out, cross_features = attend(
        meta, cross_queries, text_proj, "text", items, items, shards, "cross_attend"
    )
    branch_two = jnp.dot(cross_out, w_co, preferred_element_type=jnp.float32)
    after_cross = after_attn + branch_two
    normed_two, inverse_two = layer_norm(after_cross)
    hidden_two = (normed_two * (1.0 + per_frame(4)) + per_frame(3)).astype(jnp.bfloat16)
    pre_act = jnp.dot(hidden_two, w_up, preferred_element_type=jnp.float32)
    activated, gelu_back = jax.vjp(partial(jax.nn.gelu, approximate=True), pre_act)
    activated_low = activated.astype(jnp.bfloat16)
    gate_two = per_frame(5)
    grad_out = cotangent[0].astype(jnp.float32)
    grad_branch_three = (grad_out * gate_two).astype(jnp.bfloat16)
    grad_pre = gelu_back(times_transposed(grad_branch_three, w_down))[0].astype(jnp.bfloat16)
    branch_three = jnp.dot(activated_low, w_down, preferred_element_type=jnp.float32)
    result = after_cross + gate_two * branch_three
    grad_hidden_two = times_transposed(grad_pre, w_up)
    grad_cross = grad_out + norm_back(grad_hidden_two * (1.0 + per_frame(4)), normed_two, inverse_two)
    grad_branch_two = grad_cross.astype(jnp.bfloat16)
    grad_cross_out = times_transposed(grad_branch_two, w_co).astype(jnp.bfloat16)
    cross_features = with_deltas(cross_features, grad_cross_out, cross_exact)
    grad_cross_queries, text_terms = text_grad(
        meta, cross_queries, grad_cross_out, cross_features, text_proj, items, shards, "cross_grad"
    )
    grad_attn_res = grad_cross + norm_back(
        times_transposed(grad_cross_queries, w_cq), normed_cross, inverse_cross
    )
    grad_branch_one = (grad_attn_res * per_frame(2)).astype(jnp.bfloat16)
    grad_attended = times_transposed(grad_branch_one, w_o).astype(jnp.bfloat16)
    features = with_deltas(features, grad_attended, attn_exact)
    grad_queries = query_grad(
        meta, queries, grad_attended, features, kv, blocks, items, shards, "self_query_grad"
    )
    do_window = jnp.concatenate(
        gather_window(jnp.concatenate([grad_attended, features], axis=1), reach, shards), axis=0
    )
    q_window = window_queries(meta, hidden_window, w_qkv, blocks, items, shards)
    grad_keys, grad_values = frame_key_grad(
        meta, q_window, do_window, kv, count, blocks, items, shards, "self_key_grad"
    )
    grad_projected = jnp.concatenate([grad_queries, grad_keys, grad_values], axis=1)
    grad_hidden_one = times_transposed(grad_projected, w_qkv)
    grad_inputs = grad_attn_res + norm_back(
        grad_hidden_one * (1.0 + per_frame(1)), normed_one, inverse_one
    )

    def item_sum(values):
        return lax.dot_general(
            one_hot,
            values,
            (((0,), (0,)), ((), ())),
            precision=lax.Precision.HIGHEST,
            preferred_element_type=jnp.float32,
        )

    def item_share(terms):
        total = jnp.concatenate(terms, axis=0)
        for bit in range(shards.bit_length() - 1):
            total = total + trade(total, "seq", bit)
        own = width // shards
        mine = lax.dynamic_slice_in_dim(total, position * own, own, 1)
        return mine.reshape(len(terms), items, own).transpose(1, 0, 2)

    early = item_share(
        [
            item_sum(grad_attn_res * branch_one),
            item_sum(grad_hidden_two),
            item_sum(grad_hidden_two * normed_two),
            item_sum(grad_out * branch_three),
        ]
    )
    late = item_share([item_sum(grad_hidden_one), item_sum(grad_hidden_one * normed_one)])
    grad_mod = jnp.concatenate([late, early[:, :1]], axis=1)[None]
    grad_mod_mlp = early[:, 1:][None]
    for bit in range(shards.bit_length() - 1):
        text_terms = text_terms.reshape(2, -1, 2, *text_terms.shape[2:])
        text_terms = halve(text_terms[:, :, 0], text_terms[:, :, 1], "seq", bit).astype(jnp.bfloat16)
    share_rows = text_rows // shards
    text_grad_low = jnp.concatenate([text_terms[0, 0], text_terms[1, 0]], axis=1)

    def text_of(device):
        return lax.dynamic_slice_in_dim(text[0], device * share_rows, share_rows, 1).reshape(
            items * share_rows, text_width
        )

    grad_text = times_transposed(text_grad_low, w_ckv).reshape(1, items, share_rows, text_width)
    weights = weight_grads_fast if fast else weight_grads
    return (
        result.astype(jnp.bfloat16)[None],
        grad_inputs[None],
        grad_mod,
        grad_mod_mlp,
        grad_text,
        *weights(
            meta,
            items,
            sibling,
            (hidden_one, grad_projected),
            (attended, grad_branch_one),
            (cross_in, grad_cross_queries),
            (text_of(position), text_grad_low, text_of(position ^ 1)),
            (cross_out, grad_branch_two),
            (hidden_two, grad_pre),
            (activated_low, grad_branch_three),
        ),
    )


def weight_grads(meta, items, sibling, *pairs):
    def reduce_weight(left, right, *_):
        grad = contract_rows(left, right).astype(jnp.bfloat16)
        part = lax.psum_scatter(grad, "seq", scatter_dimension=0, tiled=True)
        return lax.psum_scatter(part, "batch", scatter_dimension=1, tiled=True).astype(jnp.float32)

    return tuple(reduce_weight(*pair) for pair in pairs)


def weight_grads_fast(meta, items, sibling, qkv, o, cq, ckv, co, up, down):
    def operands(left, right):
        return (left, sibling(left), right, sibling(right))

    def pack_and_reduce(kinds, arrays, firsts, name):
        packed = pack(meta, kinds, arrays, firsts, items, name)
        return [reduce_packed(packed[2 * i], packed[2 * i + 1], first) for i, first in enumerate(firsts)]

    X, Y = 0, 1
    [down_rows] = pack_and_reduce(("down",), operands(*down), (Y,), "pack_down")
    [up_rows] = pack_and_reduce(("up",), operands(*up), (X,), "pack_up")
    [square_rows] = pack_and_reduce(
        ("square",) * 3, operands(*co) + operands(*cq) + operands(*o), (Y,), "pack_square"
    )
    text_own, low, text_sib = ckv
    [text_rows] = pack_and_reduce(("text",), (text_own, text_sib, low, sibling(low)), (X,), "pack_text")
    plain, split = pack_and_reduce(("qkv",), operands(*qkv), (X, Y), "pack_qkv")
    split = unsplit(split)
    even = lax.axis_index("batch") % 2 == 0
    grad_qkv = jnp.where(
        even, jnp.concatenate([plain, split], axis=1), jnp.concatenate([split, plain], axis=1)
    )
    return (
        grad_qkv,
        unsplit(square_rows[96:]),
        unsplit(square_rows[48:96]),
        text_rows,
        unsplit(square_rows[:48]),
        jnp.concatenate([up_rows[:96], up_rows[96:]], axis=1),
        unsplit(down_rows),
    )


def solution(mesh):
    in_specs = (
        P("batch", "seq", None),
        P("batch", "seq", None),
        P("batch", None, None, None),
        P("batch", None),
        P("batch", None, None, None),
        P("batch", None),
        P(),
        P(),
        P(),
        P(),
        P(),
        P(),
        P(),
    )
    out_specs = (
        P("batch", "seq", None),
        P("batch", "seq", None),
        P("batch", None, None, "seq"),
        P("batch", None, None, "seq"),
        P("batch", None, "seq", None),
        P("seq", "batch"),
        P("seq", "batch"),
        P("seq", "batch"),
        P("seq", "batch"),
        P("seq", "batch"),
        P("seq", "batch"),
        P("seq", "batch"),
    )
    return jax.shard_map(body, mesh=mesh, in_specs=in_specs, out_specs=out_specs, check_vma=False)
```

```python
from functools import partial

import jax
import jax.numpy as jnp
from jax import lax
from jax.experimental import pallas as pl
from jax.experimental.pallas import tpu as pltpu
from jax.sharding import PartitionSpec as P

H = 12
LONGEST = 1024

epsilon = 1e-06
far = -1e30
LSE_LANE = 8
DELTA_LANE = 44
MIB = 1 << 20


def layer_norm(values):
    centred = values - jnp.mean(values, axis=-1, keepdims=True)
    inverse = lax.rsqrt(jnp.mean(centred * centred, axis=-1, keepdims=True) + epsilon)
    return (centred * inverse, inverse)


def norm_back(grad_normed, normed, inverse):
    return inverse * (
        grad_normed
        - jnp.mean(grad_normed, axis=-1, keepdims=True)
        - normed * jnp.mean(grad_normed * normed, axis=-1, keepdims=True)
    )


def contract_rows(left, right):
    return lax.dot_general(
        left, right, (((0,), (0,)), ((), ())), preferred_element_type=jnp.float32
    )


def times_transposed(left, right):
    return lax.dot_general(
        left, right, (((1,), (1,)), ((), ())), preferred_element_type=jnp.float32
    )


class Frame:
    def __init__(self, meta, items, count, shards):
        self.position = meta[0]
        self.items = items
        self.count = count
        self.shards = shards
        self.ends = []
        total = jnp.int32(0)
        for item in range(items):
            total = total + meta[1 + item]
            self.ends.append(total)
        self.text_len = [meta[1 + items + item] for item in range(items)]
        self.first = self.item_of(self.position * count)
        self.last = self.item_of(self.position * count + count - 1)
        self.low = jnp.int32(0)
        self.high = jnp.int32(0)
        for item in range(items):
            start = self.ends[item] - meta[1 + item]
            self.low = jnp.where(self.first == item, start, self.low)
            self.high = jnp.where(self.last == item, self.ends[item], self.high)

    def item_of(self, place):
        found = jnp.int32(0)
        for end in self.ends:
            found = found + (place >= end).astype(jnp.int32)
        return found

    def items_of_rows(self, base, rows):
        place = base + lax.broadcasted_iota(jnp.int32, (rows, 1), 0)
        found = jnp.zeros((rows, 1), jnp.int32)
        for end in self.ends:
            found = found + (place >= end).astype(jnp.int32)
        return found

    def items_of_chip(self, block):
        start, _ = self.chip(block)
        core = self.position % 2
        return jnp.concatenate(
            [
                self.items_of_rows(start + core * self.count, self.count),
                self.items_of_rows(start + (1 - core) * self.count, self.count),
            ],
            axis=0,
        )

    def chip(self, block):
        hop = (block + 1) // 2
        chip = self.position // 2 + jnp.where(block % 2 == 1, -hop, hop)
        rows = 2 * self.count
        start = chip * rows
        live = (chip >= 0) & (chip < self.shards // 2)
        return start, live & (start < self.high) & (start + rows > self.low)


def lanes(rows):
    return lax.broadcasted_iota(jnp.int32, (rows, 128), 1)


def lse_lanes(lane):
    return (lane >= LSE_LANE) & (lane < DELTA_LANE)


def delta_lanes(lane):
    return (lane >= DELTA_LANE) & (lane < DELTA_LANE + 3 * H)


def head_lanes(lane, base, head):
    start = base + 3 * head
    return (lane >= start) & (lane < start + 3)


def beside(left, right):
    return jnp.concatenate([left.astype(jnp.bfloat16), right.astype(jnp.bfloat16)], axis=1)


def pieces(values):
    high = values.astype(jnp.bfloat16).astype(jnp.float32)
    rest = values - high
    middle = rest.astype(jnp.bfloat16).astype(jnp.float32)
    return high, middle, rest - middle


def dot(left, right):
    return jnp.dot(left, right, preferred_element_type=jnp.float32)


def stack_heads(target, values, features):
    rows = values.shape[0]
    half = lanes(rows) // 64
    wide = values.astype(jnp.float32)
    for h in range(2):
        target[h * rows : (h + 1) * rows, :] = beside(jnp.where(half == h, wide, 0.0), features[h])


def merge_heads(stacked):
    rows = stacked.shape[0] // 2
    return jnp.where(lanes(rows) < 64, stacked[:rows], stacked[rows:])


def item_bias(frame, item):
    lane = lanes(item.shape[0])
    return jnp.where((lane != item) & (lane < frame.items), far, 0.0)


def text_bias(frame, block, rows):
    slot = lax.broadcasted_iota(jnp.int32, (rows, 1), 0)
    length = jnp.int32(0)
    for item in range(frame.items):
        length = jnp.where(block == item, frame.text_len[item], length)
    lane = lanes(rows)
    dead = (lane != block) | (slot >= length)
    return jnp.where(dead & (lane < frame.items), far, 0.0)


def block_rule(frame, kind, rows):
    if kind == "frames":
        return (
            lambda block: frame.chip(block)[1],
            lambda block: item_bias(frame, frame.items_of_chip(block)),
        )
    return (
        lambda block: (block >= frame.first) & (block <= frame.last),
        lambda block: text_bias(frame, block, rows),
    )


def rows_of(block, rows):
    return pl.ds(pl.multiple_of(block * rows, rows), rows)


def each_active(blocks, active, step):
    @pl.loop(0, blocks)
    def _(block):
        @pl.when(active(block))
        def _():
            step(block)


def fill_bias(blocks, rows, active, bias, target, with_lse):
    @pl.when(pl.program_id(0) == 0)
    def _():
        def step(block):
            mask = bias(block)
            if with_lse:
                mask = jnp.where(lse_lanes(lanes(rows)), -1.0, mask)
            target[rows_of(block, rows), :] = mask.astype(jnp.bfloat16)

        each_active(blocks, active, step)


def project_kernel(items, shards, chips, meta, mod_ref, w_ref, *refs):
    number = len(chips)
    x_refs = refs[: 2 * number]
    q_ref, kv_ref, own_ref, x_s, h_s, q_s, kv_s, in_sem, out_sem = refs[-9:]
    count, width = x_refs[0].shape
    rows = 2 * count
    frame = Frame(meta, items, count, shards)

    def live(index):
        return frame.chip(index + chips[0])[1]

    for index in range(number):

        @pl.when(live(jnp.int32(index)))
        def _(index=index):
            for part in range(2):
                block = 2 * index + part
                pltpu.make_async_copy(
                    x_refs[block], x_s.at[pl.ds(block * count, count), :], in_sem.at[block]
                ).start()

    def writes(index):
        here = rows_of(index, rows)
        there = rows_of(index + chips[0], rows)
        return (
            pltpu.make_async_copy(q_s.at[here, :], q_ref.at[there, :], out_sem.at[2 * index]),
            pltpu.make_async_copy(kv_s.at[here, :], kv_ref.at[there, :], out_sem.at[2 * index + 1]),
        )

    @pl.loop(0, number)
    def _(index):
        @pl.when(live(index))
        def _():
            start = frame.chip(index + chips[0])[0]
            for part in range(2):
                block = 2 * index + part
                here = rows_of(block, count)
                pltpu.make_async_copy(x_refs[0], x_s.at[here, :], in_sem.at[block]).wait()
                normed, _ = layer_norm(x_s[here, :].astype(jnp.float32))
                item = frame.items_of_rows(start + (frame.position + part) % 2 * count, count)
                shift = jnp.broadcast_to(mod_ref[0, 0:1, :], normed.shape)
                scale = jnp.broadcast_to(mod_ref[0, 1:2, :], normed.shape)
                for i in range(1, items):
                    shift = jnp.where(item == i, mod_ref[i, 0:1, :], shift)
                    scale = jnp.where(item == i, mod_ref[i, 1:2, :], scale)
                h_s[part * count : (part + 1) * count, :] = (normed * (1.0 + scale) + shift).astype(jnp.bfloat16)
            both = rows_of(index, rows)
            hidden = h_s[...]
            q = dot(hidden, w_ref[:, :width]).astype(jnp.bfloat16)
            q_s[both, :] = (q.astype(jnp.float32) * 0.125).astype(jnp.bfloat16)
            kv_s[both, :width] = dot(hidden, w_ref[:, width : 2 * width]).astype(jnp.bfloat16)
            kv_s[both, width:] = dot(hidden, w_ref[:, 2 * width :]).astype(jnp.bfloat16)
            for write in writes(index):
                write.start()

        @pl.when(index == 0)
        def _():
            own_ref[...] = h_s[:count, :]

    @pl.loop(0, number)
    def _(index):
        @pl.when(live(index))
        def _():
            for write in writes(index):
                write.wait()


def project(meta, modulation, weight, x_blocks, chips, total, earlier, items, shards, name):
    count, width = x_blocks[0].shape
    part = len(x_blocks) * count
    whole = pl.BlockSpec(memory_space=pltpu.VMEM)
    anywhere = pl.BlockSpec(memory_space=pl.ANY)
    before = 3 + len(x_blocks)
    return pl.pallas_call(
        partial(project_kernel, items, shards, chips),
        out_shape=(
            jax.ShapeDtypeStruct((total, width), jnp.bfloat16),
            jax.ShapeDtypeStruct((total, 2 * width), jnp.bfloat16),
            jax.ShapeDtypeStruct((count, width), jnp.bfloat16),
        ),
        in_specs=[pl.BlockSpec(memory_space=pltpu.SMEM), whole, whole]
        + [anywhere] * (len(x_blocks) + len(earlier)),
        out_specs=(anywhere, anywhere, whole),
        input_output_aliases={before: 0, before + 1: 1} if earlier else {},
        scratch_shapes=[
            pltpu.VMEM((part, width), jnp.bfloat16),
            pltpu.VMEM((2 * count, width), jnp.bfloat16),
            pltpu.VMEM((part, width), jnp.bfloat16),
            pltpu.VMEM((part, 2 * width), jnp.bfloat16),
            pltpu.SemaphoreType.DMA((len(x_blocks),)),
            pltpu.SemaphoreType.DMA((len(x_blocks),)),
        ],
        compiler_params=pltpu.CompilerParams(vmem_limit_bytes=40 * MIB),
        cost_estimate=pl.CostEstimate(
            flops=3 * part * width * width,
            bytes_accessed=2 * 4 * part * width,
            transcendentals=0,
        ),
        name=name,
    )(meta, modulation, weight, *x_blocks, *earlier)


def heads_of(ref, here, pair):
    return ref[here, pair * 128 : (pair + 1) * 128]


def spread(count, group, base):
    return pl.BlockSpec((count, group * 128), lambda p: (0, p + base // group))


ALL = slice(None)


def attend_kernel(items, shards, kind, blocks, group, meta, q_ref, k_ref, v_ref, o_ref, low_ref, f_ref, qa, bias_ref, s, m, l, acc):
    count = q_ref.shape[0]
    rows = k_ref.shape[0] // blocks
    frame = Frame(meta, items, count, shards)
    active, bias = block_rule(frame, kind, rows)
    step = pl.program_id(0)
    lane = lanes(count)
    own = frame.items_of_rows(frame.position * count, count)
    own_item = (lane == own).astype(jnp.float32)
    fill_bias(blocks, rows, active, bias, bias_ref, False)
    for g in range(group):
        stack_heads(qa.at[g], heads_of(q_ref, ALL, g), [own_item, own_item])
        m[g] = jnp.full((2 * count, 128), far, jnp.float32)
        l[g] = jnp.zeros((2 * count, 128), jnp.float32)
        acc[g] = jnp.zeros((2 * count, 128), jnp.float32)

    def score(block):
        here = rows_of(block, rows)
        for g in range(group):
            scores = times_transposed(qa[g], jnp.concatenate([heads_of(k_ref, here, g), bias_ref[here, :]], axis=1))
            s[g, block] = scores
            high = m[g]
            for c in range(rows // 128):
                high = jnp.maximum(high, scores[:, c * 128 : (c + 1) * 128])
            m[g] = high

    each_active(blocks, active, score)
    tops = []
    for g in range(group):
        tops.append(jnp.max(m[g], axis=1, keepdims=True))
        m[g] = jnp.broadcast_to(tops[g], (2 * count, 128))

    def weigh(block):
        here = rows_of(block, rows)
        for g in range(group):
            high = m[g]
            total = l[g]
            parts = []
            for c in range(rows // 128):
                part = jnp.exp(s[g, block, :, c * 128 : (c + 1) * 128] - high)
                total = total + part
                parts.append(part.astype(jnp.bfloat16))
            l[g] = total
            acc[g] = acc[g] + dot(jnp.concatenate(parts, axis=1), heads_of(v_ref, here, g))

    each_active(blocks, active, weigh)
    features = jnp.where(step == 0, own_item, f_ref[...].astype(jnp.float32))
    for g in range(group):
        total = jnp.sum(l[g], axis=1, keepdims=True)
        result = merge_heads(acc[g] / total)
        lse = tops[g] + jnp.log(total)
        for h in range(2):
            start = LSE_LANE + 3 * (2 * (step * group + g) + h)
            for number, piece in enumerate(pieces(lse[h * count : (h + 1) * count])):
                features = jnp.where(lane == start + number, piece, features)
        o_ref[:, g * 128 : (g + 1) * 128] = result
        low_ref[:, g * 128 : (g + 1) * 128] = result.astype(jnp.bfloat16)
    f_ref[...] = features.astype(jnp.bfloat16)


def attend(meta, count, queries, kv, kind, blocks, items, shards, name, group=3):
    width = queries.shape[1]
    pairs = width // 128
    total = kv.shape[0]
    rows = total // blocks
    tile = spread(count, group, 0)
    return pl.pallas_call(
        partial(attend_kernel, items, shards, kind, blocks, group),
        grid=(pairs // group,),
        out_shape=(
            jax.ShapeDtypeStruct((count, width), jnp.float32),
            jax.ShapeDtypeStruct((count, width), jnp.bfloat16),
            jax.ShapeDtypeStruct((count, 128), jnp.bfloat16),
        ),
        in_specs=[
            pl.BlockSpec(memory_space=pltpu.SMEM),
            tile,
            spread(total, group, 0),
            spread(total, group, pairs),
        ],
        out_specs=(tile, tile, pl.BlockSpec((count, 128), lambda p: (0, 0))),
        scratch_shapes=[
            pltpu.VMEM((group, 2 * count, 256), jnp.bfloat16),
            pltpu.VMEM((total, 128), jnp.bfloat16),
            pltpu.VMEM((group, blocks, 2 * count, rows), jnp.float32),
            pltpu.VMEM((group, 2 * count, 128), jnp.float32),
            pltpu.VMEM((group, 2 * count, 128), jnp.float32),
            pltpu.VMEM((group, 2 * count, 128), jnp.float32),
        ],
        compiler_params=pltpu.CompilerParams(vmem_limit_bytes=48 * MIB),
        cost_estimate=pl.CostEstimate(
            flops=2 * count * total * width,
            bytes_accessed=4 * total * width,
            transcendentals=count * total * H // 2,
        ),
        name=name,
    )(meta, queries, kv, kv)


def query_side(pair, features, q, do, qa, da):
    lane = lanes(q.shape[0])
    heads = [2 * pair, 2 * pair + 1]
    stack_heads(qa, q, [jnp.where((lane < LSE_LANE) | head_lanes(lane, LSE_LANE, head), features, 0.0) for head in heads])
    stack_heads(da, do, [jnp.where(head_lanes(lane, DELTA_LANE, head), features, 0.0) for head in heads])


def query_step(qa, da, keys, values, bias):
    minus = jnp.where(delta_lanes(lanes(keys.shape[0])), -1.0, 0.0)
    probs = jnp.exp(times_transposed(qa[...], jnp.concatenate([keys, bias], axis=1)))
    slope = times_transposed(da[...], beside(values, minus))
    return dot((probs * slope).astype(jnp.bfloat16), keys)


def key_side(pair, k, v, mask, ka, va):
    lane = lanes(k.shape[0])
    heads = [2 * pair, 2 * pair + 1]
    stack_heads(ka, k, [jnp.where(head_lanes(lane, LSE_LANE, head), -1.0, mask) for head in heads])
    stack_heads(va, v, [jnp.where(head_lanes(lane, DELTA_LANE, head), -1.0, 0.0) for head in heads])


def key_step(ka, va, q, do, features):
    probs = jnp.exp(times_transposed(ka[...], jnp.concatenate([q, features], axis=1)))
    slope = times_transposed(va[...], jnp.concatenate([do, features], axis=1))
    return dot((probs * slope).astype(jnp.bfloat16), q), dot(probs.astype(jnp.bfloat16), do)


def query_grad_kernel(items, shards, blocks, group, meta, q_ref, do_ref, f_ref, k_ref, v_ref, dq_ref, qa, da, bias_ref, acc):
    count = q_ref.shape[0]
    rows = k_ref.shape[0] // blocks
    frame = Frame(meta, items, count, shards)
    active, bias = block_rule(frame, "frames", rows)
    fill_bias(blocks, rows, active, bias, bias_ref, True)
    features = f_ref[...].astype(jnp.float32)
    for g in range(group):
        pair = pl.program_id(0) * group + g
        query_side(pair, features, heads_of(q_ref, ALL, g), heads_of(do_ref, ALL, g), qa.at[g], da.at[g])
        acc[g] = jnp.zeros((2 * count, 128), jnp.float32)

    def step(block):
        here = rows_of(block, rows)
        for g in range(group):
            acc[g] = acc[g] + query_step(
                qa.at[g], da.at[g], heads_of(k_ref, here, g), heads_of(v_ref, here, g), bias_ref[here, :]
            )

    each_active(blocks, active, step)
    for g in range(group):
        dq_ref[:, g * 128 : (g + 1) * 128] = (merge_heads(acc[g]) * 0.125).astype(jnp.bfloat16)


def query_grad(meta, queries, grad_out, features, kv, blocks, items, shards, name, group=3):
    count, width = grad_out.shape
    pairs = width // 128
    total = kv.shape[0]
    tile = spread(count, group, 0)
    return pl.pallas_call(
        partial(query_grad_kernel, items, shards, blocks, group),
        grid=(pairs // group,),
        out_shape=jax.ShapeDtypeStruct((count, width), jnp.bfloat16),
        in_specs=[
            pl.BlockSpec(memory_space=pltpu.SMEM),
            tile,
            tile,
            pl.BlockSpec((count, 128), lambda p: (0, 0)),
            spread(total, group, 0),
            spread(total, group, pairs),
        ],
        out_specs=tile,
        scratch_shapes=[
            pltpu.VMEM((group, 2 * count, 256), jnp.bfloat16),
            pltpu.VMEM((group, 2 * count, 256), jnp.bfloat16),
            pltpu.VMEM((total, 128), jnp.bfloat16),
            pltpu.VMEM((group, 2 * count, 128), jnp.float32),
        ],
        compiler_params=pltpu.CompilerParams(vmem_limit_bytes=48 * MIB),
        cost_estimate=pl.CostEstimate(
            flops=3 * count * total * width,
            bytes_accessed=4 * total * width,
            transcendentals=count * total * H // 2,
        ),
        name=name,
    )(meta, queries, grad_out, features, kv, kv)


def frame_key_grad_kernel(items, shards, blocks, group, meta, q_ref, k_ref, v_ref, all_ref, dk_ref, dv_ref, ka, va, dka, dva, do_s, sem):
    count, width = dk_ref.shape[0], do_s.shape[1] - 128
    rows = q_ref.shape[0] // blocks
    frame = Frame(meta, items, count, shards)

    def arrivals(act):
        @pl.when(pl.program_id(0) == 0)
        def _():
            for block in range(2 * blocks):
                start, live = frame.chip(jnp.int32(block // 2))
                first = start + (frame.position + block) % 2 * count

                @pl.when(live)
                def _(block=block, first=first):
                    act(
                        pltpu.make_async_copy(
                            all_ref.at[pl.ds(pl.multiple_of(first, count), count), :],
                            do_s.at[pl.ds(block * count, count), :],
                            sem.at[block],
                        )
                    )

    arrivals(lambda copy: copy.start())
    mask = item_bias(frame, frame.items_of_rows(frame.position * count, count))
    for g in range(group):
        pair = pl.program_id(0) * group + g
        key_side(pair, heads_of(k_ref, ALL, g), heads_of(v_ref, ALL, g), mask, ka.at[g], va.at[g])
        dka[g] = jnp.zeros((2 * count, 128), jnp.float32)
        dva[g] = jnp.zeros((2 * count, 128), jnp.float32)
    arrivals(lambda copy: copy.wait())

    def step(block):
        here = rows_of(block, rows)
        for g in range(group):
            column = pl.multiple_of((pl.program_id(0) * group + g) * 128, 128)
            dk, dv = key_step(
                ka.at[g], va.at[g], heads_of(q_ref, here, g), do_s[here, pl.ds(column, 128)], do_s[here, width:]
            )
            dka[g] = dka[g] + dk
            dva[g] = dva[g] + dv

    each_active(blocks, lambda block: frame.chip(block)[1], step)
    for g in range(group):
        dk_ref[:, g * 128 : (g + 1) * 128] = merge_heads(dka[g]).astype(jnp.bfloat16)
        dv_ref[:, g * 128 : (g + 1) * 128] = merge_heads(dva[g]).astype(jnp.bfloat16)


def frame_key_grad(meta, q_window, do_all, kv, count, blocks, items, shards, name, group=3):
    total, width = q_window.shape
    pairs = width // 128
    tile = spread(count, group, 0)
    wide = spread(total, group, 0)
    return pl.pallas_call(
        partial(frame_key_grad_kernel, items, shards, blocks, group),
        grid=(pairs // group,),
        out_shape=(jax.ShapeDtypeStruct((count, width), jnp.bfloat16),) * 2,
        in_specs=[
            pl.BlockSpec(memory_space=pltpu.SMEM),
            wide,
            tile,
            spread(count, group, pairs),
        ]
        + [pl.BlockSpec(memory_space=pl.ANY)],
        out_specs=(tile, tile),
        scratch_shapes=[pltpu.VMEM((group, 2 * count, 256), jnp.bfloat16)] * 2
        + [pltpu.VMEM((group, 2 * count, 128), jnp.float32)] * 2
        + [pltpu.VMEM((total, width + 128), jnp.bfloat16), pltpu.SemaphoreType.DMA((2 * blocks,))],
        compiler_params=pltpu.CompilerParams(vmem_limit_bytes=48 * MIB),
        cost_estimate=pl.CostEstimate(
            flops=4 * count * total * width,
            bytes_accessed=4 * total * width,
            transcendentals=count * total * H // 2,
        ),
        name=name,
    )(meta, q_window, kv, kv, do_all)


def text_grad_kernel(items, shards, group, meta, q_ref, do_ref, f_ref, k_ref, v_ref, dq_ref, dkv_ref, qa, da, ka, va, acc):
    count = q_ref.shape[0]
    rows = k_ref.shape[0] // items
    frame = Frame(meta, items, count, shards)
    features = f_ref[...].astype(jnp.float32)
    pairs = [pl.program_id(0) * group + g for g in range(group)]
    for g in range(group):
        query_side(pairs[g], features, heads_of(q_ref, ALL, g), heads_of(do_ref, ALL, g), qa.at[g], da.at[g])
        acc[g] = jnp.zeros((2 * count, 128), jnp.float32)

    @pl.loop(0, items)
    def _(item):
        here = rows_of(item, rows)
        live = (item >= frame.first) & (item <= frame.last)

        @pl.when(live)
        def _():
            mask = text_bias(frame, item, rows)
            bias = jnp.where(lse_lanes(lanes(rows)), -1.0, mask).astype(jnp.bfloat16)
            for g in range(group):
                keys, values = heads_of(k_ref, here, g), heads_of(v_ref, here, g)
                acc[g] = acc[g] + query_step(qa.at[g], da.at[g], keys, values, bias)
                key_side(pairs[g], keys, values, mask, ka.at[g], va.at[g])
                grads = key_step(ka.at[g], va.at[g], heads_of(q_ref, ALL, g), heads_of(do_ref, ALL, g), f_ref[...])
                for which, grad in enumerate(grads):
                    dkv_ref[which, here, g * 128 : (g + 1) * 128] = merge_heads(grad).astype(jnp.bfloat16)

        @pl.when(jnp.logical_not(live))
        def _():
            for which in range(2):
                dkv_ref[which, here, :] = jnp.zeros((rows, group * 128), jnp.bfloat16)

    for g in range(group):
        dq_ref[:, g * 128 : (g + 1) * 128] = (merge_heads(acc[g]) * 0.125).astype(jnp.bfloat16)


def text_grad(meta, queries, grad_out, features, kv, items, shards, name, group=3):
    count, width = queries.shape
    pairs = width // 128
    total = kv.shape[0]
    tile = spread(count, group, 0)
    rows = total // items
    return pl.pallas_call(
        partial(text_grad_kernel, items, shards, group),
        grid=(pairs // group,),
        out_shape=(
            jax.ShapeDtypeStruct((count, width), jnp.bfloat16),
            jax.ShapeDtypeStruct((2, total, width), jnp.bfloat16),
        ),
        in_specs=[
            pl.BlockSpec(memory_space=pltpu.SMEM),
            tile,
            tile,
            pl.BlockSpec((count, 128), lambda p: (0, 0)),
            spread(total, group, 0),
            spread(total, group, pairs),
        ],
        out_specs=(tile, pl.BlockSpec((2, total, group * 128), lambda p: (0, 0, p))),
        scratch_shapes=[pltpu.VMEM((group, 2 * count, 256), jnp.bfloat16)] * 2
        + [pltpu.VMEM((group, 2 * rows, 256), jnp.bfloat16)] * 2
        + [pltpu.VMEM((group, 2 * count, 128), jnp.float32)],
        compiler_params=pltpu.CompilerParams(vmem_limit_bytes=48 * MIB),
        cost_estimate=pl.CostEstimate(
            flops=7 * count * rows * 2 * width,
            bytes_accessed=8 * total * width,
            transcendentals=count * rows * H * 2,
        ),
        name=name,
    )(meta, queries, grad_out, features, kv, kv)


def mlp_kernel(h_ref, d_ref, up_ref, down_ref, act_ref, m_ref, dh_ref):
    step = pl.program_id(0)
    last = pl.num_programs(0) - 1

    @pl.when(step < last)
    def _():
        u = dot(h_ref[...], up_ref[...])
        slope = times_transposed(d_ref[...], down_ref[...])
        inner = 0.7978845608028654 * (u + 0.044715 * (u * u * u))
        t = jnp.tanh(inner)
        g = (0.5 * u * (1.0 + t)).astype(jnp.bfloat16)
        bend = 0.7978845608028654 * (1.0 + 0.134145 * (u * u))
        du = (slope * (0.5 * (1.0 + t) + 0.5 * u * (1.0 - t * t) * bend)).astype(jnp.bfloat16)
        act_ref[0, 0] = g
        act_ref[0, 1] = du
        m = dot(g, down_ref[...])
        dh = times_transposed(du, up_ref[...])

        @pl.when(step == 0)
        def _():
            m_ref[...] = m
            dh_ref[...] = dh

        @pl.when(step > 0)
        def _():
            m_ref[...] = m_ref[...] + m
            dh_ref[...] = dh_ref[...] + dh

    @pl.when(step == last)
    def _():
        act_ref[0, 0] = h_ref[...]
        act_ref[0, 1] = d_ref[...]


def mlp(hidden, grad, w_up, w_down):
    count, width = hidden.shape
    chunks = w_up.shape[1] // width
    whole = pl.BlockSpec((count, width), lambda c: (0, 0))
    held = lambda c: jnp.minimum(c, chunks - 1)
    return pl.pallas_call(
        mlp_kernel,
        grid=(chunks + 1,),
        out_shape=(
            jax.ShapeDtypeStruct((chunks + 1, 2, count, width), jnp.bfloat16),
            jax.ShapeDtypeStruct((count, width), jnp.float32),
            jax.ShapeDtypeStruct((count, width), jnp.float32),
        ),
        in_specs=[
            whole,
            whole,
            pl.BlockSpec((width, width), lambda c: (0, held(c))),
            pl.BlockSpec((width, width), lambda c: (held(c), 0)),
        ],
        out_specs=(pl.BlockSpec((1, 2, count, width), lambda c: (c, 0, 0, 0)), whole, whole),
        compiler_params=pltpu.CompilerParams(vmem_limit_bytes=40 * MIB),
        cost_estimate=pl.CostEstimate(
            flops=8 * count * width * w_up.shape[1],
            bytes_accessed=4 * width * w_up.shape[1] + 4 * count * w_up.shape[1],
            transcendentals=count * w_up.shape[1],
        ),
        name="mlp",
    )(hidden, grad, w_up, w_down)


UNIT = 192
X_BIT, Y_BIT = 0, 1


def rows_picked(x, core):
    row = lax.broadcasted_iota(jnp.int32, (384, 768), 0)
    column = lax.broadcasted_iota(jnp.int32, (384, 768), 1)
    chip = (row >= 96).astype(jnp.int32) + (row >= 192).astype(jnp.int32) + (row >= 288).astype(jnp.int32)
    pick = (column == row + 96 * (chip + core)).astype(jnp.bfloat16)
    return times_transposed(pick, x).astype(jnp.bfloat16)


def one_above_other(upper, lower):
    return jnp.concatenate([upper, lower], axis=0)


def finish_kernel(items, shards, meta, mod_ref, w_ref, d_ref, x_ref, dx_ref, a_ref, dh_ref, n_ref, dy_ref, m_ref, out_ref, sum_ref):
    count, width = x_ref.shape
    frame = Frame(meta, items, count, shards)
    item = frame.items_of_rows(frame.position * count, count)
    grad = times_transposed(d_ref[...], w_ref[...])
    normed, inverse = layer_norm(x_ref[...].astype(jnp.float32))
    scale = jnp.zeros((count, width), jnp.float32)
    for i in range(items):
        scale = jnp.where(item == i, mod_ref[i, 1:2, :], scale)
    dx = dx_ref[...]
    out_ref[...] = dx + norm_back(grad * (1.0 + scale), normed, inverse)
    dh = dh_ref[...]
    terms = (
        grad,
        grad * normed,
        dx * a_ref[...],
        dh,
        dh * n_ref[...],
        dy_ref[...].astype(jnp.float32) * m_ref[...],
    )
    for number, term in enumerate(terms):
        rows = [jnp.sum(jnp.where(item == i, term, 0.0), axis=0, keepdims=True) for i in range(items)]
        rows += [jnp.zeros((8 - items, width), jnp.float32)]
        sum_ref[number] = jnp.concatenate(rows, axis=0)


def finish(meta, modulation, weight, grads, frames, *arrays_items_shards):
    *arrays, items, shards = arrays_items_shards
    count, width = frames.shape
    whole = pl.BlockSpec(memory_space=pltpu.VMEM)
    return pl.pallas_call(
        partial(finish_kernel, items, shards),
        out_shape=(
            jax.ShapeDtypeStruct((count, width), jnp.float32),
            jax.ShapeDtypeStruct((6, 8, width), jnp.float32),
        ),
        in_specs=[pl.BlockSpec(memory_space=pltpu.SMEM)] + [whole] * (4 + len(arrays)),
        out_specs=(whole, whole),
        compiler_params=pltpu.CompilerParams(vmem_limit_bytes=40 * MIB),
        cost_estimate=pl.CostEstimate(
            flops=6 * count * width * width, bytes_accessed=6 * width * width + 30 * count * width, transcendentals=0
        ),
        name="finish",
    )(meta, modulation, weight, grads, frames, *arrays)


class Packer:
    def __init__(self, meta, items, outputs):
        self.core, self.chip = meta[0] % 2, meta[0] // 2
        self.mine = meta[1 + 2 * items]
        self.outputs = outputs

    def store(self, name, owner, owner_chip, row, values):
        scratch, first = self.outputs[name]
        relative = owner ^ self.mine
        where = ((relative >> first) % 2, (relative >> (1 - first)) % 2, owner_chip ^ self.chip)
        scratch[where + (slice(row, row + values.shape[0]),)] = values.astype(jnp.bfloat16)

    def store_split(self, name, pair, row, values, chips):
        rolled = pltpu.roll(values, UNIT, 1)
        each = values.shape[0] // len(chips)
        left = lax.broadcasted_iota(jnp.int32, (each // 2, 384), 1) < UNIT
        for number, owner_chip in enumerate(chips):
            upper = slice(number * each, number * each + each // 2)
            lower = slice(number * each + each // 2, (number + 1) * each)
            self.store(name, 2 * pair, owner_chip, row, jnp.where(left, values[upper], rolled[lower]))
            self.store(name, 2 * pair + 1, owner_chip, row, jnp.where(left, rolled[upper], values[lower]))


def core_columns(core, number, each):
    return pl.ds(pl.multiple_of(number * 2 * each + core * each, 128), each)


def third(values, number):
    return values[:, number * 384 : (number + 1) * 384]


def pack_mlp_kernel(items, meta, own, sib, down_s, up_s):
    packer = Packer(meta, items, {"down": (down_s, Y_BIT), "up": (up_s, X_BIT)})
    both = lambda chunk, which: one_above_other(own[chunk, which], sib[chunk, which])
    grad = both(4, 1)
    for owner_chip in range(4):
        here = core_columns(packer.core, 0, 384)
        left = one_above_other(own[owner_chip, 0, :, here], sib[owner_chip, 0, :, here])
        values = contract_rows(left, grad)
        for pair in range(2):
            packer.store_split("down", pair, 0, third(values, pair), [owner_chip])
    left = rows_picked(both(4, 0), packer.core)
    for owner in range(4):
        values = dot(left, both(owner, 1))
        for owner_chip in range(4):
            for half in range(2):
                packer.store(
                    "up", owner, owner_chip, half * 96, third(values, half)[owner_chip * 96 : (owner_chip + 1) * 96]
                )


def pack_middle_kernel(items, meta, own, sib, text_own, text_sib, text, rows_ref, square_s, text_s):
    packer = Packer(meta, items, {"square": (square_s, Y_BIT), "text": (text_s, X_BIT)})
    both = lambda which: one_above_other(own[which], sib[which])
    for number in range(3):
        values = dot(rows_picked(both(2 * number), packer.core), both(2 * number + 1))
        for pair in range(2):
            packer.store_split("square", pair, number * 48, third(values, pair), range(4))
    sums = [
        (text_own[which].astype(jnp.float32) + text_sib[which].astype(jnp.float32)).astype(jnp.bfloat16)
        for which in range(2)
    ]
    left = jnp.concatenate([text[:, core_columns(packer.core, chip, 128)] for chip in range(4)], axis=1)
    for which in range(2):
        values = contract_rows(left, sums[which])
        for owner_chip in range(4):
            for half in range(2):
                packer.store(
                    "text", 2 * which + half, owner_chip, 0, third(values, half)[owner_chip * 128 : (owner_chip + 1) * 128]
                )
    share = text.shape[0] // items // 8
    for item in range(items):
        for which in range(2):
            for owner_chip in range(4):
                start = (item * 8 + owner_chip * 2) * share
                pick = jnp.where(
                    packer.core == 0, sums[which][start : start + share], sums[which][start + share : start + 2 * share]
                )
                rows_ref[owner_chip ^ packer.chip, which, item * share : (item + 1) * share, :] = pick


def pack_qkv_kernel(items, meta, h_own, h_sib, own, sib, plain_s, split_s):
    packer = Packer(meta, items, {"plain": (plain_s, X_BIT), "split": (split_s, Y_BIT)})
    left = rows_picked(one_above_other(h_own[...], h_sib[...]), packer.core)
    values = []
    for number in range(3):
        product = dot(left, one_above_other(own[number], sib[number]))
        values += [third(product, 0), third(product, 1)]
    for owner, column in enumerate((0, 2, 3, 5)):
        for owner_chip in range(4):
            packer.store("plain", owner, owner_chip, 0, values[column][owner_chip * 96 : (owner_chip + 1) * 96])
    for pair, column in enumerate((1, 4)):
        packer.store_split("split", pair, 0, values[column], range(4))


def packing(kernel, items, inputs, groups, more, *refs):
    ins, refs = refs[:inputs], refs[inputs:]
    outs, extra, scratch, sem = refs[: 2 * groups], refs[2 * groups : -groups - 1], refs[-groups - 1 : -1], refs[-1]
    kernel(items, *ins, *extra, *scratch)
    copies = [
        pltpu.make_async_copy(scratch[i // 2].at[1 - i % 2], outs[i], sem.at[i]) for i in range(2 * groups)
    ]
    for copy in copies:
        copy.start()
    for copy in copies:
        copy.wait()


def pack(kernel, meta, operands, rows, items, name, more=()):
    whole = pl.BlockSpec(memory_space=pltpu.VMEM)
    shapes = [jax.ShapeDtypeStruct((2, 4, each, 384), jnp.bfloat16) for each in rows for _ in range(2)] + list(more)
    return pl.pallas_call(
        partial(packing, kernel, items, 1 + len(operands), len(rows), more),
        out_shape=tuple(shapes),
        in_specs=[pl.BlockSpec(memory_space=pltpu.SMEM)] + [whole] * len(operands),
        out_specs=tuple([pl.BlockSpec(memory_space=pl.ANY)] * (2 * len(rows)) + [whole] * len(more)),
        scratch_shapes=[pltpu.VMEM((2, 2, 4, each, 384), jnp.bfloat16) for each in rows]
        + [pltpu.SemaphoreType.DMA((2 * len(rows),))],
        compiler_params=pltpu.CompilerParams(vmem_limit_bytes=48 * MIB),
        cost_estimate=pl.CostEstimate(
            flops=2 * 512 * 16 * sum(rows) * 384,
            bytes_accessed=32 * sum(rows) * 384 + 2 * sum(each.size for each in operands),
            transcendentals=0,
        ),
        name=name,
    )(meta, *operands)


def trade(values, axis, bit):
    size = lax.axis_size(axis)
    return lax.ppermute(values, axis, [(i, i ^ (1 << bit)) for i in range(size)])


def halve(keep, send, axis, bit, after=()):
    got = trade(send, axis, bit)
    if after:
        [keep] = hold((keep,), *after)
    return keep.astype(jnp.float32) + got.astype(jnp.float32)


def over_batch(send, keep, first, after=((), ())):
    part = halve(keep, send, "batch", first, after[0]).astype(jnp.bfloat16)
    return halve(part[0], part[1], "batch", 1 - first, after[1]).astype(jnp.bfloat16)


def over_chips(part, after=((), ())):
    part = part.reshape(2, 2, *part.shape[1:])
    part = halve(part[:, 0], part[:, 1], "seq", 1, after[0]).astype(jnp.bfloat16)
    return halve(part[0], part[1], "seq", 2, after[1])


def unsplit(rows):
    return jnp.concatenate([rows[:, :UNIT], rows[:, UNIT:]], axis=0)


def with_deltas(features, grad_out, attn_exact):
    width = attn_exact.shape[1]
    lane = jnp.arange(128)[None, :]
    head = (jnp.arange(width) // (width // H))[:, None]
    pick = ((lane >= DELTA_LANE) & ((lane - DELTA_LANE) // 3 == head)).astype(jnp.float32)
    delta = jnp.dot(
        grad_out.astype(jnp.float32) * attn_exact,
        pick,
        precision=lax.Precision.HIGHEST,
        preferred_element_type=jnp.float32,
    )
    high = lax.reduce_precision(delta, 8, 7)
    middle = lax.reduce_precision(delta - high, 8, 7)
    which = (lane - DELTA_LANE) % 3
    piece = jnp.where(which == 0, high, jnp.where(which == 1, middle, delta - high - middle))
    inside = (lane >= DELTA_LANE) & (lane < DELTA_LANE + 3 * H)
    return jnp.where(inside, piece.astype(jnp.bfloat16), features)


def hop(below, above, shards):
    up = [(i, i + 2) for i in range(shards - 2)]
    return lax.ppermute(below, "seq", up), lax.ppermute(above, "seq", [(j, i) for i, j in up])


def hold(values, *first):
    held = lax.optimization_barrier((*values, *first))
    return held[: len(values)]


def body(
    frames,
    cotangent,
    modulation,
    lengths,
    text,
    text_len,
    w_qkv,
    w_o,
    w_cq,
    w_ckv,
    w_co,
    w_up,
    w_down,
):
    local = frames[0]
    count, width = local.shape
    items = lengths.shape[1]
    text_rows, text_width = text.shape[2:]
    shards = lax.axis_size("seq")
    position = lax.axis_index("seq")
    reach = min(-(-(LONGEST - 1) // (2 * count)), shards // 2 - 1)
    chips = 1 + 2 * reach
    meta = jnp.concatenate(
        [position[None].astype(jnp.int32), lengths[0], text_len[0], lax.axis_index("batch")[None].astype(jnp.int32)]
    )
    item_range = jnp.arange(items, dtype=jnp.int32)
    ends = jnp.sum(jnp.where(item_range[None, :] <= item_range[:, None], lengths[0][None, :], 0), axis=1)
    place = position * count + jnp.arange(count, dtype=jnp.int32)
    query_items = jnp.sum((place[:, None] >= ends[None, :]).astype(jnp.int32), axis=1)[:, None]
    mod = modulation[0]

    def per_frame(which):
        found = jnp.broadcast_to(mod[0, which][None, :], (count, width))
        for item in range(1, items):
            found = jnp.where(query_items == item, mod[item, which][None, :], found)
        return found

    swap = [(i, i ^ 1) for i in range(shards)]

    def sibling(values):
        return lax.ppermute(values, "seq", swap)

    fast = shards == 8 and lax.axis_size("batch") == 4 and width == 768

    text_proj = jnp.dot(
        text[0].reshape(items * text_rows, text_width), w_ckv, preferred_element_type=jnp.float32
    ).astype(jnp.bfloat16)
    sides = list(hold(hop(local, local, shards), text_proj))
    for _ in range(1, reach):
        sides += hop(*sides[-2:], shards)

    def with_siblings(blocks):
        return [each for block in blocks for each in (block, sibling(block))]

    total = 2 * chips * count
    near = with_siblings([local] + sides[:2])
    q_window, kv, hidden_one = project(meta, mod, w_qkv, near, range(3), total, (), items, shards, "project_near")
    if reach > 1:
        apart = with_siblings(hold(sides[2:], kv))
        q_window, kv, _ = project(
            meta, mod, w_qkv, apart, range(3, chips), total, (q_window, kv), items, shards, "project_far"
        )
    inputs = local.astype(jnp.float32)
    attn_exact, attended, features = attend(meta, count, q_window, kv, "frames", chips, items, shards, "self_attend")
    if fast:
        hidden_sib = sibling(hidden_one)
        [attended] = hold((attended,), hidden_sib)
    branch_one = jnp.dot(attended, w_o, preferred_element_type=jnp.float32)
    after_attn = inputs + per_frame(2) * branch_one
    normed_cross, inverse_cross = layer_norm(after_attn)
    cross_in = normed_cross.astype(jnp.bfloat16)
    cross_queries = jnp.dot(cross_in, w_cq, preferred_element_type=jnp.float32).astype(jnp.bfloat16)
    cross_queries = (cross_queries.astype(jnp.float32) * 0.125).astype(jnp.bfloat16)
    cross_exact, cross_out, cross_features = attend(
        meta, count, cross_queries, text_proj, "text", items, items, shards, "cross_attend"
    )
    branch_two = jnp.dot(cross_out, w_co, preferred_element_type=jnp.float32)
    after_cross = after_attn + branch_two
    normed_two, inverse_two = layer_norm(after_cross)
    hidden_two = (normed_two * (1.0 + per_frame(4)) + per_frame(3)).astype(jnp.bfloat16)
    gate_two = per_frame(5)
    grad_out = cotangent[0].astype(jnp.float32)
    grad_branch_three = (grad_out * gate_two).astype(jnp.bfloat16)
    acts, branch_three, grad_hidden_two = mlp(hidden_two, grad_branch_three, w_up, w_down)
    if fast:
        mlp_parts = pack(
            pack_mlp_kernel, meta, (acts, sibling(acts)), (192, 192), items, "pack_mlp"
        )
    result = after_cross + gate_two * branch_three
    grad_cross = grad_out + norm_back(grad_hidden_two * (1.0 + per_frame(4)), normed_two, inverse_two)
    grad_branch_two = grad_cross.astype(jnp.bfloat16)
    if fast:
        grad_branch_two, *mlp_parts = lax.optimization_barrier((grad_branch_two, *mlp_parts))
    grad_cross_out = times_transposed(grad_branch_two, w_co).astype(jnp.bfloat16)
    cross_features = with_deltas(cross_features, grad_cross_out, cross_exact)
    grad_cross_queries, text_terms = text_grad(
        meta, cross_queries, grad_cross_out, cross_features, text_proj, items, shards, "cross_grad"
    )
    grad_attn_res = grad_cross + norm_back(
        times_transposed(grad_cross_queries, w_cq), normed_cross, inverse_cross
    )
    grad_branch_one = (grad_attn_res * per_frame(2)).astype(jnp.bfloat16)
    if fast:
        text_sib = sibling(text_terms)
        [grad_branch_one] = hold((grad_branch_one,), text_sib)
    grad_attended = times_transposed(grad_branch_one, w_o).astype(jnp.bfloat16)
    features = with_deltas(features, grad_attended, attn_exact)
    if fast:
        middle = jnp.stack([cross_out, grad_branch_two, cross_in, grad_cross_queries, attended, grad_branch_one])
        middle_sib = sibling(middle)
    do_all = lax.all_gather(jnp.concatenate([grad_attended, features], axis=1), "seq", axis=0, tiled=True)
    grad_queries = query_grad(
        meta, q_window, grad_attended, features, kv, chips, items, shards, "self_query_grad"
    )
    share_rows = text_rows // shards
    if fast:
        middle_parts = pack(
            pack_middle_kernel,
            meta,
            (middle, middle_sib, text_terms, text_sib, text[0].reshape(items * text_rows, text_width)),
            (144, 128),
            items,
            "pack_middle",
            (jax.ShapeDtypeStruct((4, 2, items * share_rows, width), jnp.bfloat16),),
        )
        [do_all] = hold((do_all,), middle_parts[0])
    grad_keys, grad_values = frame_key_grad(
        meta, q_window, do_all, kv, count, chips, items, shards, "self_key_grad"
    )
    grad_projected = jnp.concatenate([grad_queries, grad_keys, grad_values], axis=1)
    if fast:
        kv_own = jnp.stack([grad_queries, grad_keys, grad_values])
        kv_sib = sibling(kv_own)
        qkv_parts = pack(
            pack_qkv_kernel,
            meta,
            (hidden_one, hidden_sib, kv_own, kv_sib),
            (96, 48),
            items,
            "pack_qkv",
        )
        [grad_projected] = hold((grad_projected,), *qkv_parts)
    grad_inputs, terms = finish(
        meta, mod, w_qkv, grad_projected, local, grad_attn_res, branch_one, grad_hidden_two, normed_two, cotangent[0],
        branch_three, items, shards,
    )
    for bit in range(shards.bit_length() - 1):
        terms = terms + trade(terms, "seq", bit)
    own = width // shards
    terms = lax.dynamic_slice_in_dim(terms, position * own, own, 2)
    shares = terms[:, :items].transpose(1, 0, 2)
    if fast:
        points = ((grad_queries,), (middle_parts[0],))
        down_part = over_batch(*mlp_parts[:2], Y_BIT, points)
        up_part = over_batch(*mlp_parts[2:], X_BIT, points)
        first_rows = over_chips(
            jnp.concatenate([down_part, up_part], axis=1), ((grad_keys,), (qkv_parts[0],))
        )
        points = ((grad_keys,), (qkv_parts[0],))
        square_send, square_keep, text_send, text_keep, text_part = middle_parts
        text_total = over_chips(text_part, points).astype(jnp.bfloat16)
        square_part = over_batch(square_send, square_keep, Y_BIT, points)
        text_w_part = over_batch(text_send, text_keep, X_BIT, points)
        middle_rows = over_chips(jnp.concatenate([square_part, text_w_part], axis=1))
        plain_send, plain_keep, split_send, split_keep = qkv_parts
        plain_part, split_part = over_batch(plain_send, plain_keep, X_BIT), over_batch(split_send, split_keep, Y_BIT)
        last_rows = over_chips(jnp.concatenate([plain_part, split_part], axis=1))
        plain, split = last_rows[:96], unsplit(last_rows[96:])
        even = lax.axis_index("batch") % 2 == 0
        grads = (
            jnp.where(even, jnp.concatenate([plain, split], axis=1), jnp.concatenate([split, plain], axis=1)),
            unsplit(middle_rows[96:144]),
            unsplit(middle_rows[48:96]),
            middle_rows[144:],
            unsplit(middle_rows[:48]),
            jnp.concatenate([first_rows[192:288], first_rows[288:]], axis=1),
            unsplit(first_rows[:192]),
        )
    else:
        shared = text_terms.reshape(2, items, shards, share_rows, width).transpose(2, 0, 1, 3, 4)
        text_total = lax.psum_scatter(shared, "seq", scatter_dimension=0, tiled=True)
        text_total = text_total.reshape(2, items * share_rows, width)
    text_grad_low = jnp.concatenate([text_total[0], text_total[1]], axis=1)
    grad_text = times_transposed(text_grad_low, w_ckv).reshape(1, items, share_rows, text_width)
    if not fast:
        text_mine = lax.dynamic_slice_in_dim(text[0], position * share_rows, share_rows, 1)
        grads = reduced_grads(
            (hidden_one, grad_projected),
            (attended, grad_branch_one),
            (cross_in, grad_cross_queries),
            (text_mine.reshape(items * share_rows, text_width), text_grad_low),
            (cross_out, grad_branch_two),
            (hidden_two, acts[:-1, 1].transpose(1, 0, 2).reshape(count, -1)),
            (acts[:-1, 0].transpose(1, 0, 2).reshape(count, -1), grad_branch_three),
        )
    return (
        result.astype(jnp.bfloat16)[None],
        grad_inputs[None],
        shares[:, :3][None],
        shares[:, 3:][None],
        grad_text,
        *grads,
    )


def reduced_grads(*pairs):
    def reduce_weight(left, right):
        grad = contract_rows(left, right).astype(jnp.bfloat16)
        part = lax.psum_scatter(grad, "seq", scatter_dimension=0, tiled=True)
        return lax.psum_scatter(part, "batch", scatter_dimension=1, tiled=True).astype(jnp.float32)

    return tuple(reduce_weight(*pair) for pair in pairs)


def solution(mesh):
    in_specs = (
        P("batch", "seq", None),
        P("batch", "seq", None),
        P("batch", None, None, None),
        P("batch", None),
        P("batch", None, None, None),
        P("batch", None),
        P(),
        P(),
        P(),
        P(),
        P(),
        P(),
        P(),
    )
    out_specs = (
        P("batch", "seq", None),
        P("batch", "seq", None),
        P("batch", None, None, "seq"),
        P("batch", None, None, "seq"),
        P("batch", None, "seq", None),
        P("seq", "batch"),
        P("seq", "batch"),
        P("seq", "batch"),
        P("seq", "batch"),
        P("seq", "batch"),
        P("seq", "batch"),
        P("seq", "batch"),
    )
    return jax.shard_map(body, mesh=mesh, in_specs=in_specs, out_specs=out_specs, check_vma=False)
```

```python
from functools import partial

import jax
import jax.numpy as jnp
from jax import lax
from jax.experimental import pallas as pl
from jax.experimental.pallas import tpu as pltpu
from jax.sharding import PartitionSpec as P

H = 12
LONGEST = 1024

epsilon = 1e-06
far = -1e30
LSE_LANE = 8
DELTA_LANE = 44
MIB = 1 << 20
FLOPS_EACH, BYTES_EACH = 5e+08, 1.65e+06


def layer_norm(values):
    centred = values - jnp.mean(values, axis=-1, keepdims=True)
    inverse = lax.rsqrt(jnp.mean(centred * centred, axis=-1, keepdims=True) + epsilon)
    return (centred * inverse, inverse)


def norm_back(grad_normed, normed, inverse):
    return inverse * (
        grad_normed
        - jnp.mean(grad_normed, axis=-1, keepdims=True)
        - normed * jnp.mean(grad_normed * normed, axis=-1, keepdims=True)
    )


def contract_rows(left, right):
    return lax.dot_general(
        left, right, (((0,), (0,)), ((), ())), preferred_element_type=jnp.float32
    )


def times_transposed(left, right):
    return lax.dot_general(
        left, right, (((1,), (1,)), ((), ())), preferred_element_type=jnp.float32
    )


class Frame:
    def __init__(self, meta, items, count, shards):
        self.position = meta[0]
        self.items = items
        self.count = count
        self.shards = shards
        self.ends = []
        total = jnp.int32(0)
        for item in range(items):
            total = total + meta[1 + item]
            self.ends.append(total)
        self.text_len = [meta[1 + items + item] for item in range(items)]
        self.first = self.item_of(self.position * count)
        self.last = self.item_of(self.position * count + count - 1)
        self.low = jnp.int32(0)
        self.high = jnp.int32(0)
        for item in range(items):
            start = self.ends[item] - meta[1 + item]
            self.low = jnp.where(self.first == item, start, self.low)
            self.high = jnp.where(self.last == item, self.ends[item], self.high)

    def item_of(self, place):
        found = jnp.int32(0)
        for end in self.ends:
            found = found + (place >= end).astype(jnp.int32)
        return found

    def items_of_rows(self, base, rows):
        place = base + lax.broadcasted_iota(jnp.int32, (rows, 1), 0)
        found = jnp.zeros((rows, 1), jnp.int32)
        for end in self.ends:
            found = found + (place >= end).astype(jnp.int32)
        return found

    def items_of_chip(self, block):
        start, _ = self.chip(block)
        core = self.position % 2
        return jnp.concatenate(
            [
                self.items_of_rows(start + core * self.count, self.count),
                self.items_of_rows(start + (1 - core) * self.count, self.count),
            ],
            axis=0,
        )

    def chip(self, block):
        hop = (block + 1) // 2
        chip = self.position // 2 + jnp.where(block % 2 == 1, -hop, hop)
        rows = 2 * self.count
        start = chip * rows
        live = (chip >= 0) & (chip < self.shards // 2)
        return start, live & (start < self.high) & (start + rows > self.low)


def lanes(rows):
    return lax.broadcasted_iota(jnp.int32, (rows, 128), 1)


def lse_lanes(lane):
    return (lane >= LSE_LANE) & (lane < DELTA_LANE)


def delta_lanes(lane):
    return (lane >= DELTA_LANE) & (lane < DELTA_LANE + 3 * H)


def head_lanes(lane, base, head):
    start = base + 3 * head
    return (lane >= start) & (lane < start + 3)


def cost(microseconds):
    return pl.CostEstimate(
        flops=int(microseconds * FLOPS_EACH), bytes_accessed=int(microseconds * BYTES_EACH), transcendentals=0
    )


def beside(left, right):
    return jnp.concatenate([left.astype(jnp.bfloat16), right.astype(jnp.bfloat16)], axis=1)


def pieces(values):
    high = values.astype(jnp.bfloat16).astype(jnp.float32)
    rest = values - high
    middle = rest.astype(jnp.bfloat16).astype(jnp.float32)
    return high, middle, rest - middle


def dot(left, right):
    return jnp.dot(left, right, preferred_element_type=jnp.float32)


def stack_heads(target, values, features):
    rows = values.shape[0]
    half = lanes(rows) // 64
    wide = values.astype(jnp.float32)
    for h in range(2):
        target[h * rows : (h + 1) * rows, :] = beside(jnp.where(half == h, wide, 0.0), features[h])


def merge_heads(stacked):
    rows = stacked.shape[0] // 2
    return jnp.where(lanes(rows) < 64, stacked[:rows], stacked[rows:])


def item_bias(frame, item):
    lane = lanes(item.shape[0])
    return jnp.where((lane != item) & (lane < frame.items), far, 0.0)


def text_bias(frame, block, rows):
    slot = lax.broadcasted_iota(jnp.int32, (rows, 1), 0)
    length = jnp.int32(0)
    for item in range(frame.items):
        length = jnp.where(block == item, frame.text_len[item], length)
    lane = lanes(rows)
    dead = (lane != block) | (slot >= length)
    return jnp.where(dead & (lane < frame.items), far, 0.0)


def block_rule(frame, kind, rows):
    if kind == "frames":
        return (
            lambda block: frame.chip(block)[1],
            lambda block: item_bias(frame, frame.items_of_chip(block)),
        )
    return (
        lambda block: (block >= frame.first) & (block <= frame.last),
        lambda block: text_bias(frame, block, rows),
    )


def rows_of(block, rows):
    return pl.ds(pl.multiple_of(block * rows, rows), rows)


def each_active(blocks, active, step):
    @pl.loop(0, blocks)
    def _(block):
        @pl.when(active(block))
        def _():
            step(block)


def fill_bias(blocks, rows, active, bias, target, with_lse):
    @pl.when(pl.program_id(0) == 0)
    def _():
        def step(block):
            mask = bias(block)
            if with_lse:
                mask = jnp.where(lse_lanes(lanes(rows)), -1.0, mask)
            target[rows_of(block, rows), :] = mask.astype(jnp.bfloat16)

        each_active(blocks, active, step)


def project_kernel(items, shards, chips, meta, mod_ref, w_hbm, *refs):
    number = len(chips)
    x_refs = refs[: 2 * number]
    q_ref, kv_ref, own_ref, x_s, h_s, q_s, kv_s, w_ref, in_sem, out_sem, w_sem = refs[-11:]
    weights = pltpu.make_async_copy(w_hbm, w_ref, w_sem)
    count, width = x_refs[0].shape
    rows = 2 * count
    frame = Frame(meta, items, count, shards)

    def live(index):
        return frame.chip(index + chips[0])[1]

    for index in range(number):

        @pl.when(live(jnp.int32(index)))
        def _(index=index):
            for part in range(2):
                block = 2 * index + part
                pltpu.make_async_copy(
                    x_refs[block], x_s.at[pl.ds(block * count, count), :], in_sem.at[block]
                ).start()

    weights.start()

    def writes(index):
        here = rows_of(index, rows)
        there = rows_of(index + chips[0], rows)
        return (
            pltpu.make_async_copy(q_s.at[here, :], q_ref.at[there, :], out_sem.at[2 * index]),
            pltpu.make_async_copy(kv_s.at[here, :], kv_ref.at[there, :], out_sem.at[2 * index + 1]),
        )

    def hide(index):
        @pl.when(live(index))
        def _():
            start = frame.chip(index + chips[0])[0]
            for part in range(2):
                block = 2 * index + part
                here = rows_of(block, count)
                pltpu.make_async_copy(x_refs[0], x_s.at[here, :], in_sem.at[block]).wait()
                normed, _ = layer_norm(x_s[here, :].astype(jnp.float32))
                item = frame.items_of_rows(start + (frame.position + part) % 2 * count, count)
                shift = jnp.broadcast_to(mod_ref[0, 0:1, :], normed.shape)
                scale = jnp.broadcast_to(mod_ref[0, 1:2, :], normed.shape)
                for i in range(1, items):
                    shift = jnp.where(item == i, mod_ref[i, 0:1, :], shift)
                    scale = jnp.where(item == i, mod_ref[i, 1:2, :], scale)
                h_s[part * count : (part + 1) * count, :] = (normed * (1.0 + scale) + shift).astype(jnp.bfloat16)
    def multiply(index):
        @pl.when(live(index))
        def _():
            both = rows_of(index, rows)
            hidden = h_s[...]
            q = dot(hidden, w_ref[:, :width]).astype(jnp.bfloat16)
            q_s[both, :] = (q.astype(jnp.float32) * 0.125).astype(jnp.bfloat16)
            kv_s[both, :width] = dot(hidden, w_ref[:, width : 2 * width]).astype(jnp.bfloat16)
            kv_s[both, width:] = dot(hidden, w_ref[:, 2 * width :]).astype(jnp.bfloat16)
            for write in writes(index):
                write.start()

    hide(jnp.int32(0))
    own_ref[...] = h_s[:count, :]
    weights.wait()
    multiply(jnp.int32(0))

    @pl.loop(1, number)
    def _(index):
        hide(index)
        multiply(index)

    @pl.loop(0, number)
    def _(index):
        @pl.when(live(index))
        def _():
            for write in writes(index):
                write.wait()


def project(meta, modulation, weight, x_blocks, chips, total, earlier, items, shards, name):
    count, width = x_blocks[0].shape
    part = len(x_blocks) * count
    whole = pl.BlockSpec(memory_space=pltpu.VMEM)
    anywhere = pl.BlockSpec(memory_space=pl.ANY)
    before = 3 + len(x_blocks)
    return pl.pallas_call(
        partial(project_kernel, items, shards, chips),
        out_shape=(
            jax.ShapeDtypeStruct((total, width), jnp.bfloat16),
            jax.ShapeDtypeStruct((total, 2 * width), jnp.bfloat16),
            jax.ShapeDtypeStruct((count, width), jnp.bfloat16),
        ),
        in_specs=[pl.BlockSpec(memory_space=pltpu.SMEM), whole]
        + [anywhere] * (1 + len(x_blocks) + len(earlier)),
        out_specs=(anywhere, anywhere, whole),
        input_output_aliases={before: 0, before + 1: 1} if earlier else {},
        scratch_shapes=[
            pltpu.VMEM((part, width), jnp.bfloat16),
            pltpu.VMEM((2 * count, width), jnp.bfloat16),
            pltpu.VMEM((part, width), jnp.bfloat16),
            pltpu.VMEM((part, 2 * width), jnp.bfloat16),
            pltpu.VMEM(weight.shape, jnp.bfloat16),
            pltpu.SemaphoreType.DMA((len(x_blocks),)),
            pltpu.SemaphoreType.DMA((len(x_blocks),)),
            pltpu.SemaphoreType.DMA,
        ],
        compiler_params=pltpu.CompilerParams(vmem_limit_bytes=40 * MIB),
        cost_estimate=cost(len(x_blocks) * 1.5),
        name=name,
    )(meta, modulation, weight, *x_blocks, *earlier)


def heads_of(ref, here, pair):
    return ref[here, pair * 128 : (pair + 1) * 128]


def spread(count, group, base):
    return pl.BlockSpec((count, group * 128), lambda p: (0, p + base // group))


ALL = slice(None)


def attend_kernel(items, shards, kind, blocks, group, meta, q_ref, k_ref, v_ref, o_ref, low_ref, f_ref, qa, bias_ref, s, m, l, acc):
    count = q_ref.shape[0]
    rows = k_ref.shape[0] // blocks
    frame = Frame(meta, items, count, shards)
    active, bias = block_rule(frame, kind, rows)
    step = pl.program_id(0)
    lane = lanes(count)
    own = frame.items_of_rows(frame.position * count, count)
    own_item = (lane == own).astype(jnp.float32)
    fill_bias(blocks, rows, active, bias, bias_ref, False)
    for g in range(group):
        stack_heads(qa.at[g], heads_of(q_ref, ALL, g), [own_item, own_item])
        m[g] = jnp.full((2 * count, 128), far, jnp.float32)
        l[g] = jnp.zeros((2 * count, 128), jnp.float32)
        acc[g] = jnp.zeros((2 * count, 128), jnp.float32)

    def score(block):
        here = rows_of(block, rows)
        for g in range(group):
            scores = times_transposed(qa[g], jnp.concatenate([heads_of(k_ref, here, g), bias_ref[here, :]], axis=1))
            s[g, block] = scores
            high = m[g]
            for c in range(rows // 128):
                high = jnp.maximum(high, scores[:, c * 128 : (c + 1) * 128])
            m[g] = high

    each_active(blocks, active, score)
    tops = []
    for g in range(group):
        tops.append(jnp.max(m[g], axis=1, keepdims=True))
        m[g] = jnp.broadcast_to(tops[g], (2 * count, 128))

    def weigh(block):
        here = rows_of(block, rows)
        for g in range(group):
            high = m[g]
            total = l[g]
            parts = []
            for c in range(rows // 128):
                part = jnp.exp(s[g, block, :, c * 128 : (c + 1) * 128] - high)
                total = total + part
                parts.append(part.astype(jnp.bfloat16))
            l[g] = total
            acc[g] = acc[g] + dot(jnp.concatenate(parts, axis=1), heads_of(v_ref, here, g))

    each_active(blocks, active, weigh)
    features = jnp.where(step == 0, own_item, f_ref[...].astype(jnp.float32))
    for g in range(group):
        total = jnp.sum(l[g], axis=1, keepdims=True)
        result = merge_heads(acc[g] / total)
        lse = tops[g] + jnp.log(total)
        for h in range(2):
            start = LSE_LANE + 3 * (2 * (step * group + g) + h)
            for number, piece in enumerate(pieces(lse[h * count : (h + 1) * count])):
                features = jnp.where(lane == start + number, piece, features)
        o_ref[:, g * 128 : (g + 1) * 128] = result
        low_ref[:, g * 128 : (g + 1) * 128] = result.astype(jnp.bfloat16)
    f_ref[...] = features.astype(jnp.bfloat16)


def attend(meta, count, queries, kv, kind, blocks, items, shards, name, group=3):
    width = queries.shape[1]
    pairs = width // 128
    total = kv.shape[0]
    rows = total // blocks
    tile = spread(count, group, 0)
    return pl.pallas_call(
        partial(attend_kernel, items, shards, kind, blocks, group),
        grid=(pairs // group,),
        out_shape=(
            jax.ShapeDtypeStruct((count, width), jnp.float32),
            jax.ShapeDtypeStruct((count, width), jnp.bfloat16),
            jax.ShapeDtypeStruct((count, 128), jnp.bfloat16),
        ),
        in_specs=[
            pl.BlockSpec(memory_space=pltpu.SMEM),
            tile,
            spread(total, group, 0),
            spread(total, group, pairs),
        ],
        out_specs=(tile, tile, pl.BlockSpec((count, 128), lambda p: (0, 0))),
        scratch_shapes=[
            pltpu.VMEM((group, 2 * count, 256), jnp.bfloat16),
            pltpu.VMEM((total, 128), jnp.bfloat16),
            pltpu.VMEM((group, blocks, 2 * count, rows), jnp.float32),
            pltpu.VMEM((group, 2 * count, 128), jnp.float32),
            pltpu.VMEM((group, 2 * count, 128), jnp.float32),
            pltpu.VMEM((group, 2 * count, 128), jnp.float32),
        ],
        compiler_params=pltpu.CompilerParams(vmem_limit_bytes=48 * MIB),
        cost_estimate=cost(14 if kind == "frames" else 5),
        name=name,
    )(meta, queries, kv, kv)


def query_side(pair, features, q, do, qa, da):
    lane = lanes(q.shape[0])
    heads = [2 * pair, 2 * pair + 1]
    stack_heads(qa, q, [jnp.where((lane < LSE_LANE) | head_lanes(lane, LSE_LANE, head), features, 0.0) for head in heads])
    stack_heads(da, do, [jnp.where(head_lanes(lane, DELTA_LANE, head), features, 0.0) for head in heads])


def query_step(qa, da, keys, values, bias):
    minus = jnp.where(delta_lanes(lanes(keys.shape[0])), -1.0, 0.0)
    probs = jnp.exp(times_transposed(qa[...], jnp.concatenate([keys, bias], axis=1)))
    slope = times_transposed(da[...], beside(values, minus))
    return dot((probs * slope).astype(jnp.bfloat16), keys)


def key_side(pair, k, v, mask, ka, va):
    lane = lanes(k.shape[0])
    heads = [2 * pair, 2 * pair + 1]
    stack_heads(ka, k, [jnp.where(head_lanes(lane, LSE_LANE, head), -1.0, mask) for head in heads])
    stack_heads(va, v, [jnp.where(head_lanes(lane, DELTA_LANE, head), -1.0, 0.0) for head in heads])


def key_step(ka, va, q, do, features):
    probs = jnp.exp(times_transposed(ka[...], jnp.concatenate([q, features], axis=1)))
    slope = times_transposed(va[...], jnp.concatenate([do, features], axis=1))
    return dot((probs * slope).astype(jnp.bfloat16), q), dot(probs.astype(jnp.bfloat16), do)


def query_grad_kernel(items, shards, blocks, group, meta, q_ref, do_ref, f_ref, k_ref, v_ref, dq_ref, qa, da, bias_ref, acc):
    count = q_ref.shape[0]
    rows = k_ref.shape[0] // blocks
    frame = Frame(meta, items, count, shards)
    active, bias = block_rule(frame, "frames", rows)
    fill_bias(blocks, rows, active, bias, bias_ref, True)
    features = f_ref[...].astype(jnp.float32)
    for g in range(group):
        pair = pl.program_id(0) * group + g
        query_side(pair, features, heads_of(q_ref, ALL, g), heads_of(do_ref, ALL, g), qa.at[g], da.at[g])
        acc[g] = jnp.zeros((2 * count, 128), jnp.float32)

    def step(block):
        here = rows_of(block, rows)
        for g in range(group):
            acc[g] = acc[g] + query_step(
                qa.at[g], da.at[g], heads_of(k_ref, here, g), heads_of(v_ref, here, g), bias_ref[here, :]
            )

    each_active(blocks, active, step)
    for g in range(group):
        dq_ref[:, g * 128 : (g + 1) * 128] = (merge_heads(acc[g]) * 0.125).astype(jnp.bfloat16)


def query_grad(meta, queries, grad_out, features, kv, blocks, items, shards, name, group=3):
    count, width = grad_out.shape
    pairs = width // 128
    total = kv.shape[0]
    tile = spread(count, group, 0)
    return pl.pallas_call(
        partial(query_grad_kernel, items, shards, blocks, group),
        grid=(pairs // group,),
        out_shape=jax.ShapeDtypeStruct((count, width), jnp.bfloat16),
        in_specs=[
            pl.BlockSpec(memory_space=pltpu.SMEM),
            tile,
            tile,
            pl.BlockSpec((count, 128), lambda p: (0, 0)),
            spread(total, group, 0),
            spread(total, group, pairs),
        ],
        out_specs=tile,
        scratch_shapes=[
            pltpu.VMEM((group, 2 * count, 256), jnp.bfloat16),
            pltpu.VMEM((group, 2 * count, 256), jnp.bfloat16),
            pltpu.VMEM((total, 128), jnp.bfloat16),
            pltpu.VMEM((group, 2 * count, 128), jnp.float32),
        ],
        compiler_params=pltpu.CompilerParams(vmem_limit_bytes=48 * MIB),
        cost_estimate=cost(14),
        name=name,
    )(meta, queries, grad_out, features, kv, kv)


def frame_key_grad_kernel(items, shards, blocks, group, meta, q_ref, k_ref, v_ref, dq_ref, all_ref, out_ref, ka, va, dka, dva, do_s, sem):
    count, width = dq_ref.shape[0], do_s.shape[1] - 128
    rows = q_ref.shape[0] // blocks
    frame = Frame(meta, items, count, shards)

    def arrivals(act):
        @pl.when(pl.program_id(0) == 0)
        def _():
            for block in range(2 * blocks):
                start, live = frame.chip(jnp.int32(block // 2))
                first = start + (frame.position + block) % 2 * count

                @pl.when(live)
                def _(block=block, first=first):
                    act(
                        pltpu.make_async_copy(
                            all_ref.at[pl.ds(pl.multiple_of(first, count), count), :],
                            do_s.at[pl.ds(block * count, count), :],
                            sem.at[block],
                        )
                    )

    arrivals(lambda copy: copy.start())
    mask = item_bias(frame, frame.items_of_rows(frame.position * count, count))
    for g in range(group):
        pair = pl.program_id(0) * group + g
        key_side(pair, heads_of(k_ref, ALL, g), heads_of(v_ref, ALL, g), mask, ka.at[g], va.at[g])
        dka[g] = jnp.zeros((2 * count, 128), jnp.float32)
        dva[g] = jnp.zeros((2 * count, 128), jnp.float32)
    arrivals(lambda copy: copy.wait())

    def step(block):
        here = rows_of(block, rows)
        for g in range(group):
            column = pl.multiple_of((pl.program_id(0) * group + g) * 128, 128)
            dk, dv = key_step(
                ka.at[g], va.at[g], heads_of(q_ref, here, g), do_s[here, pl.ds(column, 128)], do_s[here, width:]
            )
            dka[g] = dka[g] + dk
            dva[g] = dva[g] + dv

    each_active(blocks, lambda block: frame.chip(block)[1], step)
    for g in range(group):
        out_ref[1, :, g * 128 : (g + 1) * 128] = merge_heads(dka[g]).astype(jnp.bfloat16)
        out_ref[2, :, g * 128 : (g + 1) * 128] = merge_heads(dva[g]).astype(jnp.bfloat16)
    out_ref[0] = dq_ref[...]


def frame_key_grad(meta, q_window, do_all, kv, grad_queries, count, blocks, items, shards, name, group=3):
    total, width = q_window.shape
    pairs = width // 128
    tile = spread(count, group, 0)
    wide = spread(total, group, 0)
    return pl.pallas_call(
        partial(frame_key_grad_kernel, items, shards, blocks, group),
        grid=(pairs // group,),
        out_shape=jax.ShapeDtypeStruct((3, count, width), jnp.bfloat16),
        in_specs=[
            pl.BlockSpec(memory_space=pltpu.SMEM),
            wide,
            tile,
            spread(count, group, pairs),
            tile,
        ]
        + [pl.BlockSpec(memory_space=pl.ANY)],
        out_specs=pl.BlockSpec((3, count, group * 128), lambda p: (0, 0, p)),
        scratch_shapes=[pltpu.VMEM((group, 2 * count, 256), jnp.bfloat16)] * 2
        + [pltpu.VMEM((group, 2 * count, 128), jnp.float32)] * 2
        + [pltpu.VMEM((total, width + 128), jnp.bfloat16), pltpu.SemaphoreType.DMA((2 * blocks,))],
        compiler_params=pltpu.CompilerParams(vmem_limit_bytes=48 * MIB),
        cost_estimate=cost(18),
        name=name,
    )(meta, q_window, kv, kv, grad_queries, do_all)


def text_grad_kernel(items, shards, group, meta, q_ref, do_ref, f_ref, k_ref, v_ref, dq_ref, dkv_ref, qa, da, ka, va, acc):
    count = q_ref.shape[0]
    rows = k_ref.shape[0] // items
    share = rows // shards
    frame = Frame(meta, items, count, shards)
    features = f_ref[...].astype(jnp.float32)
    pairs = [pl.program_id(0) * group + g for g in range(group)]
    for g in range(group):
        query_side(pairs[g], features, heads_of(q_ref, ALL, g), heads_of(do_ref, ALL, g), qa.at[g], da.at[g])
        acc[g] = jnp.zeros((2 * count, 128), jnp.float32)

    @pl.loop(0, items)
    def _(item):
        here = rows_of(item, rows)
        live = (item >= frame.first) & (item <= frame.last)
        target = rows_of(item, share)

        @pl.when(live)
        def _():
            mask = text_bias(frame, item, rows)
            bias = jnp.where(lse_lanes(lanes(rows)), -1.0, mask).astype(jnp.bfloat16)
            for g in range(group):
                keys, values = heads_of(k_ref, here, g), heads_of(v_ref, here, g)
                acc[g] = acc[g] + query_step(qa.at[g], da.at[g], keys, values, bias)
                key_side(pairs[g], keys, values, mask, ka.at[g], va.at[g])
                grads = key_step(ka.at[g], va.at[g], heads_of(q_ref, ALL, g), heads_of(do_ref, ALL, g), f_ref[...])
                for which, grad in enumerate(grads):
                    merged = merge_heads(grad).astype(jnp.bfloat16)
                    for owner in range(shards):
                        dkv_ref[owner, which, target, g * 128 : (g + 1) * 128] = merged[
                            owner * share : (owner + 1) * share
                        ]

        @pl.when(jnp.logical_not(live))
        def _():
            dkv_ref[:, :, target, :] = jnp.zeros((shards, 2, share, group * 128), jnp.bfloat16)

    for g in range(group):
        dq_ref[:, g * 128 : (g + 1) * 128] = (merge_heads(acc[g]) * 0.125).astype(jnp.bfloat16)


def text_grad(meta, queries, grad_out, features, kv, items, shards, name, group=3):
    count, width = queries.shape
    pairs = width // 128
    total = kv.shape[0]
    tile = spread(count, group, 0)
    rows = total // items
    return pl.pallas_call(
        partial(text_grad_kernel, items, shards, group),
        grid=(pairs // group,),
        out_shape=(
            jax.ShapeDtypeStruct((count, width), jnp.bfloat16),
            jax.ShapeDtypeStruct((shards, 2, total // shards, width), jnp.bfloat16),
        ),
        in_specs=[
            pl.BlockSpec(memory_space=pltpu.SMEM),
            tile,
            tile,
            pl.BlockSpec((count, 128), lambda p: (0, 0)),
            spread(total, group, 0),
            spread(total, group, pairs),
        ],
        out_specs=(tile, pl.BlockSpec((shards, 2, total // shards, group * 128), lambda p: (0, 0, 0, p))),
        scratch_shapes=[pltpu.VMEM((group, 2 * count, 256), jnp.bfloat16)] * 2
        + [pltpu.VMEM((group, 2 * rows, 256), jnp.bfloat16)] * 2
        + [pltpu.VMEM((group, 2 * count, 128), jnp.float32)],
        compiler_params=pltpu.CompilerParams(vmem_limit_bytes=48 * MIB),
        cost_estimate=cost(8),
        name=name,
    )(meta, queries, grad_out, features, kv, kv)


def mlp_kernel(h_ref, d_ref, up_ref, down_ref, act_ref, m_ref, dh_ref):
    step = pl.program_id(0)
    last = pl.num_programs(0) - 1

    @pl.when(step < last)
    def _():
        u = dot(h_ref[...], up_ref[...])
        slope = times_transposed(d_ref[...], down_ref[...])
        inner = 0.7978845608028654 * (u + 0.044715 * (u * u * u))
        t = jnp.tanh(inner)
        g = (0.5 * u * (1.0 + t)).astype(jnp.bfloat16)
        bend = 0.7978845608028654 * (1.0 + 0.134145 * (u * u))
        du = (slope * (0.5 * (1.0 + t) + 0.5 * u * (1.0 - t * t) * bend)).astype(jnp.bfloat16)
        act_ref[0, 0] = g
        act_ref[0, 1] = du
        m = dot(g, down_ref[...])
        dh = times_transposed(du, up_ref[...])

        @pl.when(step == 0)
        def _():
            m_ref[...] = m
            dh_ref[...] = dh

        @pl.when(step > 0)
        def _():
            m_ref[...] = m_ref[...] + m
            dh_ref[...] = dh_ref[...] + dh

    @pl.when(step == last)
    def _():
        act_ref[0, 0] = h_ref[...]
        act_ref[0, 1] = d_ref[...]


def mlp(hidden, grad, w_up, w_down):
    count, width = hidden.shape
    chunks = w_up.shape[1] // width
    whole = pl.BlockSpec((count, width), lambda c: (0, 0))
    held = lambda c: jnp.minimum(c, chunks - 1)
    return pl.pallas_call(
        mlp_kernel,
        grid=(chunks + 1,),
        out_shape=(
            jax.ShapeDtypeStruct((chunks + 1, 2, count, width), jnp.bfloat16),
            jax.ShapeDtypeStruct((count, width), jnp.float32),
            jax.ShapeDtypeStruct((count, width), jnp.float32),
        ),
        in_specs=[
            whole,
            whole,
            pl.BlockSpec((width, width), lambda c: (0, held(c))),
            pl.BlockSpec((width, width), lambda c: (held(c), 0)),
        ],
        out_specs=(pl.BlockSpec((1, 2, count, width), lambda c: (c, 0, 0, 0)), whole, whole),
        compiler_params=pltpu.CompilerParams(vmem_limit_bytes=40 * MIB),
        cost_estimate=cost(9),
        name="mlp",
    )(hidden, grad, w_up, w_down)


UNIT = 192
X_BIT, Y_BIT = 0, 1


def rows_picked(x, core):
    row = lax.broadcasted_iota(jnp.int32, (384, 768), 0)
    column = lax.broadcasted_iota(jnp.int32, (384, 768), 1)
    chip = (row >= 96).astype(jnp.int32) + (row >= 192).astype(jnp.int32) + (row >= 288).astype(jnp.int32)
    pick = (column == row + 96 * (chip + core)).astype(jnp.bfloat16)
    return times_transposed(pick, x).astype(jnp.bfloat16)


def one_above_other(upper, lower):
    return jnp.concatenate([upper, lower], axis=0)


def finish_kernel(items, shards, meta, mod_ref, w_ref, d_ref, x_ref, dx_ref, a_ref, dh_ref, n_ref, dy_ref, m_ref, out_ref, sum_ref):
    count, width = x_ref.shape
    frame = Frame(meta, items, count, shards)
    item = frame.items_of_rows(frame.position * count, count)
    grad = sum(times_transposed(d_ref[i], w_ref[:, i * width : (i + 1) * width]) for i in range(3))
    normed, inverse = layer_norm(x_ref[...].astype(jnp.float32))
    scale = jnp.zeros((count, width), jnp.float32)
    for i in range(items):
        scale = jnp.where(item == i, mod_ref[i, 1:2, :], scale)
    dx = dx_ref[...]
    out_ref[...] = dx + norm_back(grad * (1.0 + scale), normed, inverse)
    dh = dh_ref[...]
    terms = (
        grad,
        grad * normed,
        dx * a_ref[...],
        dh,
        dh * n_ref[...],
        dy_ref[...].astype(jnp.float32) * m_ref[...],
    )
    for number, term in enumerate(terms):
        rows = [jnp.sum(jnp.where(item == i, term, 0.0), axis=0, keepdims=True) for i in range(items)]
        rows += [jnp.zeros((8 - items, width), jnp.float32)]
        sum_ref[number] = jnp.concatenate(rows, axis=0)


def finish(meta, modulation, weight, grads, frames, *arrays_items_shards):
    *arrays, items, shards = arrays_items_shards
    count, width = frames.shape
    whole = pl.BlockSpec(memory_space=pltpu.VMEM)
    return pl.pallas_call(
        partial(finish_kernel, items, shards),
        out_shape=(
            jax.ShapeDtypeStruct((count, width), jnp.float32),
            jax.ShapeDtypeStruct((6, 8, width), jnp.float32),
        ),
        in_specs=[pl.BlockSpec(memory_space=pltpu.SMEM)] + [whole] * (4 + len(arrays)),
        out_specs=(whole, whole),
        compiler_params=pltpu.CompilerParams(vmem_limit_bytes=40 * MIB),
        cost_estimate=cost(5),
        name="finish",
    )(meta, modulation, weight, grads, frames, *arrays)


class Packer:
    def __init__(self, meta, items, outputs):
        self.core, self.chip = meta[0] % 2, meta[0] // 2
        self.mine = meta[1 + 2 * items]
        self.outputs = outputs

    def steps(self, owner_chip):
        relative = owner_chip ^ self.chip
        return relative % 2, relative // 2

    def store(self, name, owner, owner_chip, row, values):
        scratch, first = self.outputs[name]
        relative = owner ^ self.mine
        where = ((relative >> first) % 2, (relative >> (1 - first)) % 2, *self.steps(owner_chip))
        scratch[where + (slice(row, row + values.shape[0]),)] = values.astype(jnp.bfloat16)

    def store_split(self, name, pair, row, values, chips):
        rolled = pltpu.roll(values, UNIT, 1)
        each = values.shape[0] // len(chips)
        left = lax.broadcasted_iota(jnp.int32, (each // 2, 384), 1) < UNIT
        for number, owner_chip in enumerate(chips):
            upper = slice(number * each, number * each + each // 2)
            lower = slice(number * each + each // 2, (number + 1) * each)
            self.store(name, 2 * pair, owner_chip, row, jnp.where(left, values[upper], rolled[lower]))
            self.store(name, 2 * pair + 1, owner_chip, row, jnp.where(left, rolled[upper], values[lower]))


def core_columns(core, number, each):
    return pl.ds(pl.multiple_of(number * 2 * each + core * each, 128), each)


def third(values, number):
    return values[:, number * 384 : (number + 1) * 384]


def pack_mlp_kernel(items, meta, own, sib, down_s, up_s):
    packer = Packer(meta, items, {"down": (down_s, Y_BIT), "up": (up_s, X_BIT)})
    both = lambda chunk, which: one_above_other(own[chunk, which], sib[chunk, which])
    grad = both(4, 1)
    for owner_chip in range(4):
        here = core_columns(packer.core, 0, 384)
        left = one_above_other(own[owner_chip, 0, :, here], sib[owner_chip, 0, :, here])
        values = contract_rows(left, grad)
        for pair in range(2):
            packer.store_split("down", pair, 0, third(values, pair), [owner_chip])
    left = rows_picked(both(4, 0), packer.core)
    for owner in range(4):
        values = dot(left, both(owner, 1))
        for owner_chip in range(4):
            for half in range(2):
                packer.store(
                    "up", owner, owner_chip, half * 96, third(values, half)[owner_chip * 96 : (owner_chip + 1) * 96]
                )


def pack_middle_kernel(items, meta, own, sib, text_own, text_sib, text, square_s, text_s):
    packer = Packer(meta, items, {"square": (square_s, Y_BIT), "text": (text_s, X_BIT)})
    both = lambda which: one_above_other(own[which], sib[which])
    for number in range(3):
        values = dot(rows_picked(both(2 * number), packer.core), both(2 * number + 1))
        for pair in range(2):
            packer.store_split("square", pair, number * 48, third(values, pair), range(4))
    share = text_own.shape[2] // items

    def chip_sum(which, item, owner):
        here = slice(item * share, (item + 1) * share)
        total = text_own[owner, which, here, :].astype(jnp.float32) + text_sib[owner, which, here, :].astype(jnp.float32)
        return total.astype(jnp.bfloat16)

    sums = [
        jnp.concatenate(
            [chip_sum(which, item, owner) for item in range(items) for owner in range(text_own.shape[0])], axis=0
        )
        for which in range(2)
    ]
    left = jnp.concatenate([text[:, core_columns(packer.core, chip, 128)] for chip in range(4)], axis=1)
    for which in range(2):
        values = contract_rows(left, sums[which])
        for owner_chip in range(4):
            for half in range(2):
                packer.store(
                    "text", 2 * which + half, owner_chip, 0, third(values, half)[owner_chip * 128 : (owner_chip + 1) * 128]
                )


def pack_qkv_kernel(items, meta, h_own, h_sib, own, sib, plain_s, split_s):
    packer = Packer(meta, items, {"plain": (plain_s, X_BIT), "split": (split_s, Y_BIT)})
    left = rows_picked(one_above_other(h_own[...], h_sib[...]), packer.core)
    values = []
    for number in range(3):
        product = dot(left, one_above_other(own[number], sib[number]))
        values += [third(product, 0), third(product, 1)]
    for owner, column in enumerate((0, 2, 3, 5)):
        for owner_chip in range(4):
            packer.store("plain", owner, owner_chip, 0, values[column][owner_chip * 96 : (owner_chip + 1) * 96])
    for pair, column in enumerate((1, 4)):
        packer.store_split("split", pair, 0, values[column], range(4))


def packing(kernel, items, inputs, groups, *refs):
    ins, outs, scratch, sem = refs[:inputs], refs[inputs:-groups - 1], refs[-groups - 1 : -1], refs[-1]
    kernel(items, *ins, *scratch)
    copies = [pltpu.make_async_copy(scratch[i // 2].at[1 - i % 2], outs[i], sem.at[i]) for i in range(2 * groups)]
    for copy in copies:
        copy.start()
    for copy in copies:
        copy.wait()


def pack(kernel, meta, operands, shapes, items, name):
    shapes = [(2, 2, 2, each, 384) if isinstance(each, int) else each for each in shapes]
    whole = pl.BlockSpec(memory_space=pltpu.VMEM)
    return pl.pallas_call(
        partial(packing, kernel, items, 1 + len(operands), len(shapes)),
        out_shape=tuple(jax.ShapeDtypeStruct(shape, jnp.bfloat16) for shape in shapes for _ in range(2)),
        in_specs=[pl.BlockSpec(memory_space=pltpu.SMEM)] + [whole] * len(operands),
        out_specs=tuple([pl.BlockSpec(memory_space=pl.ANY)] * (2 * len(shapes))),
        scratch_shapes=[pltpu.VMEM((2, *shape), jnp.bfloat16) for shape in shapes]
        + [pltpu.SemaphoreType.DMA((2 * len(shapes),))],
        compiler_params=pltpu.CompilerParams(vmem_limit_bytes=48 * MIB),
        cost_estimate=cost(8 if name != "pack_qkv" else 3),
        name=name,
    )(meta, *operands)


def bundle_kernel(*refs):
    for number, each in enumerate(refs[:-1]):
        refs[-1][number] = each[...]


def bundle(*arrays):
    whole = pl.BlockSpec(memory_space=pltpu.VMEM)
    return pl.pallas_call(
        bundle_kernel,
        out_shape=jax.ShapeDtypeStruct((len(arrays), *arrays[0].shape), arrays[0].dtype),
        in_specs=[whole] * len(arrays),
        out_specs=whole,
        cost_estimate=cost(3),
        name="bundle",
    )(*arrays)


def trade(values, axis, bit):
    size = lax.axis_size(axis)
    return lax.ppermute(values, axis, [(i, i ^ (1 << bit)) for i in range(size)])


def halve(keep, send, axis, bit, after=()):
    got = trade(send, axis, bit)
    if after:
        [keep] = hold((keep,), *after)
    return [(keep[i].astype(jnp.float32) + got[i].astype(jnp.float32)).astype(jnp.bfloat16) for i in range(2)]


def last_half(keep, send, after=()):
    got = trade(send, "seq", 2)
    if after:
        [keep] = hold((keep,), *after)
    return keep.astype(jnp.float32) + got.astype(jnp.float32)


def over_batch(send, keep, first, after=((), ())):
    keep, send = halve(keep, send, "batch", first, after[0])
    return halve(keep, send, "batch", 1 - first, after[1])


def over_chips(send, keep, after=((), ())):
    keep, send = halve(keep, send, "seq", 1, after[0])
    return last_half(keep, send, after[1])


def joined(upper, lower):
    return [jnp.concatenate([upper[i], lower[i]], axis=-2) for i in (1, 0)]


def unsplit(rows):
    return jnp.concatenate([rows[:, :UNIT], rows[:, UNIT:]], axis=0)


def with_deltas(features, grad_out, attn_exact):
    width = attn_exact.shape[1]
    lane = jnp.arange(128)[None, :]
    head = (jnp.arange(width) // (width // H))[:, None]
    pick = ((lane >= DELTA_LANE) & ((lane - DELTA_LANE) // 3 == head)).astype(jnp.float32)
    delta = jnp.dot(
        grad_out.astype(jnp.float32) * attn_exact,
        pick,
        precision=lax.Precision.HIGHEST,
        preferred_element_type=jnp.float32,
    )
    high = lax.reduce_precision(delta, 8, 7)
    middle = lax.reduce_precision(delta - high, 8, 7)
    which = (lane - DELTA_LANE) % 3
    piece = jnp.where(which == 0, high, jnp.where(which == 1, middle, delta - high - middle))
    inside = (lane >= DELTA_LANE) & (lane < DELTA_LANE + 3 * H)
    return jnp.where(inside, piece.astype(jnp.bfloat16), features)


def hop(below, above, shards):
    up = [(i, i + 2) for i in range(shards - 2)]
    return lax.ppermute(below, "seq", up), lax.ppermute(above, "seq", [(j, i) for i, j in up])


def hold(values, *first):
    held = lax.optimization_barrier((*values, *first))
    return held[: len(values)]


def body(
    frames,
    cotangent,
    modulation,
    lengths,
    text,
    text_len,
    w_qkv,
    w_o,
    w_cq,
    w_ckv,
    w_co,
    w_up,
    w_down,
):
    local = frames[0]
    count, width = local.shape
    items = lengths.shape[1]
    text_rows, text_width = text.shape[2:]
    shards = lax.axis_size("seq")
    position = lax.axis_index("seq")
    reach = min(-(-(LONGEST - 1) // (2 * count)), shards // 2 - 1)
    chips = 1 + 2 * reach
    meta = jnp.concatenate(
        [position[None].astype(jnp.int32), lengths[0], text_len[0], lax.axis_index("batch")[None].astype(jnp.int32)]
    )
    item_range = jnp.arange(items, dtype=jnp.int32)
    ends = jnp.sum(jnp.where(item_range[None, :] <= item_range[:, None], lengths[0][None, :], 0), axis=1)
    place = position * count + jnp.arange(count, dtype=jnp.int32)
    query_items = jnp.sum((place[:, None] >= ends[None, :]).astype(jnp.int32), axis=1)[:, None]
    mod = modulation[0]

    def per_frame(which):
        found = jnp.broadcast_to(mod[0, which][None, :], (count, width))
        for item in range(1, items):
            found = jnp.where(query_items == item, mod[item, which][None, :], found)
        return found

    swap = [(i, i ^ 1) for i in range(shards)]

    def sibling(values):
        return lax.ppermute(values, "seq", swap)

    fast = shards == 8 and lax.axis_size("batch") == 4 and width == 768

    text_proj = jnp.dot(
        text[0].reshape(items * text_rows, text_width), w_ckv, preferred_element_type=jnp.float32
    ).astype(jnp.bfloat16)
    sides = list(hold(hop(local, local, shards), text_proj))
    for _ in range(1, reach):
        sides += hop(*sides[-2:], shards)

    def with_siblings(blocks):
        return [each for block in blocks for each in (block, sibling(block))]

    total = 2 * chips * count
    near = with_siblings([local] + sides[:2])
    q_window, kv, hidden_one = project(meta, mod, w_qkv, near, range(3), total, (), items, shards, "project_near")
    if reach > 1:
        apart = with_siblings(hold(sides[2:], kv))
        q_window, kv, _ = project(
            meta, mod, w_qkv, apart, range(3, chips), total, (q_window, kv), items, shards, "project_far"
        )
    inputs = local.astype(jnp.float32)
    attn_exact, attended, features = attend(meta, count, q_window, kv, "frames", chips, items, shards, "self_attend")
    if fast:
        hidden_sib = sibling(hidden_one)
        [attended] = hold((attended,), hidden_sib)
    branch_one = jnp.dot(attended, w_o, preferred_element_type=jnp.float32)
    after_attn = inputs + per_frame(2) * branch_one
    normed_cross, inverse_cross = layer_norm(after_attn)
    cross_in = normed_cross.astype(jnp.bfloat16)
    cross_queries = jnp.dot(cross_in, w_cq, preferred_element_type=jnp.float32).astype(jnp.bfloat16)
    cross_queries = (cross_queries.astype(jnp.float32) * 0.125).astype(jnp.bfloat16)
    cross_exact, cross_out, cross_features = attend(
        meta, count, cross_queries, text_proj, "text", items, items, shards, "cross_attend"
    )
    branch_two = jnp.dot(cross_out, w_co, preferred_element_type=jnp.float32)
    after_cross = after_attn + branch_two
    normed_two, inverse_two = layer_norm(after_cross)
    hidden_two = (normed_two * (1.0 + per_frame(4)) + per_frame(3)).astype(jnp.bfloat16)
    gate_two = per_frame(5)
    grad_out = cotangent[0].astype(jnp.float32)
    grad_branch_three = (grad_out * gate_two).astype(jnp.bfloat16)
    acts, branch_three, grad_hidden_two = mlp(hidden_two, grad_branch_three, w_up, w_down)
    if fast:
        acts_sib = sibling(acts)
    result = after_cross + gate_two * branch_three
    grad_cross = grad_out + norm_back(grad_hidden_two * (1.0 + per_frame(4)), normed_two, inverse_two)
    grad_branch_two = grad_cross.astype(jnp.bfloat16)
    grad_cross_out = times_transposed(grad_branch_two, w_co).astype(jnp.bfloat16)
    cross_features = with_deltas(cross_features, grad_cross_out, cross_exact)
    grad_cross_queries, text_terms = text_grad(
        meta, cross_queries, grad_cross_out, cross_features, text_proj, items, shards, "cross_grad"
    )
    grad_attn_res = grad_cross + norm_back(
        times_transposed(grad_cross_queries, w_cq), normed_cross, inverse_cross
    )
    grad_branch_one = (grad_attn_res * per_frame(2)).astype(jnp.bfloat16)
    if fast:
        text_sib = sibling(text_terms)
        [grad_branch_one] = hold((grad_branch_one,), text_sib)
    grad_attended = times_transposed(grad_branch_one, w_o).astype(jnp.bfloat16)
    features = with_deltas(features, grad_attended, attn_exact)
    do_low = jnp.concatenate([grad_attended, features], axis=1)
    do_all = lax.all_gather(do_low, "seq", axis=0, tiled=True)
    if fast:
        middle = bundle(cross_out, grad_branch_two, cross_in, grad_cross_queries, attended, grad_branch_one)
        middle_sib = sibling(middle)
        [acts_sib] = hold((acts_sib,), do_low, middle)
        mlp_parts = pack(pack_mlp_kernel, meta, (acts, acts_sib), (192, 192), items, "pack_mlp")
        [grad_attended] = hold((grad_attended,), *mlp_parts)
    grad_queries = query_grad(
        meta, q_window, grad_attended, features, kv, chips, items, shards, "self_query_grad"
    )
    share_rows = text_rows // shards
    [text_terms_late] = hold((text_terms,), grad_queries)
    text_total = lax.psum_scatter(
        text_terms_late.reshape(shards * 2 * items * share_rows, width), "seq", scatter_dimension=0, tiled=True
    ).reshape(2, items * share_rows, width)
    if fast:
        middle_parts = pack(
            pack_middle_kernel,
            meta,
            (middle, middle_sib, text_terms, text_sib, text[0].reshape(items * text_rows, text_width)),
            (144, 128),
            items,
            "pack_middle",
        )
        down_part = halve(mlp_parts[1], mlp_parts[0], "batch", Y_BIT, (middle_parts[0],))
        up_part = halve(mlp_parts[3], mlp_parts[2], "batch", X_BIT, (middle_parts[0],))
        [do_all] = hold((do_all,), *middle_parts, *down_part, *up_part)
    grad_projected = frame_key_grad(
        meta, q_window, do_all, kv, grad_queries, count, chips, items, shards, "self_key_grad"
    )
    if fast:
        projected_sib = sibling(grad_projected)
        down_part = halve(*down_part, "batch", X_BIT, (grad_projected,))
        up_part = halve(*up_part, "batch", Y_BIT, (grad_projected,))
        first_send, first_keep = joined(down_part, up_part)
        qkv_parts = pack(
            pack_qkv_kernel,
            meta,
            (hidden_one, hidden_sib, grad_projected, projected_sib),
            (96, 48),
            items,
            "pack_qkv",
        )
        first_part = halve(first_keep, first_send, "seq", 1, (qkv_parts[0],))
        [grad_projected] = hold((grad_projected,), *qkv_parts)
    grad_inputs, terms = finish(
        meta, mod, w_qkv, grad_projected, local, grad_attn_res, branch_one, grad_hidden_two, normed_two, cotangent[0],
        branch_three, items, shards,
    )
    if fast:
        terms = terms + trade(terms, "seq", 0)
        points = ((qkv_parts[0],), (grad_inputs,))
        square_send, square_keep, text_send, text_keep = middle_parts
        square_part = over_batch(square_send, square_keep, Y_BIT, points)
        text_w_part = over_batch(text_send, text_keep, X_BIT, points)
        plain_send, plain_keep, split_send, split_keep = qkv_parts
        points = ((grad_inputs,), ())
        plain_part = over_batch(plain_send, plain_keep, X_BIT, points)
        split_part = over_batch(split_send, split_keep, Y_BIT, points)
        [terms] = hold((terms,), *plain_part, *split_part)
        first_rows = last_half(*first_part)
        middle_rows = over_chips(*joined(square_part, text_w_part))
        last_rows = over_chips(*joined(plain_part, split_part))
        done_bits = 1
    else:
        done_bits = 0
    for bit in range(done_bits, shards.bit_length() - 1):
        terms = terms + trade(terms, "seq", bit)
    own = width // shards
    terms = lax.dynamic_slice_in_dim(terms, position * own, own, 2)
    shares = terms[:, :items].transpose(1, 0, 2)
    if fast:
        plain, split = last_rows[:96], unsplit(last_rows[96:])
        even = lax.axis_index("batch") % 2 == 0
        grads = (
            jnp.where(even, jnp.concatenate([plain, split], axis=1), jnp.concatenate([split, plain], axis=1)),
            unsplit(middle_rows[96:144]),
            unsplit(middle_rows[48:96]),
            middle_rows[144:],
            unsplit(middle_rows[:48]),
            jnp.concatenate([first_rows[192:288], first_rows[288:]], axis=1),
            unsplit(first_rows[:192]),
        )
    [text_total] = hold((text_total,), terms)
    text_grad_low = jnp.concatenate([text_total[0], text_total[1]], axis=1)
    grad_text = times_transposed(text_grad_low, w_ckv).reshape(1, items, share_rows, text_width)
    if not fast:
        text_mine = lax.dynamic_slice_in_dim(text[0], position * share_rows, share_rows, 1)
        grads = reduced_grads(
            (hidden_one, jnp.concatenate(list(grad_projected), axis=1)),
            (attended, grad_branch_one),
            (cross_in, grad_cross_queries),
            (text_mine.reshape(items * share_rows, text_width), text_grad_low),
            (cross_out, grad_branch_two),
            (hidden_two, acts[:-1, 1].transpose(1, 0, 2).reshape(count, -1)),
            (acts[:-1, 0].transpose(1, 0, 2).reshape(count, -1), grad_branch_three),
        )
    return (
        result.astype(jnp.bfloat16)[None],
        grad_inputs[None],
        shares[:, :3][None],
        shares[:, 3:][None],
        grad_text,
        *grads,
    )


def reduced_grads(*pairs):
    def reduce_weight(left, right):
        grad = contract_rows(left, right).astype(jnp.bfloat16)
        part = lax.psum_scatter(grad, "seq", scatter_dimension=0, tiled=True)
        return lax.psum_scatter(part, "batch", scatter_dimension=1, tiled=True).astype(jnp.float32)

    return tuple(reduce_weight(*pair) for pair in pairs)


def solution(mesh):
    in_specs = (
        P("batch", "seq", None),
        P("batch", "seq", None),
        P("batch", None, None, None),
        P("batch", None),
        P("batch", None, None, None),
        P("batch", None),
        P(),
        P(),
        P(),
        P(),
        P(),
        P(),
        P(),
    )
    out_specs = (
        P("batch", "seq", None),
        P("batch", "seq", None),
        P("batch", None, None, "seq"),
        P("batch", None, None, "seq"),
        P("batch", None, "seq", None),
        P("seq", "batch"),
        P("seq", "batch"),
        P("seq", "batch"),
        P("seq", "batch"),
        P("seq", "batch"),
        P("seq", "batch"),
        P("seq", "batch"),
    )
    return jax.shard_map(body, mesh=mesh, in_specs=in_specs, out_specs=out_specs, check_vma=False)
```

```python
from functools import partial

import jax
import jax.numpy as jnp
from jax import lax
from jax.experimental import pallas as pl
from jax.experimental.pallas import tpu as pltpu
from jax.sharding import PartitionSpec as P

H = 12
LONGEST = 1024

epsilon = 1e-06
far = -1e30
LSE_LANE = 8
DELTA_LANE = 44
MIB = 1 << 20
FLOPS_EACH, BYTES_EACH = 5e+08, 1.65e+06


def layer_norm(values):
    centred = values - jnp.mean(values, axis=-1, keepdims=True)
    inverse = lax.rsqrt(jnp.mean(centred * centred, axis=-1, keepdims=True) + epsilon)
    return (centred * inverse, inverse)


def norm_back(grad_normed, normed, inverse):
    return inverse * (
        grad_normed
        - jnp.mean(grad_normed, axis=-1, keepdims=True)
        - normed * jnp.mean(grad_normed * normed, axis=-1, keepdims=True)
    )


def contract_rows(left, right):
    return lax.dot_general(
        left, right, (((0,), (0,)), ((), ())), preferred_element_type=jnp.float32
    )


def times_transposed(left, right):
    return lax.dot_general(
        left, right, (((1,), (1,)), ((), ())), preferred_element_type=jnp.float32
    )


class Frame:
    def __init__(self, meta, items, count, shards):
        self.position = meta[0]
        self.items = items
        self.count = count
        self.shards = shards
        self.ends = []
        total = jnp.int32(0)
        for item in range(items):
            total = total + meta[1 + item]
            self.ends.append(total)
        self.text_len = [meta[1 + items + item] for item in range(items)]
        self.first = self.item_of(self.position * count)
        self.last = self.item_of(self.position * count + count - 1)
        self.low = jnp.int32(0)
        self.high = jnp.int32(0)
        for item in range(items):
            start = self.ends[item] - meta[1 + item]
            self.low = jnp.where(self.first == item, start, self.low)
            self.high = jnp.where(self.last == item, self.ends[item], self.high)

    def item_of(self, place):
        found = jnp.int32(0)
        for end in self.ends:
            found = found + (place >= end).astype(jnp.int32)
        return found

    def items_of_rows(self, base, rows):
        place = base + lax.broadcasted_iota(jnp.int32, (rows, 1), 0)
        found = jnp.zeros((rows, 1), jnp.int32)
        for end in self.ends:
            found = found + (place >= end).astype(jnp.int32)
        return found

    def items_of_chip(self, block):
        start, _ = self.chip(block)
        core = self.position % 2
        return jnp.concatenate(
            [
                self.items_of_rows(start + core * self.count, self.count),
                self.items_of_rows(start + (1 - core) * self.count, self.count),
            ],
            axis=0,
        )

    def chip(self, block):
        hop = (block + 1) // 2
        chip = self.position // 2 + jnp.where(block % 2 == 1, -hop, hop)
        rows = 2 * self.count
        start = chip * rows
        live = (chip >= 0) & (chip < self.shards // 2)
        return start, live & (start < self.high) & (start + rows > self.low)


def lanes(rows):
    return lax.broadcasted_iota(jnp.int32, (rows, 128), 1)


def lse_lanes(lane):
    return (lane >= LSE_LANE) & (lane < DELTA_LANE)


def delta_lanes(lane):
    return (lane >= DELTA_LANE) & (lane < DELTA_LANE + 3 * H)


def head_lanes(lane, base, head):
    start = base + 3 * head
    return (lane >= start) & (lane < start + 3)


def cost(microseconds):
    return pl.CostEstimate(
        flops=int(microseconds * FLOPS_EACH), bytes_accessed=int(microseconds * BYTES_EACH), transcendentals=0
    )


def beside(left, right):
    return jnp.concatenate([left.astype(jnp.bfloat16), right.astype(jnp.bfloat16)], axis=1)


def pieces(values):
    high = values.astype(jnp.bfloat16).astype(jnp.float32)
    rest = values - high
    middle = rest.astype(jnp.bfloat16).astype(jnp.float32)
    return high, middle, rest - middle


def dot(left, right):
    return jnp.dot(left, right, preferred_element_type=jnp.float32)


def stack_heads(target, values, features):
    rows = values.shape[0]
    half = lanes(rows) // 64
    wide = values.astype(jnp.float32)
    for h in range(2):
        target[h * rows : (h + 1) * rows, :] = beside(jnp.where(half == h, wide, 0.0), features[h])


def merge_heads(stacked):
    rows = stacked.shape[0] // 2
    return jnp.where(lanes(rows) < 64, stacked[:rows], stacked[rows:])


def item_bias(frame, item):
    lane = lanes(item.shape[0])
    return jnp.where((lane != item) & (lane < frame.items), far, 0.0)


def text_bias(frame, block, rows):
    slot = lax.broadcasted_iota(jnp.int32, (rows, 1), 0)
    length = jnp.int32(0)
    for item in range(frame.items):
        length = jnp.where(block == item, frame.text_len[item], length)
    lane = lanes(rows)
    dead = (lane != block) | (slot >= length)
    return jnp.where(dead & (lane < frame.items), far, 0.0)


def block_rule(frame, kind, rows):
    if kind == "frames":
        return (
            lambda block: frame.chip(block)[1],
            lambda block: item_bias(frame, frame.items_of_chip(block)),
        )
    return (
        lambda block: (block >= frame.first) & (block <= frame.last),
        lambda block: text_bias(frame, block, rows),
    )


def rows_of(block, rows):
    return pl.ds(pl.multiple_of(block * rows, rows), rows)


def each_active(blocks, active, step):
    @pl.loop(0, blocks)
    def _(block):
        @pl.when(active(block))
        def _():
            step(block)


def fill_bias(blocks, rows, active, bias, target, with_lse):
    @pl.when(pl.program_id(0) == 0)
    def _():
        def step(block):
            mask = bias(block)
            if with_lse:
                mask = jnp.where(lse_lanes(lanes(rows)), -1.0, mask)
            target[rows_of(block, rows), :] = mask.astype(jnp.bfloat16)

        each_active(blocks, active, step)


def hide_kernel(items, shards, meta, mod_ref, x_ref, h_ref):
    count, _ = x_ref.shape
    frame = Frame(meta, items, count, shards)
    normed, _ = layer_norm(x_ref[...].astype(jnp.float32))
    item = frame.items_of_rows(frame.position * count, count)
    shift = jnp.broadcast_to(mod_ref[0, 0:1, :], normed.shape)
    scale = jnp.broadcast_to(mod_ref[0, 1:2, :], normed.shape)
    for i in range(1, items):
        shift = jnp.where(item == i, mod_ref[i, 0:1, :], shift)
        scale = jnp.where(item == i, mod_ref[i, 1:2, :], scale)
    h_ref[...] = (normed * (1.0 + scale) + shift).astype(jnp.bfloat16)


def hide(meta, modulation, frames, items, shards):
    whole = pl.BlockSpec(memory_space=pltpu.VMEM)
    return pl.pallas_call(
        partial(hide_kernel, items, shards),
        out_shape=jax.ShapeDtypeStruct(frames.shape, jnp.bfloat16),
        in_specs=[pl.BlockSpec(memory_space=pltpu.SMEM), whole, whole],
        out_specs=whole,
        cost_estimate=cost(2),
        name="hide",
    )(meta, modulation, frames)


def project_kernel(items, shards, chips, meta, w_hbm, *refs):
    number = len(chips)
    x_refs = refs[: 2 * number]
    q_ref, kv_ref, x_s, q_s, kv_s, w_ref, in_sem, out_sem, w_sem = refs[-9:]
    weights = pltpu.make_async_copy(w_hbm, w_ref, w_sem)
    count, width = x_refs[0].shape
    rows = 2 * count
    frame = Frame(meta, items, count, shards)

    def live(index):
        return frame.chip(index + chips[0])[1]

    weights.start()
    for index in range(number):

        @pl.when(live(jnp.int32(index)))
        def _(index=index):
            for part in range(2):
                block = 2 * index + part
                pltpu.make_async_copy(
                    x_refs[block], x_s.at[pl.ds(block * count, count), :], in_sem.at[block]
                ).start()

    def writes(index):
        here = rows_of(index, rows)
        there = rows_of(index + chips[0], rows)
        return (
            pltpu.make_async_copy(q_s.at[here, :], q_ref.at[there, :], out_sem.at[2 * index]),
            pltpu.make_async_copy(kv_s.at[here, :], kv_ref.at[there, :], out_sem.at[2 * index + 1]),
        )

    weights.wait()

    @pl.loop(0, number)
    def _(index):
        @pl.when(live(index))
        def _():
            for part in range(2):
                block = 2 * index + part
                pltpu.make_async_copy(x_refs[0], x_s.at[rows_of(block, count), :], in_sem.at[block]).wait()
            both = rows_of(index, rows)
            hidden = x_s[both, :]
            q = dot(hidden, w_ref[:, :width]).astype(jnp.bfloat16)
            q_s[both, :] = (q.astype(jnp.float32) * 0.125).astype(jnp.bfloat16)
            kv_s[both, :width] = dot(hidden, w_ref[:, width : 2 * width]).astype(jnp.bfloat16)
            kv_s[both, width:] = dot(hidden, w_ref[:, 2 * width :]).astype(jnp.bfloat16)
            for write in writes(index):
                write.start()

    @pl.loop(0, number)
    def _(index):
        @pl.when(live(index))
        def _():
            for write in writes(index):
                write.wait()


def project(meta, weight, x_blocks, chips, total, earlier, items, shards, name):
    count, width = x_blocks[0].shape
    part = len(x_blocks) * count
    anywhere = pl.BlockSpec(memory_space=pl.ANY)
    before = 2 + len(x_blocks)
    return pl.pallas_call(
        partial(project_kernel, items, shards, chips),
        out_shape=(
            jax.ShapeDtypeStruct((total, width), jnp.bfloat16),
            jax.ShapeDtypeStruct((total, 2 * width), jnp.bfloat16),
        ),
        in_specs=[pl.BlockSpec(memory_space=pltpu.SMEM)] + [anywhere] * (1 + len(x_blocks) + len(earlier)),
        out_specs=(anywhere, anywhere),
        input_output_aliases={before: 0, before + 1: 1} if earlier else {},
        scratch_shapes=[
            pltpu.VMEM((part, width), jnp.bfloat16),
            pltpu.VMEM((part, width), jnp.bfloat16),
            pltpu.VMEM((part, 2 * width), jnp.bfloat16),
            pltpu.VMEM(weight.shape, jnp.bfloat16),
            pltpu.SemaphoreType.DMA((len(x_blocks),)),
            pltpu.SemaphoreType.DMA((len(x_blocks),)),
            pltpu.SemaphoreType.DMA,
        ],
        compiler_params=pltpu.CompilerParams(vmem_limit_bytes=28 * MIB),
        cost_estimate=cost(len(x_blocks) * 1.2),
        name=name,
    )(meta, weight, *x_blocks, *earlier)


def heads_of(ref, here, pair):
    return ref[here, pair * 128 : (pair + 1) * 128]


def spread(count, group, base):
    return pl.BlockSpec((count, group * 128), lambda p: (0, p + base // group))


ALL = slice(None)


def attend_kernel(items, shards, kind, blocks, group, meta, q_ref, k_ref, v_ref, o_ref, low_ref, f_ref, qa, bias_ref, s, m, l, acc):
    count = q_ref.shape[0]
    rows = k_ref.shape[0] // blocks
    frame = Frame(meta, items, count, shards)
    active, bias = block_rule(frame, kind, rows)
    step = pl.program_id(0)
    lane = lanes(count)
    own = frame.items_of_rows(frame.position * count, count)
    own_item = (lane == own).astype(jnp.float32)
    fill_bias(blocks, rows, active, bias, bias_ref, False)
    for g in range(group):
        stack_heads(qa.at[g], heads_of(q_ref, ALL, g), [own_item, own_item])
        m[g] = jnp.full((2 * count, 128), far, jnp.float32)
        l[g] = jnp.zeros((2 * count, 128), jnp.float32)
        acc[g] = jnp.zeros((2 * count, 128), jnp.float32)

    def score(block):
        here = rows_of(block, rows)
        for g in range(group):
            scores = times_transposed(qa[g], jnp.concatenate([heads_of(k_ref, here, g), bias_ref[here, :]], axis=1))
            s[g, block] = scores
            high = m[g]
            for c in range(rows // 128):
                high = jnp.maximum(high, scores[:, c * 128 : (c + 1) * 128])
            m[g] = high

    each_active(blocks, active, score)
    tops = []
    for g in range(group):
        tops.append(jnp.max(m[g], axis=1, keepdims=True))
        m[g] = jnp.broadcast_to(tops[g], (2 * count, 128))

    def weigh(block):
        here = rows_of(block, rows)
        for g in range(group):
            high = m[g]
            total = l[g]
            parts = []
            for c in range(rows // 128):
                part = jnp.exp(s[g, block, :, c * 128 : (c + 1) * 128] - high)
                total = total + part
                parts.append(part.astype(jnp.bfloat16))
            l[g] = total
            acc[g] = acc[g] + dot(jnp.concatenate(parts, axis=1), heads_of(v_ref, here, g))

    each_active(blocks, active, weigh)
    features = jnp.where(step == 0, own_item, f_ref[...].astype(jnp.float32))
    for g in range(group):
        total = jnp.sum(l[g], axis=1, keepdims=True)
        result = merge_heads(acc[g] / total)
        lse = tops[g] + jnp.log(total)
        for h in range(2):
            start = LSE_LANE + 3 * (2 * (step * group + g) + h)
            for number, piece in enumerate(pieces(lse[h * count : (h + 1) * count])):
                features = jnp.where(lane == start + number, piece, features)
        o_ref[:, g * 128 : (g + 1) * 128] = result
        low_ref[:, g * 128 : (g + 1) * 128] = result.astype(jnp.bfloat16)
    f_ref[...] = features.astype(jnp.bfloat16)


def attend(meta, count, queries, kv, kind, blocks, items, shards, name, group=3):
    width = queries.shape[1]
    pairs = width // 128
    total = kv.shape[0]
    rows = total // blocks
    tile = spread(count, group, 0)
    return pl.pallas_call(
        partial(attend_kernel, items, shards, kind, blocks, group),
        grid=(pairs // group,),
        out_shape=(
            jax.ShapeDtypeStruct((count, width), jnp.float32),
            jax.ShapeDtypeStruct((count, width), jnp.bfloat16),
            jax.ShapeDtypeStruct((count, 128), jnp.bfloat16),
        ),
        in_specs=[
            pl.BlockSpec(memory_space=pltpu.SMEM),
            tile,
            spread(total, group, 0),
            spread(total, group, pairs),
        ],
        out_specs=(tile, tile, pl.BlockSpec((count, 128), lambda p: (0, 0))),
        scratch_shapes=[
            pltpu.VMEM((group, 2 * count, 256), jnp.bfloat16),
            pltpu.VMEM((total, 128), jnp.bfloat16),
            pltpu.VMEM((group, blocks, 2 * count, rows), jnp.float32),
            pltpu.VMEM((group, 2 * count, 128), jnp.float32),
            pltpu.VMEM((group, 2 * count, 128), jnp.float32),
            pltpu.VMEM((group, 2 * count, 128), jnp.float32),
        ],
        compiler_params=pltpu.CompilerParams(vmem_limit_bytes=34 * MIB),
        cost_estimate=cost(14 if kind == "frames" else 5),
        name=name,
    )(meta, queries, kv, kv)


def query_side(pair, features, q, do, qa, da):
    lane = lanes(q.shape[0])
    heads = [2 * pair, 2 * pair + 1]
    stack_heads(qa, q, [jnp.where((lane < LSE_LANE) | head_lanes(lane, LSE_LANE, head), features, 0.0) for head in heads])
    stack_heads(da, do, [jnp.where(head_lanes(lane, DELTA_LANE, head), features, 0.0) for head in heads])


def query_step(qa, da, keys, values, bias):
    minus = jnp.where(delta_lanes(lanes(keys.shape[0])), -1.0, 0.0)
    probs = jnp.exp(times_transposed(qa[...], jnp.concatenate([keys, bias], axis=1)))
    slope = times_transposed(da[...], beside(values, minus))
    return dot((probs * slope).astype(jnp.bfloat16), keys)


def key_side(pair, k, v, mask, ka, va):
    lane = lanes(k.shape[0])
    heads = [2 * pair, 2 * pair + 1]
    stack_heads(ka, k, [jnp.where(head_lanes(lane, LSE_LANE, head), -1.0, mask) for head in heads])
    stack_heads(va, v, [jnp.where(head_lanes(lane, DELTA_LANE, head), -1.0, 0.0) for head in heads])


def key_step(ka, va, q, do, features):
    probs = jnp.exp(times_transposed(ka[...], jnp.concatenate([q, features], axis=1)))
    slope = times_transposed(va[...], jnp.concatenate([do, features], axis=1))
    return dot((probs * slope).astype(jnp.bfloat16), q), dot(probs.astype(jnp.bfloat16), do)


def query_grad_kernel(items, shards, blocks, group, meta, q_ref, do_ref, f_ref, k_ref, v_ref, dq_ref, qa, da, bias_ref, acc):
    count = q_ref.shape[0]
    rows = k_ref.shape[0] // blocks
    frame = Frame(meta, items, count, shards)
    active, bias = block_rule(frame, "frames", rows)
    fill_bias(blocks, rows, active, bias, bias_ref, True)
    features = f_ref[...].astype(jnp.float32)
    for g in range(group):
        pair = pl.program_id(0) * group + g
        query_side(pair, features, heads_of(q_ref, ALL, g), heads_of(do_ref, ALL, g), qa.at[g], da.at[g])
        acc[g] = jnp.zeros((2 * count, 128), jnp.float32)

    def step(block):
        here = rows_of(block, rows)
        for g in range(group):
            acc[g] = acc[g] + query_step(
                qa.at[g], da.at[g], heads_of(k_ref, here, g), heads_of(v_ref, here, g), bias_ref[here, :]
            )

    each_active(blocks, active, step)
    for g in range(group):
        dq_ref[:, g * 128 : (g + 1) * 128] = (merge_heads(acc[g]) * 0.125).astype(jnp.bfloat16)


def query_grad(meta, queries, grad_out, features, kv, blocks, items, shards, name, group=3):
    count, width = grad_out.shape
    pairs = width // 128
    total = kv.shape[0]
    tile = spread(count, group, 0)
    return pl.pallas_call(
        partial(query_grad_kernel, items, shards, blocks, group),
        grid=(pairs // group,),
        out_shape=jax.ShapeDtypeStruct((count, width), jnp.bfloat16),
        in_specs=[
            pl.BlockSpec(memory_space=pltpu.SMEM),
            tile,
            tile,
            pl.BlockSpec((count, 128), lambda p: (0, 0)),
            spread(total, group, 0),
            spread(total, group, pairs),
        ],
        out_specs=tile,
        scratch_shapes=[
            pltpu.VMEM((group, 2 * count, 256), jnp.bfloat16),
            pltpu.VMEM((group, 2 * count, 256), jnp.bfloat16),
            pltpu.VMEM((total, 128), jnp.bfloat16),
            pltpu.VMEM((group, 2 * count, 128), jnp.float32),
        ],
        compiler_params=pltpu.CompilerParams(vmem_limit_bytes=58 * MIB),
        cost_estimate=cost(14),
        name=name,
    )(meta, queries, grad_out, features, kv, kv)


def frame_key_grad_kernel(items, shards, blocks, group, meta, q_ref, k_ref, v_ref, dq_ref, all_ref, out_ref, ka, va, dka, dva, do_s, sem):
    count, width = dq_ref.shape[0], do_s.shape[1] - 128
    rows = q_ref.shape[0] // blocks
    frame = Frame(meta, items, count, shards)

    def arrivals(act):
        @pl.when(pl.program_id(0) == 0)
        def _():
            for block in range(2 * blocks):
                start, live = frame.chip(jnp.int32(block // 2))
                first = start + (frame.position + block) % 2 * count

                @pl.when(live)
                def _(block=block, first=first):
                    act(
                        pltpu.make_async_copy(
                            all_ref.at[pl.ds(pl.multiple_of(first, count), count), :],
                            do_s.at[pl.ds(block * count, count), :],
                            sem.at[block],
                        )
                    )

    arrivals(lambda copy: copy.start())
    mask = item_bias(frame, frame.items_of_rows(frame.position * count, count))
    for g in range(group):
        pair = pl.program_id(0) * group + g
        key_side(pair, heads_of(k_ref, ALL, g), heads_of(v_ref, ALL, g), mask, ka.at[g], va.at[g])
        dka[g] = jnp.zeros((2 * count, 128), jnp.float32)
        dva[g] = jnp.zeros((2 * count, 128), jnp.float32)
    arrivals(lambda copy: copy.wait())

    def step(block):
        here = rows_of(block, rows)
        for g in range(group):
            column = pl.multiple_of((pl.program_id(0) * group + g) * 128, 128)
            dk, dv = key_step(
                ka.at[g], va.at[g], heads_of(q_ref, here, g), do_s[here, pl.ds(column, 128)], do_s[here, width:]
            )
            dka[g] = dka[g] + dk
            dva[g] = dva[g] + dv

    each_active(blocks, lambda block: frame.chip(block)[1], step)
    for g in range(group):
        out_ref[1, :, g * 128 : (g + 1) * 128] = merge_heads(dka[g]).astype(jnp.bfloat16)
        out_ref[2, :, g * 128 : (g + 1) * 128] = merge_heads(dva[g]).astype(jnp.bfloat16)
    out_ref[0] = dq_ref[...]


def frame_key_grad(meta, q_window, do_all, kv, grad_queries, count, blocks, items, shards, name, group=3):
    total, width = q_window.shape
    pairs = width // 128
    tile = spread(count, group, 0)
    wide = spread(total, group, 0)
    return pl.pallas_call(
        partial(frame_key_grad_kernel, items, shards, blocks, group),
        grid=(pairs // group,),
        out_shape=jax.ShapeDtypeStruct((3, count, width), jnp.bfloat16),
        in_specs=[
            pl.BlockSpec(memory_space=pltpu.SMEM),
            wide,
            tile,
            spread(count, group, pairs),
            tile,
        ]
        + [pl.BlockSpec(memory_space=pl.ANY)],
        out_specs=pl.BlockSpec((3, count, group * 128), lambda p: (0, 0, p)),
        scratch_shapes=[pltpu.VMEM((group, 2 * count, 256), jnp.bfloat16)] * 2
        + [pltpu.VMEM((group, 2 * count, 128), jnp.float32)] * 2
        + [pltpu.VMEM((total, width + 128), jnp.bfloat16), pltpu.SemaphoreType.DMA((2 * blocks,))],
        compiler_params=pltpu.CompilerParams(vmem_limit_bytes=58 * MIB),
        cost_estimate=cost(18),
        name=name,
    )(meta, q_window, kv, kv, grad_queries, do_all)


def text_grad_kernel(items, shards, group, meta, q_ref, do_ref, f_ref, k_ref, v_ref, dq_ref, dkv_ref, qa, da, ka, va, acc):
    count = q_ref.shape[0]
    rows = k_ref.shape[0] // items
    share = rows // shards
    frame = Frame(meta, items, count, shards)
    features = f_ref[...].astype(jnp.float32)
    pairs = [pl.program_id(0) * group + g for g in range(group)]
    for g in range(group):
        query_side(pairs[g], features, heads_of(q_ref, ALL, g), heads_of(do_ref, ALL, g), qa.at[g], da.at[g])
        acc[g] = jnp.zeros((2 * count, 128), jnp.float32)

    @pl.loop(0, items)
    def _(item):
        here = rows_of(item, rows)
        live = (item >= frame.first) & (item <= frame.last)
        target = rows_of(item, share)

        @pl.when(live)
        def _():
            mask = text_bias(frame, item, rows)
            bias = jnp.where(lse_lanes(lanes(rows)), -1.0, mask).astype(jnp.bfloat16)
            for g in range(group):
                keys, values = heads_of(k_ref, here, g), heads_of(v_ref, here, g)
                acc[g] = acc[g] + query_step(qa.at[g], da.at[g], keys, values, bias)
                key_side(pairs[g], keys, values, mask, ka.at[g], va.at[g])
                grads = key_step(ka.at[g], va.at[g], heads_of(q_ref, ALL, g), heads_of(do_ref, ALL, g), f_ref[...])
                for which, grad in enumerate(grads):
                    merged = merge_heads(grad).astype(jnp.bfloat16)
                    for owner in range(shards):
                        dkv_ref[owner, which, target, g * 128 : (g + 1) * 128] = merged[
                            owner * share : (owner + 1) * share
                        ]

        @pl.when(jnp.logical_not(live))
        def _():
            dkv_ref[:, :, target, :] = jnp.zeros((shards, 2, share, group * 128), jnp.bfloat16)

    for g in range(group):
        dq_ref[:, g * 128 : (g + 1) * 128] = (merge_heads(acc[g]) * 0.125).astype(jnp.bfloat16)


def text_grad(meta, queries, grad_out, features, kv, items, shards, name, group=3):
    count, width = queries.shape
    pairs = width // 128
    total = kv.shape[0]
    tile = spread(count, group, 0)
    rows = total // items
    return pl.pallas_call(
        partial(text_grad_kernel, items, shards, group),
        grid=(pairs // group,),
        out_shape=(
            jax.ShapeDtypeStruct((count, width), jnp.bfloat16),
            jax.ShapeDtypeStruct((shards, 2, total // shards, width), jnp.bfloat16),
        ),
        in_specs=[
            pl.BlockSpec(memory_space=pltpu.SMEM),
            tile,
            tile,
            pl.BlockSpec((count, 128), lambda p: (0, 0)),
            spread(total, group, 0),
            spread(total, group, pairs),
        ],
        out_specs=(tile, pl.BlockSpec((shards, 2, total // shards, group * 128), lambda p: (0, 0, 0, p))),
        scratch_shapes=[pltpu.VMEM((group, 2 * count, 256), jnp.bfloat16)] * 2
        + [pltpu.VMEM((group, 2 * rows, 256), jnp.bfloat16)] * 2
        + [pltpu.VMEM((group, 2 * count, 128), jnp.float32)],
        compiler_params=pltpu.CompilerParams(vmem_limit_bytes=18 * MIB),
        cost_estimate=cost(8),
        name=name,
    )(meta, queries, grad_out, features, kv, kv)


def mlp_kernel(h_ref, d_ref, up_ref, down_ref, act_ref, m_ref, dh_ref):
    step = pl.program_id(0)
    last = pl.num_programs(0) - 1

    @pl.when(step < last)
    def _():
        u = dot(h_ref[...], up_ref[...])
        slope = times_transposed(d_ref[...], down_ref[...])
        inner = 0.7978845608028654 * (u + 0.044715 * (u * u * u))
        t = jnp.tanh(inner)
        g = (0.5 * u * (1.0 + t)).astype(jnp.bfloat16)
        bend = 0.7978845608028654 * (1.0 + 0.134145 * (u * u))
        du = (slope * (0.5 * (1.0 + t) + 0.5 * u * (1.0 - t * t) * bend)).astype(jnp.bfloat16)
        act_ref[0, 0] = g
        act_ref[0, 1] = du
        m = dot(g, down_ref[...])
        dh = times_transposed(du, up_ref[...])

        @pl.when(step == 0)
        def _():
            m_ref[...] = m
            dh_ref[...] = dh

        @pl.when(step > 0)
        def _():
            m_ref[...] = m_ref[...] + m
            dh_ref[...] = dh_ref[...] + dh

    @pl.when(step == last)
    def _():
        act_ref[0, 0] = h_ref[...]
        act_ref[0, 1] = d_ref[...]


def mlp(hidden, grad, w_up, w_down):
    count, width = hidden.shape
    chunks = w_up.shape[1] // width
    whole = pl.BlockSpec((count, width), lambda c: (0, 0))
    held = lambda c: jnp.minimum(c, chunks - 1)
    return pl.pallas_call(
        mlp_kernel,
        grid=(chunks + 1,),
        out_shape=(
            jax.ShapeDtypeStruct((chunks + 1, 2, count, width), jnp.bfloat16),
            jax.ShapeDtypeStruct((count, width), jnp.float32),
            jax.ShapeDtypeStruct((count, width), jnp.float32),
        ),
        in_specs=[
            whole,
            whole,
            pl.BlockSpec((width, width), lambda c: (0, held(c))),
            pl.BlockSpec((width, width), lambda c: (held(c), 0)),
        ],
        out_specs=(pl.BlockSpec((1, 2, count, width), lambda c: (c, 0, 0, 0)), whole, whole),
        compiler_params=pltpu.CompilerParams(vmem_limit_bytes=20 * MIB),
        cost_estimate=cost(9),
        name="mlp",
    )(hidden, grad, w_up, w_down)


UNIT = 192
X_BIT, Y_BIT = 0, 1


def rows_picked(x, core):
    row = lax.broadcasted_iota(jnp.int32, (384, 768), 0)
    column = lax.broadcasted_iota(jnp.int32, (384, 768), 1)
    chip = (row >= 96).astype(jnp.int32) + (row >= 192).astype(jnp.int32) + (row >= 288).astype(jnp.int32)
    pick = (column == row + 96 * (chip + core)).astype(jnp.bfloat16)
    return times_transposed(pick, x).astype(jnp.bfloat16)


def one_above_other(upper, lower):
    return jnp.concatenate([upper, lower], axis=0)


def finish_kernel(items, shards, packed, meta, mod_ref, w_ref, d_ref, x_ref, dx_ref, a_ref, dh_ref, n_ref, dy_ref, m_ref, out_ref, sum_ref):
    count, width = x_ref.shape
    frame = Frame(meta, items, count, shards)
    item = frame.items_of_rows(frame.position * count, count)
    grad = sum(times_transposed(d_ref[i], w_ref[:, i * width : (i + 1) * width]) for i in range(3))
    normed, inverse = layer_norm(x_ref[...].astype(jnp.float32))
    scale = jnp.zeros((count, width), jnp.float32)
    for i in range(items):
        scale = jnp.where(item == i, mod_ref[i, 1:2, :], scale)
    dx = dx_ref[...]
    out_ref[...] = dx + norm_back(grad * (1.0 + scale), normed, inverse)
    dh = dh_ref[...]
    terms = (
        grad,
        grad * normed,
        dx * a_ref[...],
        dh,
        dh * n_ref[...],
        dy_ref[...].astype(jnp.float32) * m_ref[...],
    )
    sums = []
    for number, term in enumerate(terms):
        rows = [jnp.sum(jnp.where(item == i, term, 0.0), axis=0, keepdims=True) for i in range(items)]
        rows += [jnp.zeros((8 - items, width), jnp.float32)]
        sums.append(jnp.concatenate(rows, axis=0))
        if not packed:
            sum_ref[number] = sums[number]
    if packed:
        values = jnp.concatenate(sums, axis=0)
        left = lax.broadcasted_iota(jnp.int32, (24, 384), 1) < UNIT
        for pair in range(2):
            part = third(values, pair)
            rolled = pltpu.roll(part, UNIT, 1)
            each = (jnp.where(left, part[:24], rolled[24:]), jnp.where(left, rolled[:24], part[24:]))
            for half in range(2):
                relative = (2 * pair + half) ^ (frame.position // 2)
                sum_ref[relative % 2, relative // 2, :24, :] = each[half]
                sum_ref[relative % 2, relative // 2, 24:, :] = jnp.zeros((8, 384), jnp.float32)


def finish(meta, modulation, weight, grads, frames, *arrays_items_shards):
    *arrays, items, shards, packed = arrays_items_shards
    count, width = frames.shape
    whole = pl.BlockSpec(memory_space=pltpu.VMEM)
    return pl.pallas_call(
        partial(finish_kernel, items, shards, packed),
        out_shape=(
            jax.ShapeDtypeStruct((count, width), jnp.float32),
            jax.ShapeDtypeStruct((2, 2, 32, 384) if packed else (6, 8, width), jnp.float32),
        ),
        in_specs=[pl.BlockSpec(memory_space=pltpu.SMEM)] + [whole] * (4 + len(arrays)),
        out_specs=(whole, whole),
        compiler_params=pltpu.CompilerParams(vmem_limit_bytes=20 * MIB),
        cost_estimate=cost(5),
        name="finish",
    )(meta, modulation, weight, grads, frames, *arrays)


class Packer:
    def __init__(self, meta, items, outputs):
        self.core, self.chip = meta[0] % 2, meta[0] // 2
        self.mine = meta[1 + 2 * items]
        self.outputs = outputs

    def steps(self, owner_chip):
        relative = owner_chip ^ self.chip
        return relative % 2, relative // 2

    def store(self, name, owner, owner_chip, row, values):
        scratch, first = self.outputs[name]
        relative = owner ^ self.mine
        where = ((relative >> first) % 2, (relative >> (1 - first)) % 2, *self.steps(owner_chip))
        scratch[where + (slice(row, row + values.shape[0]),)] = values.astype(jnp.bfloat16)

    def store_split(self, name, pair, row, values, chips):
        rolled = pltpu.roll(values, UNIT, 1)
        each = values.shape[0] // len(chips)
        left = lax.broadcasted_iota(jnp.int32, (each // 2, 384), 1) < UNIT
        for number, owner_chip in enumerate(chips):
            upper = slice(number * each, number * each + each // 2)
            lower = slice(number * each + each // 2, (number + 1) * each)
            self.store(name, 2 * pair, owner_chip, row, jnp.where(left, values[upper], rolled[lower]))
            self.store(name, 2 * pair + 1, owner_chip, row, jnp.where(left, rolled[upper], values[lower]))


def core_columns(core, number, each):
    return pl.ds(pl.multiple_of(number * 2 * each + core * each, 128), each)


def third(values, number):
    return values[:, number * 384 : (number + 1) * 384]


def pack_mlp_kernel(items, meta, own, sib, down_s, up_s):
    packer = Packer(meta, items, {"down": (down_s, Y_BIT), "up": (up_s, X_BIT)})
    both = lambda chunk, which: one_above_other(own[chunk, which], sib[chunk, which])
    grad = both(4, 1)
    for owner_chip in range(4):
        here = core_columns(packer.core, 0, 384)
        left = one_above_other(own[owner_chip, 0, :, here], sib[owner_chip, 0, :, here])
        values = contract_rows(left, grad)
        for pair in range(2):
            packer.store_split("down", pair, 0, third(values, pair), [owner_chip])
    left = rows_picked(both(4, 0), packer.core)
    for owner in range(4):
        values = dot(left, both(owner, 1))
        for owner_chip in range(4):
            for half in range(2):
                packer.store(
                    "up", owner, owner_chip, half * 96, third(values, half)[owner_chip * 96 : (owner_chip + 1) * 96]
                )


def pack_middle_kernel(items, meta, own, sib, text_own, text_sib, text, square_s, text_s):
    packer = Packer(meta, items, {"square": (square_s, Y_BIT), "text": (text_s, X_BIT)})
    both = lambda which: one_above_other(own[which], sib[which])
    for number in range(3):
        values = dot(rows_picked(both(2 * number), packer.core), both(2 * number + 1))
        for pair in range(2):
            packer.store_split("square", pair, number * 48, third(values, pair), range(4))
    share = text_own.shape[2] // items

    def chip_sum(which, item, owner):
        here = slice(item * share, (item + 1) * share)
        total = text_own[owner, which, here, :].astype(jnp.float32) + text_sib[owner, which, here, :].astype(jnp.float32)
        return total.astype(jnp.bfloat16)

    sums = [
        jnp.concatenate(
            [chip_sum(which, item, owner) for item in range(items) for owner in range(text_own.shape[0])], axis=0
        )
        for which in range(2)
    ]
    left = jnp.concatenate([text[:, core_columns(packer.core, chip, 128)] for chip in range(4)], axis=1)
    for which in range(2):
        values = contract_rows(left, sums[which])
        for owner_chip in range(4):
            for half in range(2):
                packer.store(
                    "text", 2 * which + half, owner_chip, 0, third(values, half)[owner_chip * 128 : (owner_chip + 1) * 128]
                )


def pack_qkv_kernel(items, meta, h_own, h_sib, own, sib, plain_s, split_s):
    packer = Packer(meta, items, {"plain": (plain_s, X_BIT), "split": (split_s, Y_BIT)})
    left = rows_picked(one_above_other(h_own[...], h_sib[...]), packer.core)
    values = []
    for number in range(3):
        product = dot(left, one_above_other(own[number], sib[number]))
        values += [third(product, 0), third(product, 1)]
    for owner, column in enumerate((0, 2, 3, 5)):
        for owner_chip in range(4):
            packer.store("plain", owner, owner_chip, 0, values[column][owner_chip * 96 : (owner_chip + 1) * 96])
    for pair, column in enumerate((1, 4)):
        packer.store_split("split", pair, 0, values[column], range(4))


def packing(kernel, items, inputs, groups, *refs):
    ins, outs, scratch, sem = refs[:inputs], refs[inputs:-groups - 1], refs[-groups - 1 : -1], refs[-1]
    kernel(items, *ins, *scratch)
    copies = [pltpu.make_async_copy(scratch[i // 2].at[1 - i % 2], outs[i], sem.at[i]) for i in range(2 * groups)]
    for copy in copies:
        copy.start()
    for copy in copies:
        copy.wait()


def pack(kernel, meta, operands, shapes, items, name):
    shapes = [(2, 2, 2, each, 384) if isinstance(each, int) else each for each in shapes]
    whole = pl.BlockSpec(memory_space=pltpu.VMEM)
    return pl.pallas_call(
        partial(packing, kernel, items, 1 + len(operands), len(shapes)),
        out_shape=tuple(jax.ShapeDtypeStruct(shape, jnp.bfloat16) for shape in shapes for _ in range(2)),
        in_specs=[pl.BlockSpec(memory_space=pltpu.SMEM)] + [whole] * len(operands),
        out_specs=tuple([pl.BlockSpec(memory_space=pl.ANY)] * (2 * len(shapes))),
        scratch_shapes=[pltpu.VMEM((2, *shape), jnp.bfloat16) for shape in shapes]
        + [pltpu.SemaphoreType.DMA((2 * len(shapes),))],
        compiler_params=pltpu.CompilerParams(vmem_limit_bytes=58 * MIB),
        cost_estimate=cost(8 if name != "pack_qkv" else 3),
        name=name,
    )(meta, *operands)


def bundle_kernel(*refs):
    for number, each in enumerate(refs[:-1]):
        refs[-1][number] = each[...]


def bundle(*arrays):
    whole = pl.BlockSpec(memory_space=pltpu.VMEM)
    return pl.pallas_call(
        bundle_kernel,
        out_shape=jax.ShapeDtypeStruct((len(arrays), *arrays[0].shape), arrays[0].dtype),
        in_specs=[whole] * len(arrays),
        out_specs=whole,
        cost_estimate=cost(3),
        name="bundle",
    )(*arrays)


def trade(values, axis, bit):
    size = lax.axis_size(axis)
    return lax.ppermute(values, axis, [(i, i ^ (1 << bit)) for i in range(size)])


def added(keep, got):
    return [(keep[i].astype(jnp.float32) + got[i].astype(jnp.float32)).astype(jnp.bfloat16) for i in range(2)]


def halve(keep, send, axis, bit, after=()):
    got = trade(send, axis, bit)
    if after:
        [keep] = hold((keep,), *after)
    return added(keep, got)


def last_half(keep, send, after=()):
    got = trade(send, "seq", 2)
    if after:
        [keep] = hold((keep,), *after)
    return keep.astype(jnp.float32) + got.astype(jnp.float32)


def joined(upper, lower):
    return [jnp.concatenate([upper[i], lower[i]], axis=-2) for i in (1, 0)]


def unsplit(rows):
    return jnp.concatenate([rows[:, :UNIT], rows[:, UNIT:]], axis=0)


def with_deltas(features, grad_out, attn_exact):
    width = attn_exact.shape[1]
    lane = jnp.arange(128)[None, :]
    head = (jnp.arange(width) // (width // H))[:, None]
    pick = ((lane >= DELTA_LANE) & ((lane - DELTA_LANE) // 3 == head)).astype(jnp.float32)
    delta = jnp.dot(
        grad_out.astype(jnp.float32) * attn_exact,
        pick,
        precision=lax.Precision.HIGHEST,
        preferred_element_type=jnp.float32,
    )
    high = lax.reduce_precision(delta, 8, 7)
    middle = lax.reduce_precision(delta - high, 8, 7)
    which = (lane - DELTA_LANE) % 3
    piece = jnp.where(which == 0, high, jnp.where(which == 1, middle, delta - high - middle))
    inside = (lane >= DELTA_LANE) & (lane < DELTA_LANE + 3 * H)
    return jnp.where(inside, piece.astype(jnp.bfloat16), features)


def hop(below, above, shards):
    up = [(i, i + 2) for i in range(shards - 2)]
    return lax.ppermute(below, "seq", up), lax.ppermute(above, "seq", [(j, i) for i, j in up])


def hold(values, *first):
    held = lax.optimization_barrier((*values, *first))
    return held[: len(values)]


def body(
    frames,
    cotangent,
    modulation,
    lengths,
    text,
    text_len,
    w_qkv,
    w_o,
    w_cq,
    w_ckv,
    w_co,
    w_up,
    w_down,
):
    local = frames[0]
    count, width = local.shape
    items = lengths.shape[1]
    text_rows, text_width = text.shape[2:]
    shards = lax.axis_size("seq")
    position = lax.axis_index("seq")
    reach = min(-(-(LONGEST - 1) // (2 * count)), shards // 2 - 1)
    chips = 1 + 2 * reach
    meta = jnp.concatenate(
        [position[None].astype(jnp.int32), lengths[0], text_len[0], lax.axis_index("batch")[None].astype(jnp.int32)]
    )
    item_range = jnp.arange(items, dtype=jnp.int32)
    ends = jnp.sum(jnp.where(item_range[None, :] <= item_range[:, None], lengths[0][None, :], 0), axis=1)
    place = position * count + jnp.arange(count, dtype=jnp.int32)
    query_items = jnp.sum((place[:, None] >= ends[None, :]).astype(jnp.int32), axis=1)[:, None]
    mod = modulation[0]

    def per_frame(which):
        found = jnp.broadcast_to(mod[0, which][None, :], (count, width))
        for item in range(1, items):
            found = jnp.where(query_items == item, mod[item, which][None, :], found)
        return found

    swap = [(i, i ^ 1) for i in range(shards)]

    def sibling(values):
        return lax.ppermute(values, "seq", swap)

    fast = shards == 8 and lax.axis_size("batch") == 4 and width == 768

    text_proj = jnp.dot(
        text[0].reshape(items * text_rows, text_width), w_ckv, preferred_element_type=jnp.float32
    ).astype(jnp.bfloat16)
    hidden_one = hide(meta, mod, local, items, shards)
    sides = list(hold(hop(hidden_one, hidden_one, shards), text_proj))
    for _ in range(1, reach):
        sides += hop(*sides[-2:], shards)

    def with_siblings(blocks):
        return [each for block in blocks for each in (block, sibling(block))]

    total = 2 * chips * count
    near = with_siblings([hidden_one] + sides[:2])
    hidden_sib = near[1]
    q_window, kv = project(meta, w_qkv, near, range(3), total, (), items, shards, "project_near")
    if reach > 1:
        apart = with_siblings(hold(sides[2:], kv))
        q_window, kv = project(
            meta, w_qkv, apart, range(3, chips), total, (q_window, kv), items, shards, "project_far"
        )
    inputs = local.astype(jnp.float32)
    attn_exact, attended, features = attend(meta, count, q_window, kv, "frames", chips, items, shards, "self_attend")
    branch_one = jnp.dot(attended, w_o, preferred_element_type=jnp.float32)
    after_attn = inputs + per_frame(2) * branch_one
    normed_cross, inverse_cross = layer_norm(after_attn)
    cross_in = normed_cross.astype(jnp.bfloat16)
    cross_queries = jnp.dot(cross_in, w_cq, preferred_element_type=jnp.float32).astype(jnp.bfloat16)
    cross_queries = (cross_queries.astype(jnp.float32) * 0.125).astype(jnp.bfloat16)
    cross_exact, cross_out, cross_features = attend(
        meta, count, cross_queries, text_proj, "text", items, items, shards, "cross_attend"
    )
    branch_two = jnp.dot(cross_out, w_co, preferred_element_type=jnp.float32)
    after_cross = after_attn + branch_two
    normed_two, inverse_two = layer_norm(after_cross)
    hidden_two = (normed_two * (1.0 + per_frame(4)) + per_frame(3)).astype(jnp.bfloat16)
    gate_two = per_frame(5)
    grad_out = cotangent[0].astype(jnp.float32)
    grad_branch_three = (grad_out * gate_two).astype(jnp.bfloat16)
    acts, branch_three, grad_hidden_two = mlp(hidden_two, grad_branch_three, w_up, w_down)
    if fast:
        acts_sib = sibling(acts)
    result = after_cross + gate_two * branch_three
    grad_cross = grad_out + norm_back(grad_hidden_two * (1.0 + per_frame(4)), normed_two, inverse_two)
    grad_branch_two = grad_cross.astype(jnp.bfloat16)
    grad_cross_out = times_transposed(grad_branch_two, w_co).astype(jnp.bfloat16)
    cross_features = with_deltas(cross_features, grad_cross_out, cross_exact)
    grad_cross_queries, text_terms = text_grad(
        meta, cross_queries, grad_cross_out, cross_features, text_proj, items, shards, "cross_grad"
    )
    grad_attn_res = grad_cross + norm_back(
        times_transposed(grad_cross_queries, w_cq), normed_cross, inverse_cross
    )
    grad_branch_one = (grad_attn_res * per_frame(2)).astype(jnp.bfloat16)
    if fast:
        text_sib = sibling(text_terms)
        [grad_branch_one] = hold((grad_branch_one,), text_sib)
    grad_attended = times_transposed(grad_branch_one, w_o).astype(jnp.bfloat16)
    features = with_deltas(features, grad_attended, attn_exact)
    do_low = jnp.concatenate([grad_attended, features], axis=1)
    do_all = lax.all_gather(do_low, "seq", axis=0, tiled=True)
    if fast:
        middle = bundle(cross_out, grad_branch_two, cross_in, grad_cross_queries, attended, grad_branch_one)
        middle_sib = sibling(middle)
        [acts_sib] = hold((acts_sib,), do_low, middle)
        mlp_parts = pack(pack_mlp_kernel, meta, (acts, acts_sib), (192, 192), items, "pack_mlp")
        [grad_attended] = hold((grad_attended,), *mlp_parts)
    grad_queries = query_grad(
        meta, q_window, grad_attended, features, kv, chips, items, shards, "self_query_grad"
    )
    share_rows = text_rows // shards
    [text_terms_late] = hold((text_terms,), grad_queries)
    text_total = lax.psum_scatter(
        text_terms_late.reshape(shards * 2 * items * share_rows, width), "seq", scatter_dimension=0, tiled=True
    ).reshape(2, items * share_rows, width)
    if fast:
        middle_parts = pack(
            pack_middle_kernel,
            meta,
            (middle, middle_sib, text_terms, text_sib, text[0].reshape(items * text_rows, text_width)),
            (144, 128),
            items,
            "pack_middle",
        )
        down_part = halve(mlp_parts[1], mlp_parts[0], "batch", Y_BIT, (middle_parts[0],))
        up_part = halve(mlp_parts[3], mlp_parts[2], "batch", X_BIT, (middle_parts[0],))
        [do_all] = hold((do_all,), *middle_parts, *down_part, *up_part)
    grad_projected = frame_key_grad(
        meta, q_window, do_all, kv, grad_queries, count, chips, items, shards, "self_key_grad"
    )
    if fast:
        projected_sib = sibling(grad_projected)
    grad_inputs, terms = finish(
        meta, mod, w_qkv, grad_projected, local, grad_attn_res, branch_one, grad_hidden_two, normed_two, cotangent[0],
        branch_three, items, shards, fast,
    )
    if not fast:
        for bit in range(shards.bit_length() - 1):
            terms = terms + trade(terms, "seq", bit)
        own = width // shards
        terms = lax.dynamic_slice_in_dim(terms, position * own, own, 2)
        shares = terms[:, :items].transpose(1, 0, 2)
    if fast:
        [projected_sib] = hold((projected_sib,), grad_inputs)
        qkv_parts = pack(
            pack_qkv_kernel,
            meta,
            (hidden_one, hidden_sib, grad_projected, projected_sib),
            (96, 48),
            items,
            "pack_qkv",
        )
        square_send, square_keep, text_send, text_keep = middle_parts
        got = (
            trade(down_part[1], "batch", X_BIT),
            trade(up_part[1], "batch", Y_BIT),
            trade(square_send, "batch", Y_BIT),
            trade(text_send, "batch", X_BIT),
        )
        got = hold(got, grad_inputs)
        down_part, up_part = added(down_part[0], got[0]), added(up_part[0], got[1])
        square_part, text_w_part = added(square_keep, got[2]), added(text_keep, got[3])
        first_send, first_keep = joined(down_part, up_part)
        terms = (terms + trade(terms, "seq", 0)).astype(jnp.bfloat16)
        plain_send, plain_keep, split_send, split_keep = qkv_parts
        first_part = halve(first_keep, first_send, "seq", 1, (qkv_parts[0],))
        square_part = halve(*square_part, "batch", X_BIT, first_part)
        text_w_part = halve(*text_w_part, "batch", Y_BIT, first_part)
        half_way = (*square_part, *text_w_part)
        plain_part = halve(plain_keep, plain_send, "batch", X_BIT, half_way)
        split_part = halve(split_keep, split_send, "batch", Y_BIT, half_way)
        half_way = (*plain_part, *split_part)
        plain_part = halve(*plain_part, "batch", Y_BIT)
        split_part = halve(*split_part, "batch", X_BIT)
        sent = [jnp.concatenate([plain_part[i], split_part[i], terms[i]], axis=-2) for i in (1, 0)]
        middle_send, middle_keep = joined(square_part, text_w_part)
        middle_part = halve(middle_keep, middle_send, "seq", 1, half_way)
        last_part = halve(sent[1], sent[0], "seq", 1)
        last_rows = last_half(*last_part)
        middle_rows = last_half(*middle_part, last_part)
        first_rows = last_half(*first_part, sent)
        own_terms = unsplit(last_rows[144:168])
        own = width // shards
        own_terms = lax.dynamic_slice_in_dim(own_terms, (position % 2) * own, own, 1)
        shares = own_terms.reshape(6, 8, own)[:, :items].transpose(1, 0, 2)
        last_rows = last_rows[:144]
        [text_total] = hold((text_total,), *sent)
        plain, split = last_rows[:96], unsplit(last_rows[96:])
        even = lax.axis_index("batch") % 2 == 0
        grads = (
            jnp.where(even, jnp.concatenate([plain, split], axis=1), jnp.concatenate([split, plain], axis=1)),
            unsplit(middle_rows[96:144]),
            unsplit(middle_rows[48:96]),
            middle_rows[144:],
            unsplit(middle_rows[:48]),
            jnp.concatenate([first_rows[192:288], first_rows[288:]], axis=1),
            unsplit(first_rows[:192]),
        )
    text_grad_low = jnp.concatenate([text_total[0], text_total[1]], axis=1)
    grad_text = times_transposed(text_grad_low, w_ckv).reshape(1, items, share_rows, text_width)
    if not fast:
        text_mine = lax.dynamic_slice_in_dim(text[0], position * share_rows, share_rows, 1)
        grads = reduced_grads(
            (hidden_one, jnp.concatenate(list(grad_projected), axis=1)),
            (attended, grad_branch_one),
            (cross_in, grad_cross_queries),
            (text_mine.reshape(items * share_rows, text_width), text_grad_low),
            (cross_out, grad_branch_two),
            (hidden_two, acts[:-1, 1].transpose(1, 0, 2).reshape(count, -1)),
            (acts[:-1, 0].transpose(1, 0, 2).reshape(count, -1), grad_branch_three),
        )
    return (
        result.astype(jnp.bfloat16)[None],
        grad_inputs[None],
        shares[:, :3][None],
        shares[:, 3:][None],
        grad_text,
        *grads,
    )


def reduced_grads(*pairs):
    def reduce_weight(left, right):
        grad = contract_rows(left, right).astype(jnp.bfloat16)
        part = lax.psum_scatter(grad, "seq", scatter_dimension=0, tiled=True)
        return lax.psum_scatter(part, "batch", scatter_dimension=1, tiled=True).astype(jnp.float32)

    return tuple(reduce_weight(*pair) for pair in pairs)


def solution(mesh):
    in_specs = (
        P("batch", "seq", None),
        P("batch", "seq", None),
        P("batch", None, None, None),
        P("batch", None),
        P("batch", None, None, None),
        P("batch", None),
        P(),
        P(),
        P(),
        P(),
        P(),
        P(),
        P(),
    )
    out_specs = (
        P("batch", "seq", None),
        P("batch", "seq", None),
        P("batch", None, None, "seq"),
        P("batch", None, None, "seq"),
        P("batch", None, "seq", None),
        P("seq", "batch"),
        P("seq", "batch"),
        P("seq", "batch"),
        P("seq", "batch"),
        P("seq", "batch"),
        P("seq", "batch"),
        P("seq", "batch"),
    )
    return jax.shard_map(body, mesh=mesh, in_specs=in_specs, out_specs=out_specs, check_vma=False)
```

```python
from functools import partial

import jax
import jax.numpy as jnp
from jax import lax
from jax.experimental import pallas as pl
from jax.experimental.pallas import tpu as pltpu
from jax.sharding import PartitionSpec as P

H = 12
LONGEST = 1024

epsilon = 1e-06
far = -1e30
LSE_LANE = 8
DELTA_LANE = 44
MIB = 1 << 20
FLOPS_EACH, BYTES_EACH = 5e+08, 1.65e+06


def layer_norm(values):
    centred = values - jnp.mean(values, axis=-1, keepdims=True)
    inverse = lax.rsqrt(jnp.mean(centred * centred, axis=-1, keepdims=True) + epsilon)
    return (centred * inverse, inverse)


def norm_back(grad_normed, normed, inverse):
    return inverse * (
        grad_normed
        - jnp.mean(grad_normed, axis=-1, keepdims=True)
        - normed * jnp.mean(grad_normed * normed, axis=-1, keepdims=True)
    )


def contract_rows(left, right):
    return lax.dot_general(
        left, right, (((0,), (0,)), ((), ())), preferred_element_type=jnp.float32
    )


def times_transposed(left, right):
    return lax.dot_general(
        left, right, (((1,), (1,)), ((), ())), preferred_element_type=jnp.float32
    )


class Frame:
    def __init__(self, meta, items, count, shards):
        self.position = meta[0]
        self.items = items
        self.count = count
        self.shards = shards
        self.ends = []
        total = jnp.int32(0)
        for item in range(items):
            total = total + meta[1 + item]
            self.ends.append(total)
        self.text_len = [meta[1 + items + item] for item in range(items)]
        self.first = self.item_of(self.position * count)
        self.last = self.item_of(self.position * count + count - 1)
        self.low = jnp.int32(0)
        self.high = jnp.int32(0)
        for item in range(items):
            start = self.ends[item] - meta[1 + item]
            self.low = jnp.where(self.first == item, start, self.low)
            self.high = jnp.where(self.last == item, self.ends[item], self.high)

    def item_of(self, place):
        found = jnp.int32(0)
        for end in self.ends:
            found = found + (place >= end).astype(jnp.int32)
        return found

    def items_of_rows(self, base, rows):
        place = base + lax.broadcasted_iota(jnp.int32, (rows, 1), 0)
        found = jnp.zeros((rows, 1), jnp.int32)
        for end in self.ends:
            found = found + (place >= end).astype(jnp.int32)
        return found

    def items_of_chip(self, block):
        start, _ = self.chip(block)
        core = self.position % 2
        return jnp.concatenate(
            [
                self.items_of_rows(start + core * self.count, self.count),
                self.items_of_rows(start + (1 - core) * self.count, self.count),
            ],
            axis=0,
        )

    def chip(self, block):
        hop = (block + 1) // 2
        chip = self.position // 2 + jnp.where(block % 2 == 1, -hop, hop)
        rows = 2 * self.count
        start = chip * rows
        live = (chip >= 0) & (chip < self.shards // 2)
        return start, live & (start < self.high) & (start + rows > self.low)


def lanes(rows):
    return lax.broadcasted_iota(jnp.int32, (rows, 128), 1)


def lse_lanes(lane):
    return (lane >= LSE_LANE) & (lane < DELTA_LANE)


def delta_lanes(lane):
    return (lane >= DELTA_LANE) & (lane < DELTA_LANE + 3 * H)


def head_lanes(lane, base, head):
    start = base + 3 * head
    return (lane >= start) & (lane < start + 3)


def cost(microseconds):
    return pl.CostEstimate(
        flops=int(microseconds * FLOPS_EACH), bytes_accessed=int(microseconds * BYTES_EACH), transcendentals=0
    )


def beside(left, right):
    return jnp.concatenate([left.astype(jnp.bfloat16), right.astype(jnp.bfloat16)], axis=1)


def pieces(values):
    high = values.astype(jnp.bfloat16).astype(jnp.float32)
    rest = values - high
    middle = rest.astype(jnp.bfloat16).astype(jnp.float32)
    return high, middle, rest - middle


def dot(left, right):
    return jnp.dot(left, right, preferred_element_type=jnp.float32)


def stack_heads(target, values, features):
    rows = values.shape[0]
    half = lanes(rows) // 64
    wide = values.astype(jnp.float32)
    for h in range(2):
        target[h * rows : (h + 1) * rows, :] = beside(jnp.where(half == h, wide, 0.0), features[h])


def merge_heads(stacked):
    rows = stacked.shape[0] // 2
    return jnp.where(lanes(rows) < 64, stacked[:rows], stacked[rows:])


def item_bias(frame, item):
    lane = lanes(item.shape[0])
    return jnp.where((lane != item) & (lane < frame.items), far, 0.0)


def text_bias(frame, block, rows):
    slot = lax.broadcasted_iota(jnp.int32, (rows, 1), 0)
    length = jnp.int32(0)
    for item in range(frame.items):
        length = jnp.where(block == item, frame.text_len[item], length)
    lane = lanes(rows)
    dead = (lane != block) | (slot >= length)
    return jnp.where(dead & (lane < frame.items), far, 0.0)


def block_rule(frame, kind, rows):
    if kind == "frames":
        return (
            lambda block: frame.chip(block)[1],
            lambda block: item_bias(frame, frame.items_of_chip(block)),
        )
    return (
        lambda block: (block >= frame.first) & (block <= frame.last),
        lambda block: text_bias(frame, block, rows),
    )


def rows_of(block, rows):
    return pl.ds(pl.multiple_of(block * rows, rows), rows)


def each_active(blocks, active, step):
    @pl.loop(0, blocks)
    def _(block):
        @pl.when(active(block))
        def _():
            step(block)


def fill_bias(blocks, rows, active, bias, target, with_lse):
    @pl.when(pl.program_id(0) == 0)
    def _():
        def step(block):
            mask = bias(block)
            if with_lse:
                mask = jnp.where(lse_lanes(lanes(rows)), -1.0, mask)
            target[rows_of(block, rows), :] = mask.astype(jnp.bfloat16)

        each_active(blocks, active, step)


def hide_kernel(items, shards, meta, mod_ref, x_ref, h_ref):
    count, _ = x_ref.shape
    frame = Frame(meta, items, count, shards)
    normed, _ = layer_norm(x_ref[...].astype(jnp.float32))
    item = frame.items_of_rows(frame.position * count, count)
    shift = jnp.broadcast_to(mod_ref[0, 0:1, :], normed.shape)
    scale = jnp.broadcast_to(mod_ref[0, 1:2, :], normed.shape)
    for i in range(1, items):
        shift = jnp.where(item == i, mod_ref[i, 0:1, :], shift)
        scale = jnp.where(item == i, mod_ref[i, 1:2, :], scale)
    h_ref[...] = (normed * (1.0 + scale) + shift).astype(jnp.bfloat16)


def hide(meta, modulation, frames, items, shards):
    whole = pl.BlockSpec(memory_space=pltpu.VMEM)
    return pl.pallas_call(
        partial(hide_kernel, items, shards),
        out_shape=jax.ShapeDtypeStruct(frames.shape, jnp.bfloat16),
        in_specs=[pl.BlockSpec(memory_space=pltpu.SMEM), whole, whole],
        out_specs=whole,
        compiler_params=pltpu.CompilerParams(vmem_limit_bytes=58 * MIB),
        cost_estimate=cost(2),
        name="hide",
    )(meta, modulation, frames)


def project_kernel(items, shards, chips, meta, w_hbm, *refs):
    number = len(chips)
    x_refs = refs[: 2 * number]
    q_ref, kv_ref, x_s, q_s, kv_s, w_ref, in_sem, out_sem, w_sem = refs[-9:]
    weights = pltpu.make_async_copy(w_hbm, w_ref, w_sem)
    count, width = x_refs[0].shape
    rows = 2 * count
    frame = Frame(meta, items, count, shards)

    def live(index):
        return frame.chip(index + chips[0])[1]

    weights.start()
    for index in range(number):

        @pl.when(live(jnp.int32(index)))
        def _(index=index):
            for part in range(2):
                block = 2 * index + part
                pltpu.make_async_copy(
                    x_refs[block], x_s.at[pl.ds(block * count, count), :], in_sem.at[block]
                ).start()

    def writes(index):
        here = rows_of(index, rows)
        there = rows_of(index + chips[0], rows)
        return (
            pltpu.make_async_copy(q_s.at[here, :], q_ref.at[there, :], out_sem.at[2 * index]),
            pltpu.make_async_copy(kv_s.at[here, :], kv_ref.at[there, :], out_sem.at[2 * index + 1]),
        )

    weights.wait()

    @pl.loop(0, number)
    def _(index):
        @pl.when(live(index))
        def _():
            for part in range(2):
                block = 2 * index + part
                pltpu.make_async_copy(x_refs[0], x_s.at[rows_of(block, count), :], in_sem.at[block]).wait()
            both = rows_of(index, rows)
            hidden = x_s[both, :]
            q = dot(hidden, w_ref[:, :width]).astype(jnp.bfloat16)
            q_s[both, :] = (q.astype(jnp.float32) * 0.125).astype(jnp.bfloat16)
            kv_s[both, :width] = dot(hidden, w_ref[:, width : 2 * width]).astype(jnp.bfloat16)
            kv_s[both, width:] = dot(hidden, w_ref[:, 2 * width :]).astype(jnp.bfloat16)
            for write in writes(index):
                write.start()

    @pl.loop(0, number)
    def _(index):
        @pl.when(live(index))
        def _():
            for write in writes(index):
                write.wait()


def project(meta, weight, x_blocks, chips, total, earlier, items, shards, name):
    count, width = x_blocks[0].shape
    part = len(x_blocks) * count
    anywhere = pl.BlockSpec(memory_space=pl.ANY)
    before = 2 + len(x_blocks)
    return pl.pallas_call(
        partial(project_kernel, items, shards, chips),
        out_shape=(
            jax.ShapeDtypeStruct((total, width), jnp.bfloat16),
            jax.ShapeDtypeStruct((total, 2 * width), jnp.bfloat16),
        ),
        in_specs=[pl.BlockSpec(memory_space=pltpu.SMEM)] + [anywhere] * (1 + len(x_blocks) + len(earlier)),
        out_specs=(anywhere, anywhere),
        input_output_aliases={before: 0, before + 1: 1} if earlier else {},
        scratch_shapes=[
            pltpu.VMEM((part, width), jnp.bfloat16),
            pltpu.VMEM((part, width), jnp.bfloat16),
            pltpu.VMEM((part, 2 * width), jnp.bfloat16),
            pltpu.VMEM(weight.shape, jnp.bfloat16),
            pltpu.SemaphoreType.DMA((len(x_blocks),)),
            pltpu.SemaphoreType.DMA((len(x_blocks),)),
            pltpu.SemaphoreType.DMA,
        ],
        compiler_params=pltpu.CompilerParams(vmem_limit_bytes=28 * MIB),
        cost_estimate=cost(len(x_blocks) * 1.2),
        name=name,
    )(meta, weight, *x_blocks, *earlier)


def heads_of(ref, here, pair):
    return ref[here, pair * 128 : (pair + 1) * 128]


def spread(count, group, base):
    return pl.BlockSpec((count, group * 128), lambda p: (0, p + base // group))


ALL = slice(None)


def attend_kernel(items, shards, kind, blocks, group, meta, q_ref, k_ref, v_ref, o_ref, low_ref, f_ref, qa, bias_ref, s, m, l, acc):
    count = q_ref.shape[0]
    rows = k_ref.shape[0] // blocks
    frame = Frame(meta, items, count, shards)
    active, bias = block_rule(frame, kind, rows)
    step = pl.program_id(0)
    lane = lanes(count)
    own = frame.items_of_rows(frame.position * count, count)
    own_item = (lane == own).astype(jnp.float32)
    fill_bias(blocks, rows, active, bias, bias_ref, False)
    for g in range(group):
        stack_heads(qa.at[g], heads_of(q_ref, ALL, g), [own_item, own_item])
        m[g] = jnp.full((2 * count, 128), far, jnp.float32)
        l[g] = jnp.zeros((2 * count, 128), jnp.float32)
        acc[g] = jnp.zeros((2 * count, 128), jnp.float32)

    def score(block):
        here = rows_of(block, rows)
        for g in range(group):
            scores = times_transposed(qa[g], jnp.concatenate([heads_of(k_ref, here, g), bias_ref[here, :]], axis=1))
            s[g, block] = scores
            high = m[g]
            for c in range(rows // 128):
                high = jnp.maximum(high, scores[:, c * 128 : (c + 1) * 128])
            m[g] = high

    each_active(blocks, active, score)
    tops = []
    for g in range(group):
        tops.append(jnp.max(m[g], axis=1, keepdims=True))
        m[g] = jnp.broadcast_to(tops[g], (2 * count, 128))

    def weigh(block):
        here = rows_of(block, rows)
        for g in range(group):
            high = m[g]
            total = l[g]
            parts = []
            for c in range(rows // 128):
                part = jnp.exp(s[g, block, :, c * 128 : (c + 1) * 128] - high)
                total = total + part
                parts.append(part.astype(jnp.bfloat16))
            l[g] = total
            acc[g] = acc[g] + dot(jnp.concatenate(parts, axis=1), heads_of(v_ref, here, g))

    each_active(blocks, active, weigh)
    features = jnp.where(step == 0, own_item, f_ref[...].astype(jnp.float32))
    for g in range(group):
        total = jnp.sum(l[g], axis=1, keepdims=True)
        result = merge_heads(acc[g] / total)
        lse = tops[g] + jnp.log(total)
        for h in range(2):
            start = LSE_LANE + 3 * (2 * (step * group + g) + h)
            for number, piece in enumerate(pieces(lse[h * count : (h + 1) * count])):
                features = jnp.where(lane == start + number, piece, features)
        o_ref[:, g * 128 : (g + 1) * 128] = result
        low_ref[:, g * 128 : (g + 1) * 128] = result.astype(jnp.bfloat16)
    f_ref[...] = features.astype(jnp.bfloat16)


def attend(meta, count, queries, kv, kind, blocks, items, shards, name, group=3):
    width = queries.shape[1]
    pairs = width // 128
    total = kv.shape[0]
    rows = total // blocks
    tile = spread(count, group, 0)
    return pl.pallas_call(
        partial(attend_kernel, items, shards, kind, blocks, group),
        grid=(pairs // group,),
        out_shape=(
            jax.ShapeDtypeStruct((count, width), jnp.float32),
            jax.ShapeDtypeStruct((count, width), jnp.bfloat16),
            jax.ShapeDtypeStruct((count, 128), jnp.bfloat16),
        ),
        in_specs=[
            pl.BlockSpec(memory_space=pltpu.SMEM),
            tile,
            spread(total, group, 0),
            spread(total, group, pairs),
        ],
        out_specs=(tile, tile, pl.BlockSpec((count, 128), lambda p: (0, 0))),
        scratch_shapes=[
            pltpu.VMEM((group, 2 * count, 256), jnp.bfloat16),
            pltpu.VMEM((total, 128), jnp.bfloat16),
            pltpu.VMEM((group, blocks, 2 * count, rows), jnp.float32),
            pltpu.VMEM((group, 2 * count, 128), jnp.float32),
            pltpu.VMEM((group, 2 * count, 128), jnp.float32),
            pltpu.VMEM((group, 2 * count, 128), jnp.float32),
        ],
        compiler_params=pltpu.CompilerParams(vmem_limit_bytes=34 * MIB),
        cost_estimate=cost(14 if kind == "frames" else 5),
        name=name,
    )(meta, queries, kv, kv)


def query_side(pair, features, q, do, qa, da):
    lane = lanes(q.shape[0])
    heads = [2 * pair, 2 * pair + 1]
    stack_heads(qa, q, [jnp.where((lane < LSE_LANE) | head_lanes(lane, LSE_LANE, head), features, 0.0) for head in heads])
    stack_heads(da, do, [jnp.where(head_lanes(lane, DELTA_LANE, head), features, 0.0) for head in heads])


def query_step(qa, da, keys, values, bias):
    minus = jnp.where(delta_lanes(lanes(keys.shape[0])), -1.0, 0.0)
    probs = jnp.exp(times_transposed(qa[...], jnp.concatenate([keys, bias], axis=1)))
    slope = times_transposed(da[...], beside(values, minus))
    return dot((probs * slope).astype(jnp.bfloat16), keys)


def key_side(pair, k, v, mask, ka, va):
    lane = lanes(k.shape[0])
    heads = [2 * pair, 2 * pair + 1]
    stack_heads(ka, k, [jnp.where(head_lanes(lane, LSE_LANE, head), -1.0, mask) for head in heads])
    stack_heads(va, v, [jnp.where(head_lanes(lane, DELTA_LANE, head), -1.0, 0.0) for head in heads])


def key_step(ka, va, q, do, features):
    probs = jnp.exp(times_transposed(ka[...], jnp.concatenate([q, features], axis=1)))
    slope = times_transposed(va[...], jnp.concatenate([do, features], axis=1))
    return dot((probs * slope).astype(jnp.bfloat16), q), dot(probs.astype(jnp.bfloat16), do)


def query_grad_kernel(items, shards, blocks, group, meta, q_ref, do_ref, f_ref, k_ref, v_ref, dq_ref, qa, da, bias_ref, acc):
    count = q_ref.shape[0]
    rows = k_ref.shape[0] // blocks
    frame = Frame(meta, items, count, shards)
    active, bias = block_rule(frame, "frames", rows)
    fill_bias(blocks, rows, active, bias, bias_ref, True)
    features = f_ref[...].astype(jnp.float32)
    for g in range(group):
        pair = pl.program_id(0) * group + g
        query_side(pair, features, heads_of(q_ref, ALL, g), heads_of(do_ref, ALL, g), qa.at[g], da.at[g])
        acc[g] = jnp.zeros((2 * count, 128), jnp.float32)

    def step(block):
        here = rows_of(block, rows)
        for g in range(group):
            acc[g] = acc[g] + query_step(
                qa.at[g], da.at[g], heads_of(k_ref, here, g), heads_of(v_ref, here, g), bias_ref[here, :]
            )

    each_active(blocks, active, step)
    for g in range(group):
        dq_ref[:, g * 128 : (g + 1) * 128] = (merge_heads(acc[g]) * 0.125).astype(jnp.bfloat16)


def query_grad(meta, count, queries, grad_out, kv, blocks, items, shards, name, group=3):
    width = queries.shape[1]
    pairs = width // 128
    total = kv.shape[0]
    tile = spread(count, group, 0)
    return pl.pallas_call(
        partial(query_grad_kernel, items, shards, blocks, group),
        grid=(pairs // group,),
        out_shape=jax.ShapeDtypeStruct((count, width), jnp.bfloat16),
        in_specs=[
            pl.BlockSpec(memory_space=pltpu.SMEM),
            tile,
            tile,
            pl.BlockSpec((count, 128), lambda p: (0, pairs)),
            spread(total, group, 0),
            spread(total, group, pairs),
        ],
        out_specs=tile,
        scratch_shapes=[
            pltpu.VMEM((group, 2 * count, 256), jnp.bfloat16),
            pltpu.VMEM((group, 2 * count, 256), jnp.bfloat16),
            pltpu.VMEM((total, 128), jnp.bfloat16),
            pltpu.VMEM((group, 2 * count, 128), jnp.float32),
        ],
        compiler_params=pltpu.CompilerParams(vmem_limit_bytes=58 * MIB),
        cost_estimate=cost(14),
        name=name,
    )(meta, queries, grad_out, grad_out, kv, kv)


def frame_key_grad_kernel(items, shards, blocks, group, meta, q_ref, k_ref, v_ref, dq_ref, all_ref, out_ref, ka, va, dka, dva, do_s, sem):
    count, width = dq_ref.shape[0], do_s.shape[1] - 128
    rows = q_ref.shape[0] // blocks
    frame = Frame(meta, items, count, shards)

    def arrivals(act):
        @pl.when(pl.program_id(0) == 0)
        def _():
            for block in range(2 * blocks):
                start, live = frame.chip(jnp.int32(block // 2))
                first = start + (frame.position + block) % 2 * count

                @pl.when(live)
                def _(block=block, first=first):
                    act(
                        pltpu.make_async_copy(
                            all_ref.at[pl.ds(pl.multiple_of(first, count), count), :],
                            do_s.at[pl.ds(block * count, count), :],
                            sem.at[block],
                        )
                    )

    arrivals(lambda copy: copy.start())
    mask = item_bias(frame, frame.items_of_rows(frame.position * count, count))
    for g in range(group):
        pair = pl.program_id(0) * group + g
        key_side(pair, heads_of(k_ref, ALL, g), heads_of(v_ref, ALL, g), mask, ka.at[g], va.at[g])
        dka[g] = jnp.zeros((2 * count, 128), jnp.float32)
        dva[g] = jnp.zeros((2 * count, 128), jnp.float32)
    arrivals(lambda copy: copy.wait())

    def step(block):
        here = rows_of(block, rows)
        for g in range(group):
            column = pl.multiple_of((pl.program_id(0) * group + g) * 128, 128)
            dk, dv = key_step(
                ka.at[g], va.at[g], heads_of(q_ref, here, g), do_s[here, pl.ds(column, 128)], do_s[here, width:]
            )
            dka[g] = dka[g] + dk
            dva[g] = dva[g] + dv

    each_active(blocks, lambda block: frame.chip(block)[1], step)
    for g in range(group):
        out_ref[1, :, g * 128 : (g + 1) * 128] = merge_heads(dka[g]).astype(jnp.bfloat16)
        out_ref[2, :, g * 128 : (g + 1) * 128] = merge_heads(dva[g]).astype(jnp.bfloat16)
    out_ref[0] = dq_ref[...]


def frame_key_grad(meta, q_window, do_all, kv, grad_queries, count, blocks, items, shards, name, group=3):
    total, width = q_window.shape
    pairs = width // 128
    tile = spread(count, group, 0)
    wide = spread(total, group, 0)
    return pl.pallas_call(
        partial(frame_key_grad_kernel, items, shards, blocks, group),
        grid=(pairs // group,),
        out_shape=jax.ShapeDtypeStruct((3, count, width), jnp.bfloat16),
        in_specs=[
            pl.BlockSpec(memory_space=pltpu.SMEM),
            wide,
            tile,
            spread(count, group, pairs),
            tile,
        ]
        + [pl.BlockSpec(memory_space=pl.ANY)],
        out_specs=pl.BlockSpec((3, count, group * 128), lambda p: (0, 0, p)),
        scratch_shapes=[pltpu.VMEM((group, 2 * count, 256), jnp.bfloat16)] * 2
        + [pltpu.VMEM((group, 2 * count, 128), jnp.float32)] * 2
        + [pltpu.VMEM((total, width + 128), jnp.bfloat16), pltpu.SemaphoreType.DMA((2 * blocks,))],
        compiler_params=pltpu.CompilerParams(vmem_limit_bytes=58 * MIB),
        cost_estimate=cost(18),
        name=name,
    )(meta, q_window, kv, kv, grad_queries, do_all)


def text_grad_kernel(items, shards, group, meta, q_ref, do_ref, f_ref, k_ref, v_ref, dq_ref, dkv_ref, qa, da, ka, va, acc):
    count = q_ref.shape[0]
    rows = k_ref.shape[0] // items
    share = rows // shards
    frame = Frame(meta, items, count, shards)
    features = f_ref[...].astype(jnp.float32)
    pairs = [pl.program_id(0) * group + g for g in range(group)]
    for g in range(group):
        query_side(pairs[g], features, heads_of(q_ref, ALL, g), heads_of(do_ref, ALL, g), qa.at[g], da.at[g])
        acc[g] = jnp.zeros((2 * count, 128), jnp.float32)

    @pl.loop(0, items)
    def _(item):
        here = rows_of(item, rows)
        live = (item >= frame.first) & (item <= frame.last)
        target = rows_of(item, share)

        @pl.when(live)
        def _():
            mask = text_bias(frame, item, rows)
            bias = jnp.where(lse_lanes(lanes(rows)), -1.0, mask).astype(jnp.bfloat16)
            for g in range(group):
                keys, values = heads_of(k_ref, here, g), heads_of(v_ref, here, g)
                acc[g] = acc[g] + query_step(qa.at[g], da.at[g], keys, values, bias)
                key_side(pairs[g], keys, values, mask, ka.at[g], va.at[g])
                grads = key_step(ka.at[g], va.at[g], heads_of(q_ref, ALL, g), heads_of(do_ref, ALL, g), f_ref[...])
                for which, grad in enumerate(grads):
                    merged = merge_heads(grad).astype(jnp.bfloat16)
                    for owner in range(shards):
                        dkv_ref[owner, which, target, g * 128 : (g + 1) * 128] = merged[
                            owner * share : (owner + 1) * share
                        ]

        @pl.when(jnp.logical_not(live))
        def _():
            dkv_ref[:, :, target, :] = jnp.zeros((shards, 2, share, group * 128), jnp.bfloat16)

    for g in range(group):
        dq_ref[:, g * 128 : (g + 1) * 128] = (merge_heads(acc[g]) * 0.125).astype(jnp.bfloat16)


def text_grad(meta, queries, grad_out, features, kv, items, shards, name, group=3):
    count, width = queries.shape
    pairs = width // 128
    total = kv.shape[0]
    tile = spread(count, group, 0)
    rows = total // items
    return pl.pallas_call(
        partial(text_grad_kernel, items, shards, group),
        grid=(pairs // group,),
        out_shape=(
            jax.ShapeDtypeStruct((count, width), jnp.bfloat16),
            jax.ShapeDtypeStruct((shards, 2, total // shards, width), jnp.bfloat16),
        ),
        in_specs=[
            pl.BlockSpec(memory_space=pltpu.SMEM),
            tile,
            tile,
            pl.BlockSpec((count, 128), lambda p: (0, 0)),
            spread(total, group, 0),
            spread(total, group, pairs),
        ],
        out_specs=(tile, pl.BlockSpec((shards, 2, total // shards, group * 128), lambda p: (0, 0, 0, p))),
        scratch_shapes=[pltpu.VMEM((group, 2 * count, 256), jnp.bfloat16)] * 2
        + [pltpu.VMEM((group, 2 * rows, 256), jnp.bfloat16)] * 2
        + [pltpu.VMEM((group, 2 * count, 128), jnp.float32)],
        compiler_params=pltpu.CompilerParams(vmem_limit_bytes=18 * MIB),
        cost_estimate=cost(8),
        name=name,
    )(meta, queries, grad_out, features, kv, kv)


def mlp_kernel(h_ref, d_ref, up_ref, down_ref, act_ref, m_ref, dh_ref):
    step = pl.program_id(0)
    last = pl.num_programs(0) - 1

    @pl.when(step < last)
    def _():
        u = dot(h_ref[...], up_ref[...])
        slope = times_transposed(d_ref[...], down_ref[...])
        inner = 0.7978845608028654 * (u + 0.044715 * (u * u * u))
        t = jnp.tanh(inner)
        g = (0.5 * u * (1.0 + t)).astype(jnp.bfloat16)
        bend = 0.7978845608028654 * (1.0 + 0.134145 * (u * u))
        du = (slope * (0.5 * (1.0 + t) + 0.5 * u * (1.0 - t * t) * bend)).astype(jnp.bfloat16)
        act_ref[0, 0] = g
        act_ref[0, 1] = du
        m = dot(g, down_ref[...])
        dh = times_transposed(du, up_ref[...])

        @pl.when(step == 0)
        def _():
            m_ref[...] = m
            dh_ref[...] = dh

        @pl.when(step > 0)
        def _():
            m_ref[...] = m_ref[...] + m
            dh_ref[...] = dh_ref[...] + dh

    @pl.when(step == last)
    def _():
        act_ref[0, 0] = h_ref[...]
        act_ref[0, 1] = d_ref[...]


def mlp(hidden, grad, w_up, w_down):
    count, width = hidden.shape
    chunks = w_up.shape[1] // width
    whole = pl.BlockSpec((count, width), lambda c: (0, 0))
    held = lambda c: jnp.minimum(c, chunks - 1)
    return pl.pallas_call(
        mlp_kernel,
        grid=(chunks + 1,),
        out_shape=(
            jax.ShapeDtypeStruct((chunks + 1, 2, count, width), jnp.bfloat16),
            jax.ShapeDtypeStruct((count, width), jnp.float32),
            jax.ShapeDtypeStruct((count, width), jnp.float32),
        ),
        in_specs=[
            whole,
            whole,
            pl.BlockSpec((width, width), lambda c: (0, held(c))),
            pl.BlockSpec((width, width), lambda c: (held(c), 0)),
        ],
        out_specs=(pl.BlockSpec((1, 2, count, width), lambda c: (c, 0, 0, 0)), whole, whole),
        compiler_params=pltpu.CompilerParams(vmem_limit_bytes=20 * MIB),
        cost_estimate=cost(9),
        name="mlp",
    )(hidden, grad, w_up, w_down)


UNIT = 192
X_BIT, Y_BIT = 0, 1


def rows_picked(x, core):
    row = lax.broadcasted_iota(jnp.int32, (384, 768), 0)
    column = lax.broadcasted_iota(jnp.int32, (384, 768), 1)
    chip = (row >= 96).astype(jnp.int32) + (row >= 192).astype(jnp.int32) + (row >= 288).astype(jnp.int32)
    pick = (column == row + 96 * (chip + core)).astype(jnp.bfloat16)
    return times_transposed(pick, x).astype(jnp.bfloat16)


def one_above_other(upper, lower):
    return jnp.concatenate([upper, lower], axis=0)


def finish_kernel(items, shards, packed, meta, mod_ref, w_ref, d_ref, x_ref, dx_ref, a_ref, dh_ref, n_ref, dy_ref, m_ref, out_ref, sum_ref):
    count, width = x_ref.shape
    frame = Frame(meta, items, count, shards)
    item = frame.items_of_rows(frame.position * count, count)
    grad = sum(times_transposed(d_ref[i], w_ref[:, i * width : (i + 1) * width]) for i in range(3))
    normed, inverse = layer_norm(x_ref[...].astype(jnp.float32))
    scale = jnp.zeros((count, width), jnp.float32)
    for i in range(items):
        scale = jnp.where(item == i, mod_ref[i, 1:2, :], scale)
    dx = dx_ref[...]
    out_ref[...] = dx + norm_back(grad * (1.0 + scale), normed, inverse)
    dh = dh_ref[...]
    terms = (
        grad,
        grad * normed,
        dx * a_ref[...],
        dh,
        dh * n_ref[...],
        dy_ref[...].astype(jnp.float32) * m_ref[...],
    )
    sums = []
    for number, term in enumerate(terms):
        rows = [jnp.sum(jnp.where(item == i, term, 0.0), axis=0, keepdims=True) for i in range(items)]
        rows += [jnp.zeros((8 - items, width), jnp.float32)]
        sums.append(jnp.concatenate(rows, axis=0))
        if not packed:
            sum_ref[number] = sums[number]
    if packed:
        values = jnp.concatenate(sums, axis=0)
        left = lax.broadcasted_iota(jnp.int32, (24, 384), 1) < UNIT
        for pair in range(2):
            part = third(values, pair)
            rolled = pltpu.roll(part, UNIT, 1)
            each = (jnp.where(left, part[:24], rolled[24:]), jnp.where(left, rolled[:24], part[24:]))
            for half in range(2):
                relative = (2 * pair + half) ^ (frame.position // 2)
                sum_ref[relative % 2, relative // 2, :24, :] = each[half]
                sum_ref[relative % 2, relative // 2, 24:, :] = jnp.zeros((8, 384), jnp.float32)


def finish(meta, modulation, weight, grads, frames, *arrays_items_shards):
    *arrays, items, shards, packed = arrays_items_shards
    count, width = frames.shape
    whole = pl.BlockSpec(memory_space=pltpu.VMEM)
    return pl.pallas_call(
        partial(finish_kernel, items, shards, packed),
        out_shape=(
            jax.ShapeDtypeStruct((count, width), jnp.float32),
            jax.ShapeDtypeStruct((2, 2, 32, 384) if packed else (6, 8, width), jnp.float32),
        ),
        in_specs=[pl.BlockSpec(memory_space=pltpu.SMEM)] + [whole] * (4 + len(arrays)),
        out_specs=(whole, whole),
        compiler_params=pltpu.CompilerParams(vmem_limit_bytes=58 * MIB),
        cost_estimate=cost(5),
        name="finish",
    )(meta, modulation, weight, grads, frames, *arrays)


def attend_back_kernel(items, shards, meta, mod_ref, g_ref, cq_ref, o_ref, dx_ref, x_ref, exact_ref, f_ref, dx_out, low_out, do_out):
    count, width = x_ref.shape
    frame = Frame(meta, items, count, shards)
    item = frame.items_of_rows(frame.position * count, count)
    normed, inverse = layer_norm(x_ref[...])
    dx = dx_ref[...] + norm_back(times_transposed(g_ref[...], cq_ref[...]), normed, inverse)
    dx_out[...] = dx
    gate = jnp.broadcast_to(mod_ref[0, 2:3, :], dx.shape)
    for i in range(1, items):
        gate = jnp.where(item == i, mod_ref[i, 2:3, :], gate)
    low = (dx * gate).astype(jnp.bfloat16)
    low_out[...] = low
    grad = times_transposed(low, o_ref[...]).astype(jnp.bfloat16)
    do_out[:, :width] = grad
    row = lax.broadcasted_iota(jnp.int32, (width, 128), 0)
    lane = lax.broadcasted_iota(jnp.int32, (width, 128), 1)
    pick = jnp.zeros((width, 128), jnp.float32)
    for head in range(H):
        mine = (row >= head * (width // H)) & (row < (head + 1) * (width // H))
        pick = jnp.where(mine & head_lanes(lane, DELTA_LANE, head), 1.0, pick)
    pick = pick.astype(jnp.bfloat16)
    products = grad.astype(jnp.float32) * exact_ref[...]
    delta = sum(dot(piece.astype(jnp.bfloat16), pick) for piece in pieces(products))
    place = lanes(1)
    features = f_ref[...].astype(jnp.float32)
    for number, piece in enumerate(pieces(delta)):
        here = jnp.zeros((1, 128), jnp.bool_)
        for head in range(H):
            here = here | (place == DELTA_LANE + 3 * head + number)
        features = jnp.where(here, piece, features)
    do_out[:, width:] = features.astype(jnp.bfloat16)


def attend_back(meta, modulation, grads, w_cq, w_o, grad_cross, after_attn, attn_exact, features, items, shards):
    count, width = grads.shape
    whole = pl.BlockSpec(memory_space=pltpu.VMEM)
    return pl.pallas_call(
        partial(attend_back_kernel, items, shards),
        out_shape=(
            jax.ShapeDtypeStruct((count, width), jnp.float32),
            jax.ShapeDtypeStruct((count, width), jnp.bfloat16),
            jax.ShapeDtypeStruct((count, width + 128), jnp.bfloat16),
        ),
        in_specs=[pl.BlockSpec(memory_space=pltpu.SMEM)] + [whole] * 8,
        out_specs=(whole, whole, whole),
        compiler_params=pltpu.CompilerParams(vmem_limit_bytes=20 * MIB),
        cost_estimate=cost(3),
        name="attend_back",
    )(meta, modulation, grads, w_cq, w_o, grad_cross, after_attn, attn_exact, features)


class Packer:
    def __init__(self, meta, items, outputs):
        self.core, self.chip = meta[0] % 2, meta[0] // 2
        self.mine = meta[1 + 2 * items]
        self.outputs = outputs

    def steps(self, owner_chip):
        relative = owner_chip ^ self.chip
        return relative % 2, relative // 2

    def store(self, name, owner, owner_chip, row, values):
        scratch, first = self.outputs[name]
        relative = owner ^ self.mine
        where = ((relative >> first) % 2, (relative >> (1 - first)) % 2, *self.steps(owner_chip))
        scratch[where + (slice(row, row + values.shape[0]),)] = values.astype(jnp.bfloat16)

    def store_split(self, name, pair, row, values, chips):
        rolled = pltpu.roll(values, UNIT, 1)
        each = values.shape[0] // len(chips)
        left = lax.broadcasted_iota(jnp.int32, (each // 2, 384), 1) < UNIT
        for number, owner_chip in enumerate(chips):
            upper = slice(number * each, number * each + each // 2)
            lower = slice(number * each + each // 2, (number + 1) * each)
            self.store(name, 2 * pair, owner_chip, row, jnp.where(left, values[upper], rolled[lower]))
            self.store(name, 2 * pair + 1, owner_chip, row, jnp.where(left, rolled[upper], values[lower]))


def core_columns(core, number, each):
    return pl.ds(pl.multiple_of(number * 2 * each + core * each, 128), each)


def third(values, number):
    return values[:, number * 384 : (number + 1) * 384]


def pack_mlp_kernel(items, meta, own, sib, down_s, up_s):
    packer = Packer(meta, items, {"down": (down_s, Y_BIT), "up": (up_s, X_BIT)})
    both = lambda chunk, which: one_above_other(own[chunk, which], sib[chunk, which])
    grad = both(4, 1)
    for owner_chip in range(4):
        here = core_columns(packer.core, 0, 384)
        left = one_above_other(own[owner_chip, 0, :, here], sib[owner_chip, 0, :, here])
        values = contract_rows(left, grad)
        for pair in range(2):
            packer.store_split("down", pair, 0, third(values, pair), [owner_chip])
    left = rows_picked(both(4, 0), packer.core)
    for owner in range(4):
        values = dot(left, both(owner, 1))
        for owner_chip in range(4):
            for half in range(2):
                packer.store(
                    "up", owner, owner_chip, half * 96, third(values, half)[owner_chip * 96 : (owner_chip + 1) * 96]
                )


def pack_middle_kernel(items, meta, own, sib, text_own, text_sib, text, square_s, text_s):
    packer = Packer(meta, items, {"square": (square_s, Y_BIT), "text": (text_s, X_BIT)})
    both = lambda which: one_above_other(own[which], sib[which])
    for number in range(3):
        values = dot(rows_picked(both(2 * number), packer.core), both(2 * number + 1))
        for pair in range(2):
            packer.store_split("square", pair, number * 48, third(values, pair), range(4))
    share = text_own.shape[2] // items

    def chip_sum(which, item, owner):
        here = slice(item * share, (item + 1) * share)
        total = text_own[owner, which, here, :].astype(jnp.float32) + text_sib[owner, which, here, :].astype(jnp.float32)
        return total.astype(jnp.bfloat16)

    sums = [
        jnp.concatenate(
            [chip_sum(which, item, owner) for item in range(items) for owner in range(text_own.shape[0])], axis=0
        )
        for which in range(2)
    ]
    left = jnp.concatenate([text[:, core_columns(packer.core, chip, 128)] for chip in range(4)], axis=1)
    for which in range(2):
        values = contract_rows(left, sums[which])
        for owner_chip in range(4):
            for half in range(2):
                packer.store(
                    "text", 2 * which + half, owner_chip, 0, third(values, half)[owner_chip * 128 : (owner_chip + 1) * 128]
                )


def pack_qkv_kernel(items, meta, h_own, h_sib, own, sib, plain_s, split_s):
    packer = Packer(meta, items, {"plain": (plain_s, X_BIT), "split": (split_s, Y_BIT)})
    left = rows_picked(one_above_other(h_own[...], h_sib[...]), packer.core)
    values = []
    for number in range(3):
        product = dot(left, one_above_other(own[number], sib[number]))
        values += [third(product, 0), third(product, 1)]
    for owner, column in enumerate((0, 2, 3, 5)):
        for owner_chip in range(4):
            packer.store("plain", owner, owner_chip, 0, values[column][owner_chip * 96 : (owner_chip + 1) * 96])
    for pair, column in enumerate((1, 4)):
        packer.store_split("split", pair, 0, values[column], range(4))


def packing(kernel, items, inputs, groups, *refs):
    ins, outs, scratch, sem = refs[:inputs], refs[inputs:-groups - 1], refs[-groups - 1 : -1], refs[-1]
    kernel(items, *ins, *scratch)
    copies = [pltpu.make_async_copy(scratch[i // 2].at[1 - i % 2], outs[i], sem.at[i]) for i in range(2 * groups)]
    for copy in copies:
        copy.start()
    for copy in copies:
        copy.wait()


def pack(kernel, meta, operands, shapes, items, name):
    shapes = [(2, 2, 2, each, 384) if isinstance(each, int) else each for each in shapes]
    whole = pl.BlockSpec(memory_space=pltpu.VMEM)
    return pl.pallas_call(
        partial(packing, kernel, items, 1 + len(operands), len(shapes)),
        out_shape=tuple(jax.ShapeDtypeStruct(shape, jnp.bfloat16) for shape in shapes for _ in range(2)),
        in_specs=[pl.BlockSpec(memory_space=pltpu.SMEM)] + [whole] * len(operands),
        out_specs=tuple([pl.BlockSpec(memory_space=pl.ANY)] * (2 * len(shapes))),
        scratch_shapes=[pltpu.VMEM((2, *shape), jnp.bfloat16) for shape in shapes]
        + [pltpu.SemaphoreType.DMA((2 * len(shapes),))],
        compiler_params=pltpu.CompilerParams(vmem_limit_bytes=58 * MIB),
        cost_estimate=cost(8 if name != "pack_qkv" else 3),
        name=name,
    )(meta, *operands)


def bundle_kernel(*refs):
    for number, each in enumerate(refs[:-1]):
        refs[-1][number] = each[...]


def bundle(*arrays):
    whole = pl.BlockSpec(memory_space=pltpu.VMEM)
    return pl.pallas_call(
        bundle_kernel,
        out_shape=jax.ShapeDtypeStruct((len(arrays), *arrays[0].shape), arrays[0].dtype),
        in_specs=[whole] * len(arrays),
        out_specs=whole,
        cost_estimate=cost(3),
        name="bundle",
    )(*arrays)


def trade(values, axis, bit):
    size = lax.axis_size(axis)
    return lax.ppermute(values, axis, [(i, i ^ (1 << bit)) for i in range(size)])


def added(keep, got):
    return [(keep[i].astype(jnp.float32) + got[i].astype(jnp.float32)).astype(jnp.bfloat16) for i in range(2)]


def halve(keep, send, axis, bit, after=()):
    got = trade(send, axis, bit)
    if after:
        [keep] = hold((keep,), *after)
    return added(keep, got)


def last_half(keep, send, after=()):
    got = trade(send, "seq", 2)
    if after:
        [keep] = hold((keep,), *after)
    return keep.astype(jnp.float32) + got.astype(jnp.float32)


def joined(upper, lower):
    return [jnp.concatenate([upper[i], lower[i]], axis=-2) for i in (1, 0)]


def unsplit(rows):
    return jnp.concatenate([rows[:, :UNIT], rows[:, UNIT:]], axis=0)


def with_deltas(features, grad_out, attn_exact):
    width = attn_exact.shape[1]
    lane = jnp.arange(128)[None, :]
    head = (jnp.arange(width) // (width // H))[:, None]
    pick = ((lane >= DELTA_LANE) & ((lane - DELTA_LANE) // 3 == head)).astype(jnp.float32)
    delta = jnp.dot(
        grad_out.astype(jnp.float32) * attn_exact,
        pick,
        precision=lax.Precision.HIGHEST,
        preferred_element_type=jnp.float32,
    )
    high = lax.reduce_precision(delta, 8, 7)
    middle = lax.reduce_precision(delta - high, 8, 7)
    which = (lane - DELTA_LANE) % 3
    piece = jnp.where(which == 0, high, jnp.where(which == 1, middle, delta - high - middle))
    inside = (lane >= DELTA_LANE) & (lane < DELTA_LANE + 3 * H)
    return jnp.where(inside, piece.astype(jnp.bfloat16), features)


def hop(below, above, shards):
    up = [(i, i + 2) for i in range(shards - 2)]
    return lax.ppermute(below, "seq", up), lax.ppermute(above, "seq", [(j, i) for i, j in up])


def hold(values, *first):
    held = lax.optimization_barrier((*values, *first))
    return held[: len(values)]


def body(
    frames,
    cotangent,
    modulation,
    lengths,
    text,
    text_len,
    w_qkv,
    w_o,
    w_cq,
    w_ckv,
    w_co,
    w_up,
    w_down,
):
    local = frames[0]
    count, width = local.shape
    items = lengths.shape[1]
    text_rows, text_width = text.shape[2:]
    shards = lax.axis_size("seq")
    position = lax.axis_index("seq")
    reach = min(-(-(LONGEST - 1) // (2 * count)), shards // 2 - 1)
    chips = 1 + 2 * reach
    meta = jnp.concatenate(
        [position[None].astype(jnp.int32), lengths[0], text_len[0], lax.axis_index("batch")[None].astype(jnp.int32)]
    )
    item_range = jnp.arange(items, dtype=jnp.int32)
    ends = jnp.sum(jnp.where(item_range[None, :] <= item_range[:, None], lengths[0][None, :], 0), axis=1)
    place = position * count + jnp.arange(count, dtype=jnp.int32)
    query_items = jnp.sum((place[:, None] >= ends[None, :]).astype(jnp.int32), axis=1)[:, None]
    mod = modulation[0]

    def per_frame(which):
        found = jnp.broadcast_to(mod[0, which][None, :], (count, width))
        for item in range(1, items):
            found = jnp.where(query_items == item, mod[item, which][None, :], found)
        return found

    swap = [(i, i ^ 1) for i in range(shards)]

    def sibling(values):
        return lax.ppermute(values, "seq", swap)

    fast = shards == 8 and lax.axis_size("batch") == 4 and width == 768

    text_proj = jnp.dot(
        text[0].reshape(items * text_rows, text_width), w_ckv, preferred_element_type=jnp.float32
    ).astype(jnp.bfloat16)
    hidden_one = hide(meta, mod, local, items, shards)
    sides = list(hold(hop(hidden_one, hidden_one, shards), text_proj))
    for _ in range(1, reach):
        sides += hop(*sides[-2:], shards)

    def with_siblings(blocks):
        return [each for block in blocks for each in (block, sibling(block))]

    total = 2 * chips * count
    near = with_siblings([hidden_one] + sides[:2])
    hidden_sib = near[1]
    q_window, kv = project(meta, w_qkv, near, range(3), total, (), items, shards, "project_near")
    if reach > 1:
        apart = with_siblings(hold(sides[2:], kv))
        q_window, kv = project(
            meta, w_qkv, apart, range(3, chips), total, (q_window, kv), items, shards, "project_far"
        )
    inputs = local.astype(jnp.float32)
    attn_exact, attended, features = attend(meta, count, q_window, kv, "frames", chips, items, shards, "self_attend")
    branch_one = jnp.dot(attended, w_o, preferred_element_type=jnp.float32)
    after_attn = inputs + per_frame(2) * branch_one
    normed_cross, inverse_cross = layer_norm(after_attn)
    cross_in = normed_cross.astype(jnp.bfloat16)
    cross_queries = jnp.dot(cross_in, w_cq, preferred_element_type=jnp.float32).astype(jnp.bfloat16)
    cross_queries = (cross_queries.astype(jnp.float32) * 0.125).astype(jnp.bfloat16)
    cross_exact, cross_out, cross_features = attend(
        meta, count, cross_queries, text_proj, "text", items, items, shards, "cross_attend"
    )
    branch_two = jnp.dot(cross_out, w_co, preferred_element_type=jnp.float32)
    after_cross = after_attn + branch_two
    normed_two, inverse_two = layer_norm(after_cross)
    hidden_two = (normed_two * (1.0 + per_frame(4)) + per_frame(3)).astype(jnp.bfloat16)
    gate_two = per_frame(5)
    grad_out = cotangent[0].astype(jnp.float32)
    grad_branch_three = (grad_out * gate_two).astype(jnp.bfloat16)
    acts, branch_three, grad_hidden_two = mlp(hidden_two, grad_branch_three, w_up, w_down)
    if fast:
        acts_sib = sibling(acts)
    result = after_cross + gate_two * branch_three
    grad_cross = grad_out + norm_back(grad_hidden_two * (1.0 + per_frame(4)), normed_two, inverse_two)
    grad_branch_two = grad_cross.astype(jnp.bfloat16)
    grad_cross_out = times_transposed(grad_branch_two, w_co).astype(jnp.bfloat16)
    cross_features = with_deltas(cross_features, grad_cross_out, cross_exact)
    grad_cross_queries, text_terms = text_grad(
        meta, cross_queries, grad_cross_out, cross_features, text_proj, items, shards, "cross_grad"
    )
    if fast:
        [grad_cross_queries] = hold((grad_cross_queries,), acts_sib)
    grad_attn_res, grad_branch_one, do_low = attend_back(
        meta, mod, grad_cross_queries, w_cq, w_o, grad_cross, after_attn, attn_exact, features, items, shards
    )
    if fast:
        text_sib = sibling(text_terms)
    do_all = lax.all_gather(do_low, "seq", axis=0, tiled=True)
    if fast:
        middle = bundle(cross_out, grad_branch_two, cross_in, grad_cross_queries, attended, grad_branch_one)
        middle_sib = sibling(middle)
        [acts_sib] = hold((acts_sib,), do_low, middle)
        mlp_parts = pack(pack_mlp_kernel, meta, (acts, acts_sib), (192, 192), items, "pack_mlp")
        [middle] = hold((middle,), *mlp_parts)
        middle_parts = pack(
            pack_middle_kernel,
            meta,
            (middle, middle_sib, text_terms, text_sib, text[0].reshape(items * text_rows, text_width)),
            (144, 128),
            items,
            "pack_middle",
        )
        [do_own] = hold((do_low,), *middle_parts)
    else:
        do_own = do_low
    grad_queries = query_grad(
        meta, count, q_window, do_own, kv, chips, items, shards, "self_query_grad"
    )
    share_rows = text_rows // shards
    [text_terms_late] = hold((text_terms,), grad_queries)
    text_total = lax.psum_scatter(
        text_terms_late.reshape(shards * 2 * items * share_rows, width), "seq", scatter_dimension=0, tiled=True
    ).reshape(2, items * share_rows, width)
    if fast:
        down_part = halve(mlp_parts[1], mlp_parts[0], "batch", Y_BIT, (grad_queries,))
        up_part = halve(mlp_parts[3], mlp_parts[2], "batch", X_BIT, (grad_queries,))
        [do_all] = hold((do_all,), *middle_parts, *down_part, *up_part)
    grad_projected = frame_key_grad(
        meta, q_window, do_all, kv, grad_queries, count, chips, items, shards, "self_key_grad"
    )
    if fast:
        projected_sib = sibling(grad_projected)
    if fast:
        square_send, square_keep, text_send, text_keep = middle_parts
        got = (
            trade(down_part[1], "batch", X_BIT),
            trade(up_part[1], "batch", Y_BIT),
            trade(square_send, "batch", Y_BIT),
            trade(text_send, "batch", X_BIT),
        )
        got = hold(got, grad_projected)
        down_part, up_part = added(down_part[0], got[0]), added(up_part[0], got[1])
        square_part, text_w_part = added(square_keep, got[2]), added(text_keep, got[3])
        first_send, first_keep = joined(down_part, up_part)
        [projected_sib] = hold((projected_sib,), *square_part, *text_w_part, first_send)
        qkv_parts = pack(
            pack_qkv_kernel,
            meta,
            (hidden_one, hidden_sib, grad_projected, projected_sib),
            (96, 48),
            items,
            "pack_qkv",
        )
        [grad_projected] = hold((grad_projected,), *qkv_parts)
    grad_inputs, terms = finish(
        meta, mod, w_qkv, grad_projected, local, grad_attn_res, branch_one, grad_hidden_two, normed_two, cotangent[0],
        branch_three, items, shards, fast,
    )
    if not fast:
        for bit in range(shards.bit_length() - 1):
            terms = terms + trade(terms, "seq", bit)
        own = width // shards
        terms = lax.dynamic_slice_in_dim(terms, position * own, own, 2)
        shares = terms[:, :items].transpose(1, 0, 2)
    if fast:
        terms = (terms + trade(terms, "seq", 0)).astype(jnp.bfloat16)
        plain_send, plain_keep, split_send, split_keep = qkv_parts
        first_part = halve(first_keep, first_send, "seq", 1, (grad_inputs,))
        square_part = halve(*square_part, "batch", X_BIT, first_part)
        text_w_part = halve(*text_w_part, "batch", Y_BIT, first_part)
        half_way = (grad_inputs,)
        plain_part = halve(plain_keep, plain_send, "batch", X_BIT, half_way)
        split_part = halve(split_keep, split_send, "batch", Y_BIT, half_way)
        half_way = (*plain_part, *split_part)
        plain_part = halve(*plain_part, "batch", Y_BIT)
        split_part = halve(*split_part, "batch", X_BIT)
        sent = [jnp.concatenate([plain_part[i], split_part[i], terms[i]], axis=-2) for i in (1, 0)]
        middle_send, middle_keep = joined(square_part, text_w_part)
        middle_part = halve(middle_keep, middle_send, "seq", 1, sent)
        last_part = halve(sent[1], sent[0], "seq", 1)
        last_rows = last_half(*last_part)
        middle_rows = last_half(*middle_part, last_part)
        first_rows = last_half(*first_part, sent)
        own_terms = unsplit(last_rows[144:168])
        own = width // shards
        own_terms = lax.dynamic_slice_in_dim(own_terms, (position % 2) * own, own, 1)
        shares = own_terms.reshape(6, 8, own)[:, :items].transpose(1, 0, 2)
        last_rows = last_rows[:144]
        [text_total] = hold((text_total,), *sent)
        plain, split = last_rows[:96], unsplit(last_rows[96:])
        even = lax.axis_index("batch") % 2 == 0
        grads = (
            jnp.where(even, jnp.concatenate([plain, split], axis=1), jnp.concatenate([split, plain], axis=1)),
            unsplit(middle_rows[96:144]),
            unsplit(middle_rows[48:96]),
            middle_rows[144:],
            unsplit(middle_rows[:48]),
            jnp.concatenate([first_rows[192:288], first_rows[288:]], axis=1),
            unsplit(first_rows[:192]),
        )
    text_grad_low = jnp.concatenate([text_total[0], text_total[1]], axis=1)
    grad_text = times_transposed(text_grad_low, w_ckv).reshape(1, items, share_rows, text_width)
    if not fast:
        text_mine = lax.dynamic_slice_in_dim(text[0], position * share_rows, share_rows, 1)
        grads = reduced_grads(
            (hidden_one, jnp.concatenate(list(grad_projected), axis=1)),
            (attended, grad_branch_one),
            (cross_in, grad_cross_queries),
            (text_mine.reshape(items * share_rows, text_width), text_grad_low),
            (cross_out, grad_branch_two),
            (hidden_two, acts[:-1, 1].transpose(1, 0, 2).reshape(count, -1)),
            (acts[:-1, 0].transpose(1, 0, 2).reshape(count, -1), grad_branch_three),
        )
    return (
        result.astype(jnp.bfloat16)[None],
        grad_inputs[None],
        shares[:, :3][None],
        shares[:, 3:][None],
        grad_text,
        *grads,
    )


def reduced_grads(*pairs):
    def reduce_weight(left, right):
        grad = contract_rows(left, right).astype(jnp.bfloat16)
        part = lax.psum_scatter(grad, "seq", scatter_dimension=0, tiled=True)
        return lax.psum_scatter(part, "batch", scatter_dimension=1, tiled=True).astype(jnp.float32)

    return tuple(reduce_weight(*pair) for pair in pairs)


def solution(mesh):
    in_specs = (
        P("batch", "seq", None),
        P("batch", "seq", None),
        P("batch", None, None, None),
        P("batch", None),
        P("batch", None, None, None),
        P("batch", None),
        P(),
        P(),
        P(),
        P(),
        P(),
        P(),
        P(),
    )
    out_specs = (
        P("batch", "seq", None),
        P("batch", "seq", None),
        P("batch", None, None, "seq"),
        P("batch", None, None, "seq"),
        P("batch", None, "seq", None),
        P("seq", "batch"),
        P("seq", "batch"),
        P("seq", "batch"),
        P("seq", "batch"),
        P("seq", "batch"),
        P("seq", "batch"),
        P("seq", "batch"),
    )
    return jax.shard_map(body, mesh=mesh, in_specs=in_specs, out_specs=out_specs, check_vma=False)
```

```python
from functools import partial

import jax
import jax.numpy as jnp
from jax import lax
from jax.experimental import pallas as pl
from jax.experimental.pallas import tpu as pltpu
from jax.sharding import PartitionSpec as P

H = 12
LONGEST = 1024

epsilon = 1e-06
far = -1e30
LSE_LANE = 8
DELTA_LANE = 44
MIB = 1 << 20
FLOPS_EACH, BYTES_EACH = 5e+08, 1.65e+06


def layer_norm(values):
    centred = values - jnp.mean(values, axis=-1, keepdims=True)
    inverse = lax.rsqrt(jnp.mean(centred * centred, axis=-1, keepdims=True) + epsilon)
    return (centred * inverse, inverse)


def norm_back(grad_normed, normed, inverse):
    return inverse * (
        grad_normed
        - jnp.mean(grad_normed, axis=-1, keepdims=True)
        - normed * jnp.mean(grad_normed * normed, axis=-1, keepdims=True)
    )


def contract_rows(left, right):
    return lax.dot_general(
        left, right, (((0,), (0,)), ((), ())), preferred_element_type=jnp.float32
    )


def times_transposed(left, right):
    return lax.dot_general(
        left, right, (((1,), (1,)), ((), ())), preferred_element_type=jnp.float32
    )


class Frame:
    def __init__(self, meta, items, count, shards):
        self.position = meta[0]
        self.items = items
        self.count = count
        self.shards = shards
        self.ends = []
        total = jnp.int32(0)
        for item in range(items):
            total = total + meta[1 + item]
            self.ends.append(total)
        self.text_len = [meta[1 + items + item] for item in range(items)]
        self.first = self.item_of(self.position * count)
        self.last = self.item_of(self.position * count + count - 1)
        self.low = jnp.int32(0)
        self.high = jnp.int32(0)
        for item in range(items):
            start = self.ends[item] - meta[1 + item]
            self.low = jnp.where(self.first == item, start, self.low)
            self.high = jnp.where(self.last == item, self.ends[item], self.high)

    def item_of(self, place):
        found = jnp.int32(0)
        for end in self.ends:
            found = found + (place >= end).astype(jnp.int32)
        return found

    def items_of_rows(self, base, rows):
        place = base + lax.broadcasted_iota(jnp.int32, (rows, 1), 0)
        found = jnp.zeros((rows, 1), jnp.int32)
        for end in self.ends:
            found = found + (place >= end).astype(jnp.int32)
        return found

    def items_of_chip(self, block):
        start, _ = self.chip(block)
        core = self.position % 2
        return jnp.concatenate(
            [
                self.items_of_rows(start + core * self.count, self.count),
                self.items_of_rows(start + (1 - core) * self.count, self.count),
            ],
            axis=0,
        )

    def chip(self, block):
        hop = (block + 1) // 2
        chip = self.position // 2 + jnp.where(block % 2 == 1, -hop, hop)
        rows = 2 * self.count
        start = chip * rows
        live = (chip >= 0) & (chip < self.shards // 2)
        return start, live & (start < self.high) & (start + rows > self.low)


def lanes(rows):
    return lax.broadcasted_iota(jnp.int32, (rows, 128), 1)


def lse_lanes(lane):
    return (lane >= LSE_LANE) & (lane < DELTA_LANE)


def delta_lanes(lane):
    return (lane >= DELTA_LANE) & (lane < DELTA_LANE + 3 * H)


def head_lanes(lane, base, head):
    start = base + 3 * head
    return (lane >= start) & (lane < start + 3)


def cost(microseconds):
    return pl.CostEstimate(
        flops=int(microseconds * FLOPS_EACH), bytes_accessed=int(microseconds * BYTES_EACH), transcendentals=0
    )


def beside(left, right):
    return jnp.concatenate([left.astype(jnp.bfloat16), right.astype(jnp.bfloat16)], axis=1)


def pieces(values):
    high = values.astype(jnp.bfloat16).astype(jnp.float32)
    rest = values - high
    middle = rest.astype(jnp.bfloat16).astype(jnp.float32)
    return high, middle, rest - middle


def dot(left, right):
    return jnp.dot(left, right, preferred_element_type=jnp.float32)


def stack_heads(target, values, features):
    rows = values.shape[0]
    half = lanes(rows) // 64
    wide = values.astype(jnp.float32)
    for h in range(2):
        target[h * rows : (h + 1) * rows, :] = beside(jnp.where(half == h, wide, 0.0), features[h])


def merge_heads(stacked):
    rows = stacked.shape[0] // 2
    return jnp.where(lanes(rows) < 64, stacked[:rows], stacked[rows:])


def item_bias(frame, item):
    lane = lanes(item.shape[0])
    return jnp.where((lane != item) & (lane < frame.items), far, 0.0)


def text_bias(frame, block, rows):
    slot = lax.broadcasted_iota(jnp.int32, (rows, 1), 0)
    length = jnp.int32(0)
    for item in range(frame.items):
        length = jnp.where(block == item, frame.text_len[item], length)
    lane = lanes(rows)
    dead = (lane != block) | (slot >= length)
    return jnp.where(dead & (lane < frame.items), far, 0.0)


def block_rule(frame, kind, rows):
    if kind == "frames":
        return (
            lambda block: frame.chip(block)[1],
            lambda block: item_bias(frame, frame.items_of_chip(block)),
        )
    return (
        lambda block: (block >= frame.first) & (block <= frame.last),
        lambda block: text_bias(frame, block, rows),
    )


def rows_of(block, rows):
    return pl.ds(pl.multiple_of(block * rows, rows), rows)


def each_active(blocks, active, step):
    @pl.loop(0, blocks)
    def _(block):
        @pl.when(active(block))
        def _():
            step(block)


def fill_bias(blocks, rows, active, bias, target, with_lse):
    @pl.when(pl.program_id(0) == 0)
    def _():
        def step(block):
            mask = bias(block)
            if with_lse:
                mask = jnp.where(lse_lanes(lanes(rows)), -1.0, mask)
            target[rows_of(block, rows), :] = mask.astype(jnp.bfloat16)

        each_active(blocks, active, step)


def hide_kernel(items, shards, meta, mod_ref, x_ref, h_ref):
    count, _ = x_ref.shape
    frame = Frame(meta, items, count, shards)
    normed, _ = layer_norm(x_ref[...].astype(jnp.float32))
    item = frame.items_of_rows(frame.position * count, count)
    shift = jnp.broadcast_to(mod_ref[0], normed.shape)
    scale = jnp.broadcast_to(mod_ref[1], normed.shape)
    for i in range(1, items):
        shift = jnp.where(item == i, mod_ref[6 * i], shift)
        scale = jnp.where(item == i, mod_ref[6 * i + 1], scale)
    h_ref[...] = (normed * (1.0 + scale) + shift).astype(jnp.bfloat16)


def hide(meta, modulation, frames, items, shards):
    whole = pl.BlockSpec(memory_space=pltpu.VMEM)
    return pl.pallas_call(
        partial(hide_kernel, items, shards),
        out_shape=jax.ShapeDtypeStruct(frames.shape, jnp.bfloat16),
        in_specs=[pl.BlockSpec(memory_space=pltpu.SMEM), whole, whole],
        out_specs=whole,
        compiler_params=pltpu.CompilerParams(vmem_limit_bytes=58 * MIB),
        cost_estimate=cost(2),
        name="hide",
    )(meta, modulation, frames)


def project_kernel(items, shards, chips, meta, w_hbm, *refs):
    number = len(chips)
    x_refs = refs[: 2 * number]
    q_ref, kv_ref, x_s, q_s, kv_s, w_ref, in_sem, out_sem, w_sem = refs[-9:]
    weights = pltpu.make_async_copy(w_hbm, w_ref, w_sem)
    count, width = x_refs[0].shape
    rows = 2 * count
    frame = Frame(meta, items, count, shards)

    def live(index):
        return frame.chip(index + chips[0])[1]

    weights.start()
    for index in range(number):

        @pl.when(live(jnp.int32(index)))
        def _(index=index):
            for part in range(2):
                block = 2 * index + part
                pltpu.make_async_copy(
                    x_refs[block], x_s.at[pl.ds(block * count, count), :], in_sem.at[block]
                ).start()

    def writes(index):
        here = rows_of(index, rows)
        there = rows_of(index + chips[0], rows)
        return (
            pltpu.make_async_copy(q_s.at[here, :], q_ref.at[there, :], out_sem.at[2 * index]),
            pltpu.make_async_copy(kv_s.at[here, :], kv_ref.at[there, :], out_sem.at[2 * index + 1]),
        )

    weights.wait()

    @pl.loop(0, number)
    def _(index):
        @pl.when(live(index))
        def _():
            for part in range(2):
                block = 2 * index + part
                pltpu.make_async_copy(x_refs[0], x_s.at[rows_of(block, count), :], in_sem.at[block]).wait()
            both = rows_of(index, rows)
            hidden = x_s[both, :]
            q = dot(hidden, w_ref[:, :width]).astype(jnp.bfloat16)
            q_s[both, :] = (q.astype(jnp.float32) * 0.125).astype(jnp.bfloat16)
            kv_s[both, :width] = dot(hidden, w_ref[:, width : 2 * width]).astype(jnp.bfloat16)
            kv_s[both, width:] = dot(hidden, w_ref[:, 2 * width :]).astype(jnp.bfloat16)
            for write in writes(index):
                write.start()

    @pl.loop(0, number)
    def _(index):
        @pl.when(live(index))
        def _():
            for write in writes(index):
                write.wait()


def project(meta, weight, x_blocks, chips, total, earlier, items, shards, name):
    count, width = x_blocks[0].shape
    part = len(x_blocks) * count
    anywhere = pl.BlockSpec(memory_space=pl.ANY)
    before = 2 + len(x_blocks)
    return pl.pallas_call(
        partial(project_kernel, items, shards, chips),
        out_shape=(
            jax.ShapeDtypeStruct((total, width), jnp.bfloat16),
            jax.ShapeDtypeStruct((total, 2 * width), jnp.bfloat16),
        ),
        in_specs=[pl.BlockSpec(memory_space=pltpu.SMEM)] + [anywhere] * (1 + len(x_blocks) + len(earlier)),
        out_specs=(anywhere, anywhere),
        input_output_aliases={before: 0, before + 1: 1} if earlier else {},
        scratch_shapes=[
            pltpu.VMEM((part, width), jnp.bfloat16),
            pltpu.VMEM((part, width), jnp.bfloat16),
            pltpu.VMEM((part, 2 * width), jnp.bfloat16),
            pltpu.VMEM(weight.shape, jnp.bfloat16),
            pltpu.SemaphoreType.DMA((len(x_blocks),)),
            pltpu.SemaphoreType.DMA((len(x_blocks),)),
            pltpu.SemaphoreType.DMA,
        ],
        compiler_params=pltpu.CompilerParams(vmem_limit_bytes=28 * MIB),
        cost_estimate=cost(len(x_blocks) * 1.2),
        name=name,
    )(meta, weight, *x_blocks, *earlier)


def heads_of(ref, here, pair):
    return ref[here, pair * 128 : (pair + 1) * 128]


def spread(count, group, base):
    return pl.BlockSpec((count, group * 128), lambda p: (0, p + base // group))


ALL = slice(None)


def attend_kernel(items, shards, kind, blocks, group, meta, q_ref, k_ref, v_ref, o_ref, low_ref, f_ref, qa, bias_ref, s, m, l, acc):
    count = q_ref.shape[0]
    rows = k_ref.shape[0] // blocks
    frame = Frame(meta, items, count, shards)
    active, bias = block_rule(frame, kind, rows)
    step = pl.program_id(0)
    lane = lanes(count)
    own = frame.items_of_rows(frame.position * count, count)
    own_item = (lane == own).astype(jnp.float32)
    fill_bias(blocks, rows, active, bias, bias_ref, False)
    for g in range(group):
        stack_heads(qa.at[g], heads_of(q_ref, ALL, g), [own_item, own_item])
        m[g] = jnp.full((2 * count, 128), far, jnp.float32)
        l[g] = jnp.zeros((2 * count, 128), jnp.float32)
        acc[g] = jnp.zeros((2 * count, 128), jnp.float32)

    def score(block):
        here = rows_of(block, rows)
        for g in range(group):
            scores = times_transposed(qa[g], jnp.concatenate([heads_of(k_ref, here, g), bias_ref[here, :]], axis=1))
            s[g, block] = scores
            high = m[g]
            for c in range(rows // 128):
                high = jnp.maximum(high, scores[:, c * 128 : (c + 1) * 128])
            m[g] = high

    each_active(blocks, active, score)
    tops = []
    for g in range(group):
        tops.append(jnp.max(m[g], axis=1, keepdims=True))
        m[g] = jnp.broadcast_to(tops[g], (2 * count, 128))

    def weigh(block):
        here = rows_of(block, rows)
        for g in range(group):
            high = m[g]
            total = l[g]
            parts = []
            for c in range(rows // 128):
                part = jnp.exp(s[g, block, :, c * 128 : (c + 1) * 128] - high)
                total = total + part
                parts.append(part.astype(jnp.bfloat16))
            l[g] = total
            acc[g] = acc[g] + dot(jnp.concatenate(parts, axis=1), heads_of(v_ref, here, g))

    each_active(blocks, active, weigh)
    features = jnp.where(step == 0, own_item, f_ref[...].astype(jnp.float32))
    for g in range(group):
        total = jnp.sum(l[g], axis=1, keepdims=True)
        result = merge_heads(acc[g] / total)
        lse = tops[g] + jnp.log(total)
        for h in range(2):
            start = LSE_LANE + 3 * (2 * (step * group + g) + h)
            for number, piece in enumerate(pieces(lse[h * count : (h + 1) * count])):
                features = jnp.where(lane == start + number, piece, features)
        o_ref[:, g * 128 : (g + 1) * 128] = result
        low_ref[:, g * 128 : (g + 1) * 128] = result.astype(jnp.bfloat16)
    f_ref[...] = features.astype(jnp.bfloat16)


def attend(meta, count, queries, kv, kind, blocks, items, shards, name, group=3):
    width = queries.shape[1]
    pairs = width // 128
    total = kv.shape[0]
    rows = total // blocks
    tile = spread(count, group, 0)
    return pl.pallas_call(
        partial(attend_kernel, items, shards, kind, blocks, group),
        grid=(pairs // group,),
        out_shape=(
            jax.ShapeDtypeStruct((count, width), jnp.float32),
            jax.ShapeDtypeStruct((count, width), jnp.bfloat16),
            jax.ShapeDtypeStruct((count, 128), jnp.bfloat16),
        ),
        in_specs=[
            pl.BlockSpec(memory_space=pltpu.SMEM),
            tile,
            spread(total, group, 0),
            spread(total, group, pairs),
        ],
        out_specs=(tile, tile, pl.BlockSpec((count, 128), lambda p: (0, 0))),
        scratch_shapes=[
            pltpu.VMEM((group, 2 * count, 256), jnp.bfloat16),
            pltpu.VMEM((total, 128), jnp.bfloat16),
            pltpu.VMEM((group, blocks, 2 * count, rows), jnp.float32),
            pltpu.VMEM((group, 2 * count, 128), jnp.float32),
            pltpu.VMEM((group, 2 * count, 128), jnp.float32),
            pltpu.VMEM((group, 2 * count, 128), jnp.float32),
        ],
        compiler_params=pltpu.CompilerParams(vmem_limit_bytes=34 * MIB),
        cost_estimate=cost(14 if kind == "frames" else 5),
        name=name,
    )(meta, queries, kv, kv)


def query_side(pair, features, q, do, qa, da):
    lane = lanes(q.shape[0])
    heads = [2 * pair, 2 * pair + 1]
    stack_heads(qa, q, [jnp.where((lane < LSE_LANE) | head_lanes(lane, LSE_LANE, head), features, 0.0) for head in heads])
    stack_heads(da, do, [jnp.where(head_lanes(lane, DELTA_LANE, head), features, 0.0) for head in heads])


def query_step(qa, da, keys, values, bias):
    minus = jnp.where(delta_lanes(lanes(keys.shape[0])), -1.0, 0.0)
    probs = jnp.exp(times_transposed(qa[...], jnp.concatenate([keys, bias], axis=1)))
    slope = times_transposed(da[...], beside(values, minus))
    return dot((probs * slope).astype(jnp.bfloat16), keys)


def key_side(pair, k, v, mask, ka, va):
    lane = lanes(k.shape[0])
    heads = [2 * pair, 2 * pair + 1]
    stack_heads(ka, k, [jnp.where(head_lanes(lane, LSE_LANE, head), -1.0, mask) for head in heads])
    stack_heads(va, v, [jnp.where(head_lanes(lane, DELTA_LANE, head), -1.0, 0.0) for head in heads])


def key_step(ka, va, q, do, features):
    probs = jnp.exp(times_transposed(ka[...], jnp.concatenate([q, features], axis=1)))
    slope = times_transposed(va[...], jnp.concatenate([do, features], axis=1))
    return dot((probs * slope).astype(jnp.bfloat16), q), dot(probs.astype(jnp.bfloat16), do)


def query_grad_kernel(items, shards, blocks, group, meta, q_ref, do_ref, f_ref, k_ref, v_ref, dq_ref, qa, da, bias_ref, acc):
    count = q_ref.shape[0]
    rows = k_ref.shape[0] // blocks
    frame = Frame(meta, items, count, shards)
    active, bias = block_rule(frame, "frames", rows)
    fill_bias(blocks, rows, active, bias, bias_ref, True)
    features = f_ref[...].astype(jnp.float32)
    for g in range(group):
        pair = pl.program_id(0) * group + g
        query_side(pair, features, heads_of(q_ref, ALL, g), heads_of(do_ref, ALL, g), qa.at[g], da.at[g])
        acc[g] = jnp.zeros((2 * count, 128), jnp.float32)

    def step(block):
        here = rows_of(block, rows)
        for g in range(group):
            acc[g] = acc[g] + query_step(
                qa.at[g], da.at[g], heads_of(k_ref, here, g), heads_of(v_ref, here, g), bias_ref[here, :]
            )

    each_active(blocks, active, step)
    for g in range(group):
        dq_ref[:, g * 128 : (g + 1) * 128] = (merge_heads(acc[g]) * 0.125).astype(jnp.bfloat16)


def query_grad(meta, count, queries, grad_out, kv, blocks, items, shards, name, group=3):
    width = queries.shape[1]
    pairs = width // 128
    total = kv.shape[0]
    tile = spread(count, group, 0)
    return pl.pallas_call(
        partial(query_grad_kernel, items, shards, blocks, group),
        grid=(pairs // group,),
        out_shape=jax.ShapeDtypeStruct((count, width), jnp.bfloat16),
        in_specs=[
            pl.BlockSpec(memory_space=pltpu.SMEM),
            tile,
            tile,
            pl.BlockSpec((count, 128), lambda p: (0, pairs)),
            spread(total, group, 0),
            spread(total, group, pairs),
        ],
        out_specs=tile,
        scratch_shapes=[
            pltpu.VMEM((group, 2 * count, 256), jnp.bfloat16),
            pltpu.VMEM((group, 2 * count, 256), jnp.bfloat16),
            pltpu.VMEM((total, 128), jnp.bfloat16),
            pltpu.VMEM((group, 2 * count, 128), jnp.float32),
        ],
        compiler_params=pltpu.CompilerParams(vmem_limit_bytes=58 * MIB),
        cost_estimate=cost(14),
        name=name,
    )(meta, queries, grad_out, grad_out, kv, kv)


def frame_key_grad_kernel(items, shards, blocks, group, meta, q_ref, k_ref, v_ref, dq_ref, all_ref, out_ref, ka, va, dka, dva, do_s, sem):
    count, width = dq_ref.shape[0], do_s.shape[1] - 128
    rows = q_ref.shape[0] // blocks
    frame = Frame(meta, items, count, shards)

    def arrivals(act):
        @pl.when(pl.program_id(0) == 0)
        def _():
            for block in range(2 * blocks):
                start, live = frame.chip(jnp.int32(block // 2))
                first = start + (frame.position + block) % 2 * count

                @pl.when(live)
                def _(block=block, first=first):
                    act(
                        pltpu.make_async_copy(
                            all_ref.at[pl.ds(pl.multiple_of(first, count), count), :],
                            do_s.at[pl.ds(block * count, count), :],
                            sem.at[block],
                        )
                    )

    arrivals(lambda copy: copy.start())
    mask = item_bias(frame, frame.items_of_rows(frame.position * count, count))
    for g in range(group):
        pair = pl.program_id(0) * group + g
        key_side(pair, heads_of(k_ref, ALL, g), heads_of(v_ref, ALL, g), mask, ka.at[g], va.at[g])
        dka[g] = jnp.zeros((2 * count, 128), jnp.float32)
        dva[g] = jnp.zeros((2 * count, 128), jnp.float32)
    arrivals(lambda copy: copy.wait())

    def step(block):
        here = rows_of(block, rows)
        for g in range(group):
            column = pl.multiple_of((pl.program_id(0) * group + g) * 128, 128)
            dk, dv = key_step(
                ka.at[g], va.at[g], heads_of(q_ref, here, g), do_s[here, pl.ds(column, 128)], do_s[here, width:]
            )
            dka[g] = dka[g] + dk
            dva[g] = dva[g] + dv

    each_active(blocks, lambda block: frame.chip(block)[1], step)
    for g in range(group):
        out_ref[1, :, g * 128 : (g + 1) * 128] = merge_heads(dka[g]).astype(jnp.bfloat16)
        out_ref[2, :, g * 128 : (g + 1) * 128] = merge_heads(dva[g]).astype(jnp.bfloat16)
    out_ref[0] = dq_ref[...]


def frame_key_grad(meta, q_window, do_all, kv, grad_queries, count, blocks, items, shards, name, group=3):
    total, width = q_window.shape
    pairs = width // 128
    tile = spread(count, group, 0)
    wide = spread(total, group, 0)
    return pl.pallas_call(
        partial(frame_key_grad_kernel, items, shards, blocks, group),
        grid=(pairs // group,),
        out_shape=jax.ShapeDtypeStruct((3, count, width), jnp.bfloat16),
        in_specs=[
            pl.BlockSpec(memory_space=pltpu.SMEM),
            wide,
            tile,
            spread(count, group, pairs),
            tile,
        ]
        + [pl.BlockSpec(memory_space=pl.ANY)],
        out_specs=pl.BlockSpec((3, count, group * 128), lambda p: (0, 0, p)),
        scratch_shapes=[pltpu.VMEM((group, 2 * count, 256), jnp.bfloat16)] * 2
        + [pltpu.VMEM((group, 2 * count, 128), jnp.float32)] * 2
        + [pltpu.VMEM((total, width + 128), jnp.bfloat16), pltpu.SemaphoreType.DMA((2 * blocks,))],
        compiler_params=pltpu.CompilerParams(vmem_limit_bytes=58 * MIB),
        cost_estimate=cost(18),
        name=name,
    )(meta, q_window, kv, kv, grad_queries, do_all)


def text_grad_kernel(items, shards, group, meta, q_ref, do_ref, f_ref, k_ref, v_ref, dq_ref, dkv_ref, qa, da, ka, va, acc):
    count = q_ref.shape[0]
    rows = k_ref.shape[0] // items
    share = rows // shards
    frame = Frame(meta, items, count, shards)
    features = f_ref[...].astype(jnp.float32)
    pairs = [pl.program_id(0) * group + g for g in range(group)]
    for g in range(group):
        query_side(pairs[g], features, heads_of(q_ref, ALL, g), heads_of(do_ref, ALL, g), qa.at[g], da.at[g])
        acc[g] = jnp.zeros((2 * count, 128), jnp.float32)

    @pl.loop(0, items)
    def _(item):
        here = rows_of(item, rows)
        live = (item >= frame.first) & (item <= frame.last)
        target = rows_of(item, share)

        @pl.when(live)
        def _():
            mask = text_bias(frame, item, rows)
            bias = jnp.where(lse_lanes(lanes(rows)), -1.0, mask).astype(jnp.bfloat16)
            for g in range(group):
                keys, values = heads_of(k_ref, here, g), heads_of(v_ref, here, g)
                acc[g] = acc[g] + query_step(qa.at[g], da.at[g], keys, values, bias)
                key_side(pairs[g], keys, values, mask, ka.at[g], va.at[g])
                grads = key_step(ka.at[g], va.at[g], heads_of(q_ref, ALL, g), heads_of(do_ref, ALL, g), f_ref[...])
                for which, grad in enumerate(grads):
                    merged = merge_heads(grad).astype(jnp.bfloat16)
                    for owner in range(shards):
                        dkv_ref[owner, which, target, g * 128 : (g + 1) * 128] = merged[
                            owner * share : (owner + 1) * share
                        ]

        @pl.when(jnp.logical_not(live))
        def _():
            dkv_ref[:, :, target, :] = jnp.zeros((shards, 2, share, group * 128), jnp.bfloat16)

    for g in range(group):
        dq_ref[:, g * 128 : (g + 1) * 128] = (merge_heads(acc[g]) * 0.125).astype(jnp.bfloat16)


def text_grad(meta, queries, grad_out, features, kv, items, shards, name, group=3):
    count, width = queries.shape
    pairs = width // 128
    total = kv.shape[0]
    tile = spread(count, group, 0)
    rows = total // items
    return pl.pallas_call(
        partial(text_grad_kernel, items, shards, group),
        grid=(pairs // group,),
        out_shape=(
            jax.ShapeDtypeStruct((count, width), jnp.bfloat16),
            jax.ShapeDtypeStruct((shards, 2, total // shards, width), jnp.bfloat16),
        ),
        in_specs=[
            pl.BlockSpec(memory_space=pltpu.SMEM),
            tile,
            tile,
            pl.BlockSpec((count, 128), lambda p: (0, 0)),
            spread(total, group, 0),
            spread(total, group, pairs),
        ],
        out_specs=(tile, pl.BlockSpec((shards, 2, total // shards, group * 128), lambda p: (0, 0, 0, p))),
        scratch_shapes=[pltpu.VMEM((group, 2 * count, 256), jnp.bfloat16)] * 2
        + [pltpu.VMEM((group, 2 * rows, 256), jnp.bfloat16)] * 2
        + [pltpu.VMEM((group, 2 * count, 128), jnp.float32)],
        compiler_params=pltpu.CompilerParams(vmem_limit_bytes=18 * MIB),
        cost_estimate=cost(8),
        name=name,
    )(meta, queries, grad_out, features, kv, kv)


def mlp_kernel(h_ref, d_ref, up_ref, down_ref, act_ref, m_ref, dh_ref):
    step = pl.program_id(0)
    last = pl.num_programs(0) - 1

    @pl.when(step < last)
    def _():
        u = dot(h_ref[...], up_ref[...])
        slope = times_transposed(d_ref[...], down_ref[...])
        inner = 0.7978845608028654 * (u + 0.044715 * (u * u * u))
        t = jnp.tanh(inner)
        g = (0.5 * u * (1.0 + t)).astype(jnp.bfloat16)
        bend = 0.7978845608028654 * (1.0 + 0.134145 * (u * u))
        du = (slope * (0.5 * (1.0 + t) + 0.5 * u * (1.0 - t * t) * bend)).astype(jnp.bfloat16)
        act_ref[0, 0] = g
        act_ref[0, 1] = du
        m = dot(g, down_ref[...])
        dh = times_transposed(du, up_ref[...])

        @pl.when(step == 0)
        def _():
            m_ref[...] = m
            dh_ref[...] = dh

        @pl.when(step > 0)
        def _():
            m_ref[...] = m_ref[...] + m
            dh_ref[...] = dh_ref[...] + dh

    @pl.when(step == last)
    def _():
        act_ref[0, 0] = h_ref[...]
        act_ref[0, 1] = d_ref[...]


def mlp(hidden, grad, w_up, w_down):
    count, width = hidden.shape
    chunks = w_up.shape[1] // width
    whole = pl.BlockSpec((count, width), lambda c: (0, 0))
    held = lambda c: jnp.minimum(c, chunks - 1)
    return pl.pallas_call(
        mlp_kernel,
        grid=(chunks + 1,),
        out_shape=(
            jax.ShapeDtypeStruct((chunks + 1, 2, count, width), jnp.bfloat16),
            jax.ShapeDtypeStruct((count, width), jnp.float32),
            jax.ShapeDtypeStruct((count, width), jnp.float32),
        ),
        in_specs=[
            whole,
            whole,
            pl.BlockSpec((width, width), lambda c: (0, held(c))),
            pl.BlockSpec((width, width), lambda c: (held(c), 0)),
        ],
        out_specs=(pl.BlockSpec((1, 2, count, width), lambda c: (c, 0, 0, 0)), whole, whole),
        compiler_params=pltpu.CompilerParams(vmem_limit_bytes=20 * MIB),
        cost_estimate=cost(9),
        name="mlp",
    )(hidden, grad, w_up, w_down)


UNIT = 192
X_BIT, Y_BIT = 0, 1


def rows_picked(x, core):
    row = lax.broadcasted_iota(jnp.int32, (384, 768), 0)
    column = lax.broadcasted_iota(jnp.int32, (384, 768), 1)
    chip = (row >= 96).astype(jnp.int32) + (row >= 192).astype(jnp.int32) + (row >= 288).astype(jnp.int32)
    pick = (column == row + 96 * (chip + core)).astype(jnp.bfloat16)
    return times_transposed(pick, x).astype(jnp.bfloat16)


def one_above_other(upper, lower):
    return jnp.concatenate([upper, lower], axis=0)


def finish_kernel(items, shards, packed, meta, mod_ref, w_ref, d_ref, x_ref, dx_ref, a_ref, dh_ref, n_ref, dy_ref, m_ref, out_ref, sum_ref):
    count, width = x_ref.shape
    frame = Frame(meta, items, count, shards)
    item = frame.items_of_rows(frame.position * count, count)
    grad = sum(times_transposed(d_ref[i], w_ref[:, i * width : (i + 1) * width]) for i in range(3))
    normed, inverse = layer_norm(x_ref[...].astype(jnp.float32))
    scale = jnp.zeros((count, width), jnp.float32)
    for i in range(items):
        scale = jnp.where(item == i, mod_ref[6 * i + 1], scale)
    dx = dx_ref[...]
    out_ref[...] = dx + norm_back(grad * (1.0 + scale), normed, inverse)
    dh = dh_ref[...]
    terms = (
        grad,
        grad * normed,
        dx * a_ref[...],
        dh,
        dh * n_ref[...],
        dy_ref[...].astype(jnp.float32) * m_ref[...],
    )
    sums = []
    for number, term in enumerate(terms):
        rows = [jnp.sum(jnp.where(item == i, term, 0.0), axis=0, keepdims=True) for i in range(items)]
        rows += [jnp.zeros((8 - items, width), jnp.float32)]
        sums.append(jnp.concatenate(rows, axis=0))
        if not packed:
            sum_ref[number] = sums[number]
    if packed:
        values = jnp.concatenate(sums, axis=0)
        left = lax.broadcasted_iota(jnp.int32, (24, 384), 1) < UNIT
        for pair in range(2):
            part = third(values, pair)
            rolled = pltpu.roll(part, UNIT, 1)
            each = (jnp.where(left, part[:24], rolled[24:]), jnp.where(left, rolled[:24], part[24:]))
            for half in range(2):
                relative = (2 * pair + half) ^ (frame.position // 2)
                sum_ref[relative % 2, relative // 2, :24, :] = each[half]
                sum_ref[relative % 2, relative // 2, 24:, :] = jnp.zeros((8, 384), jnp.float32)


def finish(meta, modulation, weight, grads, frames, *arrays_items_shards):
    *arrays, items, shards, packed = arrays_items_shards
    count, width = frames.shape
    whole = pl.BlockSpec(memory_space=pltpu.VMEM)
    return pl.pallas_call(
        partial(finish_kernel, items, shards, packed),
        out_shape=(
            jax.ShapeDtypeStruct((count, width), jnp.float32),
            jax.ShapeDtypeStruct((2, 2, 32, 384) if packed else (6, 8, width), jnp.float32),
        ),
        in_specs=[pl.BlockSpec(memory_space=pltpu.SMEM)] + [whole] * (4 + len(arrays)),
        out_specs=(whole, whole),
        compiler_params=pltpu.CompilerParams(vmem_limit_bytes=58 * MIB),
        cost_estimate=cost(5),
        name="finish",
    )(meta, modulation, weight, grads, frames, *arrays)


def attend_back_kernel(items, shards, meta, mod_ref, g_ref, cq_ref, o_ref, dx_ref, x_ref, exact_ref, f_ref, dx_out, low_out, do_out):
    count, width = x_ref.shape
    frame = Frame(meta, items, count, shards)
    item = frame.items_of_rows(frame.position * count, count)
    normed, inverse = layer_norm(x_ref[...])
    dx = dx_ref[...] + norm_back(times_transposed(g_ref[...], cq_ref[...]), normed, inverse)
    dx_out[...] = dx
    gate = jnp.broadcast_to(mod_ref[2], dx.shape)
    for i in range(1, items):
        gate = jnp.where(item == i, mod_ref[6 * i + 2], gate)
    low = (dx * gate).astype(jnp.bfloat16)
    low_out[...] = low
    grad = times_transposed(low, o_ref[...]).astype(jnp.bfloat16)
    do_out[:, :width] = grad
    row = lax.broadcasted_iota(jnp.int32, (width, 128), 0)
    lane = lax.broadcasted_iota(jnp.int32, (width, 128), 1)
    pick = jnp.zeros((width, 128), jnp.float32)
    for head in range(H):
        mine = (row >= head * (width // H)) & (row < (head + 1) * (width // H))
        pick = jnp.where(mine & head_lanes(lane, DELTA_LANE, head), 1.0, pick)
    pick = pick.astype(jnp.bfloat16)
    products = grad.astype(jnp.float32) * exact_ref[...]
    delta = sum(dot(piece.astype(jnp.bfloat16), pick) for piece in pieces(products))
    place = lanes(1)
    features = f_ref[...].astype(jnp.float32)
    for number, piece in enumerate(pieces(delta)):
        here = jnp.zeros((1, 128), jnp.bool_)
        for head in range(H):
            here = here | (place == DELTA_LANE + 3 * head + number)
        features = jnp.where(here, piece, features)
    do_out[:, width:] = features.astype(jnp.bfloat16)


def attend_back(meta, modulation, grads, w_cq, w_o, grad_cross, after_attn, attn_exact, features, items, shards):
    count, width = grads.shape
    whole = pl.BlockSpec(memory_space=pltpu.VMEM)
    return pl.pallas_call(
        partial(attend_back_kernel, items, shards),
        out_shape=(
            jax.ShapeDtypeStruct((count, width), jnp.float32),
            jax.ShapeDtypeStruct((count, width), jnp.bfloat16),
            jax.ShapeDtypeStruct((count, width + 128), jnp.bfloat16),
        ),
        in_specs=[pl.BlockSpec(memory_space=pltpu.SMEM)] + [whole] * 8,
        out_specs=(whole, whole, whole),
        compiler_params=pltpu.CompilerParams(vmem_limit_bytes=20 * MIB),
        cost_estimate=cost(3),
        name="attend_back",
    )(meta, modulation, grads, w_cq, w_o, grad_cross, after_attn, attn_exact, features)


class Packer:
    def __init__(self, meta, items, outputs):
        self.core, self.chip = meta[0] % 2, meta[0] // 2
        self.mine = meta[1 + 2 * items]
        self.outputs = outputs

    def steps(self, owner_chip):
        relative = owner_chip ^ self.chip
        return relative % 2, relative // 2

    def store(self, name, owner, owner_chip, row, values):
        scratch, first = self.outputs[name]
        relative = owner ^ self.mine
        where = ((relative >> first) % 2, (relative >> (1 - first)) % 2, *self.steps(owner_chip))
        scratch[where + (slice(row, row + values.shape[0]),)] = values.astype(jnp.bfloat16)

    def store_split(self, name, pair, row, values, chips):
        rolled = pltpu.roll(values, UNIT, 1)
        each = values.shape[0] // len(chips)
        left = lax.broadcasted_iota(jnp.int32, (each // 2, 384), 1) < UNIT
        for number, owner_chip in enumerate(chips):
            upper = slice(number * each, number * each + each // 2)
            lower = slice(number * each + each // 2, (number + 1) * each)
            self.store(name, 2 * pair, owner_chip, row, jnp.where(left, values[upper], rolled[lower]))
            self.store(name, 2 * pair + 1, owner_chip, row, jnp.where(left, rolled[upper], values[lower]))


def core_columns(core, number, each):
    return pl.ds(pl.multiple_of(number * 2 * each + core * each, 128), each)


def third(values, number):
    return values[:, number * 384 : (number + 1) * 384]


def pack_mlp_kernel(items, meta, own, sib, down_s, up_s):
    packer = Packer(meta, items, {"down": (down_s, Y_BIT), "up": (up_s, X_BIT)})
    both = lambda chunk, which: one_above_other(own[chunk, which], sib[chunk, which])
    grad = both(4, 1)
    for owner_chip in range(4):
        here = core_columns(packer.core, 0, 384)
        left = one_above_other(own[owner_chip, 0, :, here], sib[owner_chip, 0, :, here])
        values = contract_rows(left, grad)
        for pair in range(2):
            packer.store_split("down", pair, 0, third(values, pair), [owner_chip])
    left = rows_picked(both(4, 0), packer.core)
    for owner in range(4):
        values = dot(left, both(owner, 1))
        for owner_chip in range(4):
            for half in range(2):
                packer.store(
                    "up", owner, owner_chip, half * 96, third(values, half)[owner_chip * 96 : (owner_chip + 1) * 96]
                )


def pack_middle_kernel(items, meta, own, sib, text_own, text_sib, text, square_s, text_s):
    packer = Packer(meta, items, {"square": (square_s, Y_BIT), "text": (text_s, X_BIT)})
    both = lambda which: one_above_other(own[which], sib[which])
    for number in range(3):
        values = dot(rows_picked(both(2 * number), packer.core), both(2 * number + 1))
        for pair in range(2):
            packer.store_split("square", pair, number * 48, third(values, pair), range(4))
    share = text_own.shape[2] // items

    def chip_sum(which, item, owner):
        here = slice(item * share, (item + 1) * share)
        total = text_own[owner, which, here, :].astype(jnp.float32) + text_sib[owner, which, here, :].astype(jnp.float32)
        return total.astype(jnp.bfloat16)

    sums = [
        jnp.concatenate(
            [chip_sum(which, item, owner) for item in range(items) for owner in range(text_own.shape[0])], axis=0
        )
        for which in range(2)
    ]
    left = jnp.concatenate([text[:, core_columns(packer.core, chip, 128)] for chip in range(4)], axis=1)
    for which in range(2):
        values = contract_rows(left, sums[which])
        for owner_chip in range(4):
            for half in range(2):
                packer.store(
                    "text", 2 * which + half, owner_chip, 0, third(values, half)[owner_chip * 128 : (owner_chip + 1) * 128]
                )


def pack_qkv_kernel(items, meta, h_own, h_sib, own, sib, plain_s, split_s):
    packer = Packer(meta, items, {"plain": (plain_s, X_BIT), "split": (split_s, Y_BIT)})
    left = rows_picked(one_above_other(h_own[...], h_sib[...]), packer.core)
    values = []
    for number in range(3):
        product = dot(left, one_above_other(own[number], sib[number]))
        values += [third(product, 0), third(product, 1)]
    for owner, column in enumerate((0, 2, 3, 5)):
        for owner_chip in range(4):
            packer.store("plain", owner, owner_chip, 0, values[column][owner_chip * 96 : (owner_chip + 1) * 96])
    for pair, column in enumerate((1, 4)):
        packer.store_split("split", pair, 0, values[column], range(4))


def packing(kernel, items, inputs, groups, *refs):
    ins, outs, scratch, sem = refs[:inputs], refs[inputs:-groups - 1], refs[-groups - 1 : -1], refs[-1]
    kernel(items, *ins, *scratch)
    copies = [pltpu.make_async_copy(scratch[i // 2].at[1 - i % 2], outs[i], sem.at[i]) for i in range(2 * groups)]
    for copy in copies:
        copy.start()
    for copy in copies:
        copy.wait()


def pack(kernel, meta, operands, shapes, items, name):
    shapes = [(2, 2, 2, each, 384) if isinstance(each, int) else each for each in shapes]
    whole = pl.BlockSpec(memory_space=pltpu.VMEM)
    return pl.pallas_call(
        partial(packing, kernel, items, 1 + len(operands), len(shapes)),
        out_shape=tuple(jax.ShapeDtypeStruct(shape, jnp.bfloat16) for shape in shapes for _ in range(2)),
        in_specs=[pl.BlockSpec(memory_space=pltpu.SMEM)] + [whole] * len(operands),
        out_specs=tuple([pl.BlockSpec(memory_space=pl.ANY)] * (2 * len(shapes))),
        scratch_shapes=[pltpu.VMEM((2, *shape), jnp.bfloat16) for shape in shapes]
        + [pltpu.SemaphoreType.DMA((2 * len(shapes),))],
        compiler_params=pltpu.CompilerParams(vmem_limit_bytes=58 * MIB),
        cost_estimate=cost(8 if name != "pack_qkv" else 3),
        name=name,
    )(meta, *operands)


def bundle_kernel(*refs):
    for number, each in enumerate(refs[:-1]):
        refs[-1][number] = each[...]


def bundle(*arrays):
    whole = pl.BlockSpec(memory_space=pltpu.VMEM)
    return pl.pallas_call(
        bundle_kernel,
        out_shape=jax.ShapeDtypeStruct((len(arrays), *arrays[0].shape), arrays[0].dtype),
        in_specs=[whole] * len(arrays),
        out_specs=whole,
        cost_estimate=cost(3),
        name="bundle",
    )(*arrays)


def trade(values, axis, bit):
    size = lax.axis_size(axis)
    return lax.ppermute(values, axis, [(i, i ^ (1 << bit)) for i in range(size)])


def added(keep, got):
    return [(keep[i].astype(jnp.float32) + got[i].astype(jnp.float32)).astype(jnp.bfloat16) for i in range(2)]


def halve(keep, send, axis, bit, after=()):
    got = trade(send, axis, bit)
    if after:
        [keep] = hold((keep,), *after)
    return added(keep, got)


def last_half(keep, send, after=()):
    got = trade(send, "seq", 2)
    if after:
        [keep] = hold((keep,), *after)
    return keep.astype(jnp.float32) + got.astype(jnp.float32)


def joined(upper, lower):
    return [jnp.concatenate([upper[i], lower[i]], axis=-2) for i in (1, 0)]


def unpack_kernel(items, place, last_keep, last_got, middle_keep, middle_got, qkv_ref, o_ref, cq_ref, ckv_ref, co_ref, mod_ref, mlp_ref):
    def whole(keep, got, start, rows):
        here = slice(start, start + rows)
        return keep[here, :].astype(jnp.float32) + got[here, :].astype(jnp.float32)

    def parts(values):
        return one_above_other(values, pltpu.roll(values, UNIT, 1))

    plain = whole(last_keep, last_got, 0, 96)
    split = parts(whole(last_keep, last_got, 96, 48))
    empty = jnp.zeros((96, 384), jnp.float32)
    even = jnp.concatenate([plain, split], axis=1)
    shifted = pltpu.roll(jnp.concatenate([plain, empty], axis=1), UNIT, 1)
    lane = lax.broadcasted_iota(jnp.int32, (96, 768), 1)
    odd = jnp.where(lane < UNIT, jnp.concatenate([split, empty], axis=1), shifted)

    @pl.when(place[0] == 0)
    def _():
        qkv_ref[...] = even[:, :576]

    @pl.when(place[0] == 1)
    def _():
        qkv_ref[...] = odd[:, :576]

    for number, ref in enumerate((co_ref, cq_ref, o_ref)):
        ref[...] = parts(whole(middle_keep, middle_got, number * 48, 48))[:, :UNIT]
    ckv_ref[...] = whole(middle_keep, middle_got, 144, 128)
    terms = parts(whole(last_keep, last_got, 144, 32)[:24])
    terms = jnp.where(place[1] == 0, terms, pltpu.roll(terms, 384 - UNIT // 2, 1))[:, : UNIT // 2]
    for item in range(items):
        for number in range(3):
            mod_ref[item * 3 + number] = terms[number * 8 + item : number * 8 + item + 1]
            mlp_ref[item * 3 + number] = terms[24 + number * 8 + item : 24 + number * 8 + item + 1]


def unpack(place, last, middle, items):
    whole = pl.BlockSpec(memory_space=pltpu.VMEM)
    shapes = [(96, 576), (96, UNIT), (96, UNIT), (128, 384), (96, UNIT)] + [(items * 3, 1, UNIT // 2)] * 2
    return pl.pallas_call(
        partial(unpack_kernel, items),
        out_shape=tuple(jax.ShapeDtypeStruct(shape, jnp.float32) for shape in shapes),
        in_specs=[pl.BlockSpec(memory_space=pltpu.SMEM)] + [whole] * 4,
        out_specs=tuple([whole] * len(shapes)),
        cost_estimate=cost(2),
        name="unpack",
    )(place, *last, *middle)


def unsplit(rows):
    return jnp.concatenate([rows[:, :UNIT], rows[:, UNIT:]], axis=0)


def with_deltas(features, grad_out, attn_exact):
    width = attn_exact.shape[1]
    lane = jnp.arange(128)[None, :]
    head = (jnp.arange(width) // (width // H))[:, None]
    pick = ((lane >= DELTA_LANE) & ((lane - DELTA_LANE) // 3 == head)).astype(jnp.float32)
    delta = jnp.dot(
        grad_out.astype(jnp.float32) * attn_exact,
        pick,
        precision=lax.Precision.HIGHEST,
        preferred_element_type=jnp.float32,
    )
    high = lax.reduce_precision(delta, 8, 7)
    middle = lax.reduce_precision(delta - high, 8, 7)
    which = (lane - DELTA_LANE) % 3
    piece = jnp.where(which == 0, high, jnp.where(which == 1, middle, delta - high - middle))
    inside = (lane >= DELTA_LANE) & (lane < DELTA_LANE + 3 * H)
    return jnp.where(inside, piece.astype(jnp.bfloat16), features)


def hop(below, above, shards):
    up = [(i, i + 2) for i in range(shards - 2)]
    return lax.ppermute(below, "seq", up), lax.ppermute(above, "seq", [(j, i) for i, j in up])


def hold(values, *first):
    held = lax.optimization_barrier((*values, *first))
    return held[: len(values)]


def body(
    frames,
    cotangent,
    modulation,
    lengths,
    text,
    text_len,
    w_qkv,
    w_o,
    w_cq,
    w_ckv,
    w_co,
    w_up,
    w_down,
):
    local = frames[0]
    count, width = local.shape
    items = lengths.shape[1]
    text_rows, text_width = text.shape[2:]
    shards = lax.axis_size("seq")
    position = lax.axis_index("seq")
    reach = min(-(-(LONGEST - 1) // (2 * count)), shards // 2 - 1)
    chips = 1 + 2 * reach
    meta = jnp.concatenate(
        [position[None].astype(jnp.int32), lengths[0], text_len[0], lax.axis_index("batch")[None].astype(jnp.int32)]
    )
    item_range = jnp.arange(items, dtype=jnp.int32)
    ends = jnp.sum(jnp.where(item_range[None, :] <= item_range[:, None], lengths[0][None, :], 0), axis=1)
    place = position * count + jnp.arange(count, dtype=jnp.int32)
    query_items = jnp.sum((place[:, None] >= ends[None, :]).astype(jnp.int32), axis=1)[:, None]
    mod = modulation[0]
    mod_rows = modulation.reshape(items * 6, 1, width)

    def per_frame(which):
        found = jnp.broadcast_to(mod[0, which][None, :], (count, width))
        for item in range(1, items):
            found = jnp.where(query_items == item, mod[item, which][None, :], found)
        return found

    swap = [(i, i ^ 1) for i in range(shards)]

    def sibling(values):
        return lax.ppermute(values, "seq", swap)

    fast = shards == 8 and lax.axis_size("batch") == 4 and width == 768

    text_proj = jnp.dot(
        text[0].reshape(items * text_rows, text_width), w_ckv, preferred_element_type=jnp.float32
    ).astype(jnp.bfloat16)
    hidden_one = hide(meta, mod_rows, local, items, shards)
    sides = list(hold(hop(hidden_one, hidden_one, shards), text_proj))
    for _ in range(1, reach):
        sides += hop(*sides[-2:], shards)

    def with_siblings(blocks):
        return [each for block in blocks for each in (block, sibling(block))]

    total = 2 * chips * count
    near = with_siblings([hidden_one] + sides[:2])
    hidden_sib = near[1]
    q_window, kv = project(meta, w_qkv, near, range(3), total, (), items, shards, "project_near")
    if reach > 1:
        apart = with_siblings(hold(sides[2:], kv))
        q_window, kv = project(
            meta, w_qkv, apart, range(3, chips), total, (q_window, kv), items, shards, "project_far"
        )
    inputs = local.astype(jnp.float32)
    attn_exact, attended, features = attend(meta, count, q_window, kv, "frames", chips, items, shards, "self_attend")
    branch_one = jnp.dot(attended, w_o, preferred_element_type=jnp.float32)
    after_attn = inputs + per_frame(2) * branch_one
    normed_cross, inverse_cross = layer_norm(after_attn)
    cross_in = normed_cross.astype(jnp.bfloat16)
    cross_queries = jnp.dot(cross_in, w_cq, preferred_element_type=jnp.float32).astype(jnp.bfloat16)
    cross_queries = (cross_queries.astype(jnp.float32) * 0.125).astype(jnp.bfloat16)
    cross_exact, cross_out, cross_features = attend(
        meta, count, cross_queries, text_proj, "text", items, items, shards, "cross_attend"
    )
    branch_two = jnp.dot(cross_out, w_co, preferred_element_type=jnp.float32)
    after_cross = after_attn + branch_two
    normed_two, inverse_two = layer_norm(after_cross)
    hidden_two = (normed_two * (1.0 + per_frame(4)) + per_frame(3)).astype(jnp.bfloat16)
    gate_two = per_frame(5)
    grad_out = cotangent[0].astype(jnp.float32)
    grad_branch_three = (grad_out * gate_two).astype(jnp.bfloat16)
    acts, branch_three, grad_hidden_two = mlp(hidden_two, grad_branch_three, w_up, w_down)
    if fast:
        acts_sib = sibling(acts)
    result = after_cross + gate_two * branch_three
    grad_cross = grad_out + norm_back(grad_hidden_two * (1.0 + per_frame(4)), normed_two, inverse_two)
    grad_branch_two = grad_cross.astype(jnp.bfloat16)
    grad_cross_out = times_transposed(grad_branch_two, w_co).astype(jnp.bfloat16)
    cross_features = with_deltas(cross_features, grad_cross_out, cross_exact)
    grad_cross_queries, text_terms = text_grad(
        meta, cross_queries, grad_cross_out, cross_features, text_proj, items, shards, "cross_grad"
    )
    if fast:
        [grad_cross_queries] = hold((grad_cross_queries,), acts_sib)
    grad_attn_res, grad_branch_one, do_low = attend_back(
        meta, mod_rows, grad_cross_queries, w_cq, w_o, grad_cross, after_attn, attn_exact, features, items, shards
    )
    if fast:
        text_sib = sibling(text_terms)
    do_all = lax.all_gather(do_low, "seq", axis=0, tiled=True)
    if fast:
        middle = bundle(cross_out, grad_branch_two, cross_in, grad_cross_queries, attended, grad_branch_one)
        middle_sib = sibling(middle)
        [acts_sib] = hold((acts_sib,), do_low, middle)
        mlp_parts = pack(pack_mlp_kernel, meta, (acts, acts_sib), (192, 192), items, "pack_mlp")
        [middle] = hold((middle,), *mlp_parts)
        middle_parts = pack(
            pack_middle_kernel,
            meta,
            (middle, middle_sib, text_terms, text_sib, text[0].reshape(items * text_rows, text_width)),
            (144, 128),
            items,
            "pack_middle",
        )
        [do_own] = hold((do_low,), *middle_parts)
    else:
        do_own = do_low
    grad_queries = query_grad(
        meta, count, q_window, do_own, kv, chips, items, shards, "self_query_grad"
    )
    share_rows = text_rows // shards
    [text_terms_late] = hold((text_terms,), grad_queries)
    text_total = lax.psum_scatter(
        text_terms_late.reshape(shards * 2 * items * share_rows, width), "seq", scatter_dimension=0, tiled=True
    ).reshape(2, items * share_rows, width)
    if fast:
        down_part = halve(mlp_parts[1], mlp_parts[0], "batch", Y_BIT, (grad_queries,))
        up_part = halve(mlp_parts[3], mlp_parts[2], "batch", X_BIT, (grad_queries,))
        [do_all] = hold((do_all,), *middle_parts, *down_part, *up_part)
    grad_projected = frame_key_grad(
        meta, q_window, do_all, kv, grad_queries, count, chips, items, shards, "self_key_grad"
    )
    if fast:
        projected_sib = sibling(grad_projected)
    if fast:
        square_send, square_keep, text_send, text_keep = middle_parts
        got = (
            trade(down_part[1], "batch", X_BIT),
            trade(up_part[1], "batch", Y_BIT),
            trade(square_send, "batch", Y_BIT),
            trade(text_send, "batch", X_BIT),
        )
        got = hold(got, grad_projected)
        down_part, up_part = added(down_part[0], got[0]), added(up_part[0], got[1])
        square_part, text_w_part = added(square_keep, got[2]), added(text_keep, got[3])
        first_send, first_keep = joined(down_part, up_part)
        [projected_sib] = hold((projected_sib,), *square_part, *text_w_part, first_send)
        qkv_parts = pack(
            pack_qkv_kernel,
            meta,
            (hidden_one, hidden_sib, grad_projected, projected_sib),
            (96, 48),
            items,
            "pack_qkv",
        )
        [grad_projected] = hold((grad_projected,), *qkv_parts)
    grad_inputs, terms = finish(
        meta, mod_rows, w_qkv, grad_projected, local, grad_attn_res, branch_one, grad_hidden_two, normed_two, cotangent[0],
        branch_three, items, shards, fast,
    )
    if not fast:
        for bit in range(shards.bit_length() - 1):
            terms = terms + trade(terms, "seq", bit)
        own = width // shards
        terms = lax.dynamic_slice_in_dim(terms, position * own, own, 2)
        shares = terms[:, :items].transpose(1, 0, 2)[None]
        grad_mod, grad_mod_mlp = shares[:, :, :3], shares[:, :, 3:]
    if fast:
        terms = (terms + trade(terms, "seq", 0)).astype(jnp.bfloat16)
        plain_send, plain_keep, split_send, split_keep = qkv_parts
        first_part = halve(first_keep, first_send, "seq", 1, (grad_inputs,))
        square_part = halve(*square_part, "batch", X_BIT, first_part)
        text_w_part = halve(*text_w_part, "batch", Y_BIT, first_part)
        half_way = (grad_inputs,)
        plain_part = halve(plain_keep, plain_send, "batch", X_BIT, half_way)
        split_part = halve(split_keep, split_send, "batch", Y_BIT, half_way)
        half_way = (*plain_part, *split_part)
        plain_part = halve(*plain_part, "batch", Y_BIT)
        split_part = halve(*split_part, "batch", X_BIT)
        sent = [jnp.concatenate([plain_part[i], split_part[i], terms[i]], axis=-2) for i in (1, 0)]
        middle_send, middle_keep = joined(square_part, text_w_part)
        middle_part = halve(middle_keep, middle_send, "seq", 1, sent)
        last_part = halve(sent[1], sent[0], "seq", 1)
        place = jnp.stack([lax.axis_index("batch"), position]).astype(jnp.int32) % 2
        grad_qkv, grad_o, grad_cq, grad_ckv, grad_co, grad_mod, grad_mod_mlp = unpack(
            place,
            (last_part[0], trade(last_part[1], "seq", 2)),
            (middle_part[0], trade(middle_part[1], "seq", 2)),
            items,
        )
        grad_mod = grad_mod.reshape(1, items, 3, width // shards)
        grad_mod_mlp = grad_mod_mlp.reshape(1, items, 3, width // shards)
        first_rows = last_half(*first_part, last_part)
        [text_total] = hold((text_total,), *last_part)
        grad_up = jnp.concatenate([first_rows[192:288], first_rows[288:]], axis=1)
        grads = (grad_qkv, grad_o, grad_cq, grad_ckv, grad_co, grad_up, unsplit(first_rows[:192]))
    text_grad_low = jnp.concatenate([text_total[0], text_total[1]], axis=1)
    grad_text = times_transposed(text_grad_low, w_ckv).reshape(1, items, share_rows, text_width)
    if not fast:
        text_mine = lax.dynamic_slice_in_dim(text[0], position * share_rows, share_rows, 1)
        grads = reduced_grads(
            (hidden_one, jnp.concatenate(list(grad_projected), axis=1)),
            (attended, grad_branch_one),
            (cross_in, grad_cross_queries),
            (text_mine.reshape(items * share_rows, text_width), text_grad_low),
            (cross_out, grad_branch_two),
            (hidden_two, acts[:-1, 1].transpose(1, 0, 2).reshape(count, -1)),
            (acts[:-1, 0].transpose(1, 0, 2).reshape(count, -1), grad_branch_three),
        )
    return (
        result.astype(jnp.bfloat16)[None],
        grad_inputs[None],
        grad_mod,
        grad_mod_mlp,
        grad_text,
        *grads,
    )


def reduced_grads(*pairs):
    def reduce_weight(left, right):
        grad = contract_rows(left, right).astype(jnp.bfloat16)
        part = lax.psum_scatter(grad, "seq", scatter_dimension=0, tiled=True)
        return lax.psum_scatter(part, "batch", scatter_dimension=1, tiled=True).astype(jnp.float32)

    return tuple(reduce_weight(*pair) for pair in pairs)


def solution(mesh):
    in_specs = (
        P("batch", "seq", None),
        P("batch", "seq", None),
        P("batch", None, None, None),
        P("batch", None),
        P("batch", None, None, None),
        P("batch", None),
        P(),
        P(),
        P(),
        P(),
        P(),
        P(),
        P(),
    )
    out_specs = (
        P("batch", "seq", None),
        P("batch", "seq", None),
        P("batch", None, None, "seq"),
        P("batch", None, None, "seq"),
        P("batch", None, "seq", None),
        P("seq", "batch"),
        P("seq", "batch"),
        P("seq", "batch"),
        P("seq", "batch"),
        P("seq", "batch"),
        P("seq", "batch"),
        P("seq", "batch"),
    )
    return jax.shard_map(body, mesh=mesh, in_specs=in_specs, out_specs=out_specs, check_vma=False)
```

```python
from functools import partial

import jax
import jax.numpy as jnp
from jax import lax
from jax.experimental import pallas as pl
from jax.experimental.pallas import tpu as pltpu
from jax.sharding import PartitionSpec as P

H = 12
LONGEST = 1024

epsilon = 1e-06
far = -1e30
LSE_LANE = 8
DELTA_LANE = 44
MIB = 1 << 20
FLOPS_EACH, BYTES_EACH = 7.5e+08, 2.48e+06


def layer_norm(values):
    centred = values - jnp.mean(values, axis=-1, keepdims=True)
    inverse = lax.rsqrt(jnp.mean(centred * centred, axis=-1, keepdims=True) + epsilon)
    return (centred * inverse, inverse)


def norm_back(grad_normed, normed, inverse):
    return inverse * (
        grad_normed
        - jnp.mean(grad_normed, axis=-1, keepdims=True)
        - normed * jnp.mean(grad_normed * normed, axis=-1, keepdims=True)
    )


def contract_rows(left, right):
    return lax.dot_general(
        left, right, (((0,), (0,)), ((), ())), preferred_element_type=jnp.float32
    )


def times_transposed(left, right):
    return lax.dot_general(
        left, right, (((1,), (1,)), ((), ())), preferred_element_type=jnp.float32
    )


class Frame:
    def __init__(self, meta, items, count, shards):
        self.position = meta[0]
        self.items = items
        self.count = count
        self.shards = shards
        self.ends = []
        total = jnp.int32(0)
        for item in range(items):
            total = total + meta[1 + item]
            self.ends.append(total)
        self.text_len = [meta[1 + items + item] for item in range(items)]
        self.first = self.item_of(self.position * count)
        self.last = self.item_of(self.position * count + count - 1)
        self.low = jnp.int32(0)
        self.high = jnp.int32(0)
        for item in range(items):
            start = self.ends[item] - meta[1 + item]
            self.low = jnp.where(self.first == item, start, self.low)
            self.high = jnp.where(self.last == item, self.ends[item], self.high)

    def item_of(self, place):
        found = jnp.int32(0)
        for end in self.ends:
            found = found + (place >= end).astype(jnp.int32)
        return found

    def items_of_rows(self, base, rows):
        place = base + lax.broadcasted_iota(jnp.int32, (rows, 1), 0)
        found = jnp.zeros((rows, 1), jnp.int32)
        for end in self.ends:
            found = found + (place >= end).astype(jnp.int32)
        return found

    def items_of_chip(self, block):
        start, _ = self.chip(block)
        core = self.position % 2
        return jnp.concatenate(
            [
                self.items_of_rows(start + core * self.count, self.count),
                self.items_of_rows(start + (1 - core) * self.count, self.count),
            ],
            axis=0,
        )

    def chip(self, block):
        hop = (block + 1) // 2
        chip = self.position // 2 + jnp.where(block % 2 == 1, -hop, hop)
        rows = 2 * self.count
        start = chip * rows
        live = (chip >= 0) & (chip < self.shards // 2)
        return start, live & (start < self.high) & (start + rows > self.low)


def lanes(rows):
    return lax.broadcasted_iota(jnp.int32, (rows, 128), 1)


def lse_lanes(lane):
    return (lane >= LSE_LANE) & (lane < DELTA_LANE)


def delta_lanes(lane):
    return (lane >= DELTA_LANE) & (lane < DELTA_LANE + 3 * H)


def head_lanes(lane, base, head):
    start = base + 3 * head
    return (lane >= start) & (lane < start + 3)


def cost(microseconds):
    return pl.CostEstimate(
        flops=int(microseconds * FLOPS_EACH), bytes_accessed=int(microseconds * BYTES_EACH), transcendentals=0
    )


def beside(left, right):
    return jnp.concatenate([left.astype(jnp.bfloat16), right.astype(jnp.bfloat16)], axis=1)


def pieces(values):
    high = values.astype(jnp.bfloat16).astype(jnp.float32)
    rest = values - high
    middle = rest.astype(jnp.bfloat16).astype(jnp.float32)
    return high, middle, rest - middle


def dot(left, right):
    return jnp.dot(left, right, preferred_element_type=jnp.float32)


def stack_heads(target, values, features):
    rows = values.shape[0]
    half = lanes(rows) // 64
    wide = values.astype(jnp.float32)
    for h in range(2):
        target[h * rows : (h + 1) * rows, :] = beside(jnp.where(half == h, wide, 0.0), features[h])


def merge_heads(stacked):
    rows = stacked.shape[0] // 2
    return jnp.where(lanes(rows) < 64, stacked[:rows], stacked[rows:])


def item_bias(frame, item):
    lane = lanes(item.shape[0])
    return jnp.where((lane != item) & (lane < frame.items), far, 0.0)


def text_bias(frame, block, rows):
    slot = lax.broadcasted_iota(jnp.int32, (rows, 1), 0)
    length = jnp.int32(0)
    for item in range(frame.items):
        length = jnp.where(block == item, frame.text_len[item], length)
    lane = lanes(rows)
    dead = (lane != block) | (slot >= length)
    return jnp.where(dead & (lane < frame.items), far, 0.0)


def block_rule(frame, kind, rows):
    if kind == "frames":
        return (
            lambda block: frame.chip(block)[1],
            lambda block: item_bias(frame, frame.items_of_chip(block)),
        )
    return (
        lambda block: (block >= frame.first) & (block <= frame.last),
        lambda block: text_bias(frame, block, rows),
    )


def rows_of(block, rows):
    return pl.ds(pl.multiple_of(block * rows, rows), rows)


def each_active(blocks, active, step):
    @pl.loop(0, blocks)
    def _(block):
        @pl.when(active(block))
        def _():
            step(block)


def fill_bias(blocks, rows, active, bias, target, with_lse):
    @pl.when(pl.program_id(0) == 0)
    def _():
        def step(block):
            mask = bias(block)
            if with_lse:
                mask = jnp.where(lse_lanes(lanes(rows)), -1.0, mask)
            target[rows_of(block, rows), :] = mask.astype(jnp.bfloat16)

        each_active(blocks, active, step)


def hide_kernel(items, shards, meta, mod_ref, x_ref, h_ref):
    count, _ = x_ref.shape
    frame = Frame(meta, items, count, shards)
    normed, _ = layer_norm(x_ref[...].astype(jnp.float32))
    item = frame.items_of_rows(frame.position * count, count)
    shift = jnp.broadcast_to(mod_ref[0], normed.shape)
    scale = jnp.broadcast_to(mod_ref[1], normed.shape)
    for i in range(1, items):
        shift = jnp.where(item == i, mod_ref[6 * i], shift)
        scale = jnp.where(item == i, mod_ref[6 * i + 1], scale)
    h_ref[...] = (normed * (1.0 + scale) + shift).astype(jnp.bfloat16)


def hide(meta, modulation, frames, items, shards):
    whole = pl.BlockSpec(memory_space=pltpu.VMEM)
    return pl.pallas_call(
        partial(hide_kernel, items, shards),
        out_shape=jax.ShapeDtypeStruct(frames.shape, jnp.bfloat16),
        in_specs=[pl.BlockSpec(memory_space=pltpu.SMEM), whole, whole],
        out_specs=whole,
        compiler_params=pltpu.CompilerParams(vmem_limit_bytes=58 * MIB),
        cost_estimate=cost(2),
        name="hide",
    )(meta, modulation, frames)


def project_kernel(items, shards, chips, meta, w_hbm, *refs):
    number = len(chips)
    x_refs = refs[: 2 * number]
    q_ref, kv_ref, x_s, q_s, kv_s, w_ref, in_sem, out_sem, w_sem = refs[-9:]
    weights = pltpu.make_async_copy(w_hbm, w_ref, w_sem)
    count, width = x_refs[0].shape
    rows = 2 * count
    frame = Frame(meta, items, count, shards)

    def live(index):
        return frame.chip(index + chips[0])[1]

    weights.start()
    for index in range(number):

        @pl.when(live(jnp.int32(index)))
        def _(index=index):
            for part in range(2):
                block = 2 * index + part
                pltpu.make_async_copy(
                    x_refs[block], x_s.at[pl.ds(block * count, count), :], in_sem.at[block]
                ).start()

    def writes(index):
        here = rows_of(index, rows)
        there = rows_of(index + chips[0], rows)
        return (
            pltpu.make_async_copy(q_s.at[here, :], q_ref.at[there, :], out_sem.at[2 * index]),
            pltpu.make_async_copy(kv_s.at[here, :], kv_ref.at[there, :], out_sem.at[2 * index + 1]),
        )

    weights.wait()

    @pl.loop(0, number)
    def _(index):
        @pl.when(live(index))
        def _():
            for part in range(2):
                block = 2 * index + part
                pltpu.make_async_copy(x_refs[0], x_s.at[rows_of(block, count), :], in_sem.at[block]).wait()
            both = rows_of(index, rows)
            hidden = x_s[both, :]
            q = dot(hidden, w_ref[:, :width]).astype(jnp.bfloat16)
            q_s[both, :] = (q.astype(jnp.float32) * 0.125).astype(jnp.bfloat16)
            kv_s[both, :width] = dot(hidden, w_ref[:, width : 2 * width]).astype(jnp.bfloat16)
            kv_s[both, width:] = dot(hidden, w_ref[:, 2 * width :]).astype(jnp.bfloat16)
            for write in writes(index):
                write.start()

    @pl.loop(0, number)
    def _(index):
        @pl.when(live(index))
        def _():
            for write in writes(index):
                write.wait()


def project(meta, weight, x_blocks, chips, total, earlier, items, shards, name):
    count, width = x_blocks[0].shape
    part = len(x_blocks) * count
    anywhere = pl.BlockSpec(memory_space=pl.ANY)
    before = 2 + len(x_blocks)
    return pl.pallas_call(
        partial(project_kernel, items, shards, chips),
        out_shape=(
            jax.ShapeDtypeStruct((total, width), jnp.bfloat16),
            jax.ShapeDtypeStruct((total, 2 * width), jnp.bfloat16),
        ),
        in_specs=[pl.BlockSpec(memory_space=pltpu.SMEM), pl.BlockSpec(memory_space=pltpu.HBM)]
        + [anywhere] * (len(x_blocks) + len(earlier)),
        out_specs=(anywhere, anywhere),
        input_output_aliases={before: 0, before + 1: 1} if earlier else {},
        scratch_shapes=[
            pltpu.VMEM((part, width), jnp.bfloat16),
            pltpu.VMEM((part, width), jnp.bfloat16),
            pltpu.VMEM((part, 2 * width), jnp.bfloat16),
            pltpu.VMEM(weight.shape, jnp.bfloat16),
            pltpu.SemaphoreType.DMA((len(x_blocks),)),
            pltpu.SemaphoreType.DMA((len(x_blocks),)),
            pltpu.SemaphoreType.DMA,
        ],
        compiler_params=pltpu.CompilerParams(vmem_limit_bytes=28 * MIB),
        cost_estimate=cost(len(x_blocks) * 1.2),
        name=name,
    )(meta, weight, *x_blocks, *earlier)


def heads_of(ref, here, pair):
    return ref[here, pair * 128 : (pair + 1) * 128]


def spread(count, group, base):
    return pl.BlockSpec((count, group * 128), lambda p: (0, p + base // group))


ALL = slice(None)


def attend_kernel(items, shards, kind, blocks, group, meta, q_ref, k_ref, v_ref, o_ref, low_ref, f_ref, qa, bias_ref, s, m, l, acc):
    count = q_ref.shape[0]
    rows = k_ref.shape[0] // blocks
    frame = Frame(meta, items, count, shards)
    active, bias = block_rule(frame, kind, rows)
    step = pl.program_id(0)
    lane = lanes(count)
    own = frame.items_of_rows(frame.position * count, count)
    own_item = (lane == own).astype(jnp.float32)
    fill_bias(blocks, rows, active, bias, bias_ref, False)
    for g in range(group):
        stack_heads(qa.at[g], heads_of(q_ref, ALL, g), [own_item, own_item])
        m[g] = jnp.full((2 * count, 128), far, jnp.float32)
        l[g] = jnp.zeros((2 * count, 128), jnp.float32)
        acc[g] = jnp.zeros((2 * count, 128), jnp.float32)

    def score(block):
        here = rows_of(block, rows)
        for g in range(group):
            scores = times_transposed(qa[g], jnp.concatenate([heads_of(k_ref, here, g), bias_ref[here, :]], axis=1))
            s[g, block] = scores
            high = m[g]
            for c in range(rows // 128):
                high = jnp.maximum(high, scores[:, c * 128 : (c + 1) * 128])
            m[g] = high

    each_active(blocks, active, score)
    tops = []
    for g in range(group):
        tops.append(jnp.max(m[g], axis=1, keepdims=True))
        m[g] = jnp.broadcast_to(tops[g], (2 * count, 128))

    def weigh(block):
        here = rows_of(block, rows)
        for g in range(group):
            high = m[g]
            total = l[g]
            parts = []
            for c in range(rows // 128):
                part = jnp.exp(s[g, block, :, c * 128 : (c + 1) * 128] - high)
                total = total + part
                parts.append(part.astype(jnp.bfloat16))
            l[g] = total
            acc[g] = acc[g] + dot(jnp.concatenate(parts, axis=1), heads_of(v_ref, here, g))

    each_active(blocks, active, weigh)
    features = jnp.where(step == 0, own_item, f_ref[...].astype(jnp.float32))
    for g in range(group):
        total = jnp.sum(l[g], axis=1, keepdims=True)
        result = merge_heads(acc[g] / total)
        lse = tops[g] + jnp.log(total)
        for h in range(2):
            start = LSE_LANE + 3 * (2 * (step * group + g) + h)
            for number, piece in enumerate(pieces(lse[h * count : (h + 1) * count])):
                features = jnp.where(lane == start + number, piece, features)
        o_ref[:, g * 128 : (g + 1) * 128] = result
        low_ref[:, g * 128 : (g + 1) * 128] = result.astype(jnp.bfloat16)
    f_ref[...] = features.astype(jnp.bfloat16)


def attend(meta, count, queries, kv, kind, blocks, items, shards, name, group=3):
    width = queries.shape[1]
    pairs = width // 128
    total = kv.shape[0]
    rows = total // blocks
    tile = spread(count, group, 0)
    return pl.pallas_call(
        partial(attend_kernel, items, shards, kind, blocks, group),
        grid=(pairs // group,),
        out_shape=(
            jax.ShapeDtypeStruct((count, width), jnp.float32),
            jax.ShapeDtypeStruct((count, width), jnp.bfloat16),
            jax.ShapeDtypeStruct((count, 128), jnp.bfloat16),
        ),
        in_specs=[
            pl.BlockSpec(memory_space=pltpu.SMEM),
            tile,
            spread(total, group, 0),
            spread(total, group, pairs),
        ],
        out_specs=(tile, tile, pl.BlockSpec((count, 128), lambda p: (0, 0))),
        scratch_shapes=[
            pltpu.VMEM((group, 2 * count, 256), jnp.bfloat16),
            pltpu.VMEM((total, 128), jnp.bfloat16),
            pltpu.VMEM((group, blocks, 2 * count, rows), jnp.float32),
            pltpu.VMEM((group, 2 * count, 128), jnp.float32),
            pltpu.VMEM((group, 2 * count, 128), jnp.float32),
            pltpu.VMEM((group, 2 * count, 128), jnp.float32),
        ],
        compiler_params=pltpu.CompilerParams(vmem_limit_bytes=34 * MIB),
        cost_estimate=cost(14 if kind == "frames" else 5),
        name=name,
    )(meta, queries, kv, kv)


def query_side(pair, features, q, do, qa, da):
    lane = lanes(q.shape[0])
    heads = [2 * pair, 2 * pair + 1]
    stack_heads(qa, q, [jnp.where((lane < LSE_LANE) | head_lanes(lane, LSE_LANE, head), features, 0.0) for head in heads])
    stack_heads(da, do, [jnp.where(head_lanes(lane, DELTA_LANE, head), features, 0.0) for head in heads])


def query_step(qa, da, keys, values, bias):
    minus = jnp.where(delta_lanes(lanes(keys.shape[0])), -1.0, 0.0)
    probs = jnp.exp(times_transposed(qa[...], jnp.concatenate([keys, bias], axis=1)))
    slope = times_transposed(da[...], beside(values, minus))
    return dot((probs * slope).astype(jnp.bfloat16), keys)


def key_side(pair, k, v, mask, ka, va):
    lane = lanes(k.shape[0])
    heads = [2 * pair, 2 * pair + 1]
    stack_heads(ka, k, [jnp.where(head_lanes(lane, LSE_LANE, head), -1.0, mask) for head in heads])
    stack_heads(va, v, [jnp.where(head_lanes(lane, DELTA_LANE, head), -1.0, 0.0) for head in heads])


def key_step(ka, va, q, do, features):
    probs = jnp.exp(times_transposed(ka[...], jnp.concatenate([q, features], axis=1)))
    slope = times_transposed(va[...], jnp.concatenate([do, features], axis=1))
    return dot((probs * slope).astype(jnp.bfloat16), q), dot(probs.astype(jnp.bfloat16), do)


def query_grad_kernel(items, shards, blocks, group, meta, q_ref, do_ref, f_ref, k_ref, v_ref, dq_ref, qa, da, bias_ref, acc):
    count = q_ref.shape[0]
    rows = k_ref.shape[0] // blocks
    frame = Frame(meta, items, count, shards)
    active, bias = block_rule(frame, "frames", rows)
    fill_bias(blocks, rows, active, bias, bias_ref, True)
    features = f_ref[...].astype(jnp.float32)
    for g in range(group):
        pair = pl.program_id(0) * group + g
        query_side(pair, features, heads_of(q_ref, ALL, g), heads_of(do_ref, ALL, g), qa.at[g], da.at[g])
        acc[g] = jnp.zeros((2 * count, 128), jnp.float32)

    def step(block):
        here = rows_of(block, rows)
        for g in range(group):
            acc[g] = acc[g] + query_step(
                qa.at[g], da.at[g], heads_of(k_ref, here, g), heads_of(v_ref, here, g), bias_ref[here, :]
            )

    each_active(blocks, active, step)
    for g in range(group):
        dq_ref[:, g * 128 : (g + 1) * 128] = (merge_heads(acc[g]) * 0.125).astype(jnp.bfloat16)


def query_grad(meta, count, queries, grad_out, kv, blocks, items, shards, name, group=3):
    width = queries.shape[1]
    pairs = width // 128
    total = kv.shape[0]
    tile = spread(count, group, 0)
    return pl.pallas_call(
        partial(query_grad_kernel, items, shards, blocks, group),
        grid=(pairs // group,),
        out_shape=jax.ShapeDtypeStruct((count, width), jnp.bfloat16),
        in_specs=[
            pl.BlockSpec(memory_space=pltpu.SMEM),
            tile,
            tile,
            pl.BlockSpec((count, 128), lambda p: (0, pairs)),
            spread(total, group, 0),
            spread(total, group, pairs),
        ],
        out_specs=tile,
        scratch_shapes=[
            pltpu.VMEM((group, 2 * count, 256), jnp.bfloat16),
            pltpu.VMEM((group, 2 * count, 256), jnp.bfloat16),
            pltpu.VMEM((total, 128), jnp.bfloat16),
            pltpu.VMEM((group, 2 * count, 128), jnp.float32),
        ],
        compiler_params=pltpu.CompilerParams(vmem_limit_bytes=58 * MIB),
        cost_estimate=cost(14),
        name=name,
    )(meta, queries, grad_out, grad_out, kv, kv)


def frame_key_grad_kernel(items, shards, blocks, group, meta, q_ref, k_ref, v_ref, dq_ref, all_ref, out_ref, ka, va, dka, dva, do_s, sem):
    count, width = dq_ref.shape[0], do_s.shape[1] - 128
    rows = q_ref.shape[0] // blocks
    frame = Frame(meta, items, count, shards)

    def arrivals(act):
        @pl.when(pl.program_id(0) == 0)
        def _():
            for block in range(2 * blocks):
                start, live = frame.chip(jnp.int32(block // 2))
                first = start + (frame.position + block) % 2 * count

                @pl.when(live)
                def _(block=block, first=first):
                    act(
                        pltpu.make_async_copy(
                            all_ref.at[pl.ds(pl.multiple_of(first, count), count), :],
                            do_s.at[pl.ds(block * count, count), :],
                            sem.at[block],
                        )
                    )

    arrivals(lambda copy: copy.start())
    mask = item_bias(frame, frame.items_of_rows(frame.position * count, count))
    for g in range(group):
        pair = pl.program_id(0) * group + g
        key_side(pair, heads_of(k_ref, ALL, g), heads_of(v_ref, ALL, g), mask, ka.at[g], va.at[g])
        dka[g] = jnp.zeros((2 * count, 128), jnp.float32)
        dva[g] = jnp.zeros((2 * count, 128), jnp.float32)
    arrivals(lambda copy: copy.wait())

    def step(block):
        here = rows_of(block, rows)
        for g in range(group):
            column = pl.multiple_of((pl.program_id(0) * group + g) * 128, 128)
            dk, dv = key_step(
                ka.at[g], va.at[g], heads_of(q_ref, here, g), do_s[here, pl.ds(column, 128)], do_s[here, width:]
            )
            dka[g] = dka[g] + dk
            dva[g] = dva[g] + dv

    each_active(blocks, lambda block: frame.chip(block)[1], step)
    for g in range(group):
        out_ref[1, :, g * 128 : (g + 1) * 128] = merge_heads(dka[g]).astype(jnp.bfloat16)
        out_ref[2, :, g * 128 : (g + 1) * 128] = merge_heads(dva[g]).astype(jnp.bfloat16)
    out_ref[0] = dq_ref[...]


def frame_key_grad(meta, q_window, do_all, kv, grad_queries, count, blocks, items, shards, name, group=3):
    total, width = q_window.shape
    pairs = width // 128
    tile = spread(count, group, 0)
    wide = spread(total, group, 0)
    return pl.pallas_call(
        partial(frame_key_grad_kernel, items, shards, blocks, group),
        grid=(pairs // group,),
        out_shape=jax.ShapeDtypeStruct((3, count, width), jnp.bfloat16),
        in_specs=[
            pl.BlockSpec(memory_space=pltpu.SMEM),
            wide,
            tile,
            spread(count, group, pairs),
            tile,
        ]
        + [pl.BlockSpec(memory_space=pl.ANY)],
        out_specs=pl.BlockSpec((3, count, group * 128), lambda p: (0, 0, p)),
        scratch_shapes=[pltpu.VMEM((group, 2 * count, 256), jnp.bfloat16)] * 2
        + [pltpu.VMEM((group, 2 * count, 128), jnp.float32)] * 2
        + [pltpu.VMEM((total, width + 128), jnp.bfloat16), pltpu.SemaphoreType.DMA((2 * blocks,))],
        compiler_params=pltpu.CompilerParams(vmem_limit_bytes=58 * MIB),
        cost_estimate=cost(18),
        name=name,
    )(meta, q_window, kv, kv, grad_queries, do_all)


def text_grad_kernel(items, shards, group, meta, q_ref, do_ref, f_ref, k_ref, v_ref, dq_ref, dkv_ref, qa, da, ka, va, acc):
    count = q_ref.shape[0]
    rows = k_ref.shape[0] // items
    share = rows // shards
    frame = Frame(meta, items, count, shards)
    features = f_ref[...].astype(jnp.float32)
    pairs = [pl.program_id(0) * group + g for g in range(group)]
    for g in range(group):
        query_side(pairs[g], features, heads_of(q_ref, ALL, g), heads_of(do_ref, ALL, g), qa.at[g], da.at[g])
        acc[g] = jnp.zeros((2 * count, 128), jnp.float32)

    @pl.loop(0, items)
    def _(item):
        here = rows_of(item, rows)
        live = (item >= frame.first) & (item <= frame.last)
        target = rows_of(item, share)

        @pl.when(live)
        def _():
            mask = text_bias(frame, item, rows)
            bias = jnp.where(lse_lanes(lanes(rows)), -1.0, mask).astype(jnp.bfloat16)
            for g in range(group):
                keys, values = heads_of(k_ref, here, g), heads_of(v_ref, here, g)
                acc[g] = acc[g] + query_step(qa.at[g], da.at[g], keys, values, bias)
                key_side(pairs[g], keys, values, mask, ka.at[g], va.at[g])
                grads = key_step(ka.at[g], va.at[g], heads_of(q_ref, ALL, g), heads_of(do_ref, ALL, g), f_ref[...])
                for which, grad in enumerate(grads):
                    merged = merge_heads(grad).astype(jnp.bfloat16)
                    for owner in range(shards):
                        dkv_ref[owner, which, target, g * 128 : (g + 1) * 128] = merged[
                            owner * share : (owner + 1) * share
                        ]

        @pl.when(jnp.logical_not(live))
        def _():
            dkv_ref[:, :, target, :] = jnp.zeros((shards, 2, share, group * 128), jnp.bfloat16)

    for g in range(group):
        dq_ref[:, g * 128 : (g + 1) * 128] = (merge_heads(acc[g]) * 0.125).astype(jnp.bfloat16)


def text_grad(meta, queries, grad_out, features, kv, items, shards, name, group=3):
    count, width = queries.shape
    pairs = width // 128
    total = kv.shape[0]
    tile = spread(count, group, 0)
    rows = total // items
    return pl.pallas_call(
        partial(text_grad_kernel, items, shards, group),
        grid=(pairs // group,),
        out_shape=(
            jax.ShapeDtypeStruct((count, width), jnp.bfloat16),
            jax.ShapeDtypeStruct((shards, 2, total // shards, width), jnp.bfloat16),
        ),
        in_specs=[
            pl.BlockSpec(memory_space=pltpu.SMEM),
            tile,
            tile,
            pl.BlockSpec((count, 128), lambda p: (0, 0)),
            spread(total, group, 0),
            spread(total, group, pairs),
        ],
        out_specs=(tile, pl.BlockSpec((shards, 2, total // shards, group * 128), lambda p: (0, 0, 0, p))),
        scratch_shapes=[pltpu.VMEM((group, 2 * count, 256), jnp.bfloat16)] * 2
        + [pltpu.VMEM((group, 2 * rows, 256), jnp.bfloat16)] * 2
        + [pltpu.VMEM((group, 2 * count, 128), jnp.float32)],
        compiler_params=pltpu.CompilerParams(vmem_limit_bytes=18 * MIB),
        cost_estimate=cost(8),
        name=name,
    )(meta, queries, grad_out, features, kv, kv)


def mlp_kernel(h_ref, d_ref, up_ref, down_ref, act_ref, m_ref, dh_ref):
    step = pl.program_id(0)
    last = pl.num_programs(0) - 1

    @pl.when(step < last)
    def _():
        u = dot(h_ref[...], up_ref[...])
        slope = times_transposed(d_ref[...], down_ref[...])
        inner = 0.7978845608028654 * (u + 0.044715 * (u * u * u))
        t = jnp.tanh(inner)
        g = (0.5 * u * (1.0 + t)).astype(jnp.bfloat16)
        bend = 0.7978845608028654 * (1.0 + 0.134145 * (u * u))
        du = (slope * (0.5 * (1.0 + t) + 0.5 * u * (1.0 - t * t) * bend)).astype(jnp.bfloat16)
        act_ref[0, 0] = g
        act_ref[0, 1] = du
        m = dot(g, down_ref[...])
        dh = times_transposed(du, up_ref[...])

        @pl.when(step == 0)
        def _():
            m_ref[...] = m
            dh_ref[...] = dh

        @pl.when(step > 0)
        def _():
            m_ref[...] = m_ref[...] + m
            dh_ref[...] = dh_ref[...] + dh

    @pl.when(step == last)
    def _():
        act_ref[0, 0] = h_ref[...]
        act_ref[0, 1] = d_ref[...]


def mlp(hidden, grad, w_up, w_down):
    count, width = hidden.shape
    chunks = w_up.shape[1] // width
    whole = pl.BlockSpec((count, width), lambda c: (0, 0))
    held = lambda c: jnp.minimum(c, chunks - 1)
    return pl.pallas_call(
        mlp_kernel,
        grid=(chunks + 1,),
        out_shape=(
            jax.ShapeDtypeStruct((chunks + 1, 2, count, width), jnp.bfloat16),
            jax.ShapeDtypeStruct((count, width), jnp.float32),
            jax.ShapeDtypeStruct((count, width), jnp.float32),
        ),
        in_specs=[
            whole,
            whole,
            pl.BlockSpec((width, width), lambda c: (0, held(c))),
            pl.BlockSpec((width, width), lambda c: (held(c), 0)),
        ],
        out_specs=(pl.BlockSpec((1, 2, count, width), lambda c: (c, 0, 0, 0)), whole, whole),
        compiler_params=pltpu.CompilerParams(vmem_limit_bytes=20 * MIB),
        cost_estimate=cost(9),
        name="mlp",
    )(hidden, grad, w_up, w_down)


UNIT = 192
X_BIT, Y_BIT = 0, 1


def rows_picked(x, core):
    row = lax.broadcasted_iota(jnp.int32, (384, 768), 0)
    column = lax.broadcasted_iota(jnp.int32, (384, 768), 1)
    chip = (row >= 96).astype(jnp.int32) + (row >= 192).astype(jnp.int32) + (row >= 288).astype(jnp.int32)
    pick = (column == row + 96 * (chip + core)).astype(jnp.bfloat16)
    return times_transposed(pick, x).astype(jnp.bfloat16)


def one_above_other(upper, lower):
    return jnp.concatenate([upper, lower], axis=0)


def finish_kernel(items, shards, packed, meta, mod_ref, w_ref, d_ref, x_ref, dx_ref, a_ref, dh_ref, n_ref, dy_ref, m_ref, out_ref, sum_ref):
    count, width = x_ref.shape
    frame = Frame(meta, items, count, shards)
    item = frame.items_of_rows(frame.position * count, count)
    grad = sum(times_transposed(d_ref[i], w_ref[:, i * width : (i + 1) * width]) for i in range(3))
    normed, inverse = layer_norm(x_ref[...].astype(jnp.float32))
    scale = jnp.zeros((count, width), jnp.float32)
    for i in range(items):
        scale = jnp.where(item == i, mod_ref[6 * i + 1], scale)
    dx = dx_ref[...]
    out_ref[...] = dx + norm_back(grad * (1.0 + scale), normed, inverse)
    dh = dh_ref[...]
    terms = (
        grad,
        grad * normed,
        dx * a_ref[...],
        dh,
        dh * n_ref[...],
        dy_ref[...].astype(jnp.float32) * m_ref[...],
    )
    sums = []
    for number, term in enumerate(terms):
        rows = [jnp.sum(jnp.where(item == i, term, 0.0), axis=0, keepdims=True) for i in range(items)]
        rows += [jnp.zeros((8 - items, width), jnp.float32)]
        sums.append(jnp.concatenate(rows, axis=0))
        if not packed:
            sum_ref[number] = sums[number]
    if packed:
        values = jnp.concatenate(sums, axis=0)
        left = lax.broadcasted_iota(jnp.int32, (24, 384), 1) < UNIT
        for pair in range(2):
            part = third(values, pair)
            rolled = pltpu.roll(part, UNIT, 1)
            each = (jnp.where(left, part[:24], rolled[24:]), jnp.where(left, rolled[:24], part[24:]))
            for half in range(2):
                relative = (2 * pair + half) ^ (frame.position // 2)
                sum_ref[relative % 2, relative // 2, :24, :] = each[half]
                sum_ref[relative % 2, relative // 2, 24:, :] = jnp.zeros((8, 384), jnp.float32)


def finish(meta, modulation, weight, grads, frames, *arrays_items_shards):
    *arrays, items, shards, packed = arrays_items_shards
    count, width = frames.shape
    whole = pl.BlockSpec(memory_space=pltpu.VMEM)
    return pl.pallas_call(
        partial(finish_kernel, items, shards, packed),
        out_shape=(
            jax.ShapeDtypeStruct((count, width), jnp.float32),
            jax.ShapeDtypeStruct((2, 2, 32, 384) if packed else (6, 8, width), jnp.float32),
        ),
        in_specs=[pl.BlockSpec(memory_space=pltpu.SMEM)] + [whole] * (4 + len(arrays)),
        out_specs=(whole, whole),
        compiler_params=pltpu.CompilerParams(vmem_limit_bytes=58 * MIB),
        cost_estimate=cost(5),
        name="finish",
    )(meta, modulation, weight, grads, frames, *arrays)


def attend_back_kernel(items, shards, meta, mod_ref, g_ref, cq_ref, o_ref, dx_ref, x_ref, exact_ref, f_ref, *refs):
    others, (dx_out, bundle_out, do_out) = refs[:-3], refs[-3:]
    count, width = x_ref.shape
    frame = Frame(meta, items, count, shards)
    item = frame.items_of_rows(frame.position * count, count)
    normed, inverse = layer_norm(x_ref[...])
    dx = dx_ref[...] + norm_back(times_transposed(g_ref[...], cq_ref[...]), normed, inverse)
    dx_out[...] = dx
    gate = jnp.broadcast_to(mod_ref[2], dx.shape)
    for i in range(1, items):
        gate = jnp.where(item == i, mod_ref[6 * i + 2], gate)
    low = (dx * gate).astype(jnp.bfloat16)
    for number, each in enumerate((*others[:3], g_ref, others[3])):
        bundle_out[number] = each[...]
    bundle_out[5] = low
    grad = times_transposed(low, o_ref[...]).astype(jnp.bfloat16)
    do_out[:, :width] = grad
    row = lax.broadcasted_iota(jnp.int32, (width, 128), 0)
    lane = lax.broadcasted_iota(jnp.int32, (width, 128), 1)
    pick = jnp.zeros((width, 128), jnp.float32)
    for head in range(H):
        mine = (row >= head * (width // H)) & (row < (head + 1) * (width // H))
        pick = jnp.where(mine & head_lanes(lane, DELTA_LANE, head), 1.0, pick)
    pick = pick.astype(jnp.bfloat16)
    products = grad.astype(jnp.float32) * exact_ref[...]
    delta = sum(dot(piece.astype(jnp.bfloat16), pick) for piece in pieces(products))
    place = lanes(1)
    features = f_ref[...].astype(jnp.float32)
    for number, piece in enumerate(pieces(delta)):
        here = jnp.zeros((1, 128), jnp.bool_)
        for head in range(H):
            here = here | (place == DELTA_LANE + 3 * head + number)
        features = jnp.where(here, piece, features)
    do_out[:, width:] = features.astype(jnp.bfloat16)


def attend_back(meta, modulation, grads, w_cq, w_o, grad_cross, after_attn, attn_exact, features, others, items, shards):
    count, width = grads.shape
    whole = pl.BlockSpec(memory_space=pltpu.VMEM)
    return pl.pallas_call(
        partial(attend_back_kernel, items, shards),
        out_shape=(
            jax.ShapeDtypeStruct((count, width), jnp.float32),
            jax.ShapeDtypeStruct((6, count, width), jnp.bfloat16),
            jax.ShapeDtypeStruct((count, width + 128), jnp.bfloat16),
        ),
        in_specs=[pl.BlockSpec(memory_space=pltpu.SMEM)] + [whole] * (8 + len(others)),
        out_specs=(whole, whole, whole),
        compiler_params=pltpu.CompilerParams(vmem_limit_bytes=20 * MIB),
        cost_estimate=cost(3),
        name="attend_back",
    )(meta, modulation, grads, w_cq, w_o, grad_cross, after_attn, attn_exact, features, *others)


class Packer:
    def __init__(self, meta, items, outputs):
        self.core, self.chip = meta[0] % 2, meta[0] // 2
        self.mine = meta[1 + 2 * items]
        self.outputs = outputs

    def steps(self, owner_chip):
        relative = owner_chip ^ self.chip
        return relative % 2, relative // 2

    def store(self, name, owner, owner_chip, row, values):
        scratch, first = self.outputs[name]
        relative = owner ^ self.mine
        where = ((relative >> first) % 2, (relative >> (1 - first)) % 2, *self.steps(owner_chip))
        scratch[where + (slice(row, row + values.shape[0]),)] = values.astype(jnp.bfloat16)

    def store_split(self, name, pair, row, values, chips):
        rolled = pltpu.roll(values, UNIT, 1)
        each = values.shape[0] // len(chips)
        left = lax.broadcasted_iota(jnp.int32, (each // 2, 384), 1) < UNIT
        for number, owner_chip in enumerate(chips):
            upper = slice(number * each, number * each + each // 2)
            lower = slice(number * each + each // 2, (number + 1) * each)
            self.store(name, 2 * pair, owner_chip, row, jnp.where(left, values[upper], rolled[lower]))
            self.store(name, 2 * pair + 1, owner_chip, row, jnp.where(left, rolled[upper], values[lower]))


def core_columns(core, number, each):
    return pl.ds(pl.multiple_of(number * 2 * each + core * each, 128), each)


def third(values, number):
    return values[:, number * 384 : (number + 1) * 384]


def pack_mlp_kernel(items, meta, own, sib, down_s, up_s):
    packer = Packer(meta, items, {"down": (down_s, Y_BIT), "up": (up_s, X_BIT)})
    both = lambda chunk, which: one_above_other(own[chunk, which], sib[chunk, which])
    grad = both(4, 1)
    for owner_chip in range(4):
        here = core_columns(packer.core, 0, 384)
        left = one_above_other(own[owner_chip, 0, :, here], sib[owner_chip, 0, :, here])
        values = contract_rows(left, grad)
        for pair in range(2):
            packer.store_split("down", pair, 0, third(values, pair), [owner_chip])
    left = rows_picked(both(4, 0), packer.core)
    for owner in range(4):
        values = dot(left, both(owner, 1))
        for owner_chip in range(4):
            for half in range(2):
                packer.store(
                    "up", owner, owner_chip, half * 96, third(values, half)[owner_chip * 96 : (owner_chip + 1) * 96]
                )


def pack_middle_kernel(items, meta, own, sib, text_own, text_sib, text, square_s, text_s):
    packer = Packer(meta, items, {"square": (square_s, Y_BIT), "text": (text_s, X_BIT)})
    both = lambda which: one_above_other(own[which], sib[which])
    for number in range(3):
        values = dot(rows_picked(both(2 * number), packer.core), both(2 * number + 1))
        for pair in range(2):
            packer.store_split("square", pair, number * 48, third(values, pair), range(4))
    share = text_own.shape[2] // items

    def chip_sum(which, item, owner):
        here = slice(item * share, (item + 1) * share)
        total = text_own[owner, which, here, :].astype(jnp.float32) + text_sib[owner, which, here, :].astype(jnp.float32)
        return total.astype(jnp.bfloat16)

    sums = [
        jnp.concatenate(
            [chip_sum(which, item, owner) for item in range(items) for owner in range(text_own.shape[0])], axis=0
        )
        for which in range(2)
    ]
    left = jnp.concatenate([text[:, core_columns(packer.core, chip, 128)] for chip in range(4)], axis=1)
    for which in range(2):
        values = contract_rows(left, sums[which])
        for owner_chip in range(4):
            for half in range(2):
                packer.store(
                    "text", 2 * which + half, owner_chip, 0, third(values, half)[owner_chip * 128 : (owner_chip + 1) * 128]
                )


def pack_qkv_kernel(items, meta, h_own, h_sib, own, sib, plain_s, split_s):
    packer = Packer(meta, items, {"plain": (plain_s, X_BIT), "split": (split_s, Y_BIT)})
    left = rows_picked(one_above_other(h_own[...], h_sib[...]), packer.core)
    values = []
    for number in range(3):
        product = dot(left, one_above_other(own[number], sib[number]))
        values += [third(product, 0), third(product, 1)]
    for owner, column in enumerate((0, 2, 3, 5)):
        for owner_chip in range(4):
            packer.store("plain", owner, owner_chip, 0, values[column][owner_chip * 96 : (owner_chip + 1) * 96])
    for pair, column in enumerate((1, 4)):
        packer.store_split("split", pair, 0, values[column], range(4))


def packing(kernel, items, inputs, groups, *refs):
    ins, outs, scratch, sem = refs[:inputs], refs[inputs:-groups - 1], refs[-groups - 1 : -1], refs[-1]
    kernel(items, *ins, *scratch)
    copies = [pltpu.make_async_copy(scratch[i // 2].at[1 - i % 2], outs[i], sem.at[i]) for i in range(2 * groups)]
    for copy in copies:
        copy.start()
    for copy in copies:
        copy.wait()


def pack(kernel, meta, operands, shapes, items, name):
    shapes = [(2, 2, 2, each, 384) if isinstance(each, int) else each for each in shapes]
    whole = pl.BlockSpec(memory_space=pltpu.VMEM)
    return pl.pallas_call(
        partial(packing, kernel, items, 1 + len(operands), len(shapes)),
        out_shape=tuple(jax.ShapeDtypeStruct(shape, jnp.bfloat16) for shape in shapes for _ in range(2)),
        in_specs=[pl.BlockSpec(memory_space=pltpu.SMEM)] + [whole] * len(operands),
        out_specs=tuple([pl.BlockSpec(memory_space=pl.ANY)] * (2 * len(shapes))),
        scratch_shapes=[pltpu.VMEM((2, *shape), jnp.bfloat16) for shape in shapes]
        + [pltpu.SemaphoreType.DMA((2 * len(shapes),))],
        compiler_params=pltpu.CompilerParams(vmem_limit_bytes=58 * MIB),
        cost_estimate=cost(8 if name != "pack_qkv" else 3),
        name=name,
    )(meta, *operands)


def trade(values, axis, bit):
    size = lax.axis_size(axis)
    return lax.ppermute(values, axis, [(i, i ^ (1 << bit)) for i in range(size)])


def added(keep, got):
    return [(keep[i].astype(jnp.float32) + got[i].astype(jnp.float32)).astype(jnp.bfloat16) for i in range(2)]


def halve(keep, send, axis, bit, after=()):
    got = trade(send, axis, bit)
    if after:
        [keep] = hold((keep,), *after)
    return added(keep, got)


def last_half(keep, send, after=()):
    got = trade(send, "seq", 2)
    if after:
        [keep] = hold((keep,), *after)
    return keep.astype(jnp.float32) + got.astype(jnp.float32)


def joined(upper, lower):
    return [jnp.concatenate([upper[i], lower[i]], axis=-2) for i in (1, 0)]


def unpack_kernel(items, place, last_keep, last_got, middle_keep, middle_got, qkv_ref, o_ref, cq_ref, ckv_ref, co_ref, mod_ref, mlp_ref):
    def whole(keep, got, start, rows):
        here = slice(start, start + rows)
        return keep[here, :].astype(jnp.float32) + got[here, :].astype(jnp.float32)

    def parts(values):
        return one_above_other(values, pltpu.roll(values, UNIT, 1))

    plain = whole(last_keep, last_got, 0, 96)
    split = parts(whole(last_keep, last_got, 96, 48))
    empty = jnp.zeros((96, 384), jnp.float32)
    even = jnp.concatenate([plain, split], axis=1)
    shifted = pltpu.roll(jnp.concatenate([plain, empty], axis=1), UNIT, 1)
    lane = lax.broadcasted_iota(jnp.int32, (96, 768), 1)
    odd = jnp.where(lane < UNIT, jnp.concatenate([split, empty], axis=1), shifted)

    @pl.when(place[0] == 0)
    def _():
        qkv_ref[...] = even[:, :576]

    @pl.when(place[0] == 1)
    def _():
        qkv_ref[...] = odd[:, :576]

    for number, ref in enumerate((co_ref, cq_ref, o_ref)):
        ref[...] = parts(whole(middle_keep, middle_got, number * 48, 48))[:, :UNIT]
    ckv_ref[...] = whole(middle_keep, middle_got, 144, 128)
    terms = parts(whole(last_keep, last_got, 144, 32)[:24])
    terms = jnp.where(place[1] == 0, terms, pltpu.roll(terms, 384 - UNIT // 2, 1))[:, : UNIT // 2]
    for item in range(items):
        for number in range(3):
            mod_ref[item * 3 + number] = terms[number * 8 + item : number * 8 + item + 1]
            mlp_ref[item * 3 + number] = terms[24 + number * 8 + item : 24 + number * 8 + item + 1]


def unpack(place, last, middle, items):
    whole = pl.BlockSpec(memory_space=pltpu.VMEM)
    shapes = [(96, 576), (96, UNIT), (96, UNIT), (128, 384), (96, UNIT)] + [(items * 3, 1, UNIT // 2)] * 2
    return pl.pallas_call(
        partial(unpack_kernel, items),
        out_shape=tuple(jax.ShapeDtypeStruct(shape, jnp.float32) for shape in shapes),
        in_specs=[pl.BlockSpec(memory_space=pltpu.SMEM)] + [whole] * 4,
        out_specs=tuple([whole] * len(shapes)),
        cost_estimate=cost(2),
        name="unpack",
    )(place, *last, *middle)


def unsplit(rows):
    return jnp.concatenate([rows[:, :UNIT], rows[:, UNIT:]], axis=0)


def with_deltas(features, grad_out, attn_exact):
    width = attn_exact.shape[1]
    lane = jnp.arange(128)[None, :]
    head = (jnp.arange(width) // (width // H))[:, None]
    pick = ((lane >= DELTA_LANE) & ((lane - DELTA_LANE) // 3 == head)).astype(jnp.float32)
    delta = jnp.dot(
        grad_out.astype(jnp.float32) * attn_exact,
        pick,
        precision=lax.Precision.HIGHEST,
        preferred_element_type=jnp.float32,
    )
    high = lax.reduce_precision(delta, 8, 7)
    middle = lax.reduce_precision(delta - high, 8, 7)
    which = (lane - DELTA_LANE) % 3
    piece = jnp.where(which == 0, high, jnp.where(which == 1, middle, delta - high - middle))
    inside = (lane >= DELTA_LANE) & (lane < DELTA_LANE + 3 * H)
    return jnp.where(inside, piece.astype(jnp.bfloat16), features)


def hop(below, above, shards):
    up = [(i, i + 2) for i in range(shards - 2)]
    return lax.ppermute(below, "seq", up), lax.ppermute(above, "seq", [(j, i) for i, j in up])


def hold(values, *first):
    held = lax.optimization_barrier((*values, *first))
    return held[: len(values)]


def body(
    frames,
    cotangent,
    modulation,
    lengths,
    text,
    text_len,
    w_qkv,
    w_o,
    w_cq,
    w_ckv,
    w_co,
    w_up,
    w_down,
):
    local = frames[0]
    count, width = local.shape
    items = lengths.shape[1]
    text_rows, text_width = text.shape[2:]
    shards = lax.axis_size("seq")
    position = lax.axis_index("seq")
    reach = min(-(-(LONGEST - 1) // (2 * count)), shards // 2 - 1)
    chips = 1 + 2 * reach
    meta = jnp.concatenate(
        [position[None].astype(jnp.int32), lengths[0], text_len[0], lax.axis_index("batch")[None].astype(jnp.int32)]
    )
    item_range = jnp.arange(items, dtype=jnp.int32)
    ends = jnp.sum(jnp.where(item_range[None, :] <= item_range[:, None], lengths[0][None, :], 0), axis=1)
    place = position * count + jnp.arange(count, dtype=jnp.int32)
    query_items = jnp.sum((place[:, None] >= ends[None, :]).astype(jnp.int32), axis=1)[:, None]
    mod = modulation[0]
    mod_rows = modulation.reshape(items * 6, 1, width)

    def per_frame(which):
        found = jnp.broadcast_to(mod[0, which][None, :], (count, width))
        for item in range(1, items):
            found = jnp.where(query_items == item, mod[item, which][None, :], found)
        return found

    swap = [(i, i ^ 1) for i in range(shards)]

    def sibling(values):
        return lax.ppermute(values, "seq", swap)

    fast = shards == 8 and lax.axis_size("batch") == 4 and width == 768

    text_proj = jnp.dot(
        text[0].reshape(items * text_rows, text_width), w_ckv, preferred_element_type=jnp.float32
    ).astype(jnp.bfloat16)
    hidden_one = hide(meta, mod_rows, local, items, shards)
    sides = list(hold(hop(hidden_one, hidden_one, shards), text_proj))
    for _ in range(1, reach):
        sides += hop(*sides[-2:], shards)

    def with_siblings(blocks):
        return [each for block in blocks for each in (block, sibling(block))]

    total = 2 * chips * count
    near = with_siblings([hidden_one] + sides[:2])
    hidden_sib = near[1]
    q_window, kv = project(meta, w_qkv, near, range(3), total, (), items, shards, "project_near")
    if reach > 1:
        apart = with_siblings(hold(sides[2:], kv))
        q_window, kv = project(
            meta, w_qkv, apart, range(3, chips), total, (q_window, kv), items, shards, "project_far"
        )
    inputs = local.astype(jnp.float32)
    attn_exact, attended, features = attend(meta, count, q_window, kv, "frames", chips, items, shards, "self_attend")
    branch_one = jnp.dot(attended, w_o, preferred_element_type=jnp.float32)
    after_attn = inputs + per_frame(2) * branch_one
    normed_cross, inverse_cross = layer_norm(after_attn)
    cross_in = normed_cross.astype(jnp.bfloat16)
    cross_queries = jnp.dot(cross_in, w_cq, preferred_element_type=jnp.float32).astype(jnp.bfloat16)
    cross_queries = (cross_queries.astype(jnp.float32) * 0.125).astype(jnp.bfloat16)
    cross_exact, cross_out, cross_features = attend(
        meta, count, cross_queries, text_proj, "text", items, items, shards, "cross_attend"
    )
    branch_two = jnp.dot(cross_out, w_co, preferred_element_type=jnp.float32)
    after_cross = after_attn + branch_two
    normed_two, inverse_two = layer_norm(after_cross)
    hidden_two = (normed_two * (1.0 + per_frame(4)) + per_frame(3)).astype(jnp.bfloat16)
    gate_two = per_frame(5)
    grad_out = cotangent[0].astype(jnp.float32)
    grad_branch_three = (grad_out * gate_two).astype(jnp.bfloat16)
    acts, branch_three, grad_hidden_two = mlp(hidden_two, grad_branch_three, w_up, w_down)
    if fast:
        acts_sib = sibling(acts)
    result = after_cross + gate_two * branch_three
    grad_cross = grad_out + norm_back(grad_hidden_two * (1.0 + per_frame(4)), normed_two, inverse_two)
    grad_branch_two = grad_cross.astype(jnp.bfloat16)
    grad_cross_out = times_transposed(grad_branch_two, w_co).astype(jnp.bfloat16)
    cross_features = with_deltas(cross_features, grad_cross_out, cross_exact)
    grad_cross_queries, text_terms = text_grad(
        meta, cross_queries, grad_cross_out, cross_features, text_proj, items, shards, "cross_grad"
    )
    if fast:
        [grad_cross_queries] = hold((grad_cross_queries,), acts_sib)
    others = (cross_out, grad_branch_two, cross_in, attended)
    grad_attn_res, middle, do_low = attend_back(
        meta, mod_rows, grad_cross_queries, w_cq, w_o, grad_cross, after_attn, attn_exact, features, others, items, shards
    )
    if fast:
        text_sib = sibling(text_terms)
    do_all = lax.all_gather(do_low, "seq", axis=0, tiled=True)
    if fast:
        middle_sib = sibling(middle)
        [acts_sib] = hold((acts_sib,), do_low, middle)
        mlp_parts = pack(pack_mlp_kernel, meta, (acts, acts_sib), (192, 192), items, "pack_mlp")
        [middle] = hold((middle,), *mlp_parts)
        middle_parts = pack(
            pack_middle_kernel,
            meta,
            (middle, middle_sib, text_terms, text_sib, text[0].reshape(items * text_rows, text_width)),
            (144, 128),
            items,
            "pack_middle",
        )
        [do_own] = hold((do_low,), *middle_parts)
    else:
        do_own = do_low
    grad_queries = query_grad(
        meta, count, q_window, do_own, kv, chips, items, shards, "self_query_grad"
    )
    share_rows = text_rows // shards
    [text_terms_late] = hold((text_terms,), grad_queries)
    text_total = lax.psum_scatter(
        text_terms_late.reshape(shards * 2 * items * share_rows, width), "seq", scatter_dimension=0, tiled=True
    ).reshape(2, items * share_rows, width)
    if fast:
        down_part = halve(mlp_parts[1], mlp_parts[0], "batch", Y_BIT, (grad_queries,))
        up_part = halve(mlp_parts[3], mlp_parts[2], "batch", X_BIT, (grad_queries,))
        [do_all] = hold((do_all,), *middle_parts, *down_part, *up_part)
    grad_projected = frame_key_grad(
        meta, q_window, do_all, kv, grad_queries, count, chips, items, shards, "self_key_grad"
    )
    if fast:
        projected_sib = sibling(grad_projected)
    if fast:
        square_send, square_keep, text_send, text_keep = middle_parts
        got = (
            trade(down_part[1], "batch", X_BIT),
            trade(up_part[1], "batch", Y_BIT),
            trade(square_send, "batch", Y_BIT),
            trade(text_send, "batch", X_BIT),
        )
        got = hold(got, grad_projected)
        down_part, up_part = added(down_part[0], got[0]), added(up_part[0], got[1])
        square_part, text_w_part = added(square_keep, got[2]), added(text_keep, got[3])
        first_send, first_keep = joined(down_part, up_part)
        [projected_sib] = hold((projected_sib,), *square_part, *text_w_part, first_send)
        qkv_parts = pack(
            pack_qkv_kernel,
            meta,
            (hidden_one, hidden_sib, grad_projected, projected_sib),
            (96, 48),
            items,
            "pack_qkv",
        )
        [grad_projected] = hold((grad_projected,), *qkv_parts)
    grad_inputs, terms = finish(
        meta, mod_rows, w_qkv, grad_projected, local, grad_attn_res, branch_one, grad_hidden_two, normed_two, cotangent[0],
        branch_three, items, shards, fast,
    )
    if not fast:
        for bit in range(shards.bit_length() - 1):
            terms = terms + trade(terms, "seq", bit)
        own = width // shards
        terms = lax.dynamic_slice_in_dim(terms, position * own, own, 2)
        shares = terms[:, :items].transpose(1, 0, 2)[None]
        grad_mod, grad_mod_mlp = shares[:, :, :3], shares[:, :, 3:]
    if fast:
        terms = (terms + trade(terms, "seq", 0)).astype(jnp.bfloat16)
        plain_send, plain_keep, split_send, split_keep = qkv_parts
        first_part = halve(first_keep, first_send, "seq", 1, (grad_inputs,))
        square_part = halve(*square_part, "batch", X_BIT, first_part)
        text_w_part = halve(*text_w_part, "batch", Y_BIT, first_part)
        half_way = (grad_inputs,)
        plain_part = halve(plain_keep, plain_send, "batch", X_BIT, half_way)
        split_part = halve(split_keep, split_send, "batch", Y_BIT, half_way)
        half_way = (*plain_part, *split_part)
        plain_part = halve(*plain_part, "batch", Y_BIT)
        split_part = halve(*split_part, "batch", X_BIT)
        sent = [jnp.concatenate([plain_part[i], split_part[i], terms[i]], axis=-2) for i in (1, 0)]
        middle_send, middle_keep = joined(square_part, text_w_part)
        middle_part = halve(middle_keep, middle_send, "seq", 1, sent)
        last_part = halve(sent[1], sent[0], "seq", 1)
        place = jnp.stack([lax.axis_index("batch"), position]).astype(jnp.int32) % 2
        grad_qkv, grad_o, grad_cq, grad_ckv, grad_co, grad_mod, grad_mod_mlp = unpack(
            place,
            (last_part[0], trade(last_part[1], "seq", 2)),
            (middle_part[0], trade(middle_part[1], "seq", 2)),
            items,
        )
        grad_mod = grad_mod.reshape(1, items, 3, width // shards)
        grad_mod_mlp = grad_mod_mlp.reshape(1, items, 3, width // shards)
        first_rows = last_half(*first_part, last_part)
        [text_total] = hold((text_total,), *last_part)
        grad_up = jnp.concatenate([first_rows[192:288], first_rows[288:]], axis=1)
        grads = (grad_qkv, grad_o, grad_cq, grad_ckv, grad_co, grad_up, unsplit(first_rows[:192]))
    text_grad_low = jnp.concatenate([text_total[0], text_total[1]], axis=1)
    grad_text = times_transposed(text_grad_low, w_ckv).reshape(1, items, share_rows, text_width)
    if not fast:
        text_mine = lax.dynamic_slice_in_dim(text[0], position * share_rows, share_rows, 1)
        grads = reduced_grads(
            (hidden_one, jnp.concatenate(list(grad_projected), axis=1)),
            (attended, middle[5]),
            (cross_in, grad_cross_queries),
            (text_mine.reshape(items * share_rows, text_width), text_grad_low),
            (cross_out, grad_branch_two),
            (hidden_two, acts[:-1, 1].transpose(1, 0, 2).reshape(count, -1)),
            (acts[:-1, 0].transpose(1, 0, 2).reshape(count, -1), grad_branch_three),
        )
    return (
        result.astype(jnp.bfloat16)[None],
        grad_inputs[None],
        grad_mod,
        grad_mod_mlp,
        grad_text,
        *grads,
    )


def reduced_grads(*pairs):
    def reduce_weight(left, right):
        grad = contract_rows(left, right).astype(jnp.bfloat16)
        part = lax.psum_scatter(grad, "seq", scatter_dimension=0, tiled=True)
        return lax.psum_scatter(part, "batch", scatter_dimension=1, tiled=True).astype(jnp.float32)

    return tuple(reduce_weight(*pair) for pair in pairs)


def solution(mesh):
    in_specs = (
        P("batch", "seq", None),
        P("batch", "seq", None),
        P("batch", None, None, None),
        P("batch", None),
        P("batch", None, None, None),
        P("batch", None),
        P(),
        P(),
        P(),
        P(),
        P(),
        P(),
        P(),
    )
    out_specs = (
        P("batch", "seq", None),
        P("batch", "seq", None),
        P("batch", None, None, "seq"),
        P("batch", None, None, "seq"),
        P("batch", None, "seq", None),
        P("seq", "batch"),
        P("seq", "batch"),
        P("seq", "batch"),
        P("seq", "batch"),
        P("seq", "batch"),
        P("seq", "batch"),
        P("seq", "batch"),
    )
    return jax.shard_map(body, mesh=mesh, in_specs=in_specs, out_specs=out_specs, check_vma=False)
```
